32 devices in a mesh: dp: 8 (over z, x), seq: 4 (over y, core).
Axes of the slice: x: 2, y: 2, z: 4, core: 2. Of those that a mesh axis runs over, the one named last changes fastest.
Arguments:
- x_content: bfloat16 [16, 512, 768], P('dp', 'seq'), may hold values from -6 to 6
- x_query: bfloat16 [16, 512, 768], P('dp', 'seq'), may hold values from -6 to 6
- cot_content: bfloat16 [16, 512, 768], P('dp', 'seq'), may hold values from -6 to 6
- cot_query: bfloat16 [16, 512, 768], P('dp', 'seq'), may hold values from -6 to 6
- w_query: bfloat16 [768, 768], P('dp'), may hold values from -0.21875 to 0.21875
- b_query: bfloat16 [768], P('dp'), may hold values from -1.75 to 1.75
- w_key: bfloat16 [768, 768], P('dp'), may hold values from -0.21875 to 0.21875
- w_value: bfloat16 [768, 768], P('dp'), may hold values from -0.21875 to 0.21875
- b_value: bfloat16 [768], P('dp'), may hold values from -1.75 to 1.75
- w_out: bfloat16 [768, 768], P('dp'), may hold values from -0.875 to 0.875
- b_out: bfloat16 [768], P('dp'), may hold values from -1.75 to 1.75
- gain_attn: bfloat16 [768], P('dp'), may hold values from 0.5 to 1.5
- shift_attn: bfloat16 [768], P('dp'), may hold values from -1.75 to 1.75
- w_up: bfloat16 [768, 3072], P('dp'), may hold values from -0.21875 to 0.21875
- b_up: bfloat16 [3072], P('dp'), may hold values from -1.75 to 1.75
- w_down: bfloat16 [3072, 768], P('dp'), may hold values from -0.109375 to 0.109375
- b_down: bfloat16 [768], P('dp'), may hold values from -1.75 to 1.75
- gain_ffn: bfloat16 [768], P('dp'), may hold values from 0.5 to 1.5
- shift_ffn: bfloat16 [768], P('dp'), may hold values from -1.75 to 1.75
- rel_table: bfloat16 [32, 12], replicated, may hold values from -4 to 4
- lengths: int32 [16], P('dp'), may hold values from 192 to 512, as said below
- positions: int32 [16, 512], P('dp'), may hold values from 0 to 511, as said below
- predicted: int32 [16, 512], P('dp', 'seq'), may hold values 0 or 1
Outputs:
- y_content: float32 [16, 512, 768], P('dp', 'seq')
- y_query: float32 [16, 512, 768], P('dp', 'seq')
- grad_content: float32 [16, 512, 768], P('dp', 'seq')
- grad_query: float32 [16, 512, 768], P('dp', 'seq')
- grad_w_query: float32 [768, 768], P('dp')
- grad_b_query: float32 [768], P('dp')
- grad_w_key: float32 [768, 768], P('dp')
- grad_w_value: float32 [768, 768], P('dp')
- grad_b_value: float32 [768], P('dp')
- grad_w_out: float32 [768, 768], P('dp')
- grad_b_out: float32 [768], P('dp')
- grad_gain_attn: float32 [768], P('dp')
- grad_shift_attn: float32 [768], P('dp')
- grad_w_up: float32 [768, 3072], P('dp')
- grad_b_up: float32 [3072], P('dp')
- grad_w_down: float32 [3072, 768], P('dp')
- grad_b_down: float32 [768], P('dp')
- grad_gain_ffn: float32 [768], P('dp')
- grad_shift_ffn: float32 [768], P('dp')
- grad_rel_table: float32 [32, 12], replicated
The draws below stay inside these ranges and needn't reach their ends.
Inputs may be any that keep to these rules, and one draw needn't show every extreme that they name: `lengths`: one sequence of each aligned group of 2 has exactly 512 tokens. `positions`: in row s the slots below lengths[s] hold a permutation of 0 to lengths[s] - 1; the others hold lengths[s] to 511 in order.
All inputs are finite; a program needn't handle non-finite values. No bound on the sum of `predicted` on one device may be relied on, other than what follows from the above.
Results may differ from the reference program's by a relative error of at most 0.018.
Values may be sent and summed in bfloat16 or wider, within the bound.
A program may use at most 192 MiB of HBM per device.

```python
import jax
import jax.numpy as jnp
from jax import lax

D = 768
H = 12
HD = 64
FF = 3072
NB = 32
L = 512
MINLEN = 64
SEQS = 2
NSEQ = 16


def lengths_of(key):
    key_draw, key_pick = jax.random.split(key)
    spread = jax.random.randint(key_draw, (NSEQ,), 1, 8)
    tail = jnp.minimum(L, MINLEN + (L - MINLEN) * 2 // spread)
    groups = NSEQ // SEQS
    pick = jax.random.randint(key_pick, (groups,), 0, SEQS)
    index = jnp.arange(NSEQ)
    full = index % SEQS == jnp.repeat(pick, SEQS, total_repeat_length=NSEQ)
    return jnp.where(full, L, tail).astype(jnp.int32)


def draw_lengths(key, part):
    return lengths_of(jax.random.fold_in(key, 11))


def draw_positions(key, part):
    lens = lengths_of(jax.random.fold_in(key, 11))
    keys = jax.random.split(jax.random.fold_in(key, 23), NSEQ)
    ranks = jax.vmap(lambda one: jax.random.permutation(one, L))(keys).astype(jnp.int32)
    slot = jnp.arange(L, dtype=jnp.int32)
    score = jnp.where(slot[None, :] < lens[:, None], ranks, L + slot[None, :])
    return jnp.argsort(score, axis=1, stable=True).astype(jnp.int32)


def touch_ends(values, key, smallest, top_value):
    index_at = [jax.random.randint(jax.random.fold_in(key, axis), (), 0, length) for axis, length in enumerate(values.shape)]
    longest = values.shape.index(max(values.shape))
    neighbour = index_at[:longest] + [(index_at[longest] + 1) % values.shape[longest]] + index_at[longest + 1:]
    return values.at[tuple(index_at)].set(smallest).at[tuple(neighbour)].set(top_value)


def level_of(rng, shape, cuts, low, largest):
    def one(position, shards_of):
        draws = jax.random.uniform(jax.random.fold_in(jax.random.fold_in(rng, 6), position), (shards_of,), jnp.float32, low / len(cuts), largest / len(cuts))
        return jnp.repeat(jnp.exp(draws), shape[position] // shards_of).reshape((-1,) + (1,) * (len(shape) - position - 1))

    loudness = one(*cuts[0])
    for cut in cuts[1:]:
        loudness = loudness * one(*cut)
    return loudness


def bell_draw(stream_key, dims, scale, bound, shards=(), kind=jnp.bfloat16):
    array = jax.random.normal(stream_key, dims, jnp.float32) * scale
    if len(shards) > 0:
        array = level_of(stream_key, dims, shards, -0.22, 0.18) * array
    return jnp.clip(array, min=-bound, max=bound).astype(kind)


def setup_inputs(seed: int = 0) -> dict:
    arg_keys = jax.random.split(jax.random.key(seed), 24)
    return {
        "x_content": bell_draw(arg_keys[0], (NSEQ, L, D), 1.0, 6.0, ((0, 8), (1, 4))),
        "x_query": bell_draw(arg_keys[1], (NSEQ, L, D), 1.0, 6.0, ((0, 8), (1, 4))),
        "cot_content": bell_draw(arg_keys[2], (NSEQ, L, D), 1.0, 6.0, ((0, 8), (1, 4))),
        "cot_query": bell_draw(arg_keys[3], (NSEQ, L, D), 1.0, 6.0, ((0, 8), (1, 4))),
        "w_query": bell_draw(arg_keys[4], (D, D), D ** -0.5, 0.21875, ((0, 8),)),
        "b_query": bell_draw(arg_keys[5], (D,), 0.3, 1.75, ((0, 8),)),
        "w_key": bell_draw(arg_keys[6], (D, D), D ** -0.5, 0.21875, ((0, 8),)),
        "w_value": bell_draw(arg_keys[7], (D, D), D ** -0.5, 0.21875, ((0, 8),)),
        "b_value": bell_draw(arg_keys[8], (D,), 0.3, 1.75, ((0, 8),)),
        "w_out": bell_draw(arg_keys[9], (D, D), (D // 16) ** -0.5, 0.875, ((0, 8),)),
        "b_out": bell_draw(arg_keys[10], (D,), 0.3, 1.75, ((0, 8),)),
        "gain_attn": jnp.clip(1.0 + 0.1 * jax.random.normal(arg_keys[11], (D,), jnp.float32), 0.5, 1.5).astype(jnp.bfloat16),
        "shift_attn": bell_draw(arg_keys[12], (D,), 0.3, 1.75, ((0, 8),)),
        "w_up": bell_draw(arg_keys[13], (D, FF), D ** -0.5, 0.21875, ((0, 8),)),
        "b_up": bell_draw(arg_keys[14], (FF,), 0.3, 1.75, ((0, 8),)),
        "w_down": bell_draw(arg_keys[15], (FF, D), FF ** -0.5, 0.109375, ((0, 8),)),
        "b_down": bell_draw(arg_keys[16], (D,), 0.3, 1.75, ((0, 8),)),
        "gain_ffn": jnp.clip(1.0 + 0.1 * jax.random.normal(arg_keys[17], (D,), jnp.float32), 0.5, 1.5).astype(jnp.bfloat16),
        "shift_ffn": bell_draw(arg_keys[18], (D,), 0.3, 1.75, ((0, 8),)),
        "rel_table": bell_draw(arg_keys[19], (NB, H), 0.7, 4.0),
        "lengths": draw_lengths(jax.random.fold_in(arg_keys[23], 71), 0),
        "positions": draw_positions(jax.random.fold_in(arg_keys[23], 71), 0),
        "predicted": touch_ends((jax.random.randint(arg_keys[22], (NSEQ, L), 0, 20) < 3).astype(jnp.int32), jax.random.fold_in(arg_keys[22], 1), 0, 1),
    }


@jax.custom_vjp
def low(v):
    return lax.optimization_barrier(v.astype(jnp.bfloat16)).astype(jnp.float32)

@jax.custom_vjp
def low_back(v):
    return v

def low_keep(v):
    return (low(v), None)

def low_pass(kept, grad):
    return (grad,)

def back_keep(v):
    return (v, None)

def back_low(kept, grad):
    return (low(grad),)
low.defvjp(low_keep, low_pass)
low_back.defvjp(back_keep, back_low)
bucket_marks = (12, 16, 23, 32, 46, 64, 91)

def bucket_ids(pos_rows, pos_cols):
    delta = pos_cols[..., None, :] - pos_rows[..., :, None]
    dist = jnp.abs(delta)
    far = jnp.full(dist.shape, 8, jnp.int32)
    for mark in bucket_marks:
        far = far + (dist >= mark).astype(jnp.int32)
    near = jnp.where(dist < 8, dist, far)
    return (near + 16 * (delta > 0).astype(jnp.int32)).astype(jnp.int32)

def norm_apply(value, gain, shift):
    center = value - lax.optimization_barrier(jnp.mean(value, axis=-1, keepdims=True))
    var = lax.optimization_barrier(jnp.mean(center * center, axis=-1, keepdims=True))
    return center * lax.rsqrt(var + 1e-05) * gain + shift

def matmul(left, right):
    return jnp.dot(left, right, precision=lax.Precision.HIGHEST)

def group_forward(weights, xc, xq, lens, pos, pred):
    wq, bq, wk, wv, bv, wo, bo, g1, b1, w1, c1, w2, c2, g2, b2, table = weights
    group = xc.shape[0]
    slot = jnp.arange(L)
    valid = slot[None, :] < lens[:, None]
    causal_c = slot[None, :] <= slot[:, None]
    causal_q = slot[None, :] < jnp.maximum(slot[:, None], 1)
    allowed = jnp.stack([valid[:, None, :] & causal_c[None], valid[:, None, :] & causal_q[None]])
    onehot = (bucket_ids(pos, pos)[..., None] == jnp.arange(NB)).astype(jnp.float32)
    bias = jnp.einsum('gqkn,nh->ghqk', onehot, table, precision=lax.Precision.HIGHEST)
    xs = jnp.stack([xc, xq])
    query = low(low_back(matmul(xs, wq)) + bq).reshape(2, group, L, H, HD)
    key = low(low_back(matmul(xc, wk))).reshape(group, L, H, HD)
    value = low(low_back(matmul(xc, wv)) + bv).reshape(group, L, H, HD)
    raw = jnp.einsum('tgqhe,gkhe->tghqk', query, key, precision=lax.Precision.HIGHEST)
    scores = low_back(raw) * HD ** (-0.5) + bias[None]
    scores = jnp.where(allowed[:, :, None], scores, -1e+30)
    probs = jax.nn.softmax(scores, axis=-1)
    mixed = jnp.einsum('tghqk,gkhe->tgqhe', low(probs), value, precision=lax.Precision.HIGHEST)
    attended = low(low_back(mixed.reshape(2, group, L, D)))
    out = low_back(matmul(attended, wo)) + bo
    hidden = norm_apply(xs + out, g1, b1)
    upper = low_back(matmul(low(hidden), w1)) + c1
    active = low(jax.nn.gelu(upper, approximate=False))
    feed = low_back(matmul(active, w2)) + c2
    result = norm_apply(hidden + feed, g2, b2)
    keep = jnp.stack([valid, valid & (pred > 0)])[..., None].astype(jnp.float32)
    return result * keep

def reference(x_content, x_query, cot_content, cot_query, w_query, b_query, w_key, w_value, b_value, w_out, b_out, gain_attn, shift_attn, w_up, b_up, w_down, b_down, gain_ffn, shift_ffn, rel_table, lengths, positions, predicted):
    weights = tuple((w.astype(jnp.float32) for w in (w_query, b_query, w_key, w_value, b_value, w_out, b_out, gain_attn, shift_attn, w_up, b_up, w_down, b_down, gain_ffn, shift_ffn, rel_table)))
    groups = NSEQ // SEQS
    xc = x_content.astype(jnp.float32).reshape(groups, SEQS, L, D)
    xq = x_query.astype(jnp.float32).reshape(groups, SEQS, L, D)
    lens = lengths.reshape(groups, SEQS)
    pos = positions.reshape(groups, SEQS, L)
    pred = predicted.reshape(groups, SEQS, L)

    def forward(weights, xc, xq):

        def one(item):
            return jax.checkpoint(group_forward)(weights, *item)
        return lax.map(one, (xc, xq, lens, pos, pred))
    outputs, pull = jax.vjp(forward, weights, xc, xq)
    cot = jnp.stack([cot_content.astype(jnp.float32).reshape(groups, SEQS, L, D), cot_query.astype(jnp.float32).reshape(groups, SEQS, L, D)], axis=1)
    grads, grad_c, grad_q = pull(cot)
    y_content = outputs[:, 0].reshape(NSEQ, L, D)
    y_query = outputs[:, 1].reshape(NSEQ, L, D)
    return (y_content, y_query, grad_c.reshape(NSEQ, L, D), grad_q.reshape(NSEQ, L, D), grads[0], grads[1], grads[2], grads[3], grads[4], grads[5], grads[6], grads[7], grads[8], grads[9], grads[10], grads[11], grads[12], grads[13], grads[14], grads[15])
```

```python
import functools

import jax
import jax.numpy as jnp
from jax import lax
from jax.experimental import pallas as pl
from jax.experimental.pallas import tpu as pltpu
from jax.sharding import PartitionSpec as P

H = 12
HD = 64
NB = 32

bucket_marks = (12, 16, 23, 32, 46, 64, 91)


def bucket_ids(pos_rows, pos_cols):
    delta = pos_cols[..., None, :] - pos_rows[..., :, None]
    dist = jnp.abs(delta)
    far = jnp.full(dist.shape, 8, jnp.int32)
    for mark in bucket_marks:
        far = far + (dist >= mark).astype(jnp.int32)
    near = jnp.where(dist < 8, dist, far)
    return near + 16 * (delta > 0).astype(jnp.int32)


def norm_apply(value, gain, shift):
    center = value - jnp.mean(value, axis=-1, keepdims=True)
    var = jnp.mean(center * center, axis=-1, keepdims=True)
    return center * lax.rsqrt(var + 1e-05) * gain + shift


MESH = pl.DeviceIdType.MESH
UNITS = 12
SKEW = 128


def place(mesh_sizes):
    dp, sq = lax.axis_index("dp"), lax.axis_index("seq")
    row, side = dp // 2, dp % 2
    deck, core = sq // 2, sq % 2
    return dp, sq, row, side, deck, core


def tile_of(unit, shard, shards):
    down = unit // 8
    return (1 - down) * (unit * shards + shard) + down * (8 * shards + shard * 4 + unit - 8)


def gather_kernel(
    shards, seqn,
    wq, wk, wv, wo, wu, wd, xc, vec,
    full, xall, vall,
    own, xown, load_sem, keep_sem, zup_sem, zdn_sem, xs_sem, ys_sem, cp_sem, cy_sem,
    zr_sem, xr_sem, yr_sem, cpr_sem, cyr_sem, xc_send, xc_recv, vec_send, vec_recv,
):
    dp, sq, row, side, deck, core = place(None)
    rows = shards // 2
    up = ((row + 1) * 2 + side, sq)
    down = ((row - 1) * 2 + side, sq)
    across = (row * 2 + 1 - side, sq)
    other_deck = (dp, (1 - deck) * 2 + core)
    sibling = (dp, deck * 2 + 1 - core)

    barrier = pltpu.get_barrier_semaphore()

    def greet(step, carry):
        pl.semaphore_signal(barrier, inc=1, device_id=(lax.rem(dp + step, shards), sq), device_id_type=MESH)
        return carry

    lax.fori_loop(1, shards, greet, 0)
    pl.semaphore_signal(barrier, inc=1, device_id=other_deck, device_id_type=MESH)
    pl.semaphore_signal(barrier, inc=1, device_id=sibling, device_id_type=MESH)

    pieces = [wq, wk, wv, wo] + [wu.at[:, pl.ds(j * 768, 768)] for j in range(4)] + [wd.at[j] for j in range(4)]
    loads = [pltpu.make_async_copy(piece, own.at[u], load_sem.at[u]) for u, piece in enumerate(pieces)]
    for load in loads:
        load.start()
    xload = pltpu.make_async_copy(xc, xown, load_sem.at[UNITS])
    xload.start()
    pl.semaphore_wait(barrier, shards + 1)

    plane = pl.ds(pl.multiple_of(core * 384 + deck * SKEW, 128), 256)
    solo = pl.ds(pl.multiple_of(core * 384 + deck * 256, 128), 128)

    def remote(src, dst, send, recv, device):
        return pltpu.make_async_remote_copy(
            src_ref=src, dst_ref=dst, send_sem=send, recv_sem=recv, device_id=device, device_id_type=MESH
        )

    def part(unit, shard, columns):
        return full.at[tile_of(unit, shard, shards), :, columns]

    def vec_copy(step):
        return remote(vec, vall.at[dp], vec_send, vec_recv, (lax.rem(dp + step, shards), sq))

    def send_vec(step, carry):
        vec_copy(step).start()
        return carry

    lax.fori_loop(1, shards, send_vec, 0)
    keep_vec = pltpu.make_async_copy(vec, vall.at[dp], keep_sem.at[UNITS + 1])
    keep_vec.start()

    for load in loads:
        load.wait()

    def keep_copy(u):
        return pltpu.make_async_copy(own.at[u], full.at[tile_of(u, dp, shards)], keep_sem.at[u])

    def first(u, carry):
        src = own.at[u, :, plane]
        dst = part(u, dp, plane)
        recv = zr_sem.at[u, row]

        @pl.when(row < rows - 1)
        def _():
            remote(src, dst, zup_sem.at[row], recv, up).start()

        @pl.when(row > 0)
        def _():
            remote(src, dst, zdn_sem.at[row], recv, down).start()

        remote(src, dst, xs_sem, xr_sem.at[u], across).start()
        keep_copy(u).start()
        return carry

    lax.fori_loop(0, UNITS, first, 0)

    xload.wait()
    keep_x = pltpu.make_async_copy(xown, xall.at[sq], keep_sem.at[UNITS])
    keep_x.start()
    x_deck = remote(xown, xall.at[sq], xc_send.at[0], xc_recv.at[0], other_deck)
    x_deck.start()
    x_core = remote(xown, xall.at[sq], xc_send.at[1], xc_recv.at[1], sibling)
    x_core.start()

    def to_deck(u, shard):
        ref = part(u, shard, solo)
        remote(ref, ref, ys_sem, yr_sem.at[u], other_deck).start()

    def to_core(u, shard):
        ref = part(u, shard, plane)
        remote(ref, ref, cp_sem, cpr_sem.at[u], sibling).start()

    def step(n, carry):
        def hop(t, inner):
            u = n - (t - 1)

            @pl.when((u >= 0) & (u < UNITS))
            def _():
                @pl.when(row - t >= 0)
                def _():
                    s = row - t
                    ref = part(u, s * 2 + side, plane)
                    remote(ref, ref, zup_sem.at[s], zr_sem.at[u, s], up).wait_recv()

                    @pl.when(row < rows - 1)
                    def _():
                        remote(ref, ref, zup_sem.at[s], zr_sem.at[u, s], up).start()

                    remote(ref, ref, xs_sem, xr_sem.at[u], across).start()
                    to_deck(u, s * 2 + side)
                    to_core(u, s * 2 + side)

                @pl.when(row + t < rows)
                def _():
                    s = row + t
                    ref = part(u, s * 2 + side, plane)
                    remote(ref, ref, zdn_sem.at[s], zr_sem.at[u, s], down).wait_recv()

                    @pl.when(row > 0)
                    def _():
                        remote(ref, ref, zdn_sem.at[s], zr_sem.at[u, s], down).start()

                    remote(ref, ref, xs_sem, xr_sem.at[u], across).start()
                    to_deck(u, s * 2 + side)
                    to_core(u, s * 2 + side)

            return inner

        lax.fori_loop(1, rows, hop, 0)

        ux = n - (rows - 1)

        @pl.when((ux >= 0) & (ux < UNITS))
        def _():
            whole = full.at[pl.ds(0, rows), :, pl.ds(0, 256)]
            remote(whole, whole, xs_sem, xr_sem.at[ux], across).wait_recv()

            def pass_on(s, inner):
                to_deck(ux, s * 2 + 1 - side)
                to_core(ux, s * 2 + 1 - side)
                return inner

            lax.fori_loop(0, rows, pass_on, 0)

        uy = n - rows

        @pl.when((uy >= 0) & (uy < UNITS))
        def _():
            whole = full.at[pl.ds(0, shards - 1), :, pl.ds(0, 128)]
            remote(whole, whole, ys_sem, yr_sem.at[uy], other_deck).wait_recv()
            theirs = pl.ds(pl.multiple_of(core * 384 + (1 - deck) * 256, 128), 128)

            def pass_on(k, inner):
                ref = part(uy, lax.rem(dp + k, shards), theirs)
                remote(ref, ref, cy_sem, cyr_sem.at[uy], sibling).start()
                return inner

            lax.fori_loop(1, shards, pass_on, 0)

        return carry

    lax.fori_loop(0, UNITS + rows, step, 0)

    x_theirs = xall.at[(1 - deck) * 2 + core]
    x_deck.wait_recv()
    x_forward = remote(x_theirs, x_theirs, xc_send.at[2], xc_recv.at[2], sibling)
    x_forward.start()

    def finish(u, carry):
        planes = full.at[pl.ds(0, shards - 1), :, pl.ds(0, 256)]
        solos = full.at[pl.ds(0, shards - 1), :, pl.ds(0, 128)]
        remote(planes, planes, cp_sem, cpr_sem.at[u], sibling).wait_recv()
        remote(solos, solos, cy_sem, cyr_sem.at[u], sibling).wait_recv()
        keep_copy(u).wait()
        return carry

    lax.fori_loop(0, UNITS, finish, 0)
    x_deck.wait_send()
    x_core.wait()
    x_forward.wait()
    keep_x.wait()
    keep_vec.wait()
    rest = vall.at[pl.ds(0, shards - 1)]
    remote(rest, rest, vec_send, vec_recv, sibling).wait()

    def sent(s, carry):
        ref = full.at[pl.ds(0, UNITS), :, pl.ds(0, 256)]

        @pl.when((s <= row) & (row < rows - 1))
        def _():
            remote(ref, ref, zup_sem.at[s], zr_sem.at[0, 0], sibling).wait_send()

        @pl.when((s >= row) & (row > 0))
        def _():
            remote(ref, ref, zdn_sem.at[s], zr_sem.at[0, 0], sibling).wait_send()

        return carry

    lax.fori_loop(0, rows, sent, 0)
    ref = full.at[pl.ds(0, UNITS * rows), :, pl.ds(0, 256)]
    remote(ref, ref, xs_sem, xr_sem.at[0], sibling).wait_send()
    ref = full.at[pl.ds(0, UNITS * (shards - 1)), :, pl.ds(0, 128)]
    remote(ref, ref, ys_sem, yr_sem.at[0], sibling).wait_send()
    remote(ref, ref, cy_sem, cyr_sem.at[0], sibling).wait_send()
    ref = full.at[pl.ds(0, UNITS * (shards - 1)), :, pl.ds(0, 256)]
    remote(ref, ref, cp_sem, cpr_sem.at[0], sibling).wait_send()


def gather(wq, wk, wv, wo, wu, wd, xc, vec, shards, seqn):
    rows_of = wq.shape[0]
    width = wq.shape[1]
    bf16 = jnp.bfloat16
    anywhere = pl.BlockSpec(memory_space=pl.ANY)
    dma = pltpu.SemaphoreType.DMA
    rows = shards // 2
    return pl.pallas_call(
        functools.partial(gather_kernel, shards, seqn),
        out_shape=(
            jax.ShapeDtypeStruct((UNITS * shards, rows_of, width), bf16),
            jax.ShapeDtypeStruct((seqn,) + xc.shape, bf16),
            jax.ShapeDtypeStruct((shards,) + vec.shape, jnp.float32),
        ),
        in_specs=[anywhere] * 7 + [pl.BlockSpec(memory_space=pltpu.VMEM)],
        out_specs=(anywhere, anywhere, anywhere),
        scratch_shapes=[
            pltpu.VMEM((UNITS, rows_of, width), bf16),
            pltpu.VMEM(xc.shape, bf16),
            dma((UNITS + 1,)),
            dma((UNITS + 2,)),
            dma((rows,)),
            dma((rows,)),
            dma(()),
            dma(()),
            dma(()),
            dma(()),
            dma((UNITS, rows)),
            dma((UNITS,)),
            dma((UNITS,)),
            dma((UNITS,)),
            dma((UNITS,)),
            dma((3,)),
            dma((3,)),
            dma(()),
            dma(()),
        ],
        compiler_params=pltpu.CompilerParams(collective_id=0, has_side_effects=True),
        name="gather_weights",
    )(wq, wk, wv, wo, wu, wd.reshape(4, rows_of, width), xc, vec)


def reduce_kernel(
    shards, seqn,
    grads, dxs, small,
    out, dx_out, small_out,
    acc, got_core, got_deck, got_across, line, from_below, from_above, got_plane, half, got_half,
    dx_own, dx_core, dx_deck, got_small, mid_small, got_mid,
    load_sem, core_send, core_recv, deck_send, deck_recv, across_send, across_recv,
    up_send, up_recv, down_send, down_recv, plane_send, plane_recv, half_send, half_recv,
    dx_load, dx_send, dx_recv, small_send, small_recv, mid_send, mid_recv,
):
    dp, sq, row, side, deck, core = place(None)
    rows = shards // 2
    f32, bf16 = jnp.float32, jnp.bfloat16
    up = ((row + 1) * 2 + side, sq)
    down = ((row - 1) * 2 + side, sq)
    across = (row * 2 + 1 - side, sq)
    other_deck = (dp, (1 - deck) * 2 + core)
    sibling = (dp, deck * 2 + 1 - core)

    barrier = pltpu.get_barrier_semaphore()

    def greet(step, carry):
        pl.semaphore_signal(barrier, inc=1, device_id=(lax.rem(dp + step, shards), sq), device_id_type=MESH)
        return carry

    def greet_seq(step, carry):
        pl.semaphore_signal(barrier, inc=1, device_id=(dp, lax.rem(sq + step, seqn)), device_id_type=MESH)
        return carry

    lax.fori_loop(1, shards, greet, 0)
    lax.fori_loop(1, seqn, greet_seq, 0)

    mine = pl.ds(pl.multiple_of(core * 384, 128), 384)
    siblings = pl.ds(pl.multiple_of((1 - core) * 384, 128), 384)
    plane = pl.ds(pl.multiple_of(deck * 128, 128), 256)
    solo = pl.ds(pl.multiple_of(deck * 256, 128), 128)
    other_solo = pl.ds(pl.multiple_of((1 - deck) * 256, 128), 128)

    def remote(src, dst, send, recv, device):
        return pltpu.make_async_remote_copy(
            src_ref=src, dst_ref=dst, send_sem=send, recv_sem=recv, device_id=device, device_id_type=MESH
        )

    def load_all(u, carry):
        def one(s, inner):
            for b in range(2):
                tile = tile_of(u, s * 2 + b, shards)
                pltpu.make_async_copy(grads.at[tile, :, mine], acc.at[u, s, b], load_sem.at[u]).start()
            return inner

        return lax.fori_loop(0, rows, one, carry)

    lax.fori_loop(0, UNITS, load_all, 0)
    for k in range(2):
        pltpu.make_async_copy(dxs.at[k * 2 + core], dx_own.at[k], dx_load.at[k]).start()
    got_small[dp] = small[dp]
    pl.semaphore_wait(barrier, shards + seqn - 2)

    def send_core(u, carry):
        def one(s, inner):
            for b in range(2):
                tile = tile_of(u, s * 2 + b, shards)
                remote(grads.at[tile, :, siblings], got_core.at[u, s, b], core_send, core_recv.at[u], sibling).start()
            return inner

        return lax.fori_loop(0, rows, one, carry)

    lax.fori_loop(0, UNITS, send_core, 0)
    for k in range(2):
        remote(dxs.at[k * 2 + 1 - core], dx_core.at[k], dx_send.at[k], dx_recv.at[k], sibling).start()

    def send_small(step, carry):
        to = lax.rem(dp + step, shards)
        remote(small.at[to], got_small.at[dp], small_send, small_recv, (to, sq)).start()
        return carry

    lax.fori_loop(1, shards, send_small, 0)

    def total(left, right):
        return (left.astype(f32) + right.astype(f32)).astype(bf16)

    def step(n, carry):
        @pl.when(n < UNITS)
        def _():
            u = n
            pltpu.make_async_copy(acc.at[u], acc.at[u], load_sem.at[u]).wait()
            remote(got_core.at[u], got_core.at[u], core_send, core_recv.at[u], sibling).wait_recv()

            def add(s, inner):
                for b in range(2):
                    acc[u, s, b] = total(acc[u, s, b], got_core[u, s, b])
                return inner

            lax.fori_loop(0, rows, add, 0)
            remote(acc.at[u, :, :, :, other_solo], got_deck.at[u], deck_send.at[u], deck_recv.at[u], other_deck).start()

        u2 = n - 1

        @pl.when((u2 >= 0) & (u2 < UNITS))
        def _():
            u = u2
            remote(got_deck.at[u], got_deck.at[u], deck_send.at[u], deck_recv.at[u], other_deck).wait_recv()

            def add(s, inner):
                for b in range(2):
                    acc[u, s, b, :, solo] = total(acc[u, s, b, :, solo], got_deck[u, s, b])
                return inner

            lax.fori_loop(0, rows, add, 0)
            remote(
                acc.at[u, :, 1 - side, :, plane], got_across.at[u], across_send.at[u], across_recv.at[u], across
            ).start()

        u3 = n - 2

        @pl.when((u3 >= 0) & (u3 < UNITS))
        def _():
            u = u3
            remote(got_across.at[u], got_across.at[u], across_send.at[u], across_recv.at[u], across).wait_recv()

            def add(s, inner):
                line[u, s] = total(acc[u, s, side, :, plane], got_across[u, s])
                return inner

            lax.fori_loop(0, rows, add, 0)

        u_up = n - 3 - row

        @pl.when((u_up >= 0) & (u_up < UNITS))
        def _():
            u = u_up

            def one(s, inner):
                @pl.when(row > 0)
                def _():
                    remote(line.at[u, s], from_below.at[u, s], up_send.at[u, s], up_recv.at[u, s], up).wait_recv()
                    line[u, s] = total(line[u, s], from_below[u, s])

                @pl.when(s > row)
                def _():
                    remote(line.at[u, s], from_below.at[u, s], up_send.at[u, s], up_recv.at[u, s], up).start()

                return inner

            lax.fori_loop(row, rows, one, 0)

        u_down = n - 3 - (rows - 1 - row)

        @pl.when((u_down >= 0) & (u_down < UNITS))
        def _():
            u = u_down

            def one(s, inner):
                @pl.when(row < rows - 1)
                def _():
                    remote(line.at[u, s], from_above.at[u, s], down_send.at[u, s], down_recv.at[u, s], down).wait_recv()
                    line[u, s] = total(line[u, s], from_above[u, s])

                @pl.when(s < row)
                def _():
                    remote(line.at[u, s], from_above.at[u, s], down_send.at[u, s], down_recv.at[u, s], down).start()

                return inner

            lax.fori_loop(0, row + 1, one, 0)

        u_f = n - 3 - rows

        @pl.when((u_f >= 0) & (u_f < UNITS))
        def _():
            u = u_f
            remote(line.at[u, row], got_plane.at[u], plane_send.at[u], plane_recv.at[u], other_deck).start()

        u_h = n - 4 - rows

        @pl.when((u_h >= 0) & (u_h < UNITS))
        def _():
            u = u_h
            remote(line.at[u, row], got_plane.at[u], plane_send.at[u], plane_recv.at[u], other_deck).wait_recv()
            half[u, :, plane] = line[u, row]
            half[u, :, other_solo] = got_plane[u, :, pl.ds(pl.multiple_of((1 - deck) * 128, 128), 128)]
            half[u, :, pl.ds(128, 128)] = total(
                half[u, :, pl.ds(128, 128)], got_plane[u, :, pl.ds(pl.multiple_of(deck * 128, 128), 128)]
            )
            remote(half.at[u], got_half.at[u], half_send.at[u], half_recv.at[u], sibling).start()

        u_o = n - 5 - rows

        @pl.when((u_o >= 0) & (u_o < UNITS))
        def _():
            u = u_o
            remote(half.at[u], got_half.at[u], half_send.at[u], half_recv.at[u], sibling).wait_recv()
            out[u, :, mine] = half[u].astype(f32)
            out[u, :, siblings] = got_half[u].astype(f32)

        return carry

    lax.fori_loop(0, 3, step, 0)
    for k in range(2):
        pltpu.make_async_copy(dx_own.at[k], dx_own.at[k], dx_load.at[k]).wait()
        remote(dx_core.at[k], dx_core.at[k], dx_send.at[k], dx_recv.at[k], sibling).wait()
        dx_own[k] = total(dx_own[k], dx_core[k])
    deck_dx = remote(dx_own.at[1 - deck], dx_deck, dx_send.at[2], dx_recv.at[2], other_deck)
    deck_dx.start()
    rest = got_small.at[pl.ds(0, shards - 1)]
    remote(rest, rest, small_send, small_recv, sibling).wait()
    summed = got_small[0]
    for i in range(1, shards):
        summed = summed + got_small[i]
    mid_small[...] = summed
    got_mid[sq] = summed

    def send_mid(step, carry):
        remote(mid_small, got_mid.at[sq], mid_send, mid_recv, (dp, lax.rem(sq + step, seqn))).start()
        return carry

    lax.fori_loop(1, seqn, send_mid, 0)
    lax.fori_loop(3, UNITS + 6 + rows, step, 0)

    rest = got_mid.at[pl.ds(0, seqn - 1)]
    remote(rest, rest, mid_send, mid_recv, sibling).wait()
    summed = got_mid[0]
    for i in range(1, seqn):
        summed = summed + got_mid[i]
    small_out[...] = summed
    deck_dx.wait()
    dx_out[...] = dx_own[deck].astype(f32) + dx_deck[...].astype(f32)

    ref = got_core
    remote(ref, ref, core_send, core_recv.at[0], sibling).wait_send()

    def sent(u, carry):
        remote(got_deck.at[u], got_deck.at[u], deck_send.at[u], deck_recv.at[u], other_deck).wait_send()
        remote(got_across.at[u], got_across.at[u], across_send.at[u], across_recv.at[u], across).wait_send()
        remote(got_plane.at[u], got_plane.at[u], plane_send.at[u], plane_recv.at[u], other_deck).wait_send()
        remote(half.at[u], half.at[u], half_send.at[u], half_recv.at[u], sibling).wait_send()

        def one(s, inner):
            @pl.when(s > row)
            def _():
                remote(line.at[u, s], from_below.at[u, s], up_send.at[u, s], up_recv.at[u, s], up).wait_send()

            @pl.when(s < row)
            def _():
                remote(line.at[u, s], from_above.at[u, s], down_send.at[u, s], down_recv.at[u, s], down).wait_send()

            return inner

        return lax.fori_loop(0, rows, one, carry)

    lax.fori_loop(0, UNITS, sent, 0)


def reduce_grads(grads, dxs, small, shards, seqn):
    rows_of, width = grads.shape[1:]
    f32, bf16 = jnp.float32, jnp.bfloat16
    anywhere = pl.BlockSpec(memory_space=pl.ANY)
    vmem = pl.BlockSpec(memory_space=pltpu.VMEM)
    dma = pltpu.SemaphoreType.DMA
    rows = shards // 2
    own = dxs.shape[1:]
    return pl.pallas_call(
        functools.partial(reduce_kernel, shards, seqn),
        out_shape=(
            jax.ShapeDtypeStruct((UNITS, rows_of, width), f32),
            jax.ShapeDtypeStruct(own, f32),
            jax.ShapeDtypeStruct(small.shape[1:], f32),
        ),
        in_specs=[anywhere, anywhere, vmem],
        out_specs=(vmem, vmem, vmem),
        scratch_shapes=[
            pltpu.VMEM((UNITS, rows, 2, rows_of, 384), bf16),
            pltpu.VMEM((UNITS, rows, 2, rows_of, 384), bf16),
            pltpu.VMEM((UNITS, rows, 2, rows_of, 128), bf16),
            pltpu.VMEM((UNITS, rows, rows_of, 256), bf16),
            pltpu.VMEM((UNITS, rows, rows_of, 256), bf16),
            pltpu.VMEM((UNITS, rows, rows_of, 256), bf16),
            pltpu.VMEM((UNITS, rows, rows_of, 256), bf16),
            pltpu.VMEM((UNITS, rows_of, 256), bf16),
            pltpu.VMEM((UNITS, rows_of, 384), bf16),
            pltpu.VMEM((UNITS, rows_of, 384), bf16),
            pltpu.VMEM((2,) + own, bf16),
            pltpu.VMEM((2,) + own, bf16),
            pltpu.VMEM(own, bf16),
            pltpu.VMEM(small.shape, f32),
            pltpu.VMEM(small.shape[1:], f32),
            pltpu.VMEM((seqn,) + small.shape[1:], f32),
            dma((UNITS,)),
            dma(()),
            dma((UNITS,)),
            dma((UNITS,)),
            dma((UNITS,)),
            dma((UNITS,)),
            dma((UNITS,)),
            dma((UNITS, rows)),
            dma((UNITS, rows)),
            dma((UNITS, rows)),
            dma((UNITS, rows)),
            dma((UNITS,)),
            dma((UNITS,)),
            dma((UNITS,)),
            dma((UNITS,)),
            dma((2,)),
            dma((3,)),
            dma((3,)),
            dma(()),
            dma(()),
            dma(()),
            dma(()),
        ],
        compiler_params=pltpu.CompilerParams(
            collective_id=1, has_side_effects=True, vmem_limit_bytes=60 * 1024 * 1024
        ),
        name="reduce_grads",
    )(grads, dxs, small)

def per_device(
    x_content, x_query, cot_content, cot_query,
    w_query, b_query, w_key, w_value, b_value, w_out, b_out, gain_attn, shift_attn,
    w_up, b_up, w_down, b_down, gain_ffn, shift_ffn, rel_table, lengths, positions, predicted,
    *, shards, seqn,
):
    f32 = jnp.float32
    bf16 = jnp.bfloat16
    scale = HD ** (-0.5)
    seqs, block, width = x_content.shape
    span = positions.shape[1]
    r = w_query.shape[0]
    vec = jnp.concatenate(
        [b_query, b_value, b_out, gain_attn, shift_attn, b_down, gain_ffn, shift_ffn, b_up]
    ).astype(f32)[None]
    full, xall, vall = gather(w_query, w_key, w_value, w_out, w_up, w_down, x_content, vec, shards, seqn)
    weights = full.reshape(UNITS, width, width)
    wq, wk, wv, wo = (weights[i] for i in range(4))
    w1, w2 = weights[4:8], weights[8:12]
    bq, bv, bo, g1, b1, c2, g2, b2 = (vall[:, 0, i * r : (i + 1) * r].reshape(width) for i in range(8))
    c1 = vall[:, 0, 8 * r :].reshape(4, width)
    x_every = jnp.transpose(xall, (1, 0, 2, 3)).reshape(seqs, span, width)

    base = lax.axis_index("seq") * block
    slot_q = base + jnp.arange(block)
    slot_k = jnp.arange(span)
    valid_k = slot_k[None, :] < lengths[:, None]
    valid_q = slot_q[None, :] < lengths[:, None]
    allow_c = valid_k[:, None, :] & (slot_k[None, :] <= slot_q[:, None])[None]
    allow_q = valid_k[:, None, :] & (slot_k[None, :] < jnp.maximum(slot_q[:, None], 1))[None]
    allowed = jnp.stack([allow_c, allow_q])
    pos_q = lax.dynamic_slice_in_dim(positions, base, block, 1)
    onehot = (bucket_ids(pos_q, positions)[..., None] == jnp.arange(NB)).astype(f32)
    table = rel_table.astype(f32)
    bias = jnp.einsum("sqkn,nh->shqk", onehot, table, precision=lax.Precision.HIGHEST)
    xs = jnp.stack([x_content, x_query])
    keys = jnp.einsum("sqd,de->sqe", x_every, wk, preferred_element_type=f32).astype(bf16)
    values = (jnp.einsum("sqd,de->sqe", x_every, wv, preferred_element_type=f32) + bv).astype(bf16)
    query = (jnp.einsum("tsqd,de->tsqe", xs, wq, preferred_element_type=f32) + bq).astype(bf16)
    query4 = query.reshape(2, seqs, block, H, HD)
    keys4 = keys.reshape(seqs, span, H, HD)
    values4 = values.reshape(seqs, span, H, HD)

    raw = jnp.einsum("tsqhe,skhe->tshqk", query4, keys4, preferred_element_type=f32)
    scores = jnp.where(allowed[:, :, None], raw * scale + bias[None], -1e30)
    top = jnp.max(scores, axis=-1, keepdims=True)
    expo = jnp.exp(scores - top)
    probs = expo / jnp.sum(expo, axis=-1, keepdims=True)
    mixed = jnp.einsum("tshqk,skhe->tsqhe", probs.astype(bf16), values4, preferred_element_type=f32)
    attended = mixed.reshape(2, seqs, block, width).astype(bf16)
    out = jnp.einsum("tsqd,de->tsqe", attended, wo, preferred_element_type=f32) + bo
    resid_one = xs.astype(f32) + out
    hidden, pull_one = jax.vjp(norm_apply, resid_one, g1, b1)
    hidden_low = hidden.astype(bf16)
    upper = jnp.einsum("tsqd,jdf->tsqjf", hidden_low, w1, preferred_element_type=f32) + c1
    active_full, pull_gelu = jax.vjp(lambda value: jax.nn.gelu(value, approximate=False), upper)
    active = active_full.astype(bf16)
    feed = jnp.einsum("tsqjf,jfd->tsqd", active, w2, preferred_element_type=f32) + c2
    result, pull_two = jax.vjp(norm_apply, hidden + feed, g2, b2)
    keep = jnp.stack([valid_q, valid_q & (predicted > 0)])[..., None].astype(f32)
    outputs = result * keep
    cotangent = jnp.stack([cot_content, cot_query]).astype(f32) * keep
    d_resid_two, d_g2, d_b2 = pull_two(cotangent)
    d_c2 = jnp.sum(d_resid_two, axis=(0, 1, 2))
    d_feed_low = d_resid_two.astype(bf16)
    d_w2 = jnp.einsum("tsqjf,tsqd->jfd", active, d_feed_low, preferred_element_type=f32)
    d_active = jnp.einsum("tsqd,jfd->tsqjf", d_feed_low, w2, preferred_element_type=f32)
    (d_upper,) = pull_gelu(d_active)
    d_c1 = jnp.sum(d_upper, axis=(0, 1, 2)).reshape(4 * width)
    d_upper_low = d_upper.astype(bf16)
    d_w1 = jnp.einsum("tsqd,tsqjf->jdf", hidden_low, d_upper_low, preferred_element_type=f32)
    d_hidden = d_resid_two + jnp.einsum("tsqjf,jdf->tsqd", d_upper_low, w1, preferred_element_type=f32)
    d_resid_one, d_g1, d_b1 = pull_one(d_hidden)
    d_bo = jnp.sum(d_resid_one, axis=(0, 1, 2))
    d_out_low = d_resid_one.astype(bf16)
    d_wo = jnp.einsum("tsqd,tsqe->de", attended, d_out_low, preferred_element_type=f32)
    d_attended = jnp.einsum("tsqe,de->tsqd", d_out_low, wo, preferred_element_type=f32).astype(bf16)
    d_mixed = d_attended.reshape(2, seqs, block, H, HD)
    d_probs = jnp.einsum("tsqhe,skhe->tshqk", d_mixed, values4, preferred_element_type=f32)
    d_scores = probs * (d_probs - jnp.sum(d_probs * probs, axis=-1, keepdims=True))
    d_table = jnp.einsum(
        "shqk,sqkn->nh", jnp.sum(d_scores, axis=0), onehot, precision=lax.Precision.HIGHEST
    )
    d_raw = (d_scores * scale).astype(bf16)
    d_query = jnp.einsum("tshqk,skhe->tsqhe", d_raw, keys4, preferred_element_type=f32).reshape(
        2, seqs, block, width
    )
    d_keys = jnp.einsum("tshqk,tsqhe->skhe", d_raw, query4, preferred_element_type=f32).reshape(
        seqs, span, width
    )
    d_values = jnp.einsum(
        "tshqk,tsqhe->skhe", probs.astype(bf16), d_mixed, preferred_element_type=f32
    ).reshape(seqs, span, width)
    d_bq = jnp.sum(d_query, axis=(0, 1, 2))
    d_bv = jnp.sum(d_values, axis=(0, 1))
    d_query_low = d_query.astype(bf16)
    d_key_low = d_keys.astype(bf16)
    d_value_low = d_values.astype(bf16)
    d_wq = jnp.einsum("tsqd,tsqe->de", xs, d_query_low, preferred_element_type=f32)
    d_wk = jnp.einsum("sqd,sqe->de", x_every, d_key_low, preferred_element_type=f32)
    d_wv = jnp.einsum("sqd,sqe->de", x_every, d_value_low, preferred_element_type=f32)
    d_inputs = d_resid_one + jnp.einsum("tsqe,de->tsqd", d_query_low, wq, preferred_element_type=f32)
    d_every = jnp.einsum("sqe,de->sqd", d_key_low, wk, preferred_element_type=f32) + jnp.einsum(
        "sqe,de->sqd", d_value_low, wv, preferred_element_type=f32
    )
    dxs = jnp.transpose(d_every.astype(bf16).reshape(seqs, seqn, block, width), (1, 0, 2, 3))
    grads = jnp.concatenate(
        [jnp.stack([d_wq, d_wk, d_wv, d_wo]).astype(bf16), d_w1.astype(bf16), d_w2.astype(bf16)]
    ).reshape(UNITS * shards, r, width)
    small = jnp.concatenate(
        [d.reshape(shards, 1, r) for d in (d_bq, d_bv, d_bo, d_g1, d_b1, d_c2, d_g2, d_b2)]
        + [d_c1.reshape(shards, 1, 4 * r), jnp.broadcast_to(d_table.reshape(1, 1, NB * H), (shards, 1, NB * H))],
        axis=-1,
    )
    sums, dx, tiny = reduce_grads(grads, dxs.reshape(seqn, seqs * block, width), small, shards, seqn)
    grad_content = d_inputs[0] + dx.reshape(seqs, block, width)
    tiny = tiny[0]
    pieces = [tiny[i * r : (i + 1) * r] for i in range(8)]
    g_bq, g_bv, g_bo, g_g1, g_b1, g_c2, g_g2, g_b2 = pieces
    g_c1 = tiny[8 * r : 12 * r]
    g_table = tiny[12 * r :].reshape(NB, H)
    g_w1 = jnp.transpose(sums[4:8], (1, 0, 2)).reshape(r, 4 * width)
    g_w2 = sums[8:12].reshape(4 * r, width)
    return (
        outputs[0], outputs[1], grad_content, d_inputs[1],
        sums[0], g_bq, sums[1], sums[2], g_bv, sums[3], g_bo, g_g1, g_b1,
        g_w1, g_c1, g_w2, g_c2, g_g2, g_b2, g_table,
    )

def solution(mesh):
    in_specs = (
        P("dp", "seq", None),
        P("dp", "seq", None),
        P("dp", "seq", None),
        P("dp", "seq", None),
        P("dp", None),
        P("dp"),
        P("dp", None),
        P("dp", None),
        P("dp"),
        P("dp", None),
        P("dp"),
        P("dp"),
        P("dp"),
        P("dp", None),
        P("dp"),
        P("dp", None),
        P("dp"),
        P("dp"),
        P("dp"),
        P(),
        P("dp"),
        P("dp", None),
        P("dp", "seq"),
    )
    out_specs = (
        P("dp", "seq", None),
        P("dp", "seq", None),
        P("dp", "seq", None),
        P("dp", "seq", None),
        P("dp", None),
        P("dp"),
        P("dp", None),
        P("dp", None),
        P("dp"),
        P("dp", None),
        P("dp"),
        P("dp"),
        P("dp"),
        P("dp", None),
        P("dp"),
        P("dp", None),
        P("dp"),
        P("dp"),
        P("dp"),
        P(),
    )
    return jax.shard_map(
        functools.partial(per_device, shards=mesh.shape["dp"], seqn=mesh.shape["seq"]),
        mesh=mesh, in_specs=in_specs, out_specs=out_specs, check_vma=False
    )
```

```python
import functools

import jax
import jax.numpy as jnp
from jax import lax
from jax.experimental import pallas as pl
from jax.experimental.pallas import tpu as pltpu
from jax.sharding import PartitionSpec as P

H = 12
HD = 64
NB = 32

MESH = pl.DeviceIdType.MESH
UNITS = 12
SKEW = 128


def place(mesh_sizes):
    dp, sq = lax.axis_index("dp"), lax.axis_index("seq")
    row, side = dp // 2, dp % 2
    deck, core = sq // 2, sq % 2
    return dp, sq, row, side, deck, core


def tile_of(unit, shard, shards):
    down = unit // 8
    return (1 - down) * (unit * shards + shard) + down * (8 * shards + shard * 4 + unit - 8)


def gather_kernel(
    shards, seqn,
    wq, wk, wv, wo, wu, wd, xc, vec,
    full, xall, vall,
    own, xown, load_sem, keep_sem, zup_sem, zdn_sem, xs_sem, ys_sem, cp_sem, cy_sem,
    zr_sem, xr_sem, yr_sem, cpr_sem, cyr_sem, xc_send, xc_recv, vec_send, vec_recv,
):
    dp, sq, row, side, deck, core = place(None)
    rows = shards // 2
    up = ((row + 1) * 2 + side, sq)
    down = ((row - 1) * 2 + side, sq)
    across = (row * 2 + 1 - side, sq)
    other_deck = (dp, (1 - deck) * 2 + core)
    sibling = (dp, deck * 2 + 1 - core)

    barrier = pltpu.get_barrier_semaphore()

    def greet(step, carry):
        pl.semaphore_signal(barrier, inc=1, device_id=(lax.rem(dp + step, shards), sq), device_id_type=MESH)
        return carry

    lax.fori_loop(1, shards, greet, 0)
    pl.semaphore_signal(barrier, inc=1, device_id=other_deck, device_id_type=MESH)
    pl.semaphore_signal(barrier, inc=1, device_id=sibling, device_id_type=MESH)

    pieces = [wq, wk, wv, wo] + [wu.at[:, pl.ds(j * 768, 768)] for j in range(4)] + [wd.at[j] for j in range(4)]
    loads = [pltpu.make_async_copy(piece, own.at[u], load_sem.at[u]) for u, piece in enumerate(pieces)]
    for load in loads:
        load.start()
    xload = pltpu.make_async_copy(xc, xown, load_sem.at[UNITS])
    xload.start()
    pl.semaphore_wait(barrier, shards + 1)

    plane = pl.ds(pl.multiple_of(core * 384 + deck * SKEW, 128), 256)
    solo = pl.ds(pl.multiple_of(core * 384 + deck * 256, 128), 128)

    def remote(src, dst, send, recv, device):
        return pltpu.make_async_remote_copy(
            src_ref=src, dst_ref=dst, send_sem=send, recv_sem=recv, device_id=device, device_id_type=MESH
        )

    def part(unit, shard, columns):
        return full.at[tile_of(unit, shard, shards), :, columns]

    def vec_copy(step):
        return remote(vec, vall.at[dp], vec_send, vec_recv, (lax.rem(dp + step, shards), sq))

    def send_vec(step, carry):
        vec_copy(step).start()
        return carry

    lax.fori_loop(1, shards, send_vec, 0)
    keep_vec = pltpu.make_async_copy(vec, vall.at[dp], keep_sem.at[UNITS + 1])
    keep_vec.start()

    for load in loads:
        load.wait()

    def keep_copy(u):
        return pltpu.make_async_copy(own.at[u], full.at[tile_of(u, dp, shards)], keep_sem.at[u])

    def first(u, carry):
        src = own.at[u, :, plane]
        dst = part(u, dp, plane)
        recv = zr_sem.at[u, row]

        @pl.when(row < rows - 1)
        def _():
            remote(src, dst, zup_sem.at[row], recv, up).start()

        @pl.when(row > 0)
        def _():
            remote(src, dst, zdn_sem.at[row], recv, down).start()

        remote(src, dst, xs_sem, xr_sem.at[u], across).start()
        keep_copy(u).start()
        return carry

    lax.fori_loop(0, UNITS, first, 0)

    xload.wait()
    keep_x = pltpu.make_async_copy(xown, xall.at[sq], keep_sem.at[UNITS])
    keep_x.start()
    x_deck = remote(xown, xall.at[sq], xc_send.at[0], xc_recv.at[0], other_deck)
    x_deck.start()
    x_core = remote(xown, xall.at[sq], xc_send.at[1], xc_recv.at[1], sibling)
    x_core.start()

    def to_deck(u, shard):
        ref = part(u, shard, solo)
        remote(ref, ref, ys_sem, yr_sem.at[u], other_deck).start()

    def to_core(u, shard):
        ref = part(u, shard, plane)
        remote(ref, ref, cp_sem, cpr_sem.at[u], sibling).start()

    def step(n, carry):
        def hop(t, inner):
            u = n - (t - 1)

            @pl.when((u >= 0) & (u < UNITS))
            def _():
                @pl.when(row - t >= 0)
                def _():
                    s = row - t
                    ref = part(u, s * 2 + side, plane)
                    remote(ref, ref, zup_sem.at[s], zr_sem.at[u, s], up).wait_recv()

                    @pl.when(row < rows - 1)
                    def _():
                        remote(ref, ref, zup_sem.at[s], zr_sem.at[u, s], up).start()

                    remote(ref, ref, xs_sem, xr_sem.at[u], across).start()
                    to_deck(u, s * 2 + side)
                    to_core(u, s * 2 + side)

                @pl.when(row + t < rows)
                def _():
                    s = row + t
                    ref = part(u, s * 2 + side, plane)
                    remote(ref, ref, zdn_sem.at[s], zr_sem.at[u, s], down).wait_recv()

                    @pl.when(row > 0)
                    def _():
                        remote(ref, ref, zdn_sem.at[s], zr_sem.at[u, s], down).start()

                    remote(ref, ref, xs_sem, xr_sem.at[u], across).start()
                    to_deck(u, s * 2 + side)
                    to_core(u, s * 2 + side)

            return inner

        lax.fori_loop(1, rows, hop, 0)

        ux = n - (rows - 1)

        @pl.when((ux >= 0) & (ux < UNITS))
        def _():
            whole = full.at[pl.ds(0, rows), :, pl.ds(0, 256)]
            remote(whole, whole, xs_sem, xr_sem.at[ux], across).wait_recv()

            def pass_on(s, inner):
                to_deck(ux, s * 2 + 1 - side)
                to_core(ux, s * 2 + 1 - side)
                return inner

            lax.fori_loop(0, rows, pass_on, 0)

        uy = n - rows

        @pl.when((uy >= 0) & (uy < UNITS))
        def _():
            whole = full.at[pl.ds(0, shards - 1), :, pl.ds(0, 128)]
            remote(whole, whole, ys_sem, yr_sem.at[uy], other_deck).wait_recv()
            theirs = pl.ds(pl.multiple_of(core * 384 + (1 - deck) * 256, 128), 128)

            def pass_on(k, inner):
                ref = part(uy, lax.rem(dp + k, shards), theirs)
                remote(ref, ref, cy_sem, cyr_sem.at[uy], sibling).start()
                return inner

            lax.fori_loop(1, shards, pass_on, 0)

        return carry

    lax.fori_loop(0, UNITS + rows, step, 0)

    x_theirs = xall.at[(1 - deck) * 2 + core]
    x_deck.wait_recv()
    x_forward = remote(x_theirs, x_theirs, xc_send.at[2], xc_recv.at[2], sibling)
    x_forward.start()

    def finish(u, carry):
        planes = full.at[pl.ds(0, shards - 1), :, pl.ds(0, 256)]
        solos = full.at[pl.ds(0, shards - 1), :, pl.ds(0, 128)]
        remote(planes, planes, cp_sem, cpr_sem.at[u], sibling).wait_recv()
        remote(solos, solos, cy_sem, cyr_sem.at[u], sibling).wait_recv()
        keep_copy(u).wait()
        return carry

    lax.fori_loop(0, UNITS, finish, 0)
    x_deck.wait_send()
    x_core.wait()
    x_forward.wait()
    keep_x.wait()
    keep_vec.wait()
    rest = vall.at[pl.ds(0, shards - 1)]
    remote(rest, rest, vec_send, vec_recv, sibling).wait()

    def sent(s, carry):
        ref = full.at[pl.ds(0, UNITS), :, pl.ds(0, 256)]

        @pl.when((s <= row) & (row < rows - 1))
        def _():
            remote(ref, ref, zup_sem.at[s], zr_sem.at[0, 0], sibling).wait_send()

        @pl.when((s >= row) & (row > 0))
        def _():
            remote(ref, ref, zdn_sem.at[s], zr_sem.at[0, 0], sibling).wait_send()

        return carry

    lax.fori_loop(0, rows, sent, 0)
    ref = full.at[pl.ds(0, UNITS * rows), :, pl.ds(0, 256)]
    remote(ref, ref, xs_sem, xr_sem.at[0], sibling).wait_send()
    ref = full.at[pl.ds(0, UNITS * (shards - 1)), :, pl.ds(0, 128)]
    remote(ref, ref, ys_sem, yr_sem.at[0], sibling).wait_send()
    remote(ref, ref, cy_sem, cyr_sem.at[0], sibling).wait_send()
    ref = full.at[pl.ds(0, UNITS * (shards - 1)), :, pl.ds(0, 256)]
    remote(ref, ref, cp_sem, cpr_sem.at[0], sibling).wait_send()


def gather(wq, wk, wv, wo, wu, wd, xc, vec, shards, seqn):
    rows_of = wq.shape[0]
    width = wq.shape[1]
    bf16 = jnp.bfloat16
    anywhere = pl.BlockSpec(memory_space=pl.ANY)
    dma = pltpu.SemaphoreType.DMA
    rows = shards // 2
    return pl.pallas_call(
        functools.partial(gather_kernel, shards, seqn),
        out_shape=(
            jax.ShapeDtypeStruct((UNITS * shards, rows_of, width), bf16),
            jax.ShapeDtypeStruct((seqn,) + xc.shape, bf16),
            jax.ShapeDtypeStruct((shards,) + vec.shape, jnp.float32),
        ),
        in_specs=[anywhere] * 7 + [pl.BlockSpec(memory_space=pltpu.VMEM)],
        out_specs=(anywhere, anywhere, anywhere),
        scratch_shapes=[
            pltpu.VMEM((UNITS, rows_of, width), bf16),
            pltpu.VMEM(xc.shape, bf16),
            dma((UNITS + 1,)),
            dma((UNITS + 2,)),
            dma((rows,)),
            dma((rows,)),
            dma(()),
            dma(()),
            dma(()),
            dma(()),
            dma((UNITS, rows)),
            dma((UNITS,)),
            dma((UNITS,)),
            dma((UNITS,)),
            dma((UNITS,)),
            dma((3,)),
            dma((3,)),
            dma(()),
            dma(()),
        ],
        compiler_params=pltpu.CompilerParams(collective_id=0, has_side_effects=True),
        name="gather_weights",
    )(wq, wk, wv, wo, wu, wd.reshape(4, rows_of, width), xc, vec)


def reduce_kernel(
    shards, seqn,
    grads, dxs, small,
    out, dx_out, small_out,
    acc, got_core, got_deck, got_across, line, from_below, from_above, got_plane, half, got_half,
    dx_own, dx_core, dx_deck, got_small, mid_small, got_mid,
    load_sem, core_send, core_recv, deck_send, deck_recv, across_send, across_recv,
    up_send, up_recv, down_send, down_recv, plane_send, plane_recv, half_send, half_recv,
    dx_load, dx_send, dx_recv, small_send, small_recv, mid_send, mid_recv,
):
    dp, sq, row, side, deck, core = place(None)
    rows = shards // 2
    f32, bf16 = jnp.float32, jnp.bfloat16
    up = ((row + 1) * 2 + side, sq)
    down = ((row - 1) * 2 + side, sq)
    across = (row * 2 + 1 - side, sq)
    other_deck = (dp, (1 - deck) * 2 + core)
    sibling = (dp, deck * 2 + 1 - core)

    barrier = pltpu.get_barrier_semaphore()

    def greet(step, carry):
        pl.semaphore_signal(barrier, inc=1, device_id=(lax.rem(dp + step, shards), sq), device_id_type=MESH)
        return carry

    def greet_seq(step, carry):
        pl.semaphore_signal(barrier, inc=1, device_id=(dp, lax.rem(sq + step, seqn)), device_id_type=MESH)
        return carry

    lax.fori_loop(1, shards, greet, 0)
    lax.fori_loop(1, seqn, greet_seq, 0)

    mine = pl.ds(pl.multiple_of(core * 384, 128), 384)
    siblings = pl.ds(pl.multiple_of((1 - core) * 384, 128), 384)
    plane = pl.ds(pl.multiple_of(deck * 128, 128), 256)
    solo = pl.ds(pl.multiple_of(deck * 256, 128), 128)
    other_solo = pl.ds(pl.multiple_of((1 - deck) * 256, 128), 128)

    def remote(src, dst, send, recv, device):
        return pltpu.make_async_remote_copy(
            src_ref=src, dst_ref=dst, send_sem=send, recv_sem=recv, device_id=device, device_id_type=MESH
        )

    def load_all(u, carry):
        def one(s, inner):
            for b in range(2):
                tile = tile_of(u, s * 2 + b, shards)
                pltpu.make_async_copy(grads.at[tile, :, mine], acc.at[u, s, b], load_sem.at[u]).start()
            return inner

        return lax.fori_loop(0, rows, one, carry)

    lax.fori_loop(0, UNITS, load_all, 0)
    for k in range(2):
        pltpu.make_async_copy(dxs.at[k * 2 + core], dx_own.at[k], dx_load.at[k]).start()
    got_small[dp] = small[dp]
    pl.semaphore_wait(barrier, shards + seqn - 2)

    def send_core(u, carry):
        def one(s, inner):
            for b in range(2):
                tile = tile_of(u, s * 2 + b, shards)
                remote(grads.at[tile, :, siblings], got_core.at[u, s, b], core_send, core_recv.at[u], sibling).start()
            return inner

        return lax.fori_loop(0, rows, one, carry)

    lax.fori_loop(0, UNITS, send_core, 0)
    for k in range(2):
        remote(dxs.at[k * 2 + 1 - core], dx_core.at[k], dx_send.at[k], dx_recv.at[k], sibling).start()

    def send_small(step, carry):
        to = lax.rem(dp + step, shards)
        remote(small.at[to], got_small.at[dp], small_send, small_recv, (to, sq)).start()
        return carry

    lax.fori_loop(1, shards, send_small, 0)

    def total(left, right):
        return (left.astype(f32) + right.astype(f32)).astype(bf16)

    def step(n, carry):
        @pl.when(n < UNITS)
        def _():
            u = n
            pltpu.make_async_copy(acc.at[u], acc.at[u], load_sem.at[u]).wait()
            remote(got_core.at[u], got_core.at[u], core_send, core_recv.at[u], sibling).wait_recv()

            def add(s, inner):
                for b in range(2):
                    acc[u, s, b] = total(acc[u, s, b], got_core[u, s, b])
                return inner

            lax.fori_loop(0, rows, add, 0)
            remote(acc.at[u, :, :, :, other_solo], got_deck.at[u], deck_send.at[u], deck_recv.at[u], other_deck).start()

        u2 = n - 1

        @pl.when((u2 >= 0) & (u2 < UNITS))
        def _():
            u = u2
            remote(got_deck.at[u], got_deck.at[u], deck_send.at[u], deck_recv.at[u], other_deck).wait_recv()

            def add(s, inner):
                for b in range(2):
                    acc[u, s, b, :, solo] = total(acc[u, s, b, :, solo], got_deck[u, s, b])
                return inner

            lax.fori_loop(0, rows, add, 0)
            remote(
                acc.at[u, :, 1 - side, :, plane], got_across.at[u], across_send.at[u], across_recv.at[u], across
            ).start()

        u3 = n - 2

        @pl.when((u3 >= 0) & (u3 < UNITS))
        def _():
            u = u3
            remote(got_across.at[u], got_across.at[u], across_send.at[u], across_recv.at[u], across).wait_recv()

            def add(s, inner):
                line[u, s] = total(acc[u, s, side, :, plane], got_across[u, s])
                return inner

            lax.fori_loop(0, rows, add, 0)

        u_up = n - 3 - row

        @pl.when((u_up >= 0) & (u_up < UNITS))
        def _():
            u = u_up

            def one(s, inner):
                @pl.when(row > 0)
                def _():
                    remote(line.at[u, s], from_below.at[u, s], up_send.at[u, s], up_recv.at[u, s], up).wait_recv()
                    line[u, s] = total(line[u, s], from_below[u, s])

                @pl.when(s > row)
                def _():
                    remote(line.at[u, s], from_below.at[u, s], up_send.at[u, s], up_recv.at[u, s], up).start()

                return inner

            lax.fori_loop(row, rows, one, 0)

        u_down = n - 3 - (rows - 1 - row)

        @pl.when((u_down >= 0) & (u_down < UNITS))
        def _():
            u = u_down

            def one(s, inner):
                @pl.when(row < rows - 1)
                def _():
                    remote(line.at[u, s], from_above.at[u, s], down_send.at[u, s], down_recv.at[u, s], down).wait_recv()
                    line[u, s] = total(line[u, s], from_above[u, s])

                @pl.when(s < row)
                def _():
                    remote(line.at[u, s], from_above.at[u, s], down_send.at[u, s], down_recv.at[u, s], down).start()

                return inner

            lax.fori_loop(0, row + 1, one, 0)

        u_f = n - 3 - rows

        @pl.when((u_f >= 0) & (u_f < UNITS))
        def _():
            u = u_f
            remote(line.at[u, row], got_plane.at[u], plane_send.at[u], plane_recv.at[u], other_deck).start()

        u_h = n - 4 - rows

        @pl.when((u_h >= 0) & (u_h < UNITS))
        def _():
            u = u_h
            remote(line.at[u, row], got_plane.at[u], plane_send.at[u], plane_recv.at[u], other_deck).wait_recv()
            half[u, :, plane] = line[u, row]
            half[u, :, other_solo] = got_plane[u, :, pl.ds(pl.multiple_of((1 - deck) * 128, 128), 128)]
            half[u, :, pl.ds(128, 128)] = total(
                half[u, :, pl.ds(128, 128)], got_plane[u, :, pl.ds(pl.multiple_of(deck * 128, 128), 128)]
            )
            remote(half.at[u], got_half.at[u], half_send.at[u], half_recv.at[u], sibling).start()

        u_o = n - 5 - rows

        @pl.when((u_o >= 0) & (u_o < UNITS))
        def _():
            u = u_o
            remote(half.at[u], got_half.at[u], half_send.at[u], half_recv.at[u], sibling).wait_recv()
            out[u, :, mine] = half[u].astype(f32)
            out[u, :, siblings] = got_half[u].astype(f32)

        return carry

    lax.fori_loop(0, 3, step, 0)
    for k in range(2):
        pltpu.make_async_copy(dx_own.at[k], dx_own.at[k], dx_load.at[k]).wait()
        remote(dx_core.at[k], dx_core.at[k], dx_send.at[k], dx_recv.at[k], sibling).wait()
        dx_own[k] = total(dx_own[k], dx_core[k])
    deck_dx = remote(dx_own.at[1 - deck], dx_deck, dx_send.at[2], dx_recv.at[2], other_deck)
    deck_dx.start()
    rest = got_small.at[pl.ds(0, shards - 1)]
    remote(rest, rest, small_send, small_recv, sibling).wait()
    summed = got_small[0]
    for i in range(1, shards):
        summed = summed + got_small[i]
    mid_small[...] = summed
    got_mid[sq] = summed

    def send_mid(step, carry):
        remote(mid_small, got_mid.at[sq], mid_send, mid_recv, (dp, lax.rem(sq + step, seqn))).start()
        return carry

    lax.fori_loop(1, seqn, send_mid, 0)
    lax.fori_loop(3, UNITS + 6 + rows, step, 0)

    rest = got_mid.at[pl.ds(0, seqn - 1)]
    remote(rest, rest, mid_send, mid_recv, sibling).wait()
    summed = got_mid[0]
    for i in range(1, seqn):
        summed = summed + got_mid[i]
    small_out[...] = summed
    deck_dx.wait()
    dx_out[...] = dx_own[deck].astype(f32) + dx_deck[...].astype(f32)

    ref = got_core
    remote(ref, ref, core_send, core_recv.at[0], sibling).wait_send()

    def sent(u, carry):
        remote(got_deck.at[u], got_deck.at[u], deck_send.at[u], deck_recv.at[u], other_deck).wait_send()
        remote(got_across.at[u], got_across.at[u], across_send.at[u], across_recv.at[u], across).wait_send()
        remote(got_plane.at[u], got_plane.at[u], plane_send.at[u], plane_recv.at[u], other_deck).wait_send()
        remote(half.at[u], half.at[u], half_send.at[u], half_recv.at[u], sibling).wait_send()

        def one(s, inner):
            @pl.when(s > row)
            def _():
                remote(line.at[u, s], from_below.at[u, s], up_send.at[u, s], up_recv.at[u, s], up).wait_send()

            @pl.when(s < row)
            def _():
                remote(line.at[u, s], from_above.at[u, s], down_send.at[u, s], down_recv.at[u, s], down).wait_send()

            return inner

        return lax.fori_loop(0, rows, one, carry)

    lax.fori_loop(0, UNITS, sent, 0)


def reduce_grads(grads, dxs, small, shards, seqn):
    rows_of, width = grads.shape[1:]
    f32, bf16 = jnp.float32, jnp.bfloat16
    anywhere = pl.BlockSpec(memory_space=pl.ANY)
    vmem = pl.BlockSpec(memory_space=pltpu.VMEM)
    dma = pltpu.SemaphoreType.DMA
    rows = shards // 2
    own = dxs.shape[1:]
    return pl.pallas_call(
        functools.partial(reduce_kernel, shards, seqn),
        out_shape=(
            jax.ShapeDtypeStruct((UNITS, rows_of, width), f32),
            jax.ShapeDtypeStruct(own, f32),
            jax.ShapeDtypeStruct(small.shape[1:], f32),
        ),
        in_specs=[anywhere, anywhere, vmem],
        out_specs=(vmem, vmem, vmem),
        scratch_shapes=[
            pltpu.VMEM((UNITS, rows, 2, rows_of, 384), bf16),
            pltpu.VMEM((UNITS, rows, 2, rows_of, 384), bf16),
            pltpu.VMEM((UNITS, rows, 2, rows_of, 128), bf16),
            pltpu.VMEM((UNITS, rows, rows_of, 256), bf16),
            pltpu.VMEM((UNITS, rows, rows_of, 256), bf16),
            pltpu.VMEM((UNITS, rows, rows_of, 256), bf16),
            pltpu.VMEM((UNITS, rows, rows_of, 256), bf16),
            pltpu.VMEM((UNITS, rows_of, 256), bf16),
            pltpu.VMEM((UNITS, rows_of, 384), bf16),
            pltpu.VMEM((UNITS, rows_of, 384), bf16),
            pltpu.VMEM((2,) + own, bf16),
            pltpu.VMEM((2,) + own, bf16),
            pltpu.VMEM(own, bf16),
            pltpu.VMEM(small.shape, f32),
            pltpu.VMEM(small.shape[1:], f32),
            pltpu.VMEM((seqn,) + small.shape[1:], f32),
            dma((UNITS,)),
            dma(()),
            dma((UNITS,)),
            dma((UNITS,)),
            dma((UNITS,)),
            dma((UNITS,)),
            dma((UNITS,)),
            dma((UNITS, rows)),
            dma((UNITS, rows)),
            dma((UNITS, rows)),
            dma((UNITS, rows)),
            dma((UNITS,)),
            dma((UNITS,)),
            dma((UNITS,)),
            dma((UNITS,)),
            dma((2,)),
            dma((3,)),
            dma((3,)),
            dma(()),
            dma(()),
            dma(()),
            dma(()),
        ],
        compiler_params=pltpu.CompilerParams(
            collective_id=1, has_side_effects=True, vmem_limit_bytes=60 * 1024 * 1024
        ),
        name="reduce_grads",
    )(grads, dxs, small)


bucket_marks = (12, 16, 23, 32, 46, 64, 91)
MASKED = NB
TN = (((0,), (0,)), ((), ()))
NT = (((1,), (1,)), ((), ()))


def dot(left, right, dims=None):
    if dims is None:
        dims = (((1,), (0,)), ((), ()))
    return lax.dot_general(left, right, dims, preferred_element_type=jnp.float32)


def fill_buckets(buckets, pos_rows, pos_cols, lengths, base, seqs, block, span):
    for s in range(seqs):
        delta = pos_cols[s : s + 1, :] - pos_rows[s]
        dist = jnp.abs(delta)
        far = jnp.full(dist.shape, 8, jnp.int32)
        for mark in bucket_marks:
            far = far + (dist >= mark).astype(jnp.int32)
        bucket = jnp.where(dist < 8, dist, far) + 16 * (delta > 0).astype(jnp.int32)
        i = base + lax.broadcasted_iota(jnp.int32, (block, span), 0)
        j = lax.broadcasted_iota(jnp.int32, (block, span), 1)
        valid = j < lengths[s]
        buckets[s, 0] = jnp.where(valid & (j <= i), bucket, MASKED)
        buckets[s, 1] = jnp.where(valid & (j < jnp.maximum(i, 1)), bucket, MASKED)


def head_lanes(rows, half):
    lane = lax.broadcasted_iota(jnp.int32, (rows, 2 * HD), 1)
    return (lane < HD) if half == 0 else (lane >= HD)


def attend_kernel(
    seqs, block, span, seqn,
    lengths, xc, xq, xall, weights, vectors, table, pos_rows, pos_cols,
    probs, attended, query, keys, values,
    buckets,
):
    f32, bf16 = jnp.float32, jnp.bfloat16
    step = pl.program_id(0)
    pairs = H // 2
    width = H * HD

    @pl.when(step == 0)
    def _():
        base = lax.axis_index("seq") * block
        fill_buckets(buckets, pos_rows, pos_cols, lengths, base, seqs, block, span)
        for t, x in enumerate((xc, xq)):
            rows = x[...].reshape(seqs * block, width)
            query[t] = (dot(rows, weights[0]) + vectors[0:1, :]).astype(bf16).reshape(seqs, block, width)

        def project(k, carry):
            rows = xall[k].reshape(seqs * block, width)
            at = pl.ds(pl.multiple_of(k * block, block), block)
            keys[:, at, :] = dot(rows, weights[1]).astype(bf16).reshape(seqs, block, width)
            values[:, at, :] = (dot(rows, weights[2]) + vectors[1:2, :]).astype(bf16).reshape(seqs, block, width)
            return carry

        lax.fori_loop(0, seqn, project, 0)

    s, pair = step // pairs, lax.rem(step, pairs)
    lanes = pl.ds(pl.multiple_of(pair * 128, 128), 128)
    q = query[:, s, :, lanes].reshape(2 * block, 128)
    k = keys[s, :, lanes]
    v = values[s, :, lanes]
    outs = []
    for half in range(2):
        entry = jnp.broadcast_to(table[pl.ds(pair * 2 + half, 1), :], (block, 128))
        bias = jnp.concatenate(
            [
                jnp.concatenate(
                    [
                        jnp.take_along_axis(entry, buckets[s, t, :, pl.ds(c * 128, 128)], axis=1, mode="promise_in_bounds")
                        for c in range(span // 128)
                    ],
                    axis=1,
                )
                for t in range(2)
            ],
            axis=0,
        )
        mine = head_lanes(2 * block, half)
        one = jnp.where(mine, q * 0.125, 0).astype(bf16)
        scores = dot(one, k, NT) + bias
        top = jnp.max(scores, axis=-1, keepdims=True)
        expo = jnp.exp(scores - top)
        low = (expo * (1.0 / jnp.sum(expo, axis=-1, keepdims=True))).astype(bf16)
        probs[0, half] = low
        outs.append(dot(low, v))
    mixed = jnp.where(head_lanes(2 * block, 0), outs[0], outs[1]).astype(bf16)
    attended[:, s, :, lanes] = mixed.reshape(2, block, 128)


def attend(lengths, xc, xq, xall, weights, vectors, table, pos_rows, pos_cols):
    seqs, block, width = xc.shape
    seqn = xall.shape[0]
    span = pos_cols.shape[1]
    bf16 = jnp.bfloat16
    steps = seqs * H // 2
    vmem = pl.BlockSpec(memory_space=pltpu.VMEM)
    fixed = lambda shape: pl.BlockSpec(shape, lambda i: (0,) * len(shape))
    return pl.pallas_call(
        functools.partial(attend_kernel, seqs, block, span, seqn),
        grid=(steps,),
        out_shape=(
            jax.ShapeDtypeStruct((steps, 2, 2 * block, span), bf16),
            jax.ShapeDtypeStruct((2, seqs, block, width), bf16),
            jax.ShapeDtypeStruct((2, seqs, block, width), bf16),
            jax.ShapeDtypeStruct((seqs, span, width), bf16),
            jax.ShapeDtypeStruct((seqs, span, width), bf16),
        ),
        in_specs=[pl.BlockSpec(memory_space=pltpu.SMEM), vmem, vmem, vmem]
        + [pl.BlockSpec((3, width, width), lambda i: (0, 0, 0))]
        + [vmem] * 4,
        out_specs=(
            pl.BlockSpec((1, 2, 2 * block, span), lambda i: (i, 0, 0, 0)),
            fixed((2, seqs, block, width)),
            fixed((2, seqs, block, width)),
            fixed((seqs, span, width)),
            fixed((seqs, span, width)),
        ),
        scratch_shapes=[pltpu.VMEM((seqs, 2, block, span), jnp.int32)],
        compiler_params=pltpu.CompilerParams(vmem_limit_bytes=60 * 1024 * 1024),
        name="attend",
    )(lengths, xc, xq, xall, weights, vectors, table, pos_rows, pos_cols)


def center_of(value):
    center = value - jnp.mean(value, axis=-1, keepdims=True)
    var = jnp.mean(center * center, axis=-1, keepdims=True)
    inv = lax.rsqrt(var + 1e-05)
    return center * inv, inv


def norm_back(grad, gain, normed, inv):
    scaled = grad * gain
    return inv * (
        scaled
        - jnp.mean(scaled, axis=-1, keepdims=True)
        - normed * jnp.mean(scaled * normed, axis=-1, keepdims=True)
    )


def middle_kernel(
    seqs, block,
    attended, xc, xq, cot_c, cot_q, keep, vectors, weights,
    y_c, y_q, dr1_out, da_out, grads, dvec,
    w, hidden, hidden_low, hidden_turn, normed1, inv1, active, slope, feed, dr2, dr2_low, du_low, dr1_low, y, stage,
    w_sem, y_sem, stage_sem, dr1_sem,
):
    f32, bf16 = jnp.float32, jnp.bfloat16
    width = H * HD
    half = seqs * block
    rows = 2 * half
    chunk = 128
    loads = [pltpu.make_async_copy(weights.at[3 + i], w.at[i], w_sem.at[i]) for i in range(9)]
    for load in loads:
        load.start()
    dvec[...] = jnp.zeros_like(dvec)
    vec = lambda i: vectors[i : i + 1, :]

    loads[0].wait()

    def phase_one(c, carry):
        at = pl.ds(pl.multiple_of(c * chunk, chunk), chunk)
        out = dot(attended[at, :], w[0]) + vec(2)

        def from_x(x):
            return x[pl.ds(pl.multiple_of(lax.rem(c, half // chunk) * chunk, chunk), chunk), :].astype(f32)

        x = jnp.where(c < half // chunk, from_x(xc), from_x(xq))
        normed, inv = center_of(x + out)
        normed1[at, :] = normed
        inv1[at, :] = inv
        h = normed * vec(3) + vec(4)
        hidden[at, :] = h
        hidden_low[at, :] = h.astype(bf16)
        return carry

    lax.fori_loop(0, rows // chunk, phase_one, 0)
    hidden_turn[...] = hidden_low[...].T

    tile = 256
    tiles = width // tile
    for j in range(4):
        loads[1 + j].wait()

    def phase_two(step, carry):
        j, n = step // tiles, lax.rem(step, tiles)
        cols = pl.ds(pl.multiple_of(n * tile, tile), tile)
        u = dot(hidden_low[...], w[1 + j, :, cols]) + vectors[pl.ds(8 + j, 1), cols]
        cdf = 0.5 * (1.0 + lax.erf(u * (2.0**-0.5)))
        active[j, :, cols] = (u * cdf).astype(bf16)
        slope[j, :, cols] = cdf + u * (jnp.exp(-0.5 * u * u) * ((2.0 * jnp.pi) ** -0.5))
        return carry

    lax.fori_loop(0, 4 * tiles, phase_two, 0)
    for j in range(4):
        loads[5 + j].wait()

    def phase_feed(n, carry):
        cols = pl.ds(pl.multiple_of(n * tile, tile), tile)
        feed[:, cols] = sum(dot(active[j], w[5 + j, :, cols]) for j in range(4))
        return carry

    lax.fori_loop(0, tiles, phase_feed, 0)

    def phase_three(c, carry):
        at = pl.ds(pl.multiple_of(c * chunk, chunk), chunk)
        normed, inv = center_of(hidden[at, :] + feed[at, :] + vec(5))
        kept = keep[at, :]
        y[at, :] = (normed * vec(6) + vec(7)) * kept
        inner = pl.ds(pl.multiple_of(lax.rem(c, half // chunk) * chunk, chunk), chunk)
        cot = jnp.where(c < half // chunk, cot_c[inner, :].astype(f32), cot_q[inner, :].astype(f32)) * kept
        d = norm_back(cot, vec(6), normed, inv)
        dvec[6:7, :] += jnp.sum(cot * normed, axis=0, keepdims=True)
        dvec[7:8, :] += jnp.sum(cot, axis=0, keepdims=True)
        dvec[5:6, :] += jnp.sum(d, axis=0, keepdims=True)
        dr2[at, :] = d
        dr2_low[at, :] = d.astype(bf16)
        return carry

    lax.fori_loop(0, rows // chunk, phase_three, 0)
    y_copies = [
        pltpu.make_async_copy(y.at[pl.ds(0, half)], y_c, y_sem.at[0]),
        pltpu.make_async_copy(y.at[pl.ds(half, half)], y_q, y_sem.at[1]),
    ]
    for copy in y_copies:
        copy.start()

    def phase_four(step, carry):
        j, n = step // tiles, lax.rem(step, tiles)
        cols = pl.ds(pl.multiple_of(n * tile, tile), tile)
        du = slope[j, :, cols] * dot(dr2_low[...], w[5 + j, cols, :], NT)
        dvec[pl.ds(8 + j, 1), cols] = jnp.sum(du, axis=0, keepdims=True)
        low = du.astype(bf16)
        du_low[j, :, cols] = low
        stage[j, :, cols] = dot(hidden_turn[...], low).astype(bf16)
        stage[4 + j, cols, :] = dot(active[j, :, cols], dr2_low[...], TN).astype(bf16)

        @pl.when(n == tiles - 1)
        def _():
            pltpu.make_async_copy(stage.at[j], grads.at[4 + j], stage_sem.at[j]).start()
            pltpu.make_async_copy(stage.at[4 + j], grads.at[8 + j], stage_sem.at[4 + j]).start()

        return carry

    lax.fori_loop(0, 4 * tiles, phase_four, 0)

    def phase_hidden(n, carry):
        cols = pl.ds(pl.multiple_of(n * tile, tile), tile)
        dr2[:, cols] += sum(dot(du_low[j], w[1 + j, cols, :], NT) for j in range(4))
        return carry

    lax.fori_loop(0, tiles, phase_hidden, 0)
    for copy in y_copies:
        copy.wait()

    def phase_five(c, carry):
        at = pl.ds(pl.multiple_of(c * chunk, chunk), chunk)
        dh = dr2[at, :]
        normed = normed1[at, :]
        d = norm_back(dh, vec(3), normed, inv1[at, :])
        dvec[3:4, :] += jnp.sum(dh * normed, axis=0, keepdims=True)
        dvec[4:5, :] += jnp.sum(dh, axis=0, keepdims=True)
        dvec[2:3, :] += jnp.sum(d, axis=0, keepdims=True)
        y[at, :] = d
        low = d.astype(bf16)
        dr1_low[at, :] = low
        da_out[at, :] = dot(low, w[0], NT).astype(bf16)
        return carry

    lax.fori_loop(0, rows // chunk, phase_five, 0)
    dr1_copy = pltpu.make_async_copy(y, dr1_out, dr1_sem)
    dr1_copy.start()

    def phase_out(n, carry):
        cols = pl.ds(pl.multiple_of(n * tile, tile), tile)
        stage[8, cols, :] = dot(attended[:, cols], dr1_low[...], TN).astype(bf16)
        return carry

    lax.fori_loop(0, tiles, phase_out, 0)
    last = pltpu.make_async_copy(stage.at[8], grads.at[3], stage_sem.at[8])
    last.start()
    for j in range(8):
        pltpu.make_async_copy(stage.at[j], grads.at[4 + j], stage_sem.at[j]).wait()
    last.wait()
    dr1_copy.wait()


def middle(attended, xc, xq, cot_c, cot_q, keep, vectors, weights):
    seqs, block, width = xc.shape
    f32, bf16 = jnp.float32, jnp.bfloat16
    half = seqs * block
    rows = 2 * half
    vmem = pl.BlockSpec(memory_space=pltpu.VMEM)
    anywhere = pl.BlockSpec(memory_space=pl.ANY)
    flat = lambda a: a.reshape(half, width)
    return pl.pallas_call(
        functools.partial(middle_kernel, seqs, block),
        out_shape=(
            jax.ShapeDtypeStruct((half, width), f32),
            jax.ShapeDtypeStruct((half, width), f32),
            jax.ShapeDtypeStruct((rows, width), f32),
            jax.ShapeDtypeStruct((rows, width), bf16),
            jax.ShapeDtypeStruct((UNITS, width, width), bf16),
            jax.ShapeDtypeStruct((UNITS, width), f32),
        ),
        in_specs=[vmem] * 7 + [anywhere],
        out_specs=(anywhere, anywhere, anywhere, vmem, anywhere, vmem),
        scratch_shapes=[
            pltpu.VMEM((9, width, width), bf16),
            pltpu.VMEM((rows, width), f32),
            pltpu.VMEM((rows, width), bf16),
            pltpu.VMEM((width, rows), bf16),
            pltpu.VMEM((rows, width), f32),
            pltpu.VMEM((rows, 1), f32),
            pltpu.VMEM((4, rows, width), bf16),
            pltpu.VMEM((4, rows, width), f32),
            pltpu.VMEM((rows, width), f32),
            pltpu.VMEM((rows, width), f32),
            pltpu.VMEM((rows, width), bf16),
            pltpu.VMEM((4, rows, width), bf16),
            pltpu.VMEM((rows, width), bf16),
            pltpu.VMEM((rows, width), f32),
            pltpu.VMEM((9, width, width), bf16),
            pltpu.SemaphoreType.DMA((9,)),
            pltpu.SemaphoreType.DMA((2,)),
            pltpu.SemaphoreType.DMA((9,)),
            pltpu.SemaphoreType.DMA(()),
        ],
        compiler_params=pltpu.CompilerParams(vmem_limit_bytes=63 * 1024 * 1024),
        name="middle",
    )(attended, flat(xc), flat(xq), flat(cot_c), flat(cot_q), keep, vectors, weights)


def attend_back_kernel(
    seqs, block, span, seqn,
    lengths, xc, xq, xall, weights, pos_rows, pos_cols, probs, attended, d_attended, query, keys, values, dr1, grads_in,
    grads, d_content, d_query_x, dxs, dvec, counts,
    buckets, dq, dk, dv, ds_sum, stage, grads_low, stage_sem,
):
    f32, bf16 = jnp.float32, jnp.bfloat16
    step = pl.program_id(0)
    pairs = H // 2
    width = H * HD
    rows = 2 * block

    @pl.when(step == 0)
    def _():
        base = lax.axis_index("seq") * block
        fill_buckets(buckets, pos_rows, pos_cols, lengths, base, seqs, block, span)
        counts[...] = jnp.zeros_like(counts)

    s, pair = step // pairs, lax.rem(step, pairs)
    lanes = pl.ds(pl.multiple_of(pair * 128, 128), 128)
    q = query[:, s, :, lanes].reshape(rows, 128)
    k = keys[s, :, lanes]
    v = values[s, :, lanes]
    da = d_attended[:, s, :, lanes].reshape(rows, 128)
    product = da.astype(f32) * attended[:, s, :, lanes].reshape(rows, 128).astype(f32)
    d_queries, dk_turn, dv_turn = [], 0.0, 0.0
    for half in range(2):
        mine = head_lanes(rows, half)
        one = jnp.where(mine, da, 0).astype(bf16)
        inner = jnp.sum(jnp.where(mine, product, 0.0), axis=-1, keepdims=True)
        low = probs[0, half]
        ds = low.astype(f32) * (dot(one, v, NT) - inner)
        ds_sum[pair * 2 + half] = (ds[:block] + ds[block:]).astype(bf16)
        ds_low = ds.astype(bf16)
        d_queries.append(dot(ds_low, k))
        dk_turn += dot(jnp.where(mine, q, 0).astype(bf16), ds_low, TN)
        dv_turn += dot(one, low, TN)
    d_query = jnp.where(head_lanes(rows, 0), d_queries[0], d_queries[1]) * 0.125
    dq[:, s, :, lanes] = d_query.reshape(2, block, 128)
    dk[s, :, lanes] = (dk_turn * 0.125).T.astype(bf16)
    dv[s, :, lanes] = dv_turn.T

    @pl.when(pair == pairs - 1)
    def _():
        def count(g, carry):
            at = pl.ds(pl.multiple_of(g * 16, 16), 16)
            bucket = buckets[s, 0, at, :]
            hot = jnp.concatenate(
                [jnp.where(bucket == n, 1.0, 0.0).astype(bf16) for n in range(NB)], axis=0
            )
            counts[...] += dot(hot, ds_sum[:, at, :].reshape(H * 16, span), NT)
            return carry

        lax.fori_loop(0, block // 16, count, 0)

    @pl.when(step == seqs * pairs - 1)
    def _():
        all_rows = 2 * seqs * block
        dvec[...] = jnp.zeros_like(dvec)
        dvec[0:1, :] = jnp.sum(dq[...].reshape(all_rows, width), axis=0, keepdims=True)
        dvec[1:2, :] = jnp.sum(dv[...].reshape(seqs * span, width), axis=0, keepdims=True)
        for t, (x, out) in enumerate(((xc, d_content), (xq, d_query_x))):
            low = dq[t].reshape(seqs * block, width).astype(bf16)
            out[...] = dr1[pl.ds(t * seqs * block, seqs * block), :] + dot(low, weights[0], NT)
            piece = dot(x[...].reshape(seqs * block, width), low, TN)
            stage[t] = piece
        low_q = (stage[0] + stage[1]).astype(bf16)

        def every(k, carry):
            at = pl.ds(pl.multiple_of(k * block, block), block)
            x = xall[k].reshape(seqs * block, width)
            low_k = dk[:, at, :].reshape(seqs * block, width)
            low_v = dv[:, at, :].reshape(seqs * block, width).astype(bf16)
            dxs[k] = (dot(low_k, weights[1], NT) + dot(low_v, weights[2], NT)).astype(bf16)
            turned = x.T

            @pl.when(k == 0)
            def _():
                stage[0] = dot(turned, low_k)
                stage[1] = dot(turned, low_v)

            @pl.when(k > 0)
            def _():
                stage[0] += dot(turned, low_k)
                stage[1] += dot(turned, low_v)

            return carry

        grads_low[0] = low_q
        lax.fori_loop(0, seqn, every, 0)
        grads_low[1] = stage[0].astype(bf16)
        grads_low[2] = stage[1].astype(bf16)
        for i in range(3):
            pltpu.make_async_copy(grads_low.at[i], grads.at[i], stage_sem.at[i]).start()
        for i in range(3):
            pltpu.make_async_copy(grads_low.at[i], grads.at[i], stage_sem.at[i]).wait()


def attend_back(lengths, xc, xq, xall, weights, pos_rows, pos_cols, probs, attended, d_attended, query, keys, values, dr1, grads):
    seqs, block, width = xc.shape
    seqn = xall.shape[0]
    span = pos_cols.shape[1]
    f32, bf16 = jnp.float32, jnp.bfloat16
    steps = seqs * H // 2
    vmem = pl.BlockSpec(memory_space=pltpu.VMEM)
    anywhere = pl.BlockSpec(memory_space=pl.ANY)
    fixed = lambda shape: pl.BlockSpec(shape, lambda i: (0,) * len(shape))
    own = (seqs * block, width)
    return pl.pallas_call(
        functools.partial(attend_back_kernel, seqs, block, span, seqn),
        grid=(steps,),
        out_shape=(
            jax.ShapeDtypeStruct(grads.shape, bf16),
            jax.ShapeDtypeStruct(own, f32),
            jax.ShapeDtypeStruct(own, f32),
            jax.ShapeDtypeStruct((seqn,) + own, bf16),
            jax.ShapeDtypeStruct((8, width), f32),
            jax.ShapeDtypeStruct((NB * 16, H * 16), f32),
        ),
        in_specs=[pl.BlockSpec(memory_space=pltpu.SMEM), vmem, vmem, vmem]
        + [pl.BlockSpec((3, width, width), lambda i: (0, 0, 0))]
        + [vmem] * 2
        + [pl.BlockSpec((1, 2, 2 * block, span), lambda i: (i, 0, 0, 0))]
        + [vmem] * 6
        + [anywhere],
        out_specs=(
            anywhere,
            fixed(own),
            fixed(own),
            fixed((seqn,) + own),
            fixed((8, width)),
            fixed((NB * 16, H * 16)),
        ),
        scratch_shapes=[
            pltpu.VMEM((seqs, 2, block, span), jnp.int32),
            pltpu.VMEM((2, seqs, block, width), f32),
            pltpu.VMEM((seqs, span, width), bf16),
            pltpu.VMEM((seqs, span, width), f32),
            pltpu.VMEM((H, block, span), bf16),
            pltpu.VMEM((2, width, width), f32),
            pltpu.VMEM((3, width, width), bf16),
            pltpu.SemaphoreType.DMA((3,)),
        ],
        input_output_aliases={14: 0},
        compiler_params=pltpu.CompilerParams(vmem_limit_bytes=62 * 1024 * 1024),
        name="attend_back",
    )(lengths, xc, xq, xall, weights, pos_rows, pos_cols, probs, attended, d_attended, query, keys, values, dr1, grads)


def per_device(
    x_content, x_query, cot_content, cot_query,
    w_query, b_query, w_key, w_value, b_value, w_out, b_out, gain_attn, shift_attn,
    w_up, b_up, w_down, b_down, gain_ffn, shift_ffn, rel_table, lengths, positions, predicted,
    *, shards, seqn,
):
    f32 = jnp.float32
    seqs, block, width = x_content.shape
    r = w_query.shape[0]
    vec = jnp.concatenate(
        [b_query, b_value, b_out, gain_attn, shift_attn, b_down, gain_ffn, shift_ffn, b_up]
    ).astype(f32)[None]
    full, xall, vall = gather(w_query, w_key, w_value, w_out, w_up, w_down, x_content, vec, shards, seqn)
    weights = full.reshape(UNITS, width, width)
    eight = jnp.transpose(vall[:, 0, : 8 * r].reshape(shards, 8, r), (1, 0, 2)).reshape(8, width)
    vectors = jnp.concatenate([eight, vall[:, 0, 8 * r :].reshape(4, width)])
    base = lax.axis_index("seq") * block
    pos_rows = lax.dynamic_slice_in_dim(positions, base, block, 1)[..., None]
    table = jnp.full((H, 128), -1e30, f32).at[:, :NB].set(rel_table.astype(f32).T)
    valid = (base + jnp.arange(block))[None, :] < lengths[:, None]
    keep = jnp.stack([valid, valid & (predicted > 0)]).astype(f32).reshape(2 * seqs * block, 1)

    probs, attended, query, keys, values = attend(
        lengths, x_content, x_query, xall, weights, vectors, table, pos_rows, positions
    )
    y_c, y_q, dr1, d_attended, grads, dvec = middle(
        attended.reshape(2 * seqs * block, width), x_content, x_query, cot_content, cot_query, keep, vectors, weights
    )
    grads, d_content, d_query_x, dxs, dvec_qv, counts = attend_back(
        lengths, x_content, x_query, xall, weights, pos_rows, positions, probs,
        attended, d_attended.reshape(attended.shape), query, keys, values, dr1, grads,
    )
    same = jnp.arange(16)[:, None] == jnp.arange(16)[None, :]
    d_table = jnp.sum(jnp.where(same[None, :, None, :], counts.reshape(NB, 16, H, 16), 0.0), axis=(1, 3))
    eight = jnp.concatenate([dvec_qv[:2], dvec[2:8]])
    small = jnp.concatenate(
        [
            jnp.transpose(eight.reshape(8, shards, r), (1, 0, 2)).reshape(shards, 8 * r),
            dvec[8:].reshape(shards, 4 * r),
            jnp.broadcast_to(d_table.reshape(1, NB * H), (shards, NB * H)),
        ],
        axis=-1,
    )[:, None]
    sums, dx, tiny = reduce_grads(grads.reshape(UNITS * shards, r, width), dxs, small, shards, seqn)
    shape = (seqs, block, width)
    grad_content = (d_content + dx).reshape(shape)
    tiny = tiny[0]
    g_bq, g_bv, g_bo, g_g1, g_b1, g_c2, g_g2, g_b2 = (tiny[i * r : (i + 1) * r] for i in range(8))
    g_c1 = tiny[8 * r : 12 * r]
    g_table = tiny[12 * r :].reshape(NB, H)
    g_w1 = jnp.transpose(sums[4:8], (1, 0, 2)).reshape(r, 4 * width)
    g_w2 = sums[8:12].reshape(4 * r, width)
    return (
        y_c.reshape(shape), y_q.reshape(shape), grad_content, d_query_x.reshape(shape),
        sums[0], g_bq, sums[1], sums[2], g_bv, sums[3], g_bo, g_g1, g_b1,
        g_w1, g_c1, g_w2, g_c2, g_g2, g_b2, g_table,
    )


def solution(mesh):
    in_specs = (
        P("dp", "seq", None),
        P("dp", "seq", None),
        P("dp", "seq", None),
        P("dp", "seq", None),
        P("dp", None),
        P("dp"),
        P("dp", None),
        P("dp", None),
        P("dp"),
        P("dp", None),
        P("dp"),
        P("dp"),
        P("dp"),
        P("dp", None),
        P("dp"),
        P("dp", None),
        P("dp"),
        P("dp"),
        P("dp"),
        P(),
        P("dp"),
        P("dp", None),
        P("dp", "seq"),
    )
    out_specs = (
        P("dp", "seq", None),
        P("dp", "seq", None),
        P("dp", "seq", None),
        P("dp", "seq", None),
        P("dp", None),
        P("dp"),
        P("dp", None),
        P("dp", None),
        P("dp"),
        P("dp", None),
        P("dp"),
        P("dp"),
        P("dp"),
        P("dp", None),
        P("dp"),
        P("dp", None),
        P("dp"),
        P("dp"),
        P("dp"),
        P(),
    )
    return jax.shard_map(
        functools.partial(per_device, shards=mesh.shape["dp"], seqn=mesh.shape["seq"]),
        mesh=mesh, in_specs=in_specs, out_specs=out_specs, check_vma=False
    )
```

```python
import functools

import jax
import jax.numpy as jnp
from jax import lax
from jax.experimental import pallas as pl
from jax.experimental.pallas import tpu as pltpu
from jax.sharding import PartitionSpec as P

H = 12
HD = 64
NB = 32

MESH = pl.DeviceIdType.MESH
UNITS = 12


def cutter(rows_of):
    by_rows = rows_of % 96 == 0
    piece = rows_of // 6 if by_rows else 128

    def cut(start, size):
        if not isinstance(start, int):
            start = pl.multiple_of(start * piece, 16 if by_rows else 128)
        else:
            start = start * piece
        inner = pl.ds(start, size * piece)
        return (inner, slice(None)) if by_rows else (slice(None), inner)

    def shape(size):
        return (size * piece, 768) if by_rows else (rows_of, size * piece)

    return cut, shape


def place():
    dp, sq = lax.axis_index("dp"), lax.axis_index("seq")
    row, side = dp // 2, dp % 2
    deck, core = sq // 2, sq % 2
    return dp, sq, row, side, deck, core


def tile_of(unit, shard, shards):
    down = unit // 8
    return (1 - down) * (unit * shards + shard) + down * (8 * shards + shard * 4 + unit - 8)


def remote(src, dst, send, recv, device):
    return pltpu.make_async_remote_copy(
        src_ref=src, dst_ref=dst, send_sem=send, recv_sem=recv, device_id=device, device_id_type=MESH
    )


def greet_all(dp, sq, shards, seqn):
    barrier = pltpu.get_barrier_semaphore()

    def greet(step, carry):
        pl.semaphore_signal(barrier, inc=1, device_id=(lax.rem(dp + step, shards), sq), device_id_type=MESH)
        return carry

    def greet_seq(step, carry):
        pl.semaphore_signal(barrier, inc=1, device_id=(dp, lax.rem(sq + step, seqn)), device_id_type=MESH)
        return carry

    lax.fori_loop(1, shards, greet, 0)
    lax.fori_loop(1, seqn, greet_seq, 0)
    return barrier, shards + seqn - 2


AHEAD = 2


def gather_steps(shards, seqn, ins, outs, scratch):
    wk, wv, wq, wo, wu, wd, xc, vec = ins
    full, xall, vall = outs
    (own, xown, load_sem, keep_sem, zu_sem, zd_sem, xs_sem, ys_sem, cp_sem, cy_sem,
     zr_sem, xr_sem, yr_sem, cpr_sem, cyr_sem, xc_send, xc_recv, vec_send, vec_recv) = scratch
    dp, sq, row, side, deck, core = place()
    rows = shards // 2
    across = (row * 2 + 1 - side, sq)
    other_deck = (dp, (1 - deck) * 2 + core)
    sibling = (dp, deck * 2 + 1 - core)
    cut, _ = cutter(own.shape[1])
    plane = cut(core * 3 + deck, 2)
    solo = cut(core * 3 + deck * 2, 1)
    theirs = cut(core * 3 + (1 - deck) * 2, 1)

    def many(count, size):
        return full.at[(pl.ds(0, count),) + cut(0, size)]

    def part(unit, shard, piece):
        return full.at[(tile_of(unit, shard, shards),) + piece]

    pieces = [wk, wv, wq, wo] + [wu.at[:, pl.ds(j * 768, 768)] for j in range(4)] + [wd.at[j] for j in range(4)]
    loads = [pltpu.make_async_copy(piece, own.at[u], load_sem.at[u]) for u, piece in enumerate(pieces)]
    xload = pltpu.make_async_copy(xc, xown, load_sem.at[UNITS])
    keep_x = pltpu.make_async_copy(xown, xall.at[sq], keep_sem.at[UNITS])
    keep_vec = pltpu.make_async_copy(vec, vall.at[dp], keep_sem.at[UNITS + 1])
    x_deck = remote(xown, xall.at[sq], xc_send.at[0], xc_recv.at[0], other_deck)
    x_core = remote(xown, xall.at[sq], xc_send.at[1], xc_recv.at[1], sibling)
    x_theirs = xall.at[(1 - deck) * 2 + core]
    x_forward = remote(x_theirs, x_theirs, xc_send.at[2], xc_recv.at[2], sibling)

    def keep_copy(u):
        return pltpu.make_async_copy(own.at[u], full.at[tile_of(u, dp, shards)], keep_sem.at[u])

    up = ((row + 1) * 2 + side, sq)
    down = ((row - 1) * 2 + side, sq)

    def along(u, s, src):
        dst = part(u, s * 2 + side, plane)

        @pl.when((s <= row) & (row < rows - 1))
        def _():
            remote(src, dst, zu_sem.at[s], zr_sem.at[u, s], up).start()

        @pl.when((s >= row) & (row > 0))
        def _():
            remote(src, dst, zd_sem.at[s], zr_sem.at[u, s], down).start()

    def send_own(u):
        along(u, row, own.at[(u,) + plane])
        across_own(u)

    def across_own(u):
        remote(own.at[(u,) + plane], part(u, dp, plane), xs_sem, xr_sem.at[u], across).start()

    def to_deck(u, shard):
        ref = part(u, shard, solo)
        remote(ref, ref, ys_sem, yr_sem.at[u], other_deck).start()

    def to_core(u, shard):
        ref = part(u, shard, plane)
        remote(ref, ref, cp_sem, cpr_sem.at[u], sibling).start()

    def begin():
        barrier, count = greet_all(dp, sq, shards, seqn)
        for load in loads:
            load.start()
        xload.start()
        pl.semaphore_wait(barrier, count)

        def send_vec(step, carry):
            to = (lax.rem(dp + step, shards), sq)
            remote(vec, vall.at[dp], vec_send, vec_recv, to).start()
            return carry

        lax.fori_loop(1, shards, send_vec, 0)
        keep_vec.start()
        for load in loads:
            load.wait()

        def first(u, carry):
            send_own(u)
            return carry

        lax.fori_loop(0, AHEAD, first, 0)

        def keep(u, carry):
            keep_copy(u).start()
            return carry

        lax.fori_loop(0, UNITS, keep, 0)
        xload.wait()
        keep_x.start()
        x_deck.start()
        x_core.start()

    def step(n):
        @pl.when(n + AHEAD < UNITS)
        def _():
            send_own(n + AHEAD)

        def hop(t, carry):
            u = n - (t - 1)

            def arrived(s):
                ref = part(u, s * 2 + side, plane)
                remote(ref, ref, xs_sem, zr_sem.at[u, s], across).wait_recv()
                along(u, s, ref)
                remote(ref, ref, xs_sem, xr_sem.at[u], across).start()
                to_deck(u, s * 2 + side)
                to_core(u, s * 2 + side)

            @pl.when((u >= 0) & (u < UNITS))
            def _():
                pl.when(row - t >= 0)(lambda: arrived(row - t))
                pl.when(row + t < rows)(lambda: arrived(row + t))

            return carry

        lax.fori_loop(1, rows, hop, 0)
        ux = n - (rows - 1)

        @pl.when((ux >= 0) & (ux < UNITS))
        def _():
            remote(many(rows, 2), many(rows, 2), xs_sem, xr_sem.at[ux], across).wait_recv()

            def pass_on(s, carry):
                to_deck(ux, s * 2 + 1 - side)
                to_core(ux, s * 2 + 1 - side)
                return carry

            lax.fori_loop(0, rows, pass_on, 0)

        uy = n - rows

        @pl.when((uy >= 0) & (uy < UNITS))
        def _():
            remote(many(shards - 1, 1), many(shards - 1, 1), ys_sem, yr_sem.at[uy], other_deck).wait_recv()

            def pass_on(k, carry):
                ref = part(uy, lax.rem(dp + k, shards), theirs)
                remote(ref, ref, cy_sem, cyr_sem.at[uy], sibling).start()
                return carry

            lax.fori_loop(1, shards, pass_on, 0)

    def pass_x():
        x_deck.wait_recv()
        x_forward.start()

    def wait_x():
        x_core.wait_recv()
        x_forward.wait_recv()
        keep_x.wait()

    def wait_vec():
        keep_vec.wait()
        rest = vall.at[pl.ds(0, shards - 1)]
        remote(rest, rest, vec_send, vec_recv, sibling).wait_recv()

    def whole(u):
        remote(many(shards - 1, 2), many(shards - 1, 2), cp_sem, cpr_sem.at[u], sibling).wait_recv()
        remote(many(shards - 1, 1), many(shards - 1, 1), cy_sem, cyr_sem.at[u], sibling).wait_recv()
        keep_copy(u).wait()

    def finish():
        x_deck.wait_send()
        x_core.wait_send()
        x_forward.wait_send()
        rest = vall.at[pl.ds(0, shards - 1)]
        remote(rest, rest, vec_send, vec_recv, sibling).wait_send()
        for count, size, sem in (
            (UNITS * rows, 2, xs_sem),
            (UNITS * (shards - 1), 1, ys_sem),
            (UNITS * (shards - 1), 1, cy_sem),
            (UNITS * (shards - 1), 2, cp_sem),
        ):
            ref = many(count, size)
            remote(ref, ref, sem, xr_sem.at[0], sibling).wait_send()

        def sent(s, carry):
            ref = many(UNITS, 2)

            @pl.when((s <= row) & (row < rows - 1))
            def _():
                remote(ref, ref, zu_sem.at[s], xr_sem.at[0], sibling).wait_send()

            @pl.when((s >= row) & (row > 0))
            def _():
                remote(ref, ref, zd_sem.at[s], xr_sem.at[0], sibling).wait_send()

            return carry

        lax.fori_loop(0, rows, sent, 0)

    return begin, step, whole, pass_x, wait_x, wait_vec, finish


def gather_scratch(shards, rows_of, width, xshape):
    bf16 = jnp.bfloat16
    dma = pltpu.SemaphoreType.DMA
    return [
        pltpu.VMEM((UNITS, rows_of, width), bf16),
        pltpu.VMEM(xshape, bf16),
        dma((UNITS + 1,)),
        dma((UNITS + 2,)),
    ] + [dma((shards // 2,))] * 2 + [dma(())] * 4 + [dma((UNITS, shards // 2))] + [dma((UNITS,))] * 4 + [dma((3,)), dma((3,)), dma(()), dma(())]


GATHER_SCRATCH = 19


def reduce_steps(shards, seqn, rows_of, small, out, scratch):
    f32, bf16 = jnp.float32, jnp.bfloat16
    (acc, got_core, got_deck, got_across, line, got_line, final, got_final, half, got_half,
     got_small, mid_small, got_mid, got_all,
     load_sem, core_send, core_recv, deck_send, deck_recv, across_send, across_recv,
     line_send, line_recv, final_send, final_recv, half_send, half_recv,
     small_send, small_recv) = scratch
    dp, sq, row, side, deck, core = place()
    rows = shards // 2
    across = (row * 2 + 1 - side, sq)
    other_deck = (dp, (1 - deck) * 2 + core)
    sibling = (dp, deck * 2 + 1 - core)
    cut, _ = cutter(rows_of)
    mine = cut(core * 3, 3)
    siblings = cut((1 - core) * 3, 3)
    plane = cut(deck, 2)
    solo = cut(deck * 2, 1)
    other_solo = cut((1 - deck) * 2, 1)
    every = (slice(None), slice(None))

    def total(left, right):
        return (left.astype(f32) + right.astype(f32)).astype(bf16)

    def begin():
        barrier, count = greet_all(dp, sq, shards, seqn)
        pl.semaphore_wait(barrier, count)

    def send_unit(u, tiles):
        def one(s, carry):
            for b in range(2):
                tile = tiles(s * 2 + b)
                remote(
                    tile.at[siblings], got_core.at[u, s, b], core_send.at[u], core_recv.at[u], sibling
                ).start()
                pltpu.make_async_copy(tile.at[mine], acc.at[u, s, b], load_sem.at[u]).start()
            return carry

        lax.fori_loop(0, rows, one, 0)

    def copy_of(kind, u):
        if kind == "core":
            return remote(got_core.at[u], got_core.at[u], core_send.at[u], core_recv.at[u], sibling)
        if kind == "deck":
            src = acc.at[(u,) + every + other_solo]
            return remote(src, got_deck.at[u], deck_send.at[u], deck_recv.at[u], other_deck)
        if kind == "across":
            src = acc.at[(u, slice(None), 1 - side) + plane]
            return remote(src, got_across.at[u], across_send.at[u], across_recv.at[u], across)
        if kind == "line":
            ref = got_line.at[u, pl.ds(0, rows - 1)]
            return remote(ref, ref, line_send.at[u], line_recv.at[u], across)
        if kind == "final":
            return remote(final.at[u], got_final.at[u], final_send.at[u], final_recv.at[u], other_deck)
        return remote(half.at[u], got_half.at[u], half_send.at[u], half_recv.at[u], sibling)

    def stage_core(u):
        pltpu.make_async_copy(acc.at[u], acc.at[u], load_sem.at[u]).wait()
        copy_of("core", u).wait_recv()

        def add(s, carry):
            for b in range(2):
                acc[u, s, b] = total(acc[u, s, b], got_core[u, s, b])
            return carry

        lax.fori_loop(0, rows, add, 0)
        copy_of("deck", u).start()

    def stage_deck(u):
        copy_of("deck", u).wait_recv()

        def add(s, carry):
            for b in range(2):
                at = (u, s, b) + solo
                acc[at] = total(acc[at], got_deck[u, s, b])
            return carry

        lax.fori_loop(0, rows, add, 0)
        copy_of("across", u).start()

    def stage_across(u):
        copy_of("across", u).wait_recv()

        def add(k, carry):
            s = lax.rem(row + k, rows)
            line[u, s] = total(acc[(u, s, side) + plane], got_across[u, s])

            @pl.when(k < rows)
            def _():
                remote(
                    line.at[u, s], got_line.at[u, rows - 1 - k], line_send.at[u], line_recv.at[u], (s * 2 + side, sq)
                ).start()

            return carry

        lax.fori_loop(1, rows + 1, add, 0)

    def stage_line(u):
        copy_of("line", u).wait_recv()
        summed = line[u, row].astype(f32)
        if rows <= 4:
            for k in range(rows - 1):
                summed = summed + got_line[u, k].astype(f32)
        else:
            summed = lax.fori_loop(0, rows - 1, lambda k, t: t + got_line[u, k].astype(f32), summed)
        final[u] = summed.astype(bf16)
        copy_of("final", u).start()

    def stage_final(u):
        copy_of("final", u).wait_recv()
        half[(u,) + plane] = final[u]
        half[(u,) + other_solo] = got_final[(u,) + cut(1 - deck, 1)]
        both = (u,) + cut(1, 1)
        half[both] = total(half[both], got_final[(u,) + cut(deck, 1)])
        copy_of("half", u).start()

    def stage_half(u):
        copy_of("half", u).wait_recv()
        out[(u,) + mine] = half[u].astype(f32)
        out[(u,) + siblings] = got_half[u].astype(f32)

    stages = (stage_core, stage_deck, stage_across, stage_line, stage_final, stage_half)

    def step(n, order):
        for i, stage in enumerate(stages):

            @pl.when((n - i >= 0) & (n - i < UNITS))
            def _(i=i, stage=stage):
                stage(order(n - i))

    def small_first():
        got_small[dp] = small[dp]

        def send(k, carry):
            to = lax.rem(dp + k, shards)
            remote(small.at[to], got_small.at[dp], small_send.at[0], small_recv.at[0], (to, sq)).start()
            return carry

        lax.fori_loop(1, shards, send, 0)

    def sum_of(ref, count):
        summed = ref[0]
        for i in range(1, count):
            summed = summed + ref[i]
        return summed

    def small_second():
        rest = got_small.at[pl.ds(0, shards - 1)]
        remote(rest, rest, small_send.at[0], small_recv.at[0], sibling).wait()
        summed = sum_of(got_small, shards)
        mid_small[0] = summed
        got_mid[sq] = summed

        def send(k, carry):
            to = (dp, lax.rem(sq + k, seqn))
            remote(mid_small.at[0], got_mid.at[sq], small_send.at[1], small_recv.at[1], to).start()
            return carry

        lax.fori_loop(1, seqn, send, 0)

    def small_third():
        rest = got_mid.at[pl.ds(0, seqn - 1)]
        remote(rest, rest, small_send.at[1], small_recv.at[1], sibling).wait()
        summed = sum_of(got_mid, seqn)
        mid_small[1] = summed
        got_all[dp] = summed

        def send(k, carry):
            to = (lax.rem(dp + k, shards), sq)
            remote(mid_small.at[1], got_all.at[dp], small_send.at[2], small_recv.at[2], to).start()
            return carry

        lax.fori_loop(1, shards, send, 0)

    def small_last(small_out):
        rest = got_all.at[pl.ds(0, shards - 1)]
        remote(rest, rest, small_send.at[2], small_recv.at[2], sibling).wait()
        small_out[...] = got_all[...]

    def finish():
        def sent(u, carry):
            for kind in ("core", "deck", "across", "line", "final", "half"):
                copy_of(kind, u).wait_send()
            return carry

        lax.fori_loop(0, UNITS, sent, 0)

    return begin, send_unit, step, (small_first, small_second, small_third, small_last), finish


REDUCE_STAGES = 6
REDUCE_SCRATCH = 29


def reduce_scratch(shards, seqn, rows_of, small_shape):
    f32, bf16 = jnp.float32, jnp.bfloat16
    rows = shards // 2
    _, shape = cutter(rows_of)
    dma = pltpu.SemaphoreType.DMA
    return (
        [
            pltpu.VMEM((UNITS, rows, 2) + shape(3), bf16),
            pltpu.VMEM((UNITS, rows, 2) + shape(3), bf16),
            pltpu.VMEM((UNITS, rows, 2) + shape(1), bf16),
            pltpu.VMEM((UNITS, rows) + shape(2), bf16),
            pltpu.VMEM((UNITS, rows) + shape(2), bf16),
            pltpu.VMEM((UNITS, rows) + shape(2), bf16),
            pltpu.VMEM((UNITS,) + shape(2), bf16),
            pltpu.VMEM((UNITS,) + shape(2), bf16),
            pltpu.VMEM((UNITS,) + shape(3), bf16),
            pltpu.VMEM((UNITS,) + shape(3), bf16),
            pltpu.VMEM(small_shape, f32),
            pltpu.VMEM((2,) + small_shape[1:], f32),
            pltpu.VMEM((seqn,) + small_shape[1:], f32),
            pltpu.VMEM(small_shape, f32),
        ]
        + [dma((UNITS,))] * 13
        + [dma((3,))] * 2
    )


def dx_steps(dxs, scratch):
    f32, bf16 = jnp.float32, jnp.bfloat16
    dx_own, dx_core, dx_deck, load, send, recv = scratch
    dp, sq, row, side, deck, core = place()
    other_deck = (dp, (1 - deck) * 2 + core)
    sibling = (dp, deck * 2 + 1 - core)
    deck_dx = remote(dx_own.at[1 - deck], dx_deck, send.at[2], recv.at[2], other_deck)

    def first():
        for k in range(2):
            pltpu.make_async_copy(dxs.at[k * 2 + core], dx_own.at[k], load.at[k]).start()
            remote(dxs.at[k * 2 + 1 - core], dx_core.at[k], send.at[k], recv.at[k], sibling).start()

    def second():
        for k in range(2):
            pltpu.make_async_copy(dx_own.at[k], dx_own.at[k], load.at[k]).wait()
            remote(dx_core.at[k], dx_core.at[k], send.at[k], recv.at[k], sibling).wait()
            dx_own[k] = (dx_own[k].astype(f32) + dx_core[k].astype(f32)).astype(bf16)
        deck_dx.start()

    def third(dx_out):
        deck_dx.wait()
        dx_out[...] = dx_own[deck].astype(f32) + dx_deck[...].astype(f32)

    return first, second, third


def dx_scratch(own):
    bf16 = jnp.bfloat16
    dma = pltpu.SemaphoreType.DMA
    return [pltpu.VMEM((2,) + own, bf16), pltpu.VMEM((2,) + own, bf16), pltpu.VMEM(own, bf16), dma((2,)), dma((3,)), dma((3,))]


bucket_marks = (12, 16, 23, 32, 46, 64, 91)
MASKED = NB
TN = (((0,), (0,)), ((), ()))
NT = (((1,), (1,)), ((), ()))


def dot(left, right, dims=None):
    if dims is None:
        dims = (((1,), (0,)), ((), ()))
    return lax.dot_general(left, right, dims, preferred_element_type=jnp.float32)


def fill_buckets(buckets, pos_rows, pos_cols, lengths, base, seqs, block, span):
    for s in range(seqs):
        delta = pos_cols[s : s + 1, :] - pos_rows[s]
        dist = jnp.abs(delta)
        far = jnp.full(dist.shape, 8, jnp.int32)
        for mark in bucket_marks:
            far = far + (dist >= mark).astype(jnp.int32)
        bucket = jnp.where(dist < 8, dist, far) + 16 * (delta > 0).astype(jnp.int32)
        i = base + lax.broadcasted_iota(jnp.int32, (block, span), 0)
        j = lax.broadcasted_iota(jnp.int32, (block, span), 1)
        valid = j < lengths[s]
        buckets[s, 0] = jnp.where(valid & (j <= i), bucket, MASKED)
        buckets[s, 1] = jnp.where(valid & (j < jnp.maximum(i, 1)), bucket, MASKED)


def head_lanes(rows, half):
    lane = lax.broadcasted_iota(jnp.int32, (rows, 2 * HD), 1)
    return (lane < HD) if half == 0 else (lane >= HD)


def attend_pair(i, refs, block, span, low_out):
    attended, query, keys, values, buckets, table = refs
    f32, bf16 = jnp.float32, jnp.bfloat16
    pairs = H // 2
    s, pair = i // pairs, lax.rem(i, pairs)
    lanes = pl.ds(pl.multiple_of(pair * 128, 128), 128)
    q = query[:, s, :, lanes].reshape(2 * block, 128)
    k = keys[s, :, lanes]
    v = values[s, :, lanes]
    outs = []
    for half in range(2):
        entry = jnp.broadcast_to(table[pl.ds(pair * 2 + half, 1), :], (block, 128))
        bias = jnp.concatenate(
            [
                jnp.concatenate(
                    [
                        jnp.take_along_axis(entry, buckets[s, t, :, pl.ds(c * 128, 128)], axis=1, mode="promise_in_bounds")
                        for c in range(span // 128)
                    ],
                    axis=1,
                )
                for t in range(2)
            ],
            axis=0,
        )
        mine = head_lanes(2 * block, half)
        one = jnp.where(mine, q * 0.125, 0).astype(bf16)
        scores = dot(one, k, NT) + bias
        top = jnp.max(scores, axis=-1, keepdims=True)
        expo = jnp.exp(scores - top)
        low = (expo * (1.0 / jnp.sum(expo, axis=-1, keepdims=True))).astype(bf16)
        low_out[half] = low
        outs.append(dot(low, v))
    mixed = jnp.where(head_lanes(2 * block, 0), outs[0], outs[1]).astype(bf16)
    attended[:, s, :, lanes] = mixed.reshape(2, block, 128)


EARLY = 8


def forward_kernel(
    shards, seqn, seqs, block, span,
    lengths, wk, wv, wq, wo, wu, wd, xc, xc_rows, xq_rows, table, pos_rows, pos_cols,
    bq, bv, bo, g1, b1, c2, g2, b2, c1,
    full, xall, vall, probs, attended, query, keys, values,
    buckets, w, x_every, v_every, low_two, vec, io_sem, low_sem, *scratch,
):
    f32, bf16 = jnp.float32, jnp.bfloat16
    width = H * HD
    r = vec.shape[1]
    for i, piece in enumerate((bq, bv, bo, g1, b1, c2, g2, b2)):
        vec[i : i + 1, :] = piece[...].astype(f32)
    vec[8:12, :] = c1[...].astype(f32)
    begin, step, whole, pass_x, wait_x, wait_vec, finish = gather_steps(
        shards, seqn, (wk, wv, wq, wo, wu, wd, xc, vec), (full, xall, vall), scratch
    )
    begin()
    fill_buckets(buckets, pos_rows, pos_cols, lengths, lax.axis_index("seq") * block, seqs, block, span)

    def one(n, carry):
        step(n)
        return carry

    lax.fori_loop(0, EARLY - 2, one, 0)
    pass_x()
    lax.fori_loop(EARLY - 2, EARLY, one, 0)
    wait_x()
    wait_vec()
    take_x = pltpu.make_async_copy(xall, x_every, io_sem.at[3])
    take_v = pltpu.make_async_copy(vall, v_every, io_sem.at[4])
    take_x.start()
    take_v.start()

    def take(u):
        return pltpu.make_async_copy(full.at[pl.ds(u * shards, shards)], w.at[u], io_sem.at[u])

    for u in range(3):
        whole(u)
        take(u).start()
    take_v.wait()

    def spread(i, carry):
        row = lax.broadcasted_iota(jnp.int32, (r, width), 0)
        col = lax.broadcasted_iota(jnp.int32, (r, width), 1)
        at = jnp.where(col == row + i * r, 1.0, 0.0).astype(bf16)
        return carry + dot(v_every[i].astype(bf16), at)

    biases = lax.fori_loop(0, shards, spread, jnp.zeros((UNITS, width), f32))
    take_x.wait()

    def matrix(u):
        return w[u].reshape(width, width)

    def project(k, carry):
        rows = x_every[k].reshape(seqs * block, width)
        at = pl.ds(pl.multiple_of(k * block, block), block)
        keys[:, at, :] = dot(rows, matrix(0)).astype(bf16).reshape(seqs, block, width)
        values[:, at, :] = (dot(rows, matrix(1)) + biases[1:2, :]).astype(bf16).reshape(seqs, block, width)
        return carry

    for u in range(3):
        take(u).wait()
    lax.fori_loop(0, seqn, project, 0)
    for t, x in enumerate((xc_rows, xq_rows)):
        rows = x[...].reshape(seqs * block, width)
        query[t] = (dot(rows, matrix(2)) + biases[0:1, :]).astype(bf16).reshape(seqs, block, width)

    total = seqs * H // 2

    def put(i, slot):
        return pltpu.make_async_copy(low_two.at[slot], probs.at[i], low_sem.at[slot])

    def attend_one(i, carry):
        slot = lax.rem(i, 2)

        @pl.when(EARLY + i < UNITS + shards // 2)
        def _():
            step(EARLY + i)

        @pl.when(i >= 2)
        def _():
            put(i - 2, slot).wait()

        attend_pair(i, (attended, query, keys, values, buckets, table), block, span, low_two.at[slot])
        put(i, slot).start()
        return carry

    lax.fori_loop(0, total, attend_one, 0)
    lax.fori_loop(EARLY + total, UNITS + shards // 2, one, 0)
    put(total - 2, lax.rem(total - 2, 2)).wait()
    put(total - 1, lax.rem(total - 1, 2)).wait()

    def last(u, carry):
        whole(u)
        return carry

    lax.fori_loop(3, UNITS, last, 0)
    finish()


def forward(wk, wv, wq, wo, wu, wd, xc, xq, vecs, lengths, table, pos_rows, pos_cols, shards, seqn):
    rows_of, width = wq.shape
    seqs, block, _ = xc.shape
    span = pos_cols.shape[1]
    f32, bf16 = jnp.float32, jnp.bfloat16
    steps = seqs * H // 2
    anywhere = pl.BlockSpec(memory_space=pl.ANY)
    vmem = pl.BlockSpec(memory_space=pltpu.VMEM)
    rows = shards // 2
    dma = pltpu.SemaphoreType.DMA
    return pl.pallas_call(
        functools.partial(forward_kernel, shards, seqn, seqs, block, span),
        out_shape=(
            jax.ShapeDtypeStruct((UNITS * shards, rows_of, width), bf16),
            jax.ShapeDtypeStruct((seqn,) + xc.shape, bf16),
            jax.ShapeDtypeStruct((shards, UNITS, rows_of), f32),
            jax.ShapeDtypeStruct((steps, 2, 2 * block, span), bf16),
            jax.ShapeDtypeStruct((2, seqs, block, width), bf16),
            jax.ShapeDtypeStruct((2, seqs, block, width), bf16),
            jax.ShapeDtypeStruct((seqs, span, width), bf16),
            jax.ShapeDtypeStruct((seqs, span, width), bf16),
        ),
        in_specs=[pl.BlockSpec(memory_space=pltpu.SMEM)] + [anywhere] * 7 + [vmem] * 14,
        out_specs=(anywhere,) * 4 + (vmem,) * 4,
        scratch_shapes=[
            pltpu.VMEM((seqs, 2, block, span), jnp.int32),
            pltpu.VMEM((3, shards, rows_of, width), bf16),
            pltpu.VMEM((seqn,) + xc.shape, bf16),
            pltpu.VMEM((shards, UNITS, rows_of), f32),
            pltpu.VMEM((2, 2, 2 * block, span), bf16),
            pltpu.VMEM((UNITS, rows_of), f32),
            dma((5,)),
            dma((2,)),
        ]
        + gather_scratch(shards, rows_of, width, xc.shape),
        compiler_params=pltpu.CompilerParams(
            collective_id=0, has_side_effects=True, vmem_limit_bytes=60 * 1024 * 1024
        ),
        name="gather_attend",
    )(lengths, wk, wv, wq, wo, wu, wd.reshape(4, rows_of, width), xc, xc, xq, table, pos_rows, pos_cols, *vecs)


def center_of(value):
    center = value - jnp.mean(value, axis=-1, keepdims=True)
    var = jnp.mean(center * center, axis=-1, keepdims=True)
    inv = lax.rsqrt(var + 1e-05)
    return center * inv, inv


def norm_back(grad, gain, normed, inv):
    scaled = grad * gain
    return inv * (
        scaled
        - jnp.mean(scaled, axis=-1, keepdims=True)
        - normed * jnp.mean(scaled * normed, axis=-1, keepdims=True)
    )


def middle_kernel(
    seqs, block,
    attended, xc, xq, cot_c, cot_q, keep, vectors, weights,
    y_c, y_q, dr1_out, da_out, grads, dvec,
    w, hidden, hidden_low, hidden_turn, normed1, inv1, active, slope, feed, dr2, dr2_low, du_low, dr1_low, y, stage,
    w_sem, y_sem, stage_sem, dr1_sem,
):
    f32, bf16 = jnp.float32, jnp.bfloat16
    width = H * HD
    half = seqs * block
    rows = 2 * half
    chunk = 128
    loads = [pltpu.make_async_copy(weights.at[3 + i], w.at[i], w_sem.at[i]) for i in range(9)]
    for load in loads:
        load.start()
    dvec[...] = jnp.zeros_like(dvec)
    vec = lambda i: vectors[i : i + 1, :]

    loads[0].wait()

    def phase_one(c, carry):
        at = pl.ds(pl.multiple_of(c * chunk, chunk), chunk)
        out = dot(attended[at, :], w[0]) + vec(2)

        def from_x(x):
            return x[pl.ds(pl.multiple_of(lax.rem(c, half // chunk) * chunk, chunk), chunk), :].astype(f32)

        x = jnp.where(c < half // chunk, from_x(xc), from_x(xq))
        normed, inv = center_of(x + out)
        normed1[at, :] = normed
        inv1[at, :] = inv
        h = normed * vec(3) + vec(4)
        hidden[at, :] = h
        hidden_low[at, :] = h.astype(bf16)
        return carry

    lax.fori_loop(0, rows // chunk, phase_one, 0)
    hidden_turn[...] = hidden_low[...].T

    tile = 256
    tiles = width // tile
    for j in range(4):
        loads[1 + j].wait()

    def phase_two(step, carry):
        j, n = step // tiles, lax.rem(step, tiles)
        cols = pl.ds(pl.multiple_of(n * tile, tile), tile)
        u = dot(hidden_low[...], w[1 + j, :, cols]) + vectors[pl.ds(8 + j, 1), cols]
        cdf = 0.5 * (1.0 + lax.erf(u * (2.0**-0.5)))
        active[j, :, cols] = (u * cdf).astype(bf16)
        slope[j, :, cols] = cdf + u * (jnp.exp(-0.5 * u * u) * ((2.0 * jnp.pi) ** -0.5))
        return carry

    lax.fori_loop(0, 4 * tiles, phase_two, 0)
    for j in range(4):
        loads[5 + j].wait()

    def phase_feed(n, carry):
        cols = pl.ds(pl.multiple_of(n * tile, tile), tile)
        feed[:, cols] = sum(dot(active[j], w[5 + j, :, cols]) for j in range(4))
        return carry

    lax.fori_loop(0, tiles, phase_feed, 0)

    def phase_three(c, carry):
        at = pl.ds(pl.multiple_of(c * chunk, chunk), chunk)
        normed, inv = center_of(hidden[at, :] + feed[at, :] + vec(5))
        kept = keep[at, :]
        y[at, :] = (normed * vec(6) + vec(7)) * kept
        inner = pl.ds(pl.multiple_of(lax.rem(c, half // chunk) * chunk, chunk), chunk)
        cot = jnp.where(c < half // chunk, cot_c[inner, :].astype(f32), cot_q[inner, :].astype(f32)) * kept
        d = norm_back(cot, vec(6), normed, inv)
        dvec[6:7, :] += jnp.sum(cot * normed, axis=0, keepdims=True)
        dvec[7:8, :] += jnp.sum(cot, axis=0, keepdims=True)
        dvec[5:6, :] += jnp.sum(d, axis=0, keepdims=True)
        dr2[at, :] = d
        dr2_low[at, :] = d.astype(bf16)
        return carry

    lax.fori_loop(0, rows // chunk, phase_three, 0)
    y_copies = [
        pltpu.make_async_copy(y.at[pl.ds(0, half)], y_c, y_sem.at[0]),
        pltpu.make_async_copy(y.at[pl.ds(half, half)], y_q, y_sem.at[1]),
    ]
    for copy in y_copies:
        copy.start()

    def phase_four(step, carry):
        j, n = step // tiles, lax.rem(step, tiles)
        cols = pl.ds(pl.multiple_of(n * tile, tile), tile)
        du = slope[j, :, cols] * dot(dr2_low[...], w[5 + j, cols, :], NT)
        dvec[pl.ds(8 + j, 1), cols] = jnp.sum(du, axis=0, keepdims=True)
        low = du.astype(bf16)
        du_low[j, :, cols] = low
        stage[j, :, cols] = dot(hidden_turn[...], low).astype(bf16)
        stage[4 + j, cols, :] = dot(active[j, :, cols], dr2_low[...], TN).astype(bf16)

        @pl.when(n == tiles - 1)
        def _():
            pltpu.make_async_copy(stage.at[j], grads.at[4 + j], stage_sem.at[j]).start()
            pltpu.make_async_copy(stage.at[4 + j], grads.at[8 + j], stage_sem.at[4 + j]).start()

        return carry

    lax.fori_loop(0, 4 * tiles, phase_four, 0)

    def phase_hidden(n, carry):
        cols = pl.ds(pl.multiple_of(n * tile, tile), tile)
        dr2[:, cols] += sum(dot(du_low[j], w[1 + j, cols, :], NT) for j in range(4))
        return carry

    lax.fori_loop(0, tiles, phase_hidden, 0)
    for copy in y_copies:
        copy.wait()

    def phase_five(c, carry):
        at = pl.ds(pl.multiple_of(c * chunk, chunk), chunk)
        dh = dr2[at, :]
        normed = normed1[at, :]
        d = norm_back(dh, vec(3), normed, inv1[at, :])
        dvec[3:4, :] += jnp.sum(dh * normed, axis=0, keepdims=True)
        dvec[4:5, :] += jnp.sum(dh, axis=0, keepdims=True)
        dvec[2:3, :] += jnp.sum(d, axis=0, keepdims=True)
        y[at, :] = d
        low = d.astype(bf16)
        dr1_low[at, :] = low
        da_out[at, :] = dot(low, w[0], NT).astype(bf16)
        return carry

    lax.fori_loop(0, rows // chunk, phase_five, 0)
    dr1_copy = pltpu.make_async_copy(y, dr1_out, dr1_sem)
    dr1_copy.start()

    def phase_out(n, carry):
        cols = pl.ds(pl.multiple_of(n * tile, tile), tile)
        stage[8, cols, :] = dot(attended[:, cols], dr1_low[...], TN).astype(bf16)
        return carry

    lax.fori_loop(0, tiles, phase_out, 0)
    last = pltpu.make_async_copy(stage.at[8], grads.at[3], stage_sem.at[8])
    last.start()
    for j in range(8):
        pltpu.make_async_copy(stage.at[j], grads.at[4 + j], stage_sem.at[j]).wait()
    last.wait()
    dr1_copy.wait()


def middle(attended, xc, xq, cot_c, cot_q, keep, vectors, weights):
    seqs, block, width = xc.shape
    f32, bf16 = jnp.float32, jnp.bfloat16
    half = seqs * block
    rows = 2 * half
    vmem = pl.BlockSpec(memory_space=pltpu.VMEM)
    anywhere = pl.BlockSpec(memory_space=pl.ANY)
    flat = lambda a: a.reshape(half, width)
    return pl.pallas_call(
        functools.partial(middle_kernel, seqs, block),
        out_shape=(
            jax.ShapeDtypeStruct((half, width), f32),
            jax.ShapeDtypeStruct((half, width), f32),
            jax.ShapeDtypeStruct((rows, width), f32),
            jax.ShapeDtypeStruct((rows, width), bf16),
            jax.ShapeDtypeStruct((UNITS, width, width), bf16),
            jax.ShapeDtypeStruct((UNITS, width), f32),
        ),
        in_specs=[vmem] * 7 + [anywhere],
        out_specs=(anywhere, anywhere, anywhere, vmem, anywhere, vmem),
        scratch_shapes=[
            pltpu.VMEM((9, width, width), bf16),
            pltpu.VMEM((rows, width), f32),
            pltpu.VMEM((rows, width), bf16),
            pltpu.VMEM((width, rows), bf16),
            pltpu.VMEM((rows, width), f32),
            pltpu.VMEM((rows, 1), f32),
            pltpu.VMEM((4, rows, width), bf16),
            pltpu.VMEM((4, rows, width), f32),
            pltpu.VMEM((rows, width), f32),
            pltpu.VMEM((rows, width), f32),
            pltpu.VMEM((rows, width), bf16),
            pltpu.VMEM((4, rows, width), bf16),
            pltpu.VMEM((rows, width), bf16),
            pltpu.VMEM((rows, width), f32),
            pltpu.VMEM((9, width, width), bf16),
            pltpu.SemaphoreType.DMA((9,)),
            pltpu.SemaphoreType.DMA((2,)),
            pltpu.SemaphoreType.DMA((9,)),
            pltpu.SemaphoreType.DMA(()),
        ],
        compiler_params=pltpu.CompilerParams(vmem_limit_bytes=63 * 1024 * 1024),
        name="middle",
    )(attended, flat(xc), flat(xq), flat(cot_c), flat(cot_q), keep, vectors, weights)


def attend_back_pair(i, refs, low, seqs, block, span):
    attended, d_attended, query, keys, values, buckets, dq, dk, dv, ds_sum, sums, counts = refs
    f32, bf16 = jnp.float32, jnp.bfloat16
    pairs = H // 2
    rows = 2 * block
    s, pair = i // pairs, lax.rem(i, pairs)
    lanes = pl.ds(pl.multiple_of(pair * 128, 128), 128)
    q = query[:, s, :, lanes].reshape(rows, 128)
    k = keys[s, :, lanes]
    v = values[s, :, lanes]
    da = d_attended[:, s, :, lanes].reshape(rows, 128)
    product = da.astype(f32) * attended[:, s, :, lanes].reshape(rows, 128).astype(f32)
    d_queries, dk_turn, dv_turn = [], 0.0, 0.0
    for half in range(2):
        mine = head_lanes(rows, half)
        one = jnp.where(mine, da, 0).astype(bf16)
        inner = jnp.sum(jnp.where(mine, product, 0.0), axis=-1, keepdims=True)
        ds = low[half].astype(f32) * (dot(one, v, NT) - inner)
        ds_sum[pair * 2 + half] = (ds[:block] + ds[block:]).astype(bf16)
        ds_low = ds.astype(bf16)
        d_queries.append(dot(ds_low, k))
        dk_turn += dot(jnp.where(mine, q, 0).astype(bf16), ds_low, TN)
        dv_turn += dot(one, low[half], TN)
    d_query = jnp.where(head_lanes(rows, 0), d_queries[0], d_queries[1]) * 0.125
    sums[0:1, lanes] += jnp.sum(d_query, axis=0, keepdims=True)
    dq[:, s, :, lanes] = d_query.reshape(2, block, 128).astype(bf16)
    dk[s, :, lanes] = (dk_turn * 0.125).T.astype(bf16)
    d_value = dv_turn.T
    sums[1:2, lanes] += jnp.sum(d_value, axis=0, keepdims=True)
    dv[s, :, lanes] = d_value.astype(bf16)

    @pl.when(pair == pairs - 1)
    def _():
        def count(g, carry):
            at = pl.ds(pl.multiple_of(g * 16, 16), 16)
            bucket = buckets[s, 0, at, :]
            hot = jnp.concatenate([jnp.where(bucket == n, 1.0, 0.0).astype(bf16) for n in range(NB)], axis=0)
            counts[...] += dot(hot, ds_sum[:, at, :].reshape(H * 16, span), NT)
            return carry

        lax.fori_loop(0, block // 16, count, 0)


def table_of(counts):
    row = lax.broadcasted_iota(jnp.int32, counts.shape, 0)
    col = lax.broadcasted_iota(jnp.int32, counts.shape, 1)
    kept = jnp.where(lax.rem(row, 16) == lax.rem(col, 16), counts, 0.0)
    folded = jnp.sum(kept.reshape(NB, 16, H * 16), axis=1)
    lane = lax.broadcasted_iota(jnp.int32, (H * 16, 128), 1)
    head = lax.broadcasted_iota(jnp.int32, (H * 16, 128), 0) // 16
    return jnp.dot(folded, jnp.where(lane == head, 1.0, 0.0), precision=lax.Precision.HIGHEST)


READY = 9


def backward_kernel(
    shards, seqn, seqs, block, span, rows_of,
    lengths, grads, full, xall, probs, attended_in, da_in, query_in, keys_in, values_in, dr1_in,
    xc, xq, dvec, pos_rows, pos_cols,
    out, dx_out, d_content, d_query_x, small_out,
    dq, dk, dv, late, w, x_every, dxs, sums, counts, small, io_sem, low_sem, *scratch,
):
    f32, bf16 = jnp.float32, jnp.bfloat16
    width = H * HD
    half = seqs * block
    total = seqs * H // 2
    begin, send_unit, step, (small_first, small_second, small_third, small_last), finish = reduce_steps(
        shards, seqn, rows_of, small, out, scratch[:REDUCE_SCRATCH]
    )
    dx_first, dx_second, dx_third = dx_steps(dxs, scratch[REDUCE_SCRATCH:])
    order = lambda k: UNITS - 1 - k
    weights = [pltpu.make_async_copy(full.at[pl.ds(u * shards, shards)], w.at[u], io_sem.at[5 + u]) for u in range(3)]
    slots = [
        pltpu.make_async_copy(xall.at[k], x_every.at[:, pl.ds(k * block, block)], io_sem.at[8 + k]) for k in range(seqn)
    ]

    def one(n, carry):
        step(n, order)
        return carry

    def attention(attended, d_attended, query, keys, values, buckets, low_two, ds_sum):
        loads = [
            pltpu.make_async_copy(src, dst, io_sem.at[i])
            for i, (src, dst) in enumerate(
                ((attended_in, attended), (da_in, d_attended), (query_in, query), (keys_in, keys), (values_in, values))
            )
        ]

        def take(i, slot):
            return pltpu.make_async_copy(probs.at[i], low_two.at[slot], low_sem.at[slot])

        for load in loads:
            load.start()
        take(0, 0).start()
        for load in weights + slots:
            load.start()
        begin()

        def send(k, carry):
            u = order(k)
            send_unit(u, lambda shard: grads.at[tile_of(u, shard, shards)])
            return carry

        lax.fori_loop(0, READY, send, 0)
        fill_buckets(buckets, pos_rows, pos_cols, lengths, lax.axis_index("seq") * block, seqs, block, span)
        counts[...] = jnp.zeros_like(counts)
        sums[...] = jnp.zeros_like(sums)
        for load in loads:
            load.wait()
        refs = (attended, d_attended, query, keys, values, buckets, dq, dk, dv, ds_sum, sums, counts)

        def pair(i, carry):
            slot = lax.rem(i, 2)

            @pl.when(lax.rem(i, 2) == 0)
            def _():
                step(i // 2, order)

            take(i, slot).wait()

            @pl.when(i + 1 < total)
            def _():
                take(i + 1, 1 - slot).start()

            attend_back_pair(i, refs, low_two.at[slot], seqs, block, span)
            return carry

        lax.fori_loop(0, total, pair, 0)

    pl.run_scoped(
        attention,
        pltpu.VMEM((2, seqs, block, width), bf16),
        pltpu.VMEM((2, seqs, block, width), bf16),
        pltpu.VMEM((2, seqs, block, width), bf16),
        pltpu.VMEM((seqs, span, width), bf16),
        pltpu.VMEM((seqs, span, width), bf16),
        pltpu.VMEM((seqs, 2, block, span), jnp.int32),
        pltpu.VMEM((2, 2, 2 * block, span), bf16),
        pltpu.VMEM((H, block, span), bf16),
    )

    tile = 256

    def send_late(u):
        send_unit(u, lambda shard: late.at[u, shard])

    def weight_grads(dr1, turned, x_two):
        load = pltpu.make_async_copy(dr1_in, dr1, io_sem.at[0])
        load.start()
        loads = [pltpu.make_async_copy(x, x_two.at[t], io_sem.at[1 + t]) for t, x in enumerate((xc, xq))]
        for copy in loads:
            copy.start()
        for copy in weights + slots:
            copy.wait()
        matrix = lambda u: w[u].reshape(width, width)
        turned[...] = x_every[...].reshape(seqs * span, width).T

        def late_from(u, ref):
            def tiles(n, carry):
                cols = pl.ds(pl.multiple_of(n * tile, tile), tile)
                grad = dot(turned[...], ref[:, :, cols].reshape(seqs * span, tile))
                late[u, :, :, cols] = grad.astype(bf16).reshape(shards, rows_of, tile)
                return carry

            lax.fori_loop(0, width // tile, tiles, 0)
            send_late(u)

        late_from(0, dk)
        step(6, order)
        late_from(1, dv)

        def every(n, carry):
            s, k = n // seqn, lax.rem(n, seqn)
            at = pl.ds(pl.multiple_of(k * block, block), block)
            part = dot(dk[s, at, :], matrix(0), NT) + dot(dv[s, at, :], matrix(1), NT)
            dxs[k, pl.ds(pl.multiple_of(s * block, block), block), :] = part.astype(bf16)
            return carry

        lax.fori_loop(0, seqs * seqn, every, 0)
        dx_first()
        step(7, order)
        for copy in loads:
            copy.wait()

        def tiles(n, carry):
            cols = pl.ds(pl.multiple_of(n * tile, tile), tile)
            grad = sum(
                dot(x_two[t].reshape(half, width), dq[t, :, :, cols].reshape(half, tile), TN) for t in range(2)
            )
            late[2, :, :, cols] = grad.astype(bf16).reshape(shards, rows_of, tile)
            return carry

        lax.fori_loop(0, width // tile, tiles, 0)
        send_late(2)
        load.wait()
        for t, d_x in enumerate((d_content, d_query_x)):
            d_x[...] = dr1[pl.ds(t * half, half), :] + dot(dq[t].reshape(half, width), matrix(2), NT)

    pl.run_scoped(
        weight_grads,
        pltpu.VMEM((2 * half, width), f32),
        pltpu.VMEM((width, seqs * span), bf16),
        pltpu.VMEM((2, seqs, block, width), bf16),
    )
    step(8, order)
    table = table_of(counts[...])
    vectors = jnp.concatenate([sums[0:2, :], dvec[2:, :], jnp.zeros((4, width), f32)], axis=0)
    pieces = [vectors[:, c * 128 : (c + 1) * 128] for c in range(width // 128)] + [table[:16], table[16:]]
    each = shards // 8
    size = 16 // each
    for p, piece in enumerate(pieces):
        for k in range(each):
            small[p * each + k] = piece[k * size : (k + 1) * size]
    small_first()
    dx_second()
    step(9, order)
    small_second()
    step(10, order)
    small_third()
    lax.fori_loop(11, UNITS + REDUCE_STAGES - 1, one, 0)
    dx_third(dx_out)
    small_last(small_out)
    finish()


def backward(lengths, grads, full, xall, probs, attended, d_attended, query, keys, values, dr1, xc, xq, dvec, pos_rows, pos_cols, shards, seqn):
    rows_of, width = full.shape[1:]
    seqs, block, _ = xc.shape
    span = pos_cols.shape[1]
    f32, bf16 = jnp.float32, jnp.bfloat16
    anywhere = pl.BlockSpec(memory_space=pl.ANY)
    vmem = pl.BlockSpec(memory_space=pltpu.VMEM)
    own = (seqs * block, width)
    small_shape = (shards, 128 // shards, 128)
    dma = pltpu.SemaphoreType.DMA
    return pl.pallas_call(
        functools.partial(backward_kernel, shards, seqn, seqs, block, span, rows_of),
        out_shape=(
            jax.ShapeDtypeStruct((UNITS, rows_of, width), f32),
            jax.ShapeDtypeStruct(own, f32),
            jax.ShapeDtypeStruct(own, f32),
            jax.ShapeDtypeStruct(own, f32),
            jax.ShapeDtypeStruct(small_shape, f32),
        ),
        in_specs=[pl.BlockSpec(memory_space=pltpu.SMEM)] + [anywhere] * 12 + [vmem] * 3,
        out_specs=(vmem,) * 5,
        scratch_shapes=[
            pltpu.VMEM((2, seqs, block, width), bf16),
            pltpu.VMEM((seqs, span, width), bf16),
            pltpu.VMEM((seqs, span, width), bf16),
            pltpu.VMEM((3, shards, rows_of, width), bf16),
            pltpu.VMEM((3, shards, rows_of, width), bf16),
            pltpu.VMEM((seqs, span, width), bf16),
            pltpu.VMEM((seqn,) + own, bf16),
            pltpu.VMEM((8, width), f32),
            pltpu.VMEM((NB * 16, H * 16), f32),
            pltpu.VMEM(small_shape, f32),
            dma((8 + seqn,)),
            dma((2,)),
        ]
        + reduce_scratch(shards, seqn, rows_of, small_shape)
        + dx_scratch(own),
        compiler_params=pltpu.CompilerParams(
            collective_id=1, has_side_effects=True, vmem_limit_bytes=67043328
        ),
        name="attend_back_reduce",
    )(lengths, grads, full, xall, probs, attended, d_attended, query, keys, values, dr1, xc, xq, dvec, pos_rows, pos_cols)


def per_device(
    x_content, x_query, cot_content, cot_query,
    w_query, b_query, w_key, w_value, b_value, w_out, b_out, gain_attn, shift_attn,
    w_up, b_up, w_down, b_down, gain_ffn, shift_ffn, rel_table, lengths, positions, predicted,
    *, shards, seqn,
):
    f32 = jnp.float32
    seqs, block, width = x_content.shape
    r = w_query.shape[0]
    vecs = [
        v.reshape(1, r) for v in (b_query, b_value, b_out, gain_attn, shift_attn, b_down, gain_ffn, shift_ffn)
    ] + [b_up.reshape(4, r)]
    base = lax.axis_index("seq") * block
    pos_rows = lax.dynamic_slice_in_dim(positions, base, block, 1)[..., None]
    table = jnp.full((H, 128), -1e30, f32).at[:, :NB].set(rel_table.astype(f32).T)
    valid = (base + jnp.arange(block))[None, :] < lengths[:, None]
    keep = jnp.stack([valid, valid & (predicted > 0)]).astype(f32).reshape(2 * seqs * block, 1)

    full, xall, vall, probs, attended, query, keys, values = forward(
        w_key, w_value, w_query, w_out, w_up, w_down, x_content, x_query, vecs,
        lengths, table, pos_rows, positions, shards, seqn,
    )
    weights = full.reshape(UNITS, width, width)
    vectors = jnp.concatenate(
        [jnp.transpose(vall[:, :8], (1, 0, 2)).reshape(8, width), vall[:, 8:].reshape(4, width)]
    )
    y_c, y_q, dr1, d_attended, grads, dvec = middle(
        attended.reshape(2 * seqs * block, width), x_content, x_query, cot_content, cot_query, keep, vectors, weights
    )
    sums, dx, d_content, d_query_x, small = backward(
        lengths, grads.reshape(UNITS * shards, r, width), full, xall, probs, attended,
        d_attended.reshape(attended.shape), query, keys, values, dr1, x_content, x_query, dvec,
        pos_rows, positions, shards, seqn,
    )
    small = small.reshape(8, 16, 128)
    summed = jnp.transpose(small[:6, :12], (1, 0, 2)).reshape(UNITS, width)
    mine = lax.axis_index("dp")
    tiny = lax.dynamic_slice_in_dim(summed[:8], mine * r, r, 1)
    g_c1 = lax.dynamic_slice_in_dim(summed[8:].reshape(4 * width), mine * 4 * r, 4 * r, 0)
    g_table = small[6:].reshape(NB, 128)[:, :H]
    shape = (seqs, block, width)
    grad_content = (d_content + dx).reshape(shape)
    g_bq, g_bv, g_bo, g_g1, g_b1, g_c2, g_g2, g_b2 = (tiny[i] for i in range(8))
    g_w1 = jnp.transpose(sums[4:8], (1, 0, 2)).reshape(r, 4 * width)
    g_w2 = sums[8:12].reshape(4 * r, width)
    return (
        y_c.reshape(shape), y_q.reshape(shape), grad_content, d_query_x.reshape(shape),
        sums[2], g_bq, sums[0], sums[1], g_bv, sums[3], g_bo, g_g1, g_b1,
        g_w1, g_c1, g_w2, g_c2, g_g2, g_b2, g_table,
    )


def solution(mesh):
    in_specs = (
        P("dp", "seq", None),
        P("dp", "seq", None),
        P("dp", "seq", None),
        P("dp", "seq", None),
        P("dp", None),
        P("dp"),
        P("dp", None),
        P("dp", None),
        P("dp"),
        P("dp", None),
        P("dp"),
        P("dp"),
        P("dp"),
        P("dp", None),
        P("dp"),
        P("dp", None),
        P("dp"),
        P("dp"),
        P("dp"),
        P(),
        P("dp"),
        P("dp", None),
        P("dp", "seq"),
    )
    out_specs = (
        P("dp", "seq", None),
        P("dp", "seq", None),
        P("dp", "seq", None),
        P("dp", "seq", None),
        P("dp", None),
        P("dp"),
        P("dp", None),
        P("dp", None),
        P("dp"),
        P("dp", None),
        P("dp"),
        P("dp"),
        P("dp"),
        P("dp", None),
        P("dp"),
        P("dp", None),
        P("dp"),
        P("dp"),
        P("dp"),
        P(),
    )
    return jax.shard_map(
        functools.partial(per_device, shards=mesh.shape["dp"], seqn=mesh.shape["seq"]),
        mesh=mesh, in_specs=in_specs, out_specs=out_specs, check_vma=False
    )
```

```python
import functools

import jax
import jax.numpy as jnp
from jax import lax
from jax.experimental import pallas as pl
from jax.experimental.pallas import tpu as pltpu
from jax.sharding import PartitionSpec as P

H = 12
HD = 64
NB = 32

MESH = pl.DeviceIdType.MESH
UNITS = 12


def cutter(rows_of):
    by_rows = rows_of % 96 == 0
    piece = rows_of // 6 if by_rows else 128

    def cut(start, size):
        if not isinstance(start, int):
            start = pl.multiple_of(start * piece, 16 if by_rows else 128)
        else:
            start = start * piece
        inner = pl.ds(start, size * piece)
        return (inner, slice(None)) if by_rows else (slice(None), inner)

    def shape(size):
        return (size * piece, 768) if by_rows else (rows_of, size * piece)

    return cut, shape


def place():
    dp, sq = lax.axis_index("dp"), lax.axis_index("seq")
    row, side = dp // 2, dp % 2
    deck, core = sq // 2, sq % 2
    return dp, sq, row, side, deck, core


def tile_of(unit, shard, shards):
    down = unit // 8
    return (1 - down) * (unit * shards + shard) + down * (8 * shards + shard * 4 + unit - 8)


def remote(src, dst, send, recv, device):
    return pltpu.make_async_remote_copy(
        src_ref=src, dst_ref=dst, send_sem=send, recv_sem=recv, device_id=device, device_id_type=MESH
    )


def greet_all(dp, sq, shards, seqn):
    barrier = pltpu.get_barrier_semaphore()

    def greet(step, carry):
        pl.semaphore_signal(barrier, inc=1, device_id=(lax.rem(dp + step, shards), sq), device_id_type=MESH)
        return carry

    def greet_seq(step, carry):
        pl.semaphore_signal(barrier, inc=1, device_id=(dp, lax.rem(sq + step, seqn)), device_id_type=MESH)
        return carry

    lax.fori_loop(1, shards, greet, 0)
    lax.fori_loop(1, seqn, greet_seq, 0)
    return barrier, shards + seqn - 2


AHEAD = 2


def gather_steps(shards, seqn, ins, outs, scratch):
    wk, wv, wq, wo, wu, wd, xc = ins
    full, xall, vall = outs
    (load_sem, zu_sem, zd_sem, xs_sem, ys_sem, cp_sem, cy_sem,
     zr_sem, xr_sem, yr_sem, cpr_sem, cyr_sem, xc_send, xc_recv, vec_send, vec_recv) = scratch
    dp, sq, row, side, deck, core = place()
    rows = shards // 2
    across = (row * 2 + 1 - side, sq)
    other_deck = (dp, (1 - deck) * 2 + core)
    sibling = (dp, deck * 2 + 1 - core)
    cut, _ = cutter(full.shape[1])
    plane = cut(core * 3 + deck, 2)
    solo = cut(core * 3 + deck * 2, 1)
    theirs = cut(core * 3 + (1 - deck) * 2, 1)

    def many(count, size):
        return full.at[(pl.ds(0, count),) + cut(0, size)]

    def part(unit, shard, piece):
        return full.at[(tile_of(unit, shard, shards),) + piece]

    pieces = [wk, wv, wq, wo] + [wu.at[:, pl.ds(j * 768, 768)] for j in range(4)] + [wd.at[j] for j in range(4)]
    loads = [
        pltpu.make_async_copy(piece, full.at[tile_of(u, dp, shards)], load_sem.at[u]) for u, piece in enumerate(pieces)
    ]
    x_mine = xall.at[sq]
    xload = pltpu.make_async_copy(xc, x_mine, load_sem.at[UNITS])
    x_deck = remote(x_mine, x_mine, xc_send.at[0], xc_recv.at[0], other_deck)
    x_core = remote(x_mine, x_mine, xc_send.at[1], xc_recv.at[1], sibling)
    x_theirs = xall.at[(1 - deck) * 2 + core]
    x_forward = remote(x_theirs, x_theirs, xc_send.at[2], xc_recv.at[2], sibling)

    up = ((row + 1) * 2 + side, sq)
    down = ((row - 1) * 2 + side, sq)

    def along(u, s, src):
        dst = part(u, s * 2 + side, plane)

        @pl.when((s <= row) & (row < rows - 1))
        def _():
            remote(src, dst, zu_sem.at[s], zr_sem.at[u, s], up).start()

        @pl.when((s >= row) & (row > 0))
        def _():
            remote(src, dst, zd_sem.at[s], zr_sem.at[u, s], down).start()

    def send_own(u):
        tile = full.at[tile_of(u, dp, shards)]
        pltpu.make_async_copy(tile, tile, load_sem.at[u]).wait()
        along(u, row, part(u, dp, plane))
        across_own(u)

    def across_own(u):
        ref = part(u, dp, plane)
        remote(ref, ref, xs_sem, xr_sem.at[u], across).start()

    def to_deck(u, shard):
        ref = part(u, shard, solo)
        remote(ref, ref, ys_sem, yr_sem.at[u], other_deck).start()

    def to_core(u, shard):
        ref = part(u, shard, plane)
        remote(ref, ref, cp_sem, cpr_sem.at[u], sibling).start()

    def begin():
        barrier, count = greet_all(dp, sq, shards, seqn)
        for load in loads:
            load.start()
        xload.start()
        pl.semaphore_wait(barrier, count)

        def send_vec(step, carry):
            to = (lax.rem(dp + step, shards), sq)
            remote(vall.at[dp], vall.at[dp], vec_send, vec_recv, to).start()
            return carry

        lax.fori_loop(1, shards, send_vec, 0)

        def first(u, carry):
            send_own(u)
            return carry

        lax.fori_loop(0, AHEAD, first, 0)

        xload.wait()
        x_deck.start()
        x_core.start()

    def step(n):
        @pl.when(n + AHEAD < UNITS)
        def _():
            send_own(n + AHEAD)

        def hop(t, carry):
            u = n - (t - 1)

            def arrived(s):
                ref = part(u, s * 2 + side, plane)
                remote(ref, ref, xs_sem, zr_sem.at[u, s], across).wait_recv()
                along(u, s, ref)
                remote(ref, ref, xs_sem, xr_sem.at[u], across).start()
                to_deck(u, s * 2 + side)
                to_core(u, s * 2 + side)

            @pl.when((u >= 0) & (u < UNITS))
            def _():
                pl.when(row - t >= 0)(lambda: arrived(row - t))
                pl.when(row + t < rows)(lambda: arrived(row + t))

            return carry

        lax.fori_loop(1, rows, hop, 0)
        ux = n - (rows - 1)

        @pl.when((ux >= 0) & (ux < UNITS))
        def _():
            remote(many(rows, 2), many(rows, 2), xs_sem, xr_sem.at[ux], across).wait_recv()

            def pass_on(s, carry):
                to_deck(ux, s * 2 + 1 - side)
                to_core(ux, s * 2 + 1 - side)
                return carry

            lax.fori_loop(0, rows, pass_on, 0)

        uy = n - rows

        @pl.when((uy >= 0) & (uy < UNITS))
        def _():
            remote(many(shards - 1, 1), many(shards - 1, 1), ys_sem, yr_sem.at[uy], other_deck).wait_recv()

            def pass_on(k, carry):
                ref = part(uy, lax.rem(dp + k, shards), theirs)
                remote(ref, ref, cy_sem, cyr_sem.at[uy], sibling).start()
                return carry

            lax.fori_loop(1, shards, pass_on, 0)

    def pass_x():
        x_deck.wait_recv()
        x_forward.start()

    def wait_x():
        x_core.wait_recv()
        x_forward.wait_recv()

    def wait_vec():
        rest = vall.at[pl.ds(0, shards - 1)]
        remote(rest, rest, vec_send, vec_recv, sibling).wait_recv()

    def whole(u):
        remote(many(shards - 1, 2), many(shards - 1, 2), cp_sem, cpr_sem.at[u], sibling).wait_recv()
        remote(many(shards - 1, 1), many(shards - 1, 1), cy_sem, cyr_sem.at[u], sibling).wait_recv()

    def finish():
        x_deck.wait_send()
        x_core.wait_send()
        x_forward.wait_send()
        rest = vall.at[pl.ds(0, shards - 1)]
        remote(rest, rest, vec_send, vec_recv, sibling).wait_send()
        for count, size, sem in (
            (UNITS * rows, 2, xs_sem),
            (UNITS * (shards - 1), 1, ys_sem),
            (UNITS * (shards - 1), 1, cy_sem),
            (UNITS * (shards - 1), 2, cp_sem),
        ):
            ref = many(count, size)
            remote(ref, ref, sem, xr_sem.at[0], sibling).wait_send()

        def sent(s, carry):
            ref = many(UNITS, 2)

            @pl.when((s <= row) & (row < rows - 1))
            def _():
                remote(ref, ref, zu_sem.at[s], xr_sem.at[0], sibling).wait_send()

            @pl.when((s >= row) & (row > 0))
            def _():
                remote(ref, ref, zd_sem.at[s], xr_sem.at[0], sibling).wait_send()

            return carry

        lax.fori_loop(0, rows, sent, 0)

    return begin, step, whole, pass_x, wait_x, wait_vec, finish


def gather_scratch(shards):
    dma = pltpu.SemaphoreType.DMA
    return [dma((UNITS + 1,))] + [dma((shards // 2,))] * 2 + [dma(())] * 4 + [dma((UNITS, shards // 2))] + [dma((UNITS,))] * 4 + [dma((3,)), dma((3,)), dma(()), dma(())]


GATHER_SCRATCH = 16


def reduce_front(shards, rows_of, count, scratch):
    f32, bf16 = jnp.float32, jnp.bfloat16
    acc, got_core, got_deck, load_sem, core_send, core_recv, deck_send, deck_recv = scratch
    dp, sq, row, side, deck, core = place()
    rows = shards // 2
    other_deck = (dp, (1 - deck) * 2 + core)
    sibling = (dp, deck * 2 + 1 - core)
    cut, _ = cutter(rows_of)
    mine = cut(core * 3, 3)
    siblings = cut((1 - core) * 3, 3)
    solo = cut(deck * 2, 1)
    other_solo = cut((1 - deck) * 2, 1)

    def send(u, tiles):
        def one(s, carry):
            for b in range(2):
                tile = tiles(s * 2 + b)
                remote(tile.at[siblings], got_core.at[u, s, b], core_send.at[u], core_recv.at[u], sibling).start()
                pltpu.make_async_copy(tile.at[mine], acc.at[u, s, b], load_sem.at[u]).start()
            return carry

        lax.fori_loop(0, rows, one, 0)

    def core_copy(u):
        return remote(got_core.at[u], got_core.at[u], core_send.at[u], core_recv.at[u], sibling)

    def deck_copy(u):
        src = acc.at[(u, slice(None), slice(None)) + other_solo]
        return remote(src, got_deck.at[u], deck_send.at[u], deck_recv.at[u], other_deck)

    def stage_core(u):
        pltpu.make_async_copy(acc.at[u], acc.at[u], load_sem.at[u]).wait()
        core_copy(u).wait_recv()

        def add(s, carry):
            for b in range(2):
                acc[u, s, b] = total(acc[u, s, b], got_core[u, s, b])
            return carry

        lax.fori_loop(0, rows, add, 0)
        deck_copy(u).start()

    def stage_deck(u):
        deck_copy(u).wait_recv()

        def add(s, carry):
            for b in range(2):
                at = (u, s, b) + solo
                acc[at] = total(acc[at], got_deck[u, s, b])
            return carry

        lax.fori_loop(0, rows, add, 0)

    def sent():
        def one(u, carry):
            core_copy(u).wait_send()
            deck_copy(u).wait_send()
            return carry

        lax.fori_loop(0, count, one, 0)

    return send, stage_core, stage_deck, sent


def total(left, right):
    return left + right


def front_scratch(shards, rows_of, count):
    bf16 = jnp.bfloat16
    rows = shards // 2
    _, shape = cutter(rows_of)
    return [
        pltpu.VMEM((count, rows, 2) + shape(3), bf16),
        pltpu.VMEM((count, rows, 2) + shape(3), bf16),
        pltpu.VMEM((count, rows, 2) + shape(1), bf16),
    ] + [pltpu.SemaphoreType.DMA((count,))] * 5


FRONT_SCRATCH = 8


def reduce_back(shards, rows_of, out, scratch):
    f32, bf16 = jnp.float32, jnp.bfloat16
    (own_side, got_across, line, got_line, final, got_final, half, got_half,
     side_sem, across_send, across_recv, line_send, line_recv, final_send, final_recv, half_send, half_recv) = scratch
    dp, sq, row, side, deck, core = place()
    rows = shards // 2
    across = (row * 2 + 1 - side, sq)
    other_deck = (dp, (1 - deck) * 2 + core)
    sibling = (dp, deck * 2 + 1 - core)
    cut, _ = cutter(rows_of)
    mine = cut(core * 3, 3)
    siblings = cut((1 - core) * 3, 3)
    plane = cut(deck, 2)
    other_solo = cut((1 - deck) * 2, 1)

    def send_across(u, planes):
        remote(
            planes.at[(slice(None), 1 - side) + plane], got_across.at[u], across_send.at[u], across_recv.at[u], across
        ).start()
        pltpu.make_async_copy(planes.at[(slice(None), side) + plane], own_side.at[u], side_sem.at[u]).start()

    def across_copy(u):
        return remote(got_across.at[u], got_across.at[u], across_send.at[u], across_recv.at[u], across)

    def line_copy(u):
        ref = got_line.at[u, pl.ds(0, rows - 1)]
        return remote(ref, ref, line_send.at[u], line_recv.at[u], across)

    def final_copy(u):
        return remote(final.at[u], got_final.at[u], final_send.at[u], final_recv.at[u], other_deck)

    def half_copy(u):
        return remote(half.at[u], got_half.at[u], half_send.at[u], half_recv.at[u], sibling)

    def stage_across(u):
        pltpu.make_async_copy(own_side.at[u], own_side.at[u], side_sem.at[u]).wait()
        across_copy(u).wait_recv()

        def add(k, carry):
            s = lax.rem(row + k, rows)
            line[u, s] = total(own_side[u, s], got_across[u, s])

            @pl.when(k < rows)
            def _():
                remote(
                    line.at[u, s], got_line.at[u, rows - 1 - k], line_send.at[u], line_recv.at[u], (s * 2 + side, sq)
                ).start()

            return carry

        lax.fori_loop(1, rows + 1, add, 0)

    def stage_line(u):
        line_copy(u).wait_recv()
        summed = line[u, row].astype(f32)
        if rows <= 4:
            for k in range(rows - 1):
                summed = summed + got_line[u, k].astype(f32)
        else:
            summed = lax.fori_loop(0, rows - 1, lambda k, t: t + got_line[u, k].astype(f32), summed)
        final[u] = summed.astype(bf16)
        final_copy(u).start()

    def stage_final(u):
        final_copy(u).wait_recv()
        half[(u,) + plane] = final[u]
        half[(u,) + other_solo] = got_final[(u,) + cut(1 - deck, 1)]
        both = (u,) + cut(1, 1)
        half[both] = total(half[both], got_final[(u,) + cut(deck, 1)])
        half_copy(u).start()

    def stage_half(u):
        half_copy(u).wait_recv()
        out[(u,) + mine] = half[u].astype(f32)
        out[(u,) + siblings] = got_half[u].astype(f32)

    def sent():
        def one(u, carry):
            for copy in (across_copy, line_copy, final_copy, half_copy):
                copy(u).wait_send()
            return carry

        lax.fori_loop(0, UNITS, one, 0)

    return send_across, (stage_across, stage_line, stage_final, stage_half), sent


def back_scratch(shards, rows_of):
    bf16 = jnp.bfloat16
    rows = shards // 2
    _, shape = cutter(rows_of)
    return [pltpu.VMEM((UNITS, rows) + shape(2), bf16)] * 4 + [
        pltpu.VMEM((UNITS,) + shape(2), bf16),
        pltpu.VMEM((UNITS,) + shape(2), bf16),
        pltpu.VMEM((UNITS,) + shape(3), bf16),
        pltpu.VMEM((UNITS,) + shape(3), bf16),
    ] + [pltpu.SemaphoreType.DMA((UNITS,))] * 9


BACK_SCRATCH = 17


def small_steps(shards, seqn, small, scratch):
    got_small, mid_small, got_mid, got_all, small_send, small_recv = scratch
    dp, sq, row, side, deck, core = place()
    sibling = (dp, deck * 2 + 1 - core)

    def small_first():
        got_small[dp] = small[dp]

        def send(k, carry):
            to = lax.rem(dp + k, shards)
            remote(small.at[to], got_small.at[dp], small_send.at[0], small_recv.at[0], (to, sq)).start()
            return carry

        lax.fori_loop(1, shards, send, 0)

    def sum_of(ref, count):
        summed = ref[0]
        for i in range(1, count):
            summed = summed + ref[i]
        return summed

    def small_second():
        rest = got_small.at[pl.ds(0, shards - 1)]
        remote(rest, rest, small_send.at[0], small_recv.at[0], sibling).wait()
        summed = sum_of(got_small, shards)
        mid_small[0] = summed
        got_mid[sq] = summed

        def send(k, carry):
            to = (dp, lax.rem(sq + k, seqn))
            remote(mid_small.at[0], got_mid.at[sq], small_send.at[1], small_recv.at[1], to).start()
            return carry

        lax.fori_loop(1, seqn, send, 0)

    def small_third():
        rest = got_mid.at[pl.ds(0, seqn - 1)]
        remote(rest, rest, small_send.at[1], small_recv.at[1], sibling).wait()
        summed = sum_of(got_mid, seqn)
        mid_small[1] = summed
        got_all[dp] = summed

        def send(k, carry):
            to = (lax.rem(dp + k, shards), sq)
            remote(mid_small.at[1], got_all.at[dp], small_send.at[2], small_recv.at[2], to).start()
            return carry

        lax.fori_loop(1, shards, send, 0)

    def small_last(small_out):
        rest = got_all.at[pl.ds(0, shards - 1)]
        remote(rest, rest, small_send.at[2], small_recv.at[2], sibling).wait()
        small_out[...] = got_all[...]

    return small_first, small_second, small_third, small_last


def small_scratch(shards, seqn, small_shape):
    f32 = jnp.float32
    return [
        pltpu.VMEM(small_shape, f32),
        pltpu.VMEM((2,) + small_shape[1:], f32),
        pltpu.VMEM((seqn,) + small_shape[1:], f32),
        pltpu.VMEM(small_shape, f32),
    ] + [pltpu.SemaphoreType.DMA((3,))] * 2


SMALL_SCRATCH = 6


def dx_steps(dxs, scratch):
    f32, bf16 = jnp.float32, jnp.bfloat16
    dx_own, dx_core, dx_deck, load, send, recv = scratch
    dp, sq, row, side, deck, core = place()
    other_deck = (dp, (1 - deck) * 2 + core)
    sibling = (dp, deck * 2 + 1 - core)
    deck_dx = remote(dx_own.at[1 - deck], dx_deck, send.at[2], recv.at[2], other_deck)

    def first():
        for k in range(2):
            pltpu.make_async_copy(dxs.at[k * 2 + core], dx_own.at[k], load.at[k]).start()
            remote(dxs.at[k * 2 + 1 - core], dx_core.at[k], send.at[k], recv.at[k], sibling).start()

    def second():
        for k in range(2):
            pltpu.make_async_copy(dx_own.at[k], dx_own.at[k], load.at[k]).wait()
            remote(dx_core.at[k], dx_core.at[k], send.at[k], recv.at[k], sibling).wait()
            dx_own[k] = (dx_own[k].astype(f32) + dx_core[k].astype(f32)).astype(bf16)
        deck_dx.start()

    def third(dx_out):
        deck_dx.wait()
        dx_out[...] = dx_own[deck].astype(f32) + dx_deck[...].astype(f32)

    return first, second, third


def dx_scratch(own):
    bf16 = jnp.bfloat16
    dma = pltpu.SemaphoreType.DMA
    return [pltpu.VMEM((2,) + own, bf16), pltpu.VMEM((2,) + own, bf16), pltpu.VMEM(own, bf16), dma((2,)), dma((3,)), dma((3,))]


bucket_marks = (12, 16, 23, 32, 46, 64, 91)
MASKED = NB
TN = (((0,), (0,)), ((), ()))
NT = (((1,), (1,)), ((), ()))


def dot(left, right, dims=None):
    if dims is None:
        dims = (((1,), (0,)), ((), ()))
    return lax.dot_general(left, right, dims, preferred_element_type=jnp.float32)


def column_of(row):
    return jnp.broadcast_to(row.astype(jnp.float32), (row.shape[1], row.shape[1])).T


def fill_buckets(buckets, positions, lengths, base, seqs, block, span):
    for s in range(seqs):
        mine = column_of(positions[s : s + 1, pl.ds(pl.multiple_of(base, block), block)]).astype(jnp.int32)
        for c in range(span // block):
            cols = slice(c * block, (c + 1) * block)
            delta = positions[s : s + 1, cols] - mine
            dist = jnp.abs(delta)
            far = jnp.full(dist.shape, 8, jnp.int32)
            for mark in bucket_marks:
                far = far + (dist >= mark).astype(jnp.int32)
            bucket = jnp.where(dist < 8, dist, far) + 16 * (delta > 0).astype(jnp.int32)
            i = base + lax.broadcasted_iota(jnp.int32, (block, block), 0)
            j = c * block + lax.broadcasted_iota(jnp.int32, (block, block), 1)
            valid = j < lengths[s]
            buckets[s, 0, :, cols] = jnp.where(valid & (j <= i), bucket, MASKED)
            buckets[s, 1, :, cols] = jnp.where(valid & (j < jnp.maximum(i, 1)), bucket, MASKED)


def head_lanes(rows, half):
    lane = lax.broadcasted_iota(jnp.int32, (rows, 2 * HD), 1)
    return (lane < HD) if half == 0 else (lane >= HD)


def fill_bias(i, biases, buckets, table, block, span):
    s, head = i // H, lax.rem(i, H)
    entry = jnp.broadcast_to(table[pl.ds(head, 1), :], (block, 128))
    for c in range(span // 128):
        cols = slice(c * 128, (c + 1) * 128)
        value = jnp.take_along_axis(entry, buckets[s, 0, :, cols], axis=1, mode="promise_in_bounds")
        biases[i, 0, :, cols] = value
        biases[i, 1, :, cols] = jnp.where(buckets[s, 1, :, cols] == MASKED, -1e30, value)


def attend_pair(i, refs, block, span, low_out):
    attended, query, keys, values, biases = refs
    f32, bf16 = jnp.float32, jnp.bfloat16
    pairs = H // 2
    s, pair = i // pairs, lax.rem(i, pairs)
    lanes = pl.ds(pl.multiple_of(pair * 128, 128), 128)
    q = query[:, s, :, lanes].reshape(2 * block, 128)
    k = keys[s, :, lanes]
    v = values[s, :, lanes]
    outs = []
    for half in range(2):
        mine = head_lanes(2 * block, half)
        one = jnp.where(mine, q * 0.125, 0).astype(bf16)
        scores = dot(one, k, NT) + biases[i * 2 + half].reshape(2 * block, span)
        top = jnp.max(scores, axis=-1, keepdims=True)
        expo = jnp.exp(scores - top)
        low = (expo * (1.0 / jnp.sum(expo, axis=-1, keepdims=True))).astype(bf16)
        low_out[half] = low
        outs.append(dot(low, v))
    mixed = jnp.where(head_lanes(2 * block, 0), outs[0], outs[1]).astype(bf16)
    attended[:, s, :, lanes] = mixed.reshape(2, block, 128)


def center_of(value):
    center = value - jnp.mean(value, axis=-1, keepdims=True)
    var = jnp.mean(center * center, axis=-1, keepdims=True)
    inv = lax.rsqrt(var + 1e-05)
    return center * inv, inv


def norm_back(grad, gain, normed, inv):
    scaled = grad * gain
    return inv * (
        scaled
        - jnp.mean(scaled, axis=-1, keepdims=True)
        - normed * jnp.mean(scaled * normed, axis=-1, keepdims=True)
    )


EARLY = 8
TILE = 256
LONG = 384
DOWNS = 4


def forward_kernel(
    shards, seqn, seqs, block, span, rows_of,
    lengths, wk, wv, wq, wo, wu, wd, xc, xc_rows, xq_rows, cot_c, cot_q, positions, predicted, rel_table,
    bq, bv, bo, g1, b1, c2, g2, b2, c1,
    squares, x_out, probs, attended_out, query_out, keys_out, values_out, y_c, y_q, dr1_out, da_out, grads, downs, dvec,
    full, xall, vall, vectors, keep, attended, table, io_sem, low_sem, *scratch,
):
    f32, bf16 = jnp.float32, jnp.bfloat16
    width = H * HD
    half = seqs * block
    rows = 2 * half
    r = rows_of
    wide = 4 * r
    base = lax.axis_index("seq") * block
    me = lax.axis_index("dp")
    begin, step, whole, pass_x, wait_x, wait_vec, finish = gather_steps(
        shards, seqn, (wk, wv, wq, wo, wu, wd, xc), (full, xall, vall), scratch[: -FRONT_SCRATCH]
    )
    send_front, stage_core, stage_deck, front_sent = reduce_front(shards, r, DOWNS, scratch[-FRONT_SCRATCH:])
    acc = scratch[-FRONT_SCRATCH]
    vall[me] = jnp.zeros(vall.shape[1:], f32)
    for i, piece in enumerate((bq, bv, bo, g1, b1, c2, g2, b2)):
        vall[me, i : i + 1, 0:r] = piece[...].astype(f32)
    vall[me, 8:9, :] = c1[...].astype(f32)
    begin()

    def one(n, carry):
        step(n)
        return carry

    def matrix(u):
        return full[pl.ds(u * shards, shards)].reshape(width, width)

    def columns(u, cols):
        size = cols.size
        return full[pl.ds(u * shards, shards), :, cols].reshape(width, size)

    def row_block(u, n):
        per = LONG // r
        return full[pl.ds(u * shards + n * per, per)].reshape(LONG, width)

    def attention(query, keys, values, buckets, low_two, biases):
        fill_buckets(buckets, positions, lengths, base, seqs, block, span)
        eye = (
            lax.broadcasted_iota(jnp.int32, (NB, 128), 0) == lax.broadcasted_iota(jnp.int32, (NB, 128), 1)
        )
        by_head = dot(rel_table[...], jnp.where(eye, 1.0, 0.0).astype(bf16), TN)
        lane = lax.broadcasted_iota(jnp.int32, by_head.shape, 1)
        table[...] = jnp.where(lane < NB, by_head, -1e30)
        for s in range(seqs):
            live = base + lax.broadcasted_iota(jnp.int32, (block, 1), 0) < lengths[s]
            chosen = column_of(predicted[s : s + 1, :])[:, 0:1] > 0
            keep[s * block : (s + 1) * block, :] = jnp.where(live, 1.0, 0.0)
            keep[half + s * block : half + (s + 1) * block, :] = jnp.where(live & chosen, 1.0, 0.0)
        share = seqs * H // EARLY

        def one_and_bias(n, carry):
            step(n)

            def bias(k, inner):
                fill_bias(n * share + k, biases, buckets, table, block, span)
                return inner

            return lax.fori_loop(0, share, bias, carry)

        lax.fori_loop(0, EARLY - 2, one_and_bias, 0)
        pass_x()
        lax.fori_loop(EARLY - 2, EARLY, one_and_bias, 0)
        wait_x()
        wait_vec()
        vectors[...] = jnp.zeros_like(vectors)

        def spread(i, carry):
            row = lax.broadcasted_iota(jnp.int32, (r, width), 0)
            col = lax.broadcasted_iota(jnp.int32, (r, width), 1)
            at = jnp.where(col == row + i * r, 1.0, 0.0).astype(bf16)
            vectors[0:8, :] += dot(vall[i, 0:8, 0:r].astype(bf16), at)
            per = width // wide
            row = lax.broadcasted_iota(jnp.int32, (wide, width), 0)
            col = lax.broadcasted_iota(jnp.int32, (wide, width), 1)
            at = jnp.where(col == row + lax.rem(i, per) * wide, 1.0, 0.0).astype(bf16)
            vectors[pl.ds(8 + i // per, 1), :] += dot(vall[i, 8:9, :].astype(bf16), at)
            return carry

        lax.fori_loop(0, shards, spread, 0)
        for u in range(3):
            whole(u)

        def project(k, carry):
            x = xall[k].reshape(half, width)
            at = pl.ds(pl.multiple_of(k * block, block), block)
            keys[:, at, :] = dot(x, matrix(0)).astype(bf16).reshape(seqs, block, width)
            values[:, at, :] = (dot(x, matrix(1)) + vectors[1:2, :]).astype(bf16).reshape(seqs, block, width)
            return carry

        lax.fori_loop(0, seqn, project, 0)
        for t, x in enumerate((xc_rows, xq_rows)):
            query[t] = (dot(x[...], matrix(2)) + vectors[0:1, :]).astype(bf16).reshape(seqs, block, width)
        puts = [
            pltpu.make_async_copy(src, dst, io_sem.at[i])
            for i, (src, dst) in enumerate(((query, query_out), (keys, keys_out), (values, values_out)))
        ]
        for copy in puts:
            copy.start()
        total = seqs * H // 2

        def put(i, slot):
            return pltpu.make_async_copy(low_two.at[slot], probs.at[i], low_sem.at[slot])

        def attend_one(i, carry):
            slot = lax.rem(i, 2)

            @pl.when(lax.rem(i, 4) == 0)
            def _():
                step(EARLY + i // 4)

            @pl.when(i >= 2)
            def _():
                put(i - 2, slot).wait()

            attend_pair(i, (attended, query, keys, values, biases), block, span, low_two.at[slot])
            put(i, slot).start()
            return carry

        lax.fori_loop(0, total, attend_one, 0)
        put(total - 2, (total - 2) % 2).wait()
        put(total - 1, (total - 1) % 2).wait()
        for copy in puts:
            copy.wait()

    pl.run_scoped(
        attention,
        pltpu.VMEM((2, seqs, block, width), bf16),
        pltpu.VMEM((seqs, span, width), bf16),
        pltpu.VMEM((seqs, span, width), bf16),
        pltpu.VMEM((seqs, 2, block, span), jnp.int32),
        pltpu.VMEM((2, 2, 2 * block, span), bf16),
        pltpu.VMEM((seqs * H, 2, block, span), f32),
    )
    done = EARLY + seqs * H // 8
    more = [
        pltpu.make_async_copy(full.at[pl.ds(0, 3 * shards)], squares, io_sem.at[3]),
        pltpu.make_async_copy(xall, x_out, io_sem.at[4]),
        pltpu.make_async_copy(attended, attended_out, io_sem.at[5]),
    ]
    for copy in more:
        copy.start()
    dvec[...] = jnp.zeros_like(dvec)
    vec = lambda i: vectors[i : i + 1, :]
    chunk = 128
    chunks = half // chunk

    def ffn(hidden, hidden_low, hidden_turn, normed1, inv1, active, slope, feed, dr2, dr2_low, dr1_low, da, stage, stage_down):
        step(done)
        whole(3)

        def phase_one(c, carry):
            t, s = c // seqs, lax.rem(c, seqs)
            at = pl.ds(pl.multiple_of(c * chunk, chunk), chunk)
            out = dot(attended[t, s], matrix(3)) + vec(2)
            inner = pl.ds(pl.multiple_of(s * chunk, chunk), chunk)
            x = jnp.where(t == 0, xc_rows[inner, :].astype(f32), xq_rows[inner, :].astype(f32))
            normed, inv = center_of(x + out)
            normed1[at, :] = normed
            inv1[at, :] = inv
            h = normed * vec(3) + vec(4)
            hidden[at, :] = h
            hidden_low[at, :] = h.astype(bf16)
            return carry

        lax.fori_loop(0, rows // chunk, phase_one, 0)
        hidden_turn[...] = hidden_low[...].T
        tiles = width // TILE

        def phase_two(j, carry):
            step(done + 1 + j)
            whole(4 + j)

            def tile(n, inner):
                cols = pl.ds(pl.multiple_of(n * TILE, TILE), TILE)
                u = dot(hidden_low[...], columns(4 + j, cols)) + vectors[pl.ds(8 + j, 1), cols]
                cdf = 0.5 * (1.0 + lax.erf(u * (2.0**-0.5)))
                active[j, :, cols] = (u * cdf).astype(bf16)
                slope[j, :, cols] = (cdf + u * (jnp.exp(-0.5 * u * u) * ((2.0 * jnp.pi) ** -0.5))).astype(bf16)
                return inner

            return lax.fori_loop(0, tiles, tile, carry)

        lax.fori_loop(0, 4, phase_two, 0)

        def last(u, carry):
            whole(u)
            return carry

        lax.fori_loop(done + 5, UNITS + shards // 2, one, 0)
        lax.fori_loop(8, UNITS, last, 0)

        def phase_feed(n, carry):
            cols = pl.ds(pl.multiple_of(n * TILE, TILE), TILE)
            feed[:, cols] = sum(dot(active[j], columns(8 + j, cols)) for j in range(4))
            return carry

        lax.fori_loop(0, tiles, phase_feed, 0)

        def phase_three(c, carry):
            t, s = c // seqs, lax.rem(c, seqs)
            at = pl.ds(pl.multiple_of(c * chunk, chunk), chunk)
            normed, inv = center_of(hidden[at, :] + feed[at, :] + vec(5))
            kept = keep[at, :]
            feed[at, :] = (normed * vec(6) + vec(7)) * kept
            inner = pl.ds(pl.multiple_of(s * chunk, chunk), chunk)
            cot = jnp.where(t == 0, cot_c[inner, :].astype(f32), cot_q[inner, :].astype(f32)) * kept
            d = norm_back(cot, vec(6), normed, inv)
            dvec[6:7, :] += jnp.sum(cot * normed, axis=0, keepdims=True)
            dvec[7:8, :] += jnp.sum(cot, axis=0, keepdims=True)
            dvec[5:6, :] += jnp.sum(d, axis=0, keepdims=True)
            dr2[at, :] = d
            dr2_low[at, :] = d.astype(bf16)
            return carry

        lax.fori_loop(0, rows // chunk, phase_three, 0)
        y_copies = [
            pltpu.make_async_copy(feed.at[pl.ds(0, half)], y_c, io_sem.at[6]),
            pltpu.make_async_copy(feed.at[pl.ds(half, half)], y_q, io_sem.at[7]),
        ]
        for copy in y_copies:
            copy.start()
        longs = width // LONG

        def phase_down(step_, carry):
            j, n = step_ // longs, lax.rem(step_, longs)
            cols = pl.ds(pl.multiple_of(n * LONG, 128), LONG)
            grad = dot(active[j, :, cols], dr2_low[...], TN).astype(bf16)
            per = LONG // r
            stage_down[pl.ds(step_ * per, per)] = grad.reshape(per, r, width)
            return carry

        lax.fori_loop(0, 4 * longs, phase_down, 0)

        def start_down(k, carry):
            send_front(k, lambda shard: stage_down.at[shard * 4 + k])
            return carry

        lax.fori_loop(0, DOWNS, start_down, 0)

        def phase_slope(step_, carry):
            j, n = step_ // longs, lax.rem(step_, longs)
            cols = pl.ds(pl.multiple_of(n * LONG, 128), LONG)
            du = slope[j, :, cols].astype(f32) * dot(dr2_low[...], row_block(8 + j, n), NT)
            dvec[pl.ds(8 + j, 1), cols] = jnp.sum(du, axis=0, keepdims=True)
            active[j, :, cols] = du.astype(bf16)

            @pl.when(n == longs - 1)
            def _():
                stage_core(j)

            return carry

        lax.fori_loop(0, 4 * longs, phase_slope, 0)

        def phase_up(j, carry):
            def tile(n, inner):
                cols = pl.ds(pl.multiple_of(n * TILE, TILE), TILE)
                grad = dot(hidden_turn[...], active[j, :, cols]).astype(bf16)
                stage[1 + j, :, :, cols] = grad.reshape(shards, r, TILE)
                return inner

            lax.fori_loop(0, tiles, tile, 0)
            pltpu.make_async_copy(
                stage.at[1 + j], grads.at[pl.ds((1 + j) * shards, shards)], io_sem.at[10 + j]
            ).start()
            return carry

        lax.fori_loop(0, 4, phase_up, 0)

        def put_down(k):
            return pltpu.make_async_copy(acc.at[k], downs.at[k], io_sem.at[14 + k])

        def finish_down(k):
            stage_deck(k)
            put_down(k).start()

        finish_down(0)

        def phase_hidden(n, carry):
            cols = pl.ds(pl.multiple_of(n * LONG, 128), LONG)
            dr2[:, cols] += sum(dot(active[j], row_block(4 + j, n), NT) for j in range(4))
            return carry

        lax.fori_loop(0, longs, phase_hidden, 0)
        for copy in y_copies:
            copy.wait()
        finish_down(1)

        def phase_five(c, carry):
            at = pl.ds(pl.multiple_of(c * chunk, chunk), chunk)
            dh = dr2[at, :]
            normed = normed1[at, :]
            d = norm_back(dh, vec(3), normed, inv1[at, :])
            dvec[3:4, :] += jnp.sum(dh * normed, axis=0, keepdims=True)
            dvec[4:5, :] += jnp.sum(dh, axis=0, keepdims=True)
            dvec[2:3, :] += jnp.sum(d, axis=0, keepdims=True)
            feed[at, :] = d
            low = d.astype(bf16)
            dr1_low[at, :] = low
            da[at, :] = dot(low, matrix(3), NT).astype(bf16)
            return carry

        lax.fori_loop(0, rows // chunk, phase_five, 0)
        finals = [
            pltpu.make_async_copy(feed, dr1_out, io_sem.at[6]),
            pltpu.make_async_copy(da, da_out, io_sem.at[7]),
        ]
        for copy in finals:
            copy.start()
        finish_down(2)
        turned = attended[...].reshape(rows, width).T

        def phase_out(n, carry):
            cols = pl.ds(pl.multiple_of(n * TILE, TILE), TILE)
            grad = dot(hidden_turn[...], dr1_low[:, cols]).astype(bf16)
            stage[0, :, :, cols] = grad.reshape(shards, r, TILE)
            return carry

        hidden_turn[...] = turned
        lax.fori_loop(0, tiles, phase_out, 0)
        out_copy = pltpu.make_async_copy(stage.at[0], grads.at[pl.ds(0, shards)], io_sem.at[9])
        out_copy.start()
        finish_down(3)
        for j in range(4):
            pltpu.make_async_copy(
                stage.at[1 + j], grads.at[pl.ds((1 + j) * shards, shards)], io_sem.at[10 + j]
            ).wait()
            put_down(j).wait()
        out_copy.wait()
        for copy in finals + more:
            copy.wait()
        front_sent()
        finish()

    pl.run_scoped(
        ffn,
        pltpu.VMEM((rows, width), f32),
        pltpu.VMEM((rows, width), bf16),
        pltpu.VMEM((width, rows), bf16),
        pltpu.VMEM((rows, width), f32),
        pltpu.VMEM((rows, 1), f32),
        pltpu.VMEM((4, rows, width), bf16),
        pltpu.VMEM((4, rows, width), bf16),
        pltpu.VMEM((rows, width), f32),
        pltpu.VMEM((rows, width), f32),
        pltpu.VMEM((rows, width), bf16),
        pltpu.VMEM((rows, width), bf16),
        pltpu.VMEM((rows, width), bf16),
        pltpu.VMEM((5, shards, r, width), bf16),
        pltpu.VMEM((4 * shards, r, width), bf16),
    )


def forward(wk, wv, wq, wo, wu, wd, xc, xq, cot_c, cot_q, vecs, lengths, positions, predicted, rel_table, shards, seqn):
    rows_of, width = wq.shape
    seqs, block, _ = xc.shape
    span = positions.shape[1]
    f32, bf16 = jnp.float32, jnp.bfloat16
    steps = seqs * H // 2
    half = seqs * block
    anywhere = pl.BlockSpec(memory_space=pl.ANY)
    vmem = pl.BlockSpec(memory_space=pltpu.VMEM)
    rows = shards // 2
    _, shape = cutter(rows_of)
    dma = pltpu.SemaphoreType.DMA
    flat = lambda a: a.reshape(half, width)
    stream = (2, seqs, block, width)
    return pl.pallas_call(
        functools.partial(forward_kernel, shards, seqn, seqs, block, span, rows_of),
        out_shape=(
            jax.ShapeDtypeStruct((3 * shards, rows_of, width), bf16),
            jax.ShapeDtypeStruct((seqn,) + xc.shape, bf16),
            jax.ShapeDtypeStruct((steps, 2, 2 * block, span), bf16),
            jax.ShapeDtypeStruct(stream, bf16),
            jax.ShapeDtypeStruct(stream, bf16),
            jax.ShapeDtypeStruct((seqs, span, width), bf16),
            jax.ShapeDtypeStruct((seqs, span, width), bf16),
            jax.ShapeDtypeStruct((half, width), f32),
            jax.ShapeDtypeStruct((half, width), f32),
            jax.ShapeDtypeStruct((2 * half, width), f32),
            jax.ShapeDtypeStruct((2 * half, width), bf16),
            jax.ShapeDtypeStruct((5 * shards, rows_of, width), bf16),
            jax.ShapeDtypeStruct((DOWNS, rows, 2) + shape(3), bf16),
            jax.ShapeDtypeStruct((UNITS, width), f32),
        ),
        in_specs=[pl.BlockSpec(memory_space=pltpu.SMEM)] + [anywhere] * 7 + [vmem] * 16,
        out_specs=(anywhere,) * 13 + (vmem,),
        scratch_shapes=[
            pltpu.VMEM((UNITS * shards, rows_of, width), bf16),
            pltpu.VMEM((seqn,) + xc.shape, bf16),
            pltpu.VMEM((shards, 9, 4 * rows_of), f32),
            pltpu.VMEM((UNITS, width), f32),
            pltpu.VMEM((2 * half, 1), f32),
            pltpu.VMEM(stream, bf16),
            pltpu.VMEM((H, 128), f32),
            dma((18,)),
            dma((2,)),
        ]
        + gather_scratch(shards)
        + front_scratch(shards, rows_of, DOWNS),
        compiler_params=pltpu.CompilerParams(collective_id=0, has_side_effects=True, vmem_limit_bytes=67043328),
        name="gather_attend_ffn",
    )(
        lengths, wk, wv, wq, wo, wu, wd.reshape(4, rows_of, width), xc, flat(xc), flat(xq), flat(cot_c), flat(cot_q),
        positions, predicted, rel_table, *vecs,
    )


def attend_back_pair(i, refs, low, seqs, block, span):
    attended, d_attended, query, keys, values, buckets, dq, dk, dv, ds_sum, sums, counts = refs
    f32, bf16 = jnp.float32, jnp.bfloat16
    pairs = H // 2
    rows = 2 * block
    s, pair = i // pairs, lax.rem(i, pairs)
    lanes = pl.ds(pl.multiple_of(pair * 128, 128), 128)
    q = query[:, s, :, lanes].reshape(rows, 128)
    k = keys[s, :, lanes]
    v = values[s, :, lanes]
    da = d_attended[:, s, :, lanes].reshape(rows, 128)
    product = da.astype(f32) * attended[:, s, :, lanes].reshape(rows, 128).astype(f32)
    d_queries, dk_turn, dv_turn = [], 0.0, 0.0
    for half in range(2):
        mine = head_lanes(rows, half)
        one = jnp.where(mine, da, 0).astype(bf16)
        inner = jnp.sum(jnp.where(mine, product, 0.0), axis=-1, keepdims=True)
        ds = low[half].astype(f32) * (dot(one, v, NT) - inner)
        ds_sum[pair * 2 + half] = (ds[:block] + ds[block:]).astype(bf16)
        ds_low = ds.astype(bf16)
        d_queries.append(dot(ds_low, k))
        dk_turn += dot(jnp.where(mine, q, 0).astype(bf16), ds_low, TN)
        dv_turn += dot(one, low[half], TN)
    d_query = jnp.where(head_lanes(rows, 0), d_queries[0], d_queries[1]) * 0.125
    sums[0:1, lanes] += jnp.sum(d_query, axis=0, keepdims=True)
    dq[:, s, :, lanes] = d_query.reshape(2, block, 128).astype(bf16)
    dk[s, :, lanes] = (dk_turn * 0.125).T.astype(bf16)
    d_value = dv_turn.T
    sums[1:2, lanes] += jnp.sum(d_value, axis=0, keepdims=True)
    dv[s, :, lanes] = d_value.astype(bf16)

    @pl.when(pair == pairs - 1)
    def _():
        def count(g, carry):
            at = pl.ds(pl.multiple_of(g * 16, 16), 16)
            bucket = buckets[s, 0, at, :]
            hot = jnp.concatenate([jnp.where(bucket == n, 1.0, 0.0).astype(bf16) for n in range(NB)], axis=0)
            counts[...] += dot(hot, ds_sum[:, at, :].reshape(H * 16, span), NT)
            return carry

        lax.fori_loop(0, block // 16, count, 0)


def table_of(counts):
    row = lax.broadcasted_iota(jnp.int32, counts.shape, 0)
    col = lax.broadcasted_iota(jnp.int32, counts.shape, 1)
    kept = jnp.where(lax.rem(row, 16) == lax.rem(col, 16), counts, 0.0)
    folded = jnp.sum(kept.reshape(NB, 16, H * 16), axis=1)
    lane = lax.broadcasted_iota(jnp.int32, (H * 16, 128), 1)
    head = lax.broadcasted_iota(jnp.int32, (H * 16, 128), 0) // 16
    return jnp.dot(folded, jnp.where(lane == head, 1.0, 0.0), precision=lax.Precision.HIGHEST)


def backward_kernel(
    shards, seqn, seqs, block, span, rows_of,
    lengths, grads, downs, squares, xall, probs, attended_in, da_in, query_in, keys_in, values_in, dr1_in,
    xc, xq, dvec, positions,
    out, dx_out, d_content, d_query_x, small_out,
    dq, dk, dv, late, w, x_every, dxs, sums, counts, small, io_sem, low_sem, *scratch,
):
    f32, bf16 = jnp.float32, jnp.bfloat16
    width = H * HD
    half = seqs * block
    total_pairs = seqs * H // 2
    front, scratch = scratch[:FRONT_SCRATCH], scratch[FRONT_SCRATCH:]
    back, scratch = scratch[:BACK_SCRATCH], scratch[BACK_SCRATCH:]
    send_front, stage_core, stage_deck, front_sent = reduce_front(shards, rows_of, UNITS - DOWNS, front)
    send_across, later, back_sent = reduce_back(shards, rows_of, out, back)
    small_first, small_second, small_third, small_last = small_steps(shards, seqn, small, scratch[:SMALL_SCRATCH])
    dx_first, dx_second, dx_third = dx_steps(dxs, scratch[SMALL_SCRATCH:])
    dp, sq = lax.axis_index("dp"), lax.axis_index("seq")
    acc = front[0]
    early = UNITS - DOWNS - 3
    order = lambda k: UNITS - 1 - k
    weights = [pltpu.make_async_copy(squares.at[pl.ds(u * shards, shards)], w.at[u], io_sem.at[5 + u]) for u in range(3)]
    slots = [
        pltpu.make_async_copy(xall.at[k], x_every.at[:, pl.ds(k * block, block)], io_sem.at[8 + k]) for k in range(seqn)
    ]

    def deck_and_across(u):
        stage_deck(u)
        send_across(u, acc.at[u])

    across, line, final, half_stage = later
    ready, late_from_unit = DOWNS, DOWNS + early
    plan = (
        (stage_core, ready, early, 1, 1),
        (deck_and_across, ready, early, 4, 2),
        (across, 0, DOWNS, 3, 2),
        (line, 0, DOWNS, 6, 2),
        (final, 0, DOWNS, 8, 2),
        (half_stage, 0, DOWNS, 10, 2),
        (across, ready, early, 11, 4),
        (stage_core, late_from_unit, 3, 15, 3),
        (line, ready, early, 16, 4),
        (final, ready, early, 18, 4),
        (half_stage, ready, early, 20, 4),
        (deck_and_across, late_from_unit, 3, 22, 3),
        (across, late_from_unit, 3, 29, 2),
        (line, late_from_unit, 3, 32, 2),
        (final, late_from_unit, 3, 34, 2),
        (half_stage, late_from_unit, 3, 36, 2),
    )
    ticks = 41

    def tick(t):
        for stage, first, count, start, gap in plan:
            d = t - start

            @pl.when((d >= 0) & (d < count * gap) & (lax.rem(d, gap) == 0))
            def _(stage=stage, first=first, d=d, gap=gap):
                stage(order(first + d // gap))

    def one(t, carry):
        tick(t)
        return carry

    def attention(attended, d_attended, query, keys, values, buckets, low_two, ds_sum):
        loads = [
            pltpu.make_async_copy(src, dst, io_sem.at[i])
            for i, (src, dst) in enumerate(
                ((attended_in, attended), (da_in, d_attended), (query_in, query), (keys_in, keys), (values_in, values))
            )
        ]

        def take(i, slot):
            return pltpu.make_async_copy(probs.at[i], low_two.at[slot], low_sem.at[slot])

        barrier, count = greet_all(dp, sq, shards, seqn)
        for load in loads:
            load.start()
        take(0, 0).start()
        for load in weights + slots:
            load.start()
        pl.semaphore_wait(barrier, count)

        def send(k, carry):
            u = order(DOWNS + k)
            send_front(u, lambda shard: grads.at[(u - 3) * shards + shard])
            return carry

        def send_down(k, carry):
            send_across(order(k), downs.at[order(k) - 8])
            return carry

        lax.fori_loop(0, early, send, 0)
        lax.fori_loop(0, DOWNS, send_down, 0)
        fill_buckets(buckets, positions, lengths, sq * block, seqs, block, span)
        counts[...] = jnp.zeros_like(counts)
        sums[...] = jnp.zeros_like(sums)
        for load in loads:
            load.wait()
        refs = (attended, d_attended, query, keys, values, buckets, dq, dk, dv, ds_sum, sums, counts)

        def pair(i, carry):
            slot = lax.rem(i, 2)

            tick(i)
            take(i, slot).wait()

            @pl.when(i + 1 < total_pairs)
            def _():
                take(i + 1, 1 - slot).start()

            attend_back_pair(i, refs, low_two.at[slot], seqs, block, span)
            return carry

        lax.fori_loop(0, total_pairs, pair, 0)

    pl.run_scoped(
        attention,
        pltpu.VMEM((2, seqs, block, width), bf16),
        pltpu.VMEM((2, seqs, block, width), bf16),
        pltpu.VMEM((2, seqs, block, width), bf16),
        pltpu.VMEM((seqs, span, width), bf16),
        pltpu.VMEM((seqs, span, width), bf16),
        pltpu.VMEM((seqs, 2, block, span), jnp.int32),
        pltpu.VMEM((2, 2, 2 * block, span), bf16),
        pltpu.VMEM((H, block, span), bf16),
    )

    tile = 256

    def weight_grads(dr1, turned, x_two):
        load = pltpu.make_async_copy(dr1_in, dr1, io_sem.at[0])
        load.start()
        loads = [pltpu.make_async_copy(x, x_two.at[t], io_sem.at[1 + t]) for t, x in enumerate((xc, xq))]
        for copy in loads:
            copy.start()
        for copy in weights + slots:
            copy.wait()
        matrix = lambda u: w[u].reshape(width, width)
        turned[...] = x_every[...].reshape(seqs * span, width).T

        def late_from(u, ref, first_tick):
            def tiles(n, carry):
                tick(first_tick + n)
                cols = pl.ds(pl.multiple_of(n * tile, tile), tile)
                grad = dot(turned[...], ref[:, :, cols].reshape(seqs * span, tile))
                late[u, :, :, cols] = grad.astype(bf16).reshape(shards, rows_of, tile)
                return carry

            lax.fori_loop(0, width // tile, tiles, 0)
            send_front(u, lambda shard: late.at[u, shard])

        for copy in loads:
            copy.wait()

        def tiles(n, carry):
            tick(12 + n)
            cols = pl.ds(pl.multiple_of(n * tile, tile), tile)
            grad = sum(
                dot(x_two[t].reshape(half, width), dq[t, :, :, cols].reshape(half, tile), TN) for t in range(2)
            )
            late[2, :, :, cols] = grad.astype(bf16).reshape(shards, rows_of, tile)
            return carry

        lax.fori_loop(0, width // tile, tiles, 0)
        send_front(2, lambda shard: late.at[2, shard])
        late_from(1, dv, 15)
        late_from(0, dk, 18)

        def every(n, carry):
            tick(21 + n)
            s, k = n // seqn, lax.rem(n, seqn)
            at = pl.ds(pl.multiple_of(k * block, block), block)
            part = dot(dk[s, at, :], matrix(0), NT) + dot(dv[s, at, :], matrix(1), NT)
            dxs[k, pl.ds(pl.multiple_of(s * block, block), block), :] = part.astype(bf16)
            return carry

        lax.fori_loop(0, seqs * seqn, every, 0)
        dx_first()
        load.wait()
        for t, d_x in enumerate((d_content, d_query_x)):
            d_x[...] = dr1[pl.ds(t * half, half), :] + dot(dq[t].reshape(half, width), matrix(2), NT)

    pl.run_scoped(
        weight_grads,
        pltpu.VMEM((2 * half, width), f32),
        pltpu.VMEM((width, seqs * span), bf16),
        pltpu.VMEM((2, seqs, block, width), bf16),
    )
    table = table_of(counts[...])
    vectors = jnp.concatenate([sums[0:2, :], dvec[2:, :], jnp.zeros((4, width), f32)], axis=0)
    pieces = [vectors[:, c * 128 : (c + 1) * 128] for c in range(width // 128)] + [table[:16], table[16:]]
    each = shards // 8
    size = 16 // each
    for p, piece in enumerate(pieces):
        for k in range(each):
            small[p * each + k] = piece[k * size : (k + 1) * size]
    small_first()
    lax.fori_loop(29, 31, one, 0)
    dx_second()
    lax.fori_loop(31, 33, one, 0)
    small_second()
    lax.fori_loop(33, 36, one, 0)
    small_third()
    lax.fori_loop(36, ticks, one, 0)
    dx_third(dx_out)
    small_last(small_out)
    front_sent()
    back_sent()


def backward(lengths, grads, downs, squares, xall, probs, attended, d_attended, query, keys, values, dr1, xc, xq, dvec, positions, shards, seqn):
    rows_of, width = squares.shape[1:]
    seqs, block, _ = xc.shape
    span = positions.shape[1]
    f32, bf16 = jnp.float32, jnp.bfloat16
    anywhere = pl.BlockSpec(memory_space=pl.ANY)
    vmem = pl.BlockSpec(memory_space=pltpu.VMEM)
    own = (seqs * block, width)
    small_shape = (shards, 128 // shards, 128)
    dma = pltpu.SemaphoreType.DMA
    return pl.pallas_call(
        functools.partial(backward_kernel, shards, seqn, seqs, block, span, rows_of),
        out_shape=(
            jax.ShapeDtypeStruct((UNITS, rows_of, width), f32),
            jax.ShapeDtypeStruct(own, f32),
            jax.ShapeDtypeStruct(own, f32),
            jax.ShapeDtypeStruct(own, f32),
            jax.ShapeDtypeStruct(small_shape, f32),
        ),
        in_specs=[pl.BlockSpec(memory_space=pltpu.SMEM)] + [anywhere] * 13 + [vmem] * 2,
        out_specs=(vmem,) * 5,
        scratch_shapes=[
            pltpu.VMEM((2, seqs, block, width), bf16),
            pltpu.VMEM((seqs, span, width), bf16),
            pltpu.VMEM((seqs, span, width), bf16),
            pltpu.VMEM((3, shards, rows_of, width), bf16),
            pltpu.VMEM((3, shards, rows_of, width), bf16),
            pltpu.VMEM((seqs, span, width), bf16),
            pltpu.VMEM((seqn,) + own, bf16),
            pltpu.VMEM((8, width), f32),
            pltpu.VMEM((NB * 16, H * 16), f32),
            pltpu.VMEM(small_shape, f32),
            dma((8 + seqn,)),
            dma((2,)),
        ]
        + front_scratch(shards, rows_of, UNITS - DOWNS)
        + back_scratch(shards, rows_of)
        + small_scratch(shards, seqn, small_shape)
        + dx_scratch(own),
        compiler_params=pltpu.CompilerParams(
            collective_id=1, has_side_effects=True, vmem_limit_bytes=67043328
        ),
        name="attend_back_reduce",
    )(lengths, grads, downs, squares, xall, probs, attended, d_attended, query, keys, values, dr1, xc, xq, dvec, positions)


def per_device(
    x_content, x_query, cot_content, cot_query,
    w_query, b_query, w_key, w_value, b_value, w_out, b_out, gain_attn, shift_attn,
    w_up, b_up, w_down, b_down, gain_ffn, shift_ffn, rel_table, lengths, positions, predicted,
    *, shards, seqn,
):
    f32 = jnp.float32
    seqs, block, width = x_content.shape
    r = w_query.shape[0]
    vecs = [
        v.reshape(1, v.shape[0])
        for v in (b_query, b_value, b_out, gain_attn, shift_attn, b_down, gain_ffn, shift_ffn, b_up)
    ]
    (squares, xall, probs, attended, query, keys, values, y_c, y_q, dr1, d_attended, grads, downs, dvec) = forward(
        w_key, w_value, w_query, w_out, w_up, w_down, x_content, x_query, cot_content, cot_query, vecs,
        lengths, positions, predicted, rel_table, shards, seqn,
    )
    sums, dx, d_content, d_query_x, small = backward(
        lengths, grads, downs, squares, xall, probs, attended, d_attended.reshape(attended.shape),
        query, keys, values, dr1, x_content, x_query, dvec, positions, shards, seqn,
    )
    small = small.reshape(8, 16, 128)
    summed = jnp.transpose(small[:6, :12], (1, 0, 2)).reshape(UNITS, width)
    mine = lax.axis_index("dp")
    tiny = lax.dynamic_slice_in_dim(summed[:8], mine * r, r, 1)
    g_c1 = lax.dynamic_slice_in_dim(summed[8:].reshape(4 * width), mine * 4 * r, 4 * r, 0)
    g_table = small[6:].reshape(NB, 128)[:, :H]
    shape = (seqs, block, width)
    grad_content = (d_content + dx).reshape(shape)
    g_bq, g_bv, g_bo, g_g1, g_b1, g_c2, g_g2, g_b2 = (tiny[i] for i in range(8))
    g_w1 = jnp.transpose(sums[4:8], (1, 0, 2)).reshape(r, 4 * width)
    g_w2 = sums[8:12].reshape(4 * r, width)
    return (
        y_c.reshape(shape), y_q.reshape(shape), grad_content, d_query_x.reshape(shape),
        sums[2], g_bq, sums[0], sums[1], g_bv, sums[3], g_bo, g_g1, g_b1,
        g_w1, g_c1, g_w2, g_c2, g_g2, g_b2, g_table,
    )


def solution(mesh):
    in_specs = (
        P("dp", "seq", None),
        P("dp", "seq", None),
        P("dp", "seq", None),
        P("dp", "seq", None),
        P("dp", None),
        P("dp"),
        P("dp", None),
        P("dp", None),
        P("dp"),
        P("dp", None),
        P("dp"),
        P("dp"),
        P("dp"),
        P("dp", None),
        P("dp"),
        P("dp", None),
        P("dp"),
        P("dp"),
        P("dp"),
        P(),
        P("dp"),
        P("dp", None),
        P("dp", "seq"),
    )
    out_specs = (
        P("dp", "seq", None),
        P("dp", "seq", None),
        P("dp", "seq", None),
        P("dp", "seq", None),
        P("dp", None),
        P("dp"),
        P("dp", None),
        P("dp", None),
        P("dp"),
        P("dp", None),
        P("dp"),
        P("dp"),
        P("dp"),
        P("dp", None),
        P("dp"),
        P("dp", None),
        P("dp"),
        P("dp"),
        P("dp"),
        P(),
    )
    return jax.shard_map(
        functools.partial(per_device, shards=mesh.shape["dp"], seqn=mesh.shape["seq"]),
        mesh=mesh, in_specs=in_specs, out_specs=out_specs, check_vma=False
    )
```

```python
import functools

import jax
import jax.numpy as jnp
from jax import lax
from jax.experimental import pallas as pl
from jax.experimental.pallas import tpu as pltpu
from jax.sharding import PartitionSpec as P

H = 12
HD = 64
NB = 32

MESH = pl.DeviceIdType.MESH
UNITS = 12


def cutter(rows_of):
    by_rows = rows_of % 96 == 0
    piece = rows_of // 6 if by_rows else 128

    def cut(start, size):
        if not isinstance(start, int):
            start = pl.multiple_of(start * piece, 16 if by_rows else 128)
        else:
            start = start * piece
        inner = pl.ds(start, size * piece)
        return (inner, slice(None)) if by_rows else (slice(None), inner)

    def shape(size):
        return (size * piece, 768) if by_rows else (rows_of, size * piece)

    return cut, shape


def place():
    dp, sq = lax.axis_index("dp"), lax.axis_index("seq")
    row, side = dp // 2, dp % 2
    deck, core = sq // 2, sq % 2
    return dp, sq, row, side, deck, core


def tile_of(unit, shard, shards):
    down = unit // 8
    return (1 - down) * (unit * shards + shard) + down * (8 * shards + shard * 4 + unit - 8)


def remote(src, dst, send, recv, device):
    return pltpu.make_async_remote_copy(
        src_ref=src, dst_ref=dst, send_sem=send, recv_sem=recv, device_id=device, device_id_type=MESH
    )


def greet_all(dp, sq, shards, seqn):
    barrier = pltpu.get_barrier_semaphore()

    def greet(step, carry):
        pl.semaphore_signal(barrier, inc=1, device_id=(lax.rem(dp + step, shards), sq), device_id_type=MESH)
        return carry

    def greet_seq(step, carry):
        pl.semaphore_signal(barrier, inc=1, device_id=(dp, lax.rem(sq + step, seqn)), device_id_type=MESH)
        return carry

    lax.fori_loop(1, shards, greet, 0)
    lax.fori_loop(1, seqn, greet_seq, 0)
    return barrier, shards + seqn - 2


AHEAD = 2
X_LAG = 1
Y_LAG = 1


def gather_steps(shards, seqn, ins, outs, scratch):
    wk, wv, wq, wo, wu, wd, xc = ins
    full, xall, vall = outs
    (load_sem, zu_sem, zd_sem, xs_sem, ys_sem, cp_sem, cy_sem,
     zr_sem, xr_sem, yr_sem, cpr_sem, cyr_sem, xc_send, xc_recv, vec_send, vec_recv) = scratch
    dp, sq, row, side, deck, core = place()
    rows = shards // 2
    across = (row * 2 + 1 - side, sq)
    other_deck = (dp, (1 - deck) * 2 + core)
    sibling = (dp, deck * 2 + 1 - core)
    cut, _ = cutter(full.shape[1])
    plane = cut(core * 3 + deck, 2)
    solo = cut(core * 3 + deck * 2, 1)
    theirs = cut(core * 3 + (1 - deck) * 2, 1)

    def many(count, size):
        return full.at[(pl.ds(0, count),) + cut(0, size)]

    def part(unit, shard, piece):
        return full.at[(tile_of(unit, shard, shards),) + piece]

    pieces = [wk, wv, wq, wo] + [wu.at[:, pl.ds(j * 768, 768)] for j in range(4)] + [wd.at[j] for j in range(4)]
    loads = [
        pltpu.make_async_copy(piece, full.at[tile_of(u, dp, shards)], load_sem.at[u]) for u, piece in enumerate(pieces)
    ]
    x_mine = xall.at[sq]
    xload = pltpu.make_async_copy(xc, x_mine, load_sem.at[UNITS])
    x_deck = remote(x_mine, x_mine, xc_send.at[0], xc_recv.at[0], other_deck)
    x_core = remote(x_mine, x_mine, xc_send.at[1], xc_recv.at[1], sibling)
    x_theirs = xall.at[(1 - deck) * 2 + core]
    x_forward = remote(x_theirs, x_theirs, xc_send.at[2], xc_recv.at[2], sibling)

    up = ((row + 1) * 2 + side, sq)
    down = ((row - 1) * 2 + side, sq)

    def along(u, s, src):
        dst = part(u, s * 2 + side, plane)

        @pl.when((s <= row) & (row < rows - 1))
        def _():
            remote(src, dst, zu_sem.at[s], zr_sem.at[u, s], up).start()

        @pl.when((s >= row) & (row > 0))
        def _():
            remote(src, dst, zd_sem.at[s], zr_sem.at[u, s], down).start()

    def send_own(u):
        tile = full.at[tile_of(u, dp, shards)]
        pltpu.make_async_copy(tile, tile, load_sem.at[u]).wait()
        along(u, row, part(u, dp, plane))
        across_own(u)

    def across_own(u):
        ref = part(u, dp, plane)
        remote(ref, ref, xs_sem, xr_sem.at[u], across).start()

    def to_deck(u, shard):
        ref = part(u, shard, solo)
        remote(ref, ref, ys_sem, yr_sem.at[u], other_deck).start()

    def to_core(u, shard):
        ref = part(u, shard, plane)
        remote(ref, ref, cp_sem, cpr_sem.at[u], sibling).start()

    def begin():
        barrier, count = greet_all(dp, sq, shards, seqn)
        for load in loads:
            load.start()
        xload.start()
        pl.semaphore_wait(barrier, count)

        def send_vec(step, carry):
            to = (lax.rem(dp + step, shards), sq)
            remote(vall.at[dp], vall.at[dp], vec_send, vec_recv, to).start()
            return carry

        lax.fori_loop(1, shards, send_vec, 0)

        def first(u, carry):
            send_own(u)
            return carry

        lax.fori_loop(0, AHEAD, first, 0)

        xload.wait()
        x_deck.start()
        x_core.start()

    def step(n):
        @pl.when(n + AHEAD < UNITS)
        def _():
            send_own(n + AHEAD)

        def hop(t, carry):
            u = n - (t - 1)

            def arrived(s):
                ref = part(u, s * 2 + side, plane)
                remote(ref, ref, xs_sem, zr_sem.at[u, s], across).wait_recv()
                along(u, s, ref)
                remote(ref, ref, xs_sem, xr_sem.at[u], across).start()
                to_deck(u, s * 2 + side)
                to_core(u, s * 2 + side)

            @pl.when((u >= 0) & (u < UNITS))
            def _():
                pl.when(row - t >= 0)(lambda: arrived(row - t))
                pl.when(row + t < rows)(lambda: arrived(row + t))

            return carry

        lax.fori_loop(1, rows, hop, 0)
        ux = n - (rows - 1) - X_LAG

        @pl.when((ux >= 0) & (ux < UNITS))
        def _():
            remote(many(rows, 2), many(rows, 2), xs_sem, xr_sem.at[ux], across).wait_recv()

            def pass_on(s, carry):
                to_deck(ux, s * 2 + 1 - side)
                to_core(ux, s * 2 + 1 - side)
                return carry

            lax.fori_loop(0, rows, pass_on, 0)

        uy = n - rows - X_LAG - Y_LAG

        @pl.when((uy >= 0) & (uy < UNITS))
        def _():
            remote(many(shards - 1, 1), many(shards - 1, 1), ys_sem, yr_sem.at[uy], other_deck).wait_recv()

            def pass_on(k, carry):
                ref = part(uy, lax.rem(dp + k, shards), theirs)
                remote(ref, ref, cy_sem, cyr_sem.at[uy], sibling).start()
                return carry

            lax.fori_loop(1, shards, pass_on, 0)

    def pass_x():
        x_deck.wait_recv()
        x_forward.start()

    def wait_x():
        x_core.wait_recv()
        x_forward.wait_recv()

    def wait_vec():
        rest = vall.at[pl.ds(0, shards - 1)]
        remote(rest, rest, vec_send, vec_recv, sibling).wait_recv()

    def whole(u):
        remote(many(shards - 1, 2), many(shards - 1, 2), cp_sem, cpr_sem.at[u], sibling).wait_recv()
        remote(many(shards - 1, 1), many(shards - 1, 1), cy_sem, cyr_sem.at[u], sibling).wait_recv()

    def finish():
        x_deck.wait_send()
        x_core.wait_send()
        x_forward.wait_send()
        rest = vall.at[pl.ds(0, shards - 1)]
        remote(rest, rest, vec_send, vec_recv, sibling).wait_send()
        for count, size, sem in (
            (UNITS * rows, 2, xs_sem),
            (UNITS * (shards - 1), 1, ys_sem),
            (UNITS * (shards - 1), 1, cy_sem),
            (UNITS * (shards - 1), 2, cp_sem),
        ):
            ref = many(count, size)
            remote(ref, ref, sem, xr_sem.at[0], sibling).wait_send()

        def sent(s, carry):
            ref = many(UNITS, 2)

            @pl.when((s <= row) & (row < rows - 1))
            def _():
                remote(ref, ref, zu_sem.at[s], xr_sem.at[0], sibling).wait_send()

            @pl.when((s >= row) & (row > 0))
            def _():
                remote(ref, ref, zd_sem.at[s], xr_sem.at[0], sibling).wait_send()

            return carry

        lax.fori_loop(0, rows, sent, 0)

    return begin, step, whole, pass_x, wait_x, wait_vec, finish


def gather_scratch(shards):
    dma = pltpu.SemaphoreType.DMA
    return [dma((UNITS + 1,))] + [dma((shards // 2,))] * 2 + [dma(())] * 4 + [dma((UNITS, shards // 2))] + [dma((UNITS,))] * 4 + [dma((3,)), dma((3,)), dma(()), dma(())]


GATHER_SCRATCH = 16


def reduce_front(shards, rows_of, count, scratch):
    f32, bf16 = jnp.float32, jnp.bfloat16
    acc, got_core, got_deck, load_sem, core_send, core_recv, deck_send, deck_recv = scratch
    dp, sq, row, side, deck, core = place()
    rows = shards // 2
    other_deck = (dp, (1 - deck) * 2 + core)
    sibling = (dp, deck * 2 + 1 - core)
    cut, _ = cutter(rows_of)
    mine = cut(core * 3, 3)
    siblings = cut((1 - core) * 3, 3)
    solo = cut(deck * 2, 1)
    other_solo = cut((1 - deck) * 2, 1)

    def send(u, tiles):
        def one(s, carry):
            for b in range(2):
                tile = tiles(s * 2 + b)
                remote(tile.at[siblings], got_core.at[u, s, b], core_send.at[u], core_recv.at[u], sibling).start()
                pltpu.make_async_copy(tile.at[mine], acc.at[u, s, b], load_sem.at[u]).start()
            return carry

        lax.fori_loop(0, rows, one, 0)

    def core_copy(u):
        return remote(got_core.at[u], got_core.at[u], core_send.at[u], core_recv.at[u], sibling)

    def deck_copy(u):
        src = acc.at[(u, slice(None), slice(None)) + other_solo]
        return remote(src, got_deck.at[u], deck_send.at[u], deck_recv.at[u], other_deck)

    def stage_core(u):
        pltpu.make_async_copy(acc.at[u], acc.at[u], load_sem.at[u]).wait()
        core_copy(u).wait_recv()

        def add(s, carry):
            for b in range(2):
                acc[u, s, b] = total(acc[u, s, b], got_core[u, s, b])
            return carry

        lax.fori_loop(0, rows, add, 0)
        deck_copy(u).start()

    def stage_deck(u):
        deck_copy(u).wait_recv()

        def add(s, carry):
            for b in range(2):
                at = (u, s, b) + solo
                acc[at] = total(acc[at], got_deck[u, s, b])
            return carry

        lax.fori_loop(0, rows, add, 0)

    def sent():
        def one(u, carry):
            core_copy(u).wait_send()
            deck_copy(u).wait_send()
            return carry

        lax.fori_loop(0, count, one, 0)

    return send, stage_core, stage_deck, sent


def total(left, right):
    return left + right


def front_scratch(shards, rows_of, count):
    bf16 = jnp.bfloat16
    rows = shards // 2
    _, shape = cutter(rows_of)
    return [
        pltpu.VMEM((count, rows, 2) + shape(3), bf16),
        pltpu.VMEM((count, rows, 2) + shape(3), bf16),
        pltpu.VMEM((count, rows, 2) + shape(1), bf16),
    ] + [pltpu.SemaphoreType.DMA((count,))] * 5


FRONT_SCRATCH = 8


def reduce_back(shards, rows_of, out, scratch):
    f32, bf16 = jnp.float32, jnp.bfloat16
    (own_side, got_across, line, got_line, final, got_final, half, got_half,
     side_sem, across_send, across_recv, line_send, line_recv, final_send, final_recv, half_send, half_recv) = scratch
    dp, sq, row, side, deck, core = place()
    rows = shards // 2
    across = (row * 2 + 1 - side, sq)
    other_deck = (dp, (1 - deck) * 2 + core)
    sibling = (dp, deck * 2 + 1 - core)
    cut, _ = cutter(rows_of)
    mine = cut(core * 3, 3)
    siblings = cut((1 - core) * 3, 3)
    plane = cut(deck, 2)
    other_solo = cut((1 - deck) * 2, 1)

    def send_across(u, planes):
        remote(
            planes.at[(slice(None), 1 - side) + plane], got_across.at[u], across_send.at[u], across_recv.at[u], across
        ).start()
        pltpu.make_async_copy(planes.at[(slice(None), side) + plane], own_side.at[u], side_sem.at[u]).start()

    def across_copy(u):
        return remote(got_across.at[u], got_across.at[u], across_send.at[u], across_recv.at[u], across)

    def line_copy(u):
        ref = got_line.at[u, pl.ds(0, rows - 1)]
        return remote(ref, ref, line_send.at[u], line_recv.at[u], across)

    def final_copy(u):
        return remote(final.at[u], got_final.at[u], final_send.at[u], final_recv.at[u], other_deck)

    def half_copy(u):
        return remote(half.at[u], got_half.at[u], half_send.at[u], half_recv.at[u], sibling)

    def stage_across(u):
        pltpu.make_async_copy(own_side.at[u], own_side.at[u], side_sem.at[u]).wait()
        across_copy(u).wait_recv()

        def add(k, carry):
            s = lax.rem(row + k, rows)
            line[u, s] = total(own_side[u, s], got_across[u, s])

            @pl.when(k < rows)
            def _():
                remote(
                    line.at[u, s], got_line.at[u, rows - 1 - k], line_send.at[u], line_recv.at[u], (s * 2 + side, sq)
                ).start()

            return carry

        lax.fori_loop(1, rows + 1, add, 0)

    def stage_line(u):
        line_copy(u).wait_recv()
        summed = line[u, row].astype(f32)
        if rows <= 4:
            for k in range(rows - 1):
                summed = summed + got_line[u, k].astype(f32)
        else:
            summed = lax.fori_loop(0, rows - 1, lambda k, t: t + got_line[u, k].astype(f32), summed)
        final[u] = summed.astype(bf16)
        final_copy(u).start()

    def stage_final(u):
        final_copy(u).wait_recv()
        half[(u,) + plane] = final[u]
        half[(u,) + other_solo] = got_final[(u,) + cut(1 - deck, 1)]
        both = (u,) + cut(1, 1)
        half[both] = total(half[both], got_final[(u,) + cut(deck, 1)])
        half_copy(u).start()

    def stage_half(u):
        half_copy(u).wait_recv()
        out[(u,) + mine] = half[u]
        out[(u,) + siblings] = got_half[u]

    def sent():
        def one(u, carry):
            for copy in (across_copy, line_copy, final_copy, half_copy):
                copy(u).wait_send()
            return carry

        lax.fori_loop(0, UNITS, one, 0)

    return send_across, (stage_across, stage_line, stage_final, stage_half), sent


def back_scratch(shards, rows_of):
    bf16 = jnp.bfloat16
    rows = shards // 2
    _, shape = cutter(rows_of)
    return [pltpu.VMEM((UNITS, rows) + shape(2), bf16)] * 4 + [
        pltpu.VMEM((UNITS,) + shape(2), bf16),
        pltpu.VMEM((UNITS,) + shape(2), bf16),
        pltpu.VMEM((UNITS,) + shape(3), bf16),
        pltpu.VMEM((UNITS,) + shape(3), bf16),
    ] + [pltpu.SemaphoreType.DMA((UNITS,))] * 9


BACK_SCRATCH = 17


def small_steps(shards, seqn, small, scratch):
    got_small, mid_small, got_mid, got_all, small_send, small_recv = scratch
    dp, sq, row, side, deck, core = place()
    sibling = (dp, deck * 2 + 1 - core)

    def small_first():
        got_small[dp] = small[dp]

        def send(k, carry):
            to = lax.rem(dp + k, shards)
            remote(small.at[to], got_small.at[dp], small_send.at[0], small_recv.at[0], (to, sq)).start()
            return carry

        lax.fori_loop(1, shards, send, 0)

    def sum_of(ref, count):
        summed = ref[0]
        for i in range(1, count):
            summed = summed + ref[i]
        return summed

    def small_second():
        rest = got_small.at[pl.ds(0, shards - 1)]
        remote(rest, rest, small_send.at[0], small_recv.at[0], sibling).wait()
        summed = sum_of(got_small, shards)
        mid_small[0] = summed
        got_mid[sq] = summed

        def send(k, carry):
            to = (dp, lax.rem(sq + k, seqn))
            remote(mid_small.at[0], got_mid.at[sq], small_send.at[1], small_recv.at[1], to).start()
            return carry

        lax.fori_loop(1, seqn, send, 0)

    def small_third():
        rest = got_mid.at[pl.ds(0, seqn - 1)]
        remote(rest, rest, small_send.at[1], small_recv.at[1], sibling).wait()
        summed = sum_of(got_mid, seqn)
        mid_small[1] = summed
        got_all[dp] = summed

        def send(k, carry):
            to = (lax.rem(dp + k, shards), sq)
            remote(mid_small.at[1], got_all.at[dp], small_send.at[2], small_recv.at[2], to).start()
            return carry

        lax.fori_loop(1, shards, send, 0)

    def small_last(small_out):
        rest = got_all.at[pl.ds(0, shards - 1)]
        remote(rest, rest, small_send.at[2], small_recv.at[2], sibling).wait()
        small_out[...] = got_all[...]

    return small_first, small_second, small_third, small_last


def small_scratch(shards, seqn, small_shape):
    f32 = jnp.float32
    return [
        pltpu.VMEM(small_shape, f32),
        pltpu.VMEM((2,) + small_shape[1:], f32),
        pltpu.VMEM((seqn,) + small_shape[1:], f32),
        pltpu.VMEM(small_shape, f32),
    ] + [pltpu.SemaphoreType.DMA((3,))] * 2


SMALL_SCRATCH = 6


def dx_steps(dxs, scratch):
    f32, bf16 = jnp.float32, jnp.bfloat16
    dx_own, dx_core, dx_deck, load, send, recv = scratch
    dp, sq, row, side, deck, core = place()
    other_deck = (dp, (1 - deck) * 2 + core)
    sibling = (dp, deck * 2 + 1 - core)
    deck_dx = remote(dx_own.at[1 - deck], dx_deck, send.at[2], recv.at[2], other_deck)

    def first():
        for k in range(2):
            pltpu.make_async_copy(dxs.at[k * 2 + core], dx_own.at[k], load.at[k]).start()
            remote(dxs.at[k * 2 + 1 - core], dx_core.at[k], send.at[k], recv.at[k], sibling).start()

    def second():
        for k in range(2):
            pltpu.make_async_copy(dx_own.at[k], dx_own.at[k], load.at[k]).wait()
            remote(dx_core.at[k], dx_core.at[k], send.at[k], recv.at[k], sibling).wait()
            dx_own[k] = (dx_own[k].astype(f32) + dx_core[k].astype(f32)).astype(bf16)
        deck_dx.start()

    def third(dx_out):
        deck_dx.wait()
        dx_out[...] += dx_own[deck].astype(f32) + dx_deck[...].astype(f32)

    return first, second, third


def dx_scratch(own):
    bf16 = jnp.bfloat16
    dma = pltpu.SemaphoreType.DMA
    return [pltpu.VMEM((2,) + own, bf16), pltpu.VMEM((2,) + own, bf16), pltpu.VMEM(own, bf16), dma((2,)), dma((3,)), dma((3,))]


bucket_marks = (12, 16, 23, 32, 46, 64, 91)
MASKED = NB
TN = (((0,), (0,)), ((), ()))
NT = (((1,), (1,)), ((), ()))


def dot(left, right, dims=None):
    if dims is None:
        dims = (((1,), (0,)), ((), ()))
    return lax.dot_general(left, right, dims, preferred_element_type=jnp.float32)


def column_of(row):
    return jnp.broadcast_to(row.astype(jnp.float32), (row.shape[1], row.shape[1])).T


def fill_buckets(buckets, positions, lengths, base, seqs, block, span):
    for s in range(seqs):
        mine = column_of(positions[s : s + 1, pl.ds(pl.multiple_of(base, block), block)]).astype(jnp.int32)
        for c in range(span // block):
            cols = slice(c * block, (c + 1) * block)
            delta = positions[s : s + 1, cols] - mine
            dist = jnp.abs(delta)
            far = jnp.full(dist.shape, 8, jnp.int32)
            for mark in bucket_marks:
                far = far + (dist >= mark).astype(jnp.int32)
            bucket = jnp.where(dist < 8, dist, far) + 16 * (delta > 0).astype(jnp.int32)
            i = base + lax.broadcasted_iota(jnp.int32, (block, block), 0)
            j = c * block + lax.broadcasted_iota(jnp.int32, (block, block), 1)
            valid = j < lengths[s]
            buckets[s, 0, :, cols] = jnp.where(valid & (j <= i), bucket, MASKED)
            buckets[s, 1, :, cols] = jnp.where(valid & (j < jnp.maximum(i, 1)), bucket, MASKED)


def head_lanes(rows, half):
    lane = lax.broadcasted_iota(jnp.int32, (rows, 2 * HD), 1)
    return (lane < HD) if half == 0 else (lane >= HD)


def fill_bias(i, biases, buckets, table, block, span):
    s, head = i // H, lax.rem(i, H)
    entry = jnp.broadcast_to(table[pl.ds(head, 1), :], (block, 128))
    for c in range(span // 128):
        cols = slice(c * 128, (c + 1) * 128)
        value = jnp.take_along_axis(entry, buckets[s, 0, :, cols], axis=1, mode="promise_in_bounds")
        biases[i, 0, :, cols] = value
        biases[i, 1, :, cols] = jnp.where(buckets[s, 1, :, cols] == MASKED, -1e30, value)


def attend_pair(i, refs, block, span, low_out):
    attended, query, keys, values, biases = refs
    f32, bf16 = jnp.float32, jnp.bfloat16
    pairs = H // 2
    s, pair = i // pairs, lax.rem(i, pairs)
    lanes = pl.ds(pl.multiple_of(pair * 128, 128), 128)
    q = query[:, s, :, lanes].reshape(2 * block, 128)
    k = keys[s, :, lanes]
    v = values[s, :, lanes]
    outs = []
    for half in range(2):
        mine = head_lanes(2 * block, half)
        one = jnp.where(mine, q * 0.125, 0).astype(bf16)
        scores = dot(one, k, NT) + biases[i * 2 + half].reshape(2 * block, span)
        top = jnp.max(scores, axis=-1, keepdims=True)
        expo = jnp.exp(scores - top)
        low = (expo * (1.0 / jnp.sum(expo, axis=-1, keepdims=True))).astype(bf16)
        low_out[half] = low
        outs.append(dot(low, v))
    mixed = jnp.where(head_lanes(2 * block, 0), outs[0], outs[1]).astype(bf16)
    attended[:, s, :, lanes] = mixed.reshape(2, block, 128)


def center_of(value):
    center = value - jnp.mean(value, axis=-1, keepdims=True)
    var = jnp.mean(center * center, axis=-1, keepdims=True)
    inv = lax.rsqrt(var + 1e-05)
    return center * inv, inv


def norm_back(grad, gain, normed, inv):
    scaled = grad * gain
    return inv * (
        scaled
        - jnp.mean(scaled, axis=-1, keepdims=True)
        - normed * jnp.mean(scaled * normed, axis=-1, keepdims=True)
    )


EARLY = 9
BIAS_STEPS = 8
TILE = 256
LONG = 384
DOWNS = 4


def forward_kernel(
    shards, seqn, seqs, block, span, rows_of,
    lengths, wk, wv, wq, wo, wu, wd, xc, xc_rows, xq_rows, cot_c, cot_q, positions, predicted, rel_table,
    bq, bv, bo, g1, b1, c2, g2, b2, c1,
    squares, x_out, probs, attended_out, query_out, keys_out, values_out, y_c, y_q, dr1_out, da_out, grads, downs, dvec,
    full, xall, vall, vectors, keep, attended, table, io_sem, low_sem, *scratch,
):
    f32, bf16 = jnp.float32, jnp.bfloat16
    width = H * HD
    half = seqs * block
    rows = 2 * half
    r = rows_of
    wide = 4 * r
    base = lax.axis_index("seq") * block
    me = lax.axis_index("dp")
    begin, step, whole, pass_x, wait_x, wait_vec, finish = gather_steps(
        shards, seqn, (wk, wv, wq, wo, wu, wd, xc), (full, xall, vall), scratch[: -FRONT_SCRATCH]
    )
    send_front, stage_core, stage_deck, front_sent = reduce_front(shards, r, DOWNS, scratch[-FRONT_SCRATCH:])
    acc = scratch[-FRONT_SCRATCH]
    vall[me] = jnp.zeros(vall.shape[1:], f32)
    for i, piece in enumerate((bq, bv, bo, g1, b1, c2, g2, b2)):
        vall[me, i : i + 1, 0:r] = piece[...].astype(f32)
    vall[me, 8:9, :] = c1[...].astype(f32).reshape(1, wide)
    begin()

    def one(n, carry):
        step(n)
        return carry

    def matrix(u):
        return full[pl.ds(u * shards, shards)].reshape(width, width)

    def columns(u, cols):
        size = cols.size
        return full[pl.ds(u * shards, shards), :, cols].reshape(width, size)

    def row_block(u, n):
        per = LONG // r
        return full[pl.ds(u * shards + n * per, per)].reshape(LONG, width)

    def attention(query, keys, values, buckets, low_two, biases):
        fill_buckets(buckets, positions, lengths, base, seqs, block, span)
        eye = (
            lax.broadcasted_iota(jnp.int32, (NB, 128), 0) == lax.broadcasted_iota(jnp.int32, (NB, 128), 1)
        )
        by_head = dot(rel_table[...], jnp.where(eye, 1.0, 0.0).astype(bf16))
        lane = lax.broadcasted_iota(jnp.int32, by_head.shape, 1)
        table[...] = jnp.where(lane < NB, by_head, -1e30)
        for s in range(seqs):
            live = base + lax.broadcasted_iota(jnp.int32, (block, 1), 0) < lengths[s]
            chosen = column_of(predicted[s : s + 1, :])[:, 0:1] > 0
            keep[s * block : (s + 1) * block, :] = jnp.where(live, 1.0, 0.0)
            keep[half + s * block : half + (s + 1) * block, :] = jnp.where(live & chosen, 1.0, 0.0)
        share = seqs * H // BIAS_STEPS

        def one_and_bias(n, carry):
            step(n)

            def bias(k, inner):
                fill_bias(n * share + k, biases, buckets, table, block, span)
                return inner

            return lax.fori_loop(0, share, bias, carry)

        lax.fori_loop(0, BIAS_STEPS - 2, one_and_bias, 0)
        pass_x()
        lax.fori_loop(BIAS_STEPS - 2, BIAS_STEPS, one_and_bias, 0)
        lax.fori_loop(BIAS_STEPS, EARLY, one, 0)
        wait_x()
        wait_vec()
        vectors[...] = jnp.zeros_like(vectors)

        def spread(i, carry):
            row = lax.broadcasted_iota(jnp.int32, (r, width), 0)
            col = lax.broadcasted_iota(jnp.int32, (r, width), 1)
            at = jnp.where(col == row + i * r, 1.0, 0.0).astype(bf16)
            vectors[0:8, :] += dot(vall[i, 0:8, 0:r].astype(bf16), at)
            per = width // wide
            row = lax.broadcasted_iota(jnp.int32, (wide, width), 0)
            col = lax.broadcasted_iota(jnp.int32, (wide, width), 1)
            at = jnp.where(col == row + lax.rem(i, per) * wide, 1.0, 0.0).astype(bf16)
            vectors[pl.ds(8 + i // per, 1), :] += dot(vall[i, 8:9, :].astype(bf16), at)
            return carry

        lax.fori_loop(0, shards, spread, 0)
        for u in range(3):
            whole(u)

        def project(k, carry):
            @pl.when(k == 2)
            def _():
                step(EARLY)

            x = xall[k].reshape(half, width)
            at = pl.ds(pl.multiple_of(k * block, block), block)
            keys[:, at, :] = dot(x, matrix(0)).astype(bf16).reshape(seqs, block, width)
            values[:, at, :] = (dot(x, matrix(1)) + vectors[1:2, :]).astype(bf16).reshape(seqs, block, width)
            return carry

        lax.fori_loop(0, seqn, project, 0)
        for t, x in enumerate((xc_rows, xq_rows)):
            query[t] = (dot(x[...], matrix(2)) + vectors[0:1, :]).astype(bf16).reshape(seqs, block, width)
        puts = [
            pltpu.make_async_copy(src, dst, io_sem.at[i])
            for i, (src, dst) in enumerate(((query, query_out), (keys, keys_out), (values, values_out)))
        ]
        for copy in puts:
            copy.start()
        total = seqs * H // 2

        def put(i, slot):
            return pltpu.make_async_copy(low_two.at[slot], probs.at[i], low_sem.at[slot])

        def attend_one(i, carry):
            slot = lax.rem(i, 2)

            @pl.when(lax.rem(i, 3) == 1)
            def _():
                step(EARLY + 1 + i // 3)

            @pl.when(i >= 2)
            def _():
                put(i - 2, slot).wait()

            attend_pair(i, (attended, query, keys, values, biases), block, span, low_two.at[slot])
            put(i, slot).start()
            return carry

        lax.fori_loop(0, total, attend_one, 0)
        put(total - 2, (total - 2) % 2).wait()
        put(total - 1, (total - 1) % 2).wait()
        for copy in puts:
            copy.wait()

    pl.run_scoped(
        attention,
        pltpu.VMEM((2, seqs, block, width), bf16),
        pltpu.VMEM((seqs, span, width), bf16),
        pltpu.VMEM((seqs, span, width), bf16),
        pltpu.VMEM((seqs, 2, block, span), jnp.int32),
        pltpu.VMEM((2, 2, 2 * block, span), bf16),
        pltpu.VMEM((seqs * H, 2, block, span), f32),
    )
    done = EARLY + 1 + seqs * H // 6
    more = [
        pltpu.make_async_copy(full.at[pl.ds(0, 3 * shards)], squares, io_sem.at[3]),
        pltpu.make_async_copy(xall, x_out, io_sem.at[4]),
        pltpu.make_async_copy(attended, attended_out, io_sem.at[5]),
    ]
    for copy in more:
        copy.start()
    dvec[...] = jnp.zeros_like(dvec)
    vec = lambda i: vectors[i : i + 1, :]
    chunk = 128
    chunks = half // chunk

    def ffn(hidden, hidden_low, hidden_turn, normed1, inv1, active, slope, feed, dr2, dr2_low, dr1_low, da, stage, stage_down):
        step(done)
        whole(3)

        def phase_one(c, carry):
            t, s = c // seqs, lax.rem(c, seqs)
            at = pl.ds(pl.multiple_of(c * chunk, chunk), chunk)
            out = dot(attended[t, s], matrix(3)) + vec(2)
            inner = pl.ds(pl.multiple_of(s * chunk, chunk), chunk)
            x = jnp.where(t == 0, xc_rows[inner, :].astype(f32), xq_rows[inner, :].astype(f32))
            normed, inv = center_of(x + out)
            normed1[at, :] = normed
            inv1[at, :] = inv
            h = normed * vec(3) + vec(4)
            hidden[at, :] = h
            hidden_low[at, :] = h.astype(bf16)
            return carry

        lax.fori_loop(0, rows // chunk, phase_one, 0)
        hidden_turn[...] = hidden_low[...].T
        tiles = width // TILE

        def phase_two(j, carry):
            step(done + 1 + j)
            whole(4 + j)

            def tile(n, inner):
                cols = pl.ds(pl.multiple_of(n * TILE, TILE), TILE)
                u = dot(hidden_low[...], columns(4 + j, cols)) + vectors[pl.ds(8 + j, 1), cols]
                cdf = 0.5 * (1.0 + lax.erf(u * (2.0**-0.5)))
                active[j, :, cols] = (u * cdf).astype(bf16)
                slope[j, :, cols] = (cdf + u * (jnp.exp(-0.5 * u * u) * ((2.0 * jnp.pi) ** -0.5))).astype(bf16)
                return inner

            return lax.fori_loop(0, tiles, tile, carry)

        lax.fori_loop(0, 4, phase_two, 0)

        def last(u, carry):
            whole(u)
            return carry

        lax.fori_loop(done + 5, UNITS + shards // 2 + X_LAG + Y_LAG, one, 0)
        lax.fori_loop(8, UNITS, last, 0)

        def phase_feed(n, carry):
            cols = pl.ds(pl.multiple_of(n * TILE, TILE), TILE)
            feed[:, cols] = sum(dot(active[j], columns(8 + j, cols)) for j in range(4))
            return carry

        lax.fori_loop(0, tiles, phase_feed, 0)

        def phase_three(c, carry):
            t, s = c // seqs, lax.rem(c, seqs)
            at = pl.ds(pl.multiple_of(c * chunk, chunk), chunk)
            normed, inv = center_of(hidden[at, :] + feed[at, :] + vec(5))
            kept = keep[at, :]
            feed[at, :] = (normed * vec(6) + vec(7)) * kept
            inner = pl.ds(pl.multiple_of(s * chunk, chunk), chunk)
            cot = jnp.where(t == 0, cot_c[inner, :].astype(f32), cot_q[inner, :].astype(f32)) * kept
            d = norm_back(cot, vec(6), normed, inv)
            dvec[6:7, :] += jnp.sum(cot * normed, axis=0, keepdims=True)
            dvec[7:8, :] += jnp.sum(cot, axis=0, keepdims=True)
            dvec[5:6, :] += jnp.sum(d, axis=0, keepdims=True)
            dr2[at, :] = d
            dr2_low[at, :] = d.astype(bf16)
            return carry

        lax.fori_loop(0, rows // chunk, phase_three, 0)
        y_copies = [
            pltpu.make_async_copy(feed.at[pl.ds(0, half)], y_c, io_sem.at[6]),
            pltpu.make_async_copy(feed.at[pl.ds(half, half)], y_q, io_sem.at[7]),
        ]
        for copy in y_copies:
            copy.start()
        longs = width // LONG

        def phase_down(j, carry):
            grad = dot(active[j], dr2_low[...], TN).astype(bf16)
            stage_down[pl.ds(j * shards, shards)] = grad.reshape(shards, r, width)
            return carry

        lax.fori_loop(0, 4, phase_down, 0)

        def start_down(k, carry):
            send_front(k, lambda shard: stage_down.at[shard * 4 + k])
            return carry

        lax.fori_loop(0, DOWNS, start_down, 0)

        def phase_slope(j, carry):
            du = slope[j].astype(f32) * dot(dr2_low[...], matrix(8 + j), NT)
            dvec[pl.ds(8 + j, 1), :] = jnp.sum(du, axis=0, keepdims=True)
            active[j] = du.astype(bf16)
            stage_core(j)
            return carry

        lax.fori_loop(0, 4, phase_slope, 0)

        def phase_up(j, carry):
            grad = dot(hidden_turn[...], active[j]).astype(bf16)
            stage[1 + j] = grad.reshape(shards, r, width)
            pltpu.make_async_copy(
                stage.at[1 + j], grads.at[pl.ds((1 + j) * shards, shards)], io_sem.at[10 + j]
            ).start()
            return carry

        lax.fori_loop(0, 4, phase_up, 0)

        def put_down(k):
            return pltpu.make_async_copy(acc.at[k], downs.at[k], io_sem.at[14 + k])

        def finish_down(k):
            stage_deck(k)
            put_down(k).start()

        finish_down(0)

        def phase_hidden(n, carry):
            cols = pl.ds(pl.multiple_of(n * LONG, 128), LONG)
            dr2[:, cols] += sum(dot(active[j], row_block(4 + j, n), NT) for j in range(4))
            return carry

        lax.fori_loop(0, longs, phase_hidden, 0)
        for copy in y_copies:
            copy.wait()
        finish_down(1)

        def phase_five(c, carry):
            at = pl.ds(pl.multiple_of(c * chunk, chunk), chunk)
            dh = dr2[at, :]
            normed = normed1[at, :]
            d = norm_back(dh, vec(3), normed, inv1[at, :])
            dvec[3:4, :] += jnp.sum(dh * normed, axis=0, keepdims=True)
            dvec[4:5, :] += jnp.sum(dh, axis=0, keepdims=True)
            dvec[2:3, :] += jnp.sum(d, axis=0, keepdims=True)
            feed[at, :] = d
            low = d.astype(bf16)
            dr1_low[at, :] = low
            da[at, :] = dot(low, matrix(3), NT).astype(bf16)
            return carry

        lax.fori_loop(0, rows // chunk, phase_five, 0)
        finals = [
            pltpu.make_async_copy(feed, dr1_out, io_sem.at[6]),
            pltpu.make_async_copy(da, da_out, io_sem.at[7]),
        ]
        for copy in finals:
            copy.start()
        finish_down(2)
        turned = attended[...].reshape(rows, width).T

        def phase_out(n, carry):
            cols = pl.ds(pl.multiple_of(n * TILE, TILE), TILE)
            grad = dot(hidden_turn[...], dr1_low[:, cols]).astype(bf16)
            stage[0, :, :, cols] = grad.reshape(shards, r, TILE)
            return carry

        hidden_turn[...] = turned
        lax.fori_loop(0, tiles, phase_out, 0)
        out_copy = pltpu.make_async_copy(stage.at[0], grads.at[pl.ds(0, shards)], io_sem.at[9])
        out_copy.start()
        finish_down(3)
        for j in range(4):
            pltpu.make_async_copy(
                stage.at[1 + j], grads.at[pl.ds((1 + j) * shards, shards)], io_sem.at[10 + j]
            ).wait()
            put_down(j).wait()
        out_copy.wait()
        for copy in finals + more:
            copy.wait()
        front_sent()
        finish()

    pl.run_scoped(
        ffn,
        pltpu.VMEM((rows, width), f32),
        pltpu.VMEM((rows, width), bf16),
        pltpu.VMEM((width, rows), bf16),
        pltpu.VMEM((rows, width), f32),
        pltpu.VMEM((rows, 1), f32),
        pltpu.VMEM((4, rows, width), bf16),
        pltpu.VMEM((4, rows, width), bf16),
        pltpu.VMEM((rows, width), f32),
        pltpu.VMEM((rows, width), f32),
        pltpu.VMEM((rows, width), bf16),
        pltpu.VMEM((rows, width), bf16),
        pltpu.VMEM((rows, width), bf16),
        pltpu.VMEM((5, shards, r, width), bf16),
        pltpu.VMEM((4 * shards, r, width), bf16),
    )


def forward(wk, wv, wq, wo, wu, wd, xc, xq, cot_c, cot_q, vecs, lengths, positions, predicted, rel_table, shards, seqn):
    rows_of, width = wq.shape
    seqs, block, _ = xc.shape
    span = positions.shape[1]
    f32, bf16 = jnp.float32, jnp.bfloat16
    steps = seqs * H // 2
    half = seqs * block
    anywhere = pl.BlockSpec(memory_space=pl.ANY)
    vmem = pl.BlockSpec(memory_space=pltpu.VMEM)
    rows = shards // 2
    _, shape = cutter(rows_of)
    dma = pltpu.SemaphoreType.DMA
    flat = lambda a: a.reshape(half, width)
    stream = (2, seqs, block, width)
    return pl.pallas_call(
        functools.partial(forward_kernel, shards, seqn, seqs, block, span, rows_of),
        out_shape=(
            jax.ShapeDtypeStruct((3 * shards, rows_of, width), bf16),
            jax.ShapeDtypeStruct((seqn,) + xc.shape, bf16),
            jax.ShapeDtypeStruct((steps, 2, 2 * block, span), bf16),
            jax.ShapeDtypeStruct(stream, bf16),
            jax.ShapeDtypeStruct(stream, bf16),
            jax.ShapeDtypeStruct((seqs, span, width), bf16),
            jax.ShapeDtypeStruct((seqs, span, width), bf16),
            jax.ShapeDtypeStruct((half, width), f32),
            jax.ShapeDtypeStruct((half, width), f32),
            jax.ShapeDtypeStruct((2 * half, width), f32),
            jax.ShapeDtypeStruct((2 * half, width), bf16),
            jax.ShapeDtypeStruct((5 * shards, rows_of, width), bf16),
            jax.ShapeDtypeStruct((DOWNS, rows, 2) + shape(3), bf16),
            jax.ShapeDtypeStruct((UNITS, width), f32),
        ),
        in_specs=[pl.BlockSpec(memory_space=pltpu.SMEM)] + [anywhere] * 7 + [vmem] * 16,
        out_specs=(anywhere,) * 13 + (vmem,),
        scratch_shapes=[
            pltpu.VMEM((UNITS * shards, rows_of, width), bf16),
            pltpu.VMEM((seqn,) + xc.shape, bf16),
            pltpu.VMEM((shards, 9, 4 * rows_of), f32),
            pltpu.VMEM((UNITS, width), f32),
            pltpu.VMEM((2 * half, 1), f32),
            pltpu.VMEM(stream, bf16),
            pltpu.VMEM((H, 128), f32),
            dma((18,)),
            dma((2,)),
        ]
        + gather_scratch(shards)
        + front_scratch(shards, rows_of, DOWNS),
        compiler_params=pltpu.CompilerParams(collective_id=0, has_side_effects=True, vmem_limit_bytes=67043328),
        name="gather_attend_ffn",
    )(
        lengths, wk, wv, wq, wo, wu, wd.reshape(4, rows_of, width), xc, flat(xc), flat(xq), flat(cot_c), flat(cot_q),
        positions, predicted, rel_table.T, *vecs,
    )


def attend_back_pair(i, refs, low, seqs, block, span):
    attended, d_attended, query, keys, values, buckets, dq, dk, dv, ds_sum, sums, counts = refs
    f32, bf16 = jnp.float32, jnp.bfloat16
    pairs = H // 2
    rows = 2 * block
    s, pair = i // pairs, lax.rem(i, pairs)
    lanes = pl.ds(pl.multiple_of(pair * 128, 128), 128)
    q = query[:, s, :, lanes].reshape(rows, 128)
    k = keys[s, :, lanes]
    v = values[s, :, lanes]
    da = d_attended[:, s, :, lanes].reshape(rows, 128)
    product = da.astype(f32) * attended[:, s, :, lanes].reshape(rows, 128).astype(f32)
    d_queries, dk_turn, dv_turn = [], 0.0, 0.0
    for half in range(2):
        mine = head_lanes(rows, half)
        one = jnp.where(mine, da, 0).astype(bf16)
        inner = jnp.sum(jnp.where(mine, product, 0.0), axis=-1, keepdims=True)
        ds = low[half].astype(f32) * (dot(one, v, NT) - inner)
        ds_sum[pair * 2 + half] = (ds[:block] + ds[block:]).astype(bf16)
        ds_low = ds.astype(bf16)
        d_queries.append(dot(ds_low, k))
        dk_turn += dot(jnp.where(mine, q, 0).astype(bf16), ds_low, TN)
        dv_turn += dot(one, low[half], TN)
    d_query = jnp.where(head_lanes(rows, 0), d_queries[0], d_queries[1]) * 0.125
    sums[0:1, lanes] += jnp.sum(d_query, axis=0, keepdims=True)
    dq[:, s, :, lanes] = d_query.reshape(2, block, 128).astype(bf16)
    dk[s, :, lanes] = (dk_turn * 0.125).T.astype(bf16)
    d_value = dv_turn.T
    sums[1:2, lanes] += jnp.sum(d_value, axis=0, keepdims=True)
    dv[s, :, lanes] = d_value.astype(bf16)

    @pl.when(pair == pairs - 1)
    def _():
        def count(g, carry):
            at = pl.ds(pl.multiple_of(g * 16, 16), 16)
            bucket = buckets[s, 0, at, :]
            hot = jnp.concatenate([jnp.where(bucket == n, 1.0, 0.0).astype(bf16) for n in range(NB)], axis=0)
            counts[...] += dot(hot, ds_sum[:, at, :].reshape(H * 16, span), NT)
            return carry

        lax.fori_loop(0, block // 16, count, 0)


def table_of(counts):
    row = lax.broadcasted_iota(jnp.int32, counts.shape, 0)
    col = lax.broadcasted_iota(jnp.int32, counts.shape, 1)
    kept = jnp.where(lax.rem(row, 16) == lax.rem(col, 16), counts, 0.0)
    folded = jnp.sum(kept.reshape(NB, 16, H * 16), axis=1)
    lane = lax.broadcasted_iota(jnp.int32, (H * 16, 128), 1)
    head = lax.broadcasted_iota(jnp.int32, (H * 16, 128), 0) // 16
    return jnp.dot(folded, jnp.where(lane == head, 1.0, 0.0), precision=lax.Precision.HIGHEST)


def backward_kernel(
    shards, seqn, seqs, block, span, rows_of,
    lengths, grads, downs, squares, xall, probs, attended_in, da_in, query_in, keys_in, values_in, dr1_in,
    xc, xq, dvec, positions,
    out, d_content, d_query_x, small_out,
    dq, dk, dv, late, w, x_every, dxs, sums, counts, small, io_sem, low_sem, *scratch,
):
    f32, bf16 = jnp.float32, jnp.bfloat16
    width = H * HD
    half = seqs * block
    total_pairs = seqs * H // 2
    front, scratch = scratch[:FRONT_SCRATCH], scratch[FRONT_SCRATCH:]
    back, scratch = scratch[:BACK_SCRATCH], scratch[BACK_SCRATCH:]
    send_front, stage_core, stage_deck, front_sent = reduce_front(shards, rows_of, UNITS - DOWNS, front)
    send_across, later, back_sent = reduce_back(shards, rows_of, out, back)
    small_first, small_second, small_third, small_last = small_steps(shards, seqn, small, scratch[:SMALL_SCRATCH])
    dx_first, dx_second, dx_third = dx_steps(dxs, scratch[SMALL_SCRATCH:])
    dp, sq = lax.axis_index("dp"), lax.axis_index("seq")
    acc = front[0]
    early = UNITS - DOWNS - 3
    order = lambda k: UNITS - 1 - k
    weights = [pltpu.make_async_copy(squares.at[pl.ds(u * shards, shards)], w.at[u], io_sem.at[5 + u]) for u in range(3)]
    slots = [
        pltpu.make_async_copy(xall.at[k], x_every.at[:, pl.ds(k * block, block)], io_sem.at[8 + k]) for k in range(seqn)
    ]

    def deck_and_across(u):
        stage_deck(u)
        send_across(u, acc.at[u])

    across, line, final, half_stage = later
    ready, late_from_unit = DOWNS, DOWNS + early
    plan = (
        (stage_core, ready, early, 1, 1),
        (deck_and_across, ready, early, 4, 2),
        (across, 0, DOWNS, 3, 2),
        (line, 0, DOWNS, 6, 2),
        (final, 0, DOWNS, 8, 2),
        (half_stage, 0, DOWNS, 10, 2),
        (across, ready, early, 11, 4),
        (stage_core, late_from_unit, 3, 15, 3),
        (line, ready, early, 16, 4),
        (final, ready, early, 18, 4),
        (half_stage, ready, early, 20, 4),
        (deck_and_across, late_from_unit, 3, 22, 3),
        (across, late_from_unit, 3, 29, 2),
        (line, late_from_unit, 3, 32, 2),
        (final, late_from_unit, 3, 34, 2),
        (half_stage, late_from_unit, 3, 36, 2),
    )
    ticks = 41

    def tick(t):
        for stage, first, count, start, gap in plan:
            d = t - start

            @pl.when((d >= 0) & (d < count * gap) & (lax.rem(d, gap) == 0))
            def _(stage=stage, first=first, d=d, gap=gap):
                stage(order(first + d // gap))

    def one(t, carry):
        tick(t)
        return carry

    def attention(attended, d_attended, query, keys, values, buckets, low_two, ds_sum):
        loads = [
            pltpu.make_async_copy(src, dst, io_sem.at[i])
            for i, (src, dst) in enumerate(
                ((attended_in, attended), (da_in, d_attended), (query_in, query), (keys_in, keys), (values_in, values))
            )
        ]

        def take(i, slot):
            return pltpu.make_async_copy(probs.at[i], low_two.at[slot], low_sem.at[slot])

        barrier, count = greet_all(dp, sq, shards, seqn)
        for load in loads:
            load.start()
        take(0, 0).start()
        for load in weights + slots:
            load.start()
        pl.semaphore_wait(barrier, count)

        def send(k, carry):
            u = order(DOWNS + k)
            send_front(u, lambda shard: grads.at[(u - 3) * shards + shard])
            return carry

        def send_down(k, carry):
            send_across(order(k), downs.at[order(k) - 8])
            return carry

        lax.fori_loop(0, early, send, 0)
        lax.fori_loop(0, DOWNS, send_down, 0)
        fill_buckets(buckets, positions, lengths, sq * block, seqs, block, span)
        counts[...] = jnp.zeros_like(counts)
        sums[...] = jnp.zeros_like(sums)
        for load in loads:
            load.wait()
        refs = (attended, d_attended, query, keys, values, buckets, dq, dk, dv, ds_sum, sums, counts)

        def pair(i, carry):
            slot = lax.rem(i, 2)

            tick(i)
            take(i, slot).wait()

            @pl.when(i + 1 < total_pairs)
            def _():
                take(i + 1, 1 - slot).start()

            attend_back_pair(i, refs, low_two.at[slot], seqs, block, span)
            return carry

        lax.fori_loop(0, total_pairs, pair, 0)

    pl.run_scoped(
        attention,
        pltpu.VMEM((2, seqs, block, width), bf16),
        pltpu.VMEM((2, seqs, block, width), bf16),
        pltpu.VMEM((2, seqs, block, width), bf16),
        pltpu.VMEM((seqs, span, width), bf16),
        pltpu.VMEM((seqs, span, width), bf16),
        pltpu.VMEM((seqs, 2, block, span), jnp.int32),
        pltpu.VMEM((2, 2, 2 * block, span), bf16),
        pltpu.VMEM((H, block, span), bf16),
    )

    tile = 256

    def weight_grads(dr1, turned, x_two):
        load = pltpu.make_async_copy(dr1_in, dr1, io_sem.at[0])
        load.start()
        loads = [pltpu.make_async_copy(x, x_two.at[t], io_sem.at[1 + t]) for t, x in enumerate((xc, xq))]
        for copy in loads:
            copy.start()
        for copy in weights + slots:
            copy.wait()
        matrix = lambda u: w[u].reshape(width, width)
        turned[...] = x_every[...].reshape(seqs * span, width).T

        def late_from(u, ref, first_tick):
            def tiles(n, carry):
                tick(first_tick + n)
                cols = pl.ds(pl.multiple_of(n * tile, tile), tile)
                grad = dot(turned[...], ref[:, :, cols].reshape(seqs * span, tile))
                late[u, :, :, cols] = grad.astype(bf16).reshape(shards, rows_of, tile)
                return carry

            lax.fori_loop(0, width // tile, tiles, 0)
            send_front(u, lambda shard: late.at[u, shard])

        for copy in loads:
            copy.wait()

        def tiles(n, carry):
            tick(12 + n)
            cols = pl.ds(pl.multiple_of(n * tile, tile), tile)
            grad = sum(
                dot(x_two[t].reshape(half, width), dq[t, :, :, cols].reshape(half, tile), TN) for t in range(2)
            )
            late[2, :, :, cols] = grad.astype(bf16).reshape(shards, rows_of, tile)
            return carry

        lax.fori_loop(0, width // tile, tiles, 0)
        send_front(2, lambda shard: late.at[2, shard])
        late_from(1, dv, 15)
        late_from(0, dk, 18)

        def every(n, carry):
            tick(21 + n)
            s, k = n // seqn, lax.rem(n, seqn)
            at = pl.ds(pl.multiple_of(k * block, block), block)
            part = dot(dk[s, at, :], matrix(0), NT) + dot(dv[s, at, :], matrix(1), NT)
            dxs[k, pl.ds(pl.multiple_of(s * block, block), block), :] = part.astype(bf16)
            return carry

        lax.fori_loop(0, seqs * seqn, every, 0)
        dx_first()
        load.wait()
        for t, d_x in enumerate((d_content, d_query_x)):
            d_x[...] = dr1[pl.ds(t * half, half), :] + dot(dq[t].reshape(half, width), matrix(2), NT)

    pl.run_scoped(
        weight_grads,
        pltpu.VMEM((2 * half, width), f32),
        pltpu.VMEM((width, seqs * span), bf16),
        pltpu.VMEM((2, seqs, block, width), bf16),
    )
    table = table_of(counts[...])
    vectors = jnp.concatenate([sums[0:2, :], dvec[2:, :], jnp.zeros((4, width), f32)], axis=0)
    pieces = [vectors[:, c * 128 : (c + 1) * 128] for c in range(width // 128)] + [table[:16], table[16:]]
    each = shards // 8
    size = 16 // each
    for p, piece in enumerate(pieces):
        for k in range(each):
            small[p * each + k] = piece[k * size : (k + 1) * size]
    small_first()
    lax.fori_loop(29, 31, one, 0)
    dx_second()
    lax.fori_loop(31, 33, one, 0)
    small_second()
    lax.fori_loop(33, 36, one, 0)
    small_third()
    lax.fori_loop(36, ticks, one, 0)
    dx_third(d_content)
    small_last(small_out)
    front_sent()
    back_sent()


def backward(lengths, grads, downs, squares, xall, probs, attended, d_attended, query, keys, values, dr1, xc, xq, dvec, positions, shards, seqn):
    rows_of, width = squares.shape[1:]
    seqs, block, _ = xc.shape
    span = positions.shape[1]
    f32, bf16 = jnp.float32, jnp.bfloat16
    anywhere = pl.BlockSpec(memory_space=pl.ANY)
    vmem = pl.BlockSpec(memory_space=pltpu.VMEM)
    own = (seqs * block, width)
    small_shape = (shards, 128 // shards, 128)
    dma = pltpu.SemaphoreType.DMA
    return pl.pallas_call(
        functools.partial(backward_kernel, shards, seqn, seqs, block, span, rows_of),
        out_shape=(
            jax.ShapeDtypeStruct((UNITS, rows_of, width), bf16),
            jax.ShapeDtypeStruct(own, f32),
            jax.ShapeDtypeStruct(own, f32),
            jax.ShapeDtypeStruct(small_shape, f32),
        ),
        in_specs=[pl.BlockSpec(memory_space=pltpu.SMEM)] + [anywhere] * 13 + [vmem] * 2,
        out_specs=(vmem,) * 4,
        scratch_shapes=[
            pltpu.VMEM((2, seqs, block, width), bf16),
            pltpu.VMEM((seqs, span, width), bf16),
            pltpu.VMEM((seqs, span, width), bf16),
            pltpu.VMEM((3, shards, rows_of, width), bf16),
            pltpu.VMEM((3, shards, rows_of, width), bf16),
            pltpu.VMEM((seqs, span, width), bf16),
            pltpu.VMEM((seqn,) + own, bf16),
            pltpu.VMEM((8, width), f32),
            pltpu.VMEM((NB * 16, H * 16), f32),
            pltpu.VMEM(small_shape, f32),
            dma((8 + seqn,)),
            dma((2,)),
        ]
        + front_scratch(shards, rows_of, UNITS - DOWNS)
        + back_scratch(shards, rows_of)
        + small_scratch(shards, seqn, small_shape)
        + dx_scratch(own),
        compiler_params=pltpu.CompilerParams(
            collective_id=1, has_side_effects=True, vmem_limit_bytes=67043328
        ),
        name="attend_back_reduce",
    )(lengths, grads, downs, squares, xall, probs, attended, d_attended, query, keys, values, dr1, xc, xq, dvec, positions)


def present_kernel(
    shards, rows_of,
    sums, small, y_c_in, y_q_in, g_c_in, g_q_in,
    y_c, y_q, g_c, g_q, wk, wv, wq, wo, wu, wd, *rest,
):
    vectors, table, wide_rows, low, units, passing, in_sem, out_sem, pass_sem = rest[:9], rest[9], *rest[10:]
    f32 = jnp.float32
    width = H * HD
    r = rows_of
    get = pltpu.make_async_copy(sums, low, in_sem.at[4])
    get.start()
    moves = []
    for i, (src, dst) in enumerate(((y_c_in, y_c), (y_q_in, y_q), (g_c_in, g_c), (g_q_in, g_q))):
        come = pltpu.make_async_copy(src, passing.at[i], in_sem.at[i])
        come.start()
        moves.append((come, pltpu.make_async_copy(passing.at[i], dst, pass_sem.at[i])))
    get.wait()
    pieces = [wk, wv, wq, wo] + [wu.at[:, pl.ds(j * width, width)] for j in range(4)]
    pieces += [wd.at[j] for j in range(4)]
    outs = [pltpu.make_async_copy(units.at[u], piece, out_sem.at[u]) for u, piece in enumerate(pieces)]
    for u, out in enumerate(outs):
        units[u] = low[u].astype(f32)
        out.start()
        if u % 3 == 2:
            come, go = moves[u // 3]
            come.wait()
            go.start()
    me = lax.axis_index("dp")
    whole = jnp.concatenate([small[c] for c in range(width // 128)], axis=1)
    place_of = lax.broadcasted_iota(jnp.int32, (width, r), 0)
    lane = lax.broadcasted_iota(jnp.int32, (width, r), 1)
    mine = jnp.dot(whole, jnp.where(place_of == me * r + lane, 1.0, 0.0), precision=lax.Precision.HIGHEST)
    for i in range(8):
        vectors[i][...] = mine[i]
    per = width // (4 * r)
    place_of = lax.broadcasted_iota(jnp.int32, (width, 4 * r), 0)
    lane = lax.broadcasted_iota(jnp.int32, (width, 4 * r), 1)
    at = jnp.where(place_of == lax.rem(me, per) * (4 * r) + lane, 1.0, 0.0)
    wide_rows[...] = jnp.dot(whole, at, precision=lax.Precision.HIGHEST)
    vectors[8][...] = wide_rows[pl.ds(8 + me // per, 1), :].reshape(4 * r)
    table[...] = jnp.concatenate([small[6], small[7]], axis=0).T[:H, :]
    for out in outs:
        out.wait()
    for come, go in moves:
        go.wait()


def present(sums, small, y_c, y_q, g_c, g_q, shards):
    _, r, width = sums.shape
    f32, bf16 = jnp.float32, jnp.bfloat16
    anywhere = pl.BlockSpec(memory_space=pl.ANY)
    vmem = pl.BlockSpec(memory_space=pltpu.VMEM)
    own = y_c.shape
    shape = lambda *dims: jax.ShapeDtypeStruct(dims, f32)
    dma = pltpu.SemaphoreType.DMA
    return pl.pallas_call(
        functools.partial(present_kernel, shards, r),
        out_shape=(shape(*own),) * 4
        + (shape(r, width),) * 4
        + (shape(r, 4 * width), shape(4, r, width))
        + (shape(r),) * 8
        + (shape(4 * r), shape(H, NB)),
        in_specs=[anywhere, vmem] + [anywhere] * 4,
        out_specs=(anywhere,) * 10 + (vmem,) * 10,
        scratch_shapes=[
            pltpu.VMEM((16, 4 * r), f32),
            pltpu.VMEM((UNITS, r, width), bf16),
            pltpu.VMEM((UNITS, r, width), f32),
            pltpu.VMEM((4,) + own, f32),
            dma((5,)),
            dma((UNITS,)),
            dma((4,)),
        ],
        compiler_params=pltpu.CompilerParams(vmem_limit_bytes=67043328),
        name="present",
    )(sums, small.reshape(8, 16, 128), y_c, y_q, g_c, g_q)


def per_device(
    x_content, x_query, cot_content, cot_query,
    w_query, b_query, w_key, w_value, b_value, w_out, b_out, gain_attn, shift_attn,
    w_up, b_up, w_down, b_down, gain_ffn, shift_ffn, rel_table, lengths, positions, predicted,
    *, shards, seqn,
):
    f32 = jnp.float32
    seqs, block, width = x_content.shape
    r = w_query.shape[0]
    vecs = [
        v.reshape(1, r) for v in (b_query, b_value, b_out, gain_attn, shift_attn, b_down, gain_ffn, shift_ffn)
    ] + [b_up]
    (squares, xall, probs, attended, query, keys, values, y_c, y_q, dr1, d_attended, grads, downs, dvec) = forward(
        w_key, w_value, w_query, w_out, w_up, w_down, x_content, x_query, cot_content, cot_query, vecs,
        lengths, positions, predicted, rel_table, shards, seqn,
    )
    sums, g_content, g_x_query, small = backward(
        lengths, grads, downs, squares, xall, probs, attended, d_attended.reshape(attended.shape),
        query, keys, values, dr1, x_content, x_query, dvec, positions, shards, seqn,
    )
    (
        y_c, y_q, g_content, g_x_query, g_wk, g_wv, g_wq, g_wo, g_w1, g_w2,
        g_bq, g_bv, g_bo, g_g1, g_b1, g_c2, g_g2, g_b2, g_c1, g_table,
    ) = present(sums, small, y_c, y_q, g_content, g_x_query, shards)
    shape = (seqs, block, width)
    return (
        y_c.reshape(shape), y_q.reshape(shape), g_content.reshape(shape), g_x_query.reshape(shape),
        g_wq, g_bq, g_wk, g_wv, g_bv, g_wo, g_bo, g_g1, g_b1,
        g_w1, g_c1, g_w2.reshape(4 * r, width), g_c2, g_g2, g_b2, g_table.T,
    )


def solution(mesh):
    in_specs = (
        P("dp", "seq", None),
        P("dp", "seq", None),
        P("dp", "seq", None),
        P("dp", "seq", None),
        P("dp", None),
        P("dp"),
        P("dp", None),
        P("dp", None),
        P("dp"),
        P("dp", None),
        P("dp"),
        P("dp"),
        P("dp"),
        P("dp", None),
        P("dp"),
        P("dp", None),
        P("dp"),
        P("dp"),
        P("dp"),
        P(),
        P("dp"),
        P("dp", None),
        P("dp", "seq"),
    )
    out_specs = (
        P("dp", "seq", None),
        P("dp", "seq", None),
        P("dp", "seq", None),
        P("dp", "seq", None),
        P("dp", None),
        P("dp"),
        P("dp", None),
        P("dp", None),
        P("dp"),
        P("dp", None),
        P("dp"),
        P("dp"),
        P("dp"),
        P("dp", None),
        P("dp"),
        P("dp", None),
        P("dp"),
        P("dp"),
        P("dp"),
        P(),
    )
    return jax.shard_map(
        functools.partial(per_device, shards=mesh.shape["dp"], seqn=mesh.shape["seq"]),
        mesh=mesh, in_specs=in_specs, out_specs=out_specs, check_vma=False
    )
```

```python
import functools

import jax
import jax.numpy as jnp
from jax import lax
from jax.experimental import pallas as pl
from jax.experimental.pallas import tpu as pltpu
from jax.sharding import PartitionSpec as P

H = 12
HD = 64
NB = 32

MESH = pl.DeviceIdType.MESH
UNITS = 12


def cutter(rows_of):
    by_rows = rows_of % 96 == 0
    piece = rows_of // 6 if by_rows else 128

    def cut(start, size):
        if not isinstance(start, int):
            start = pl.multiple_of(start * piece, 16 if by_rows else 128)
        else:
            start = start * piece
        inner = pl.ds(start, size * piece)
        return (inner, slice(None)) if by_rows else (slice(None), inner)

    def shape(size):
        return (size * piece, 768) if by_rows else (rows_of, size * piece)

    return cut, shape


def place():
    dp, sq = lax.axis_index("dp"), lax.axis_index("seq")
    row, side = dp // 2, dp % 2
    deck, core = sq // 2, sq % 2
    return dp, sq, row, side, deck, core


def tile_of(unit, shard, shards):
    down = unit // 8
    return (1 - down) * (unit * shards + shard) + down * (8 * shards + shard * 4 + unit - 8)


def remote(src, dst, send, recv, device):
    return pltpu.make_async_remote_copy(
        src_ref=src, dst_ref=dst, send_sem=send, recv_sem=recv, device_id=device, device_id_type=MESH
    )


def greet_all(dp, sq, shards, seqn):
    barrier = pltpu.get_barrier_semaphore()

    def greet(step, carry):
        pl.semaphore_signal(barrier, inc=1, device_id=(lax.rem(dp + step, shards), sq), device_id_type=MESH)
        return carry

    def greet_seq(step, carry):
        pl.semaphore_signal(barrier, inc=1, device_id=(dp, lax.rem(sq + step, seqn)), device_id_type=MESH)
        return carry

    lax.fori_loop(1, shards, greet, 0)
    lax.fori_loop(1, seqn, greet_seq, 0)
    return barrier, shards + seqn - 2


AHEAD = 2
X_LAG = 1
Y_LAG = 1


def gather_steps(shards, seqn, ins, outs, scratch):
    wk, wv, wq, wo, wu, wd, xc = ins
    full, xall, vall = outs
    (load_sem, zu_sem, zd_sem, xs_sem, ys_sem, cp_sem, cy_sem,
     zr_sem, xr_sem, yr_sem, cpr_sem, cyr_sem, xc_send, xc_recv, vec_send, vec_recv) = scratch
    dp, sq, row, side, deck, core = place()
    rows = shards // 2
    across = (row * 2 + 1 - side, sq)
    other_deck = (dp, (1 - deck) * 2 + core)
    sibling = (dp, deck * 2 + 1 - core)
    cut, _ = cutter(full.shape[1])
    plane = cut(core * 3 + deck, 2)
    solo = cut(core * 3 + deck * 2, 1)
    theirs = cut(core * 3 + (1 - deck) * 2, 1)

    def many(count, size):
        return full.at[(pl.ds(0, count),) + cut(0, size)]

    def part(unit, shard, piece):
        return full.at[(tile_of(unit, shard, shards),) + piece]

    pieces = [wk, wv, wq, wo] + [wu.at[:, pl.ds(j * 768, 768)] for j in range(4)] + [wd.at[j] for j in range(4)]
    loads = [
        pltpu.make_async_copy(piece, full.at[tile_of(u, dp, shards)], load_sem.at[u]) for u, piece in enumerate(pieces)
    ]
    x_mine = xall.at[sq]
    xload = pltpu.make_async_copy(xc, x_mine, load_sem.at[UNITS])
    x_deck = remote(x_mine, x_mine, xc_send.at[0], xc_recv.at[0], other_deck)
    x_core = remote(x_mine, x_mine, xc_send.at[1], xc_recv.at[1], sibling)
    x_theirs = xall.at[(1 - deck) * 2 + core]
    x_forward = remote(x_theirs, x_theirs, xc_send.at[2], xc_recv.at[2], sibling)

    up = ((row + 1) * 2 + side, sq)
    down = ((row - 1) * 2 + side, sq)

    def along(u, s, src):
        dst = part(u, s * 2 + side, plane)

        @pl.when((s <= row) & (row < rows - 1))
        def _():
            remote(src, dst, zu_sem.at[s], zr_sem.at[u, s], up).start()

        @pl.when((s >= row) & (row > 0))
        def _():
            remote(src, dst, zd_sem.at[s], zr_sem.at[u, s], down).start()

    def send_own(u):
        tile = full.at[tile_of(u, dp, shards)]
        pltpu.make_async_copy(tile, tile, load_sem.at[u]).wait()
        along(u, row, part(u, dp, plane))
        across_own(u)

    def across_own(u):
        ref = part(u, dp, plane)
        remote(ref, ref, xs_sem, xr_sem.at[u], across).start()

    def to_deck(u, shard):
        ref = part(u, shard, solo)
        remote(ref, ref, ys_sem, yr_sem.at[u], other_deck).start()

    def to_core(u, shard):
        ref = part(u, shard, plane)
        remote(ref, ref, cp_sem, cpr_sem.at[u], sibling).start()

    def begin():
        barrier, count = greet_all(dp, sq, shards, seqn)
        for load in loads:
            load.start()
        xload.start()
        pl.semaphore_wait(barrier, count)

        def send_vec(step, carry):
            to = (lax.rem(dp + step, shards), sq)
            remote(vall.at[dp], vall.at[dp], vec_send, vec_recv, to).start()
            return carry

        lax.fori_loop(1, shards, send_vec, 0)

        def first(u, carry):
            send_own(u)
            return carry

        lax.fori_loop(0, AHEAD, first, 0)

        xload.wait()
        x_deck.start()
        x_core.start()

    def step(n):
        @pl.when(n + AHEAD < UNITS)
        def _():
            send_own(n + AHEAD)

        def hop(t, carry):
            u = n - (t - 1)

            def arrived(s):
                ref = part(u, s * 2 + side, plane)
                remote(ref, ref, xs_sem, zr_sem.at[u, s], across).wait_recv()
                along(u, s, ref)
                remote(ref, ref, xs_sem, xr_sem.at[u], across).start()
                to_deck(u, s * 2 + side)
                to_core(u, s * 2 + side)

            @pl.when((u >= 0) & (u < UNITS))
            def _():
                pl.when(row - t >= 0)(lambda: arrived(row - t))
                pl.when(row + t < rows)(lambda: arrived(row + t))

            return carry

        lax.fori_loop(1, rows, hop, 0)
        ux = n - (rows - 1) - X_LAG

        @pl.when((ux >= 0) & (ux < UNITS))
        def _():
            remote(many(rows, 2), many(rows, 2), xs_sem, xr_sem.at[ux], across).wait_recv()

            def pass_on(s, carry):
                to_deck(ux, s * 2 + 1 - side)
                to_core(ux, s * 2 + 1 - side)
                return carry

            lax.fori_loop(0, rows, pass_on, 0)

        uy = n - rows - X_LAG - Y_LAG

        @pl.when((uy >= 0) & (uy < UNITS))
        def _():
            remote(many(shards - 1, 1), many(shards - 1, 1), ys_sem, yr_sem.at[uy], other_deck).wait_recv()

            def pass_on(k, carry):
                ref = part(uy, lax.rem(dp + k, shards), theirs)
                remote(ref, ref, cy_sem, cyr_sem.at[uy], sibling).start()
                return carry

            lax.fori_loop(1, shards, pass_on, 0)

    def pass_x():
        x_deck.wait_recv()
        x_forward.start()

    def wait_x():
        x_core.wait_recv()
        x_forward.wait_recv()

    def wait_vec():
        rest = vall.at[pl.ds(0, shards - 1)]
        remote(rest, rest, vec_send, vec_recv, sibling).wait_recv()

    def whole(u):
        remote(many(shards - 1, 2), many(shards - 1, 2), cp_sem, cpr_sem.at[u], sibling).wait_recv()
        remote(many(shards - 1, 1), many(shards - 1, 1), cy_sem, cyr_sem.at[u], sibling).wait_recv()

    def finish():
        x_deck.wait_send()
        x_core.wait_send()
        x_forward.wait_send()
        rest = vall.at[pl.ds(0, shards - 1)]
        remote(rest, rest, vec_send, vec_recv, sibling).wait_send()
        for count, size, sem in (
            (UNITS * rows, 2, xs_sem),
            (UNITS * (shards - 1), 1, ys_sem),
            (UNITS * (shards - 1), 1, cy_sem),
            (UNITS * (shards - 1), 2, cp_sem),
        ):
            ref = many(count, size)
            remote(ref, ref, sem, xr_sem.at[0], sibling).wait_send()

        def sent(s, carry):
            ref = many(UNITS, 2)

            @pl.when((s <= row) & (row < rows - 1))
            def _():
                remote(ref, ref, zu_sem.at[s], xr_sem.at[0], sibling).wait_send()

            @pl.when((s >= row) & (row > 0))
            def _():
                remote(ref, ref, zd_sem.at[s], xr_sem.at[0], sibling).wait_send()

            return carry

        lax.fori_loop(0, rows, sent, 0)

    return begin, step, whole, pass_x, wait_x, wait_vec, finish


def gather_scratch(shards):
    dma = pltpu.SemaphoreType.DMA
    return [dma((UNITS + 1,))] + [dma((shards // 2,))] * 2 + [dma(())] * 4 + [dma((UNITS, shards // 2))] + [dma((UNITS,))] * 4 + [dma((3,)), dma((3,)), dma(()), dma(())]


GATHER_SCRATCH = 16


def reduce_front(shards, rows_of, count, scratch):
    f32, bf16 = jnp.float32, jnp.bfloat16
    acc, got_core, got_deck, load_sem, core_send, core_recv, deck_send, deck_recv = scratch
    dp, sq, row, side, deck, core = place()
    rows = shards // 2
    other_deck = (dp, (1 - deck) * 2 + core)
    sibling = (dp, deck * 2 + 1 - core)
    cut, _ = cutter(rows_of)
    mine = cut(core * 3, 3)
    siblings = cut((1 - core) * 3, 3)
    solo = cut(deck * 2, 1)
    other_solo = cut((1 - deck) * 2, 1)

    def send(u, tiles):
        def one(s, carry):
            for b in range(2):
                tile = tiles(s * 2 + b)
                remote(tile.at[siblings], got_core.at[u, s, b], core_send.at[u], core_recv.at[u], sibling).start()
                pltpu.make_async_copy(tile.at[mine], acc.at[u, s, b], load_sem.at[u]).start()
            return carry

        lax.fori_loop(0, rows, one, 0)

    def core_copy(u):
        return remote(got_core.at[u], got_core.at[u], core_send.at[u], core_recv.at[u], sibling)

    def deck_copy(u):
        src = acc.at[(u, slice(None), slice(None)) + other_solo]
        return remote(src, got_deck.at[u], deck_send.at[u], deck_recv.at[u], other_deck)

    def stage_core(u):
        pltpu.make_async_copy(acc.at[u], acc.at[u], load_sem.at[u]).wait()
        core_copy(u).wait_recv()

        def add(s, carry):
            for b in range(2):
                acc[u, s, b] = total(acc[u, s, b], got_core[u, s, b])
            return carry

        lax.fori_loop(0, rows, add, 0)
        deck_copy(u).start()

    def stage_deck(u):
        deck_copy(u).wait_recv()

        def add(s, carry):
            for b in range(2):
                at = (u, s, b) + solo
                acc[at] = total(acc[at], got_deck[u, s, b])
            return carry

        lax.fori_loop(0, rows, add, 0)

    def sent():
        def one(u, carry):
            core_copy(u).wait_send()
            deck_copy(u).wait_send()
            return carry

        lax.fori_loop(0, count, one, 0)

    return send, stage_core, stage_deck, sent


def total(left, right):
    return left + right


def front_scratch(shards, rows_of, count):
    bf16 = jnp.bfloat16
    rows = shards // 2
    _, shape = cutter(rows_of)
    return [
        pltpu.VMEM((count, rows, 2) + shape(3), bf16),
        pltpu.VMEM((count, rows, 2) + shape(3), bf16),
        pltpu.VMEM((count, rows, 2) + shape(1), bf16),
    ] + [pltpu.SemaphoreType.DMA((count,))] * 5


FRONT_SCRATCH = 8


def reduce_back(shards, rows_of, out, scratch):
    f32, bf16 = jnp.float32, jnp.bfloat16
    (own_side, got_across, line, got_line, final, got_final, half, got_half,
     side_sem, across_send, across_recv, line_send, line_recv, final_send, final_recv, half_send, half_recv) = scratch
    dp, sq, row, side, deck, core = place()
    rows = shards // 2
    across = (row * 2 + 1 - side, sq)
    other_deck = (dp, (1 - deck) * 2 + core)
    sibling = (dp, deck * 2 + 1 - core)
    cut, _ = cutter(rows_of)
    mine = cut(core * 3, 3)
    siblings = cut((1 - core) * 3, 3)
    plane = cut(deck, 2)
    other_solo = cut((1 - deck) * 2, 1)

    def send_across(u, planes):
        remote(
            planes.at[(slice(None), 1 - side) + plane], got_across.at[u], across_send.at[u], across_recv.at[u], across
        ).start()
        pltpu.make_async_copy(planes.at[(slice(None), side) + plane], own_side.at[u], side_sem.at[u]).start()

    def across_copy(u):
        return remote(got_across.at[u], got_across.at[u], across_send.at[u], across_recv.at[u], across)

    def line_copy(u):
        ref = got_line.at[u, pl.ds(0, rows - 1)]
        return remote(ref, ref, line_send.at[u], line_recv.at[u], across)

    def final_copy(u):
        return remote(final.at[u], got_final.at[u], final_send.at[u], final_recv.at[u], other_deck)

    def half_copy(u):
        return remote(half.at[u], got_half.at[u], half_send.at[u], half_recv.at[u], sibling)

    def stage_across(u):
        pltpu.make_async_copy(own_side.at[u], own_side.at[u], side_sem.at[u]).wait()
        across_copy(u).wait_recv()

        def add(k, carry):
            s = lax.rem(row + k, rows)
            line[u, s] = total(own_side[u, s], got_across[u, s])

            @pl.when(k < rows)
            def _():
                remote(
                    line.at[u, s], got_line.at[u, rows - 1 - k], line_send.at[u], line_recv.at[u], (s * 2 + side, sq)
                ).start()

            return carry

        lax.fori_loop(1, rows + 1, add, 0)

    def stage_line(u):
        line_copy(u).wait_recv()
        summed = line[u, row].astype(f32)
        if rows <= 4:
            for k in range(rows - 1):
                summed = summed + got_line[u, k].astype(f32)
        else:
            summed = lax.fori_loop(0, rows - 1, lambda k, t: t + got_line[u, k].astype(f32), summed)
        final[u] = summed.astype(bf16)
        final_copy(u).start()

    def stage_final(u):
        final_copy(u).wait_recv()
        half[(u,) + plane] = final[u]
        half[(u,) + other_solo] = got_final[(u,) + cut(1 - deck, 1)]
        both = (u,) + cut(1, 1)
        half[both] = total(half[both], got_final[(u,) + cut(deck, 1)])
        half_copy(u).start()

    def stage_half(u):
        half_copy(u).wait_recv()
        out[(u,) + mine] = half[u]
        out[(u,) + siblings] = got_half[u]

    def sent():
        def one(u, carry):
            for copy in (across_copy, line_copy, final_copy, half_copy):
                copy(u).wait_send()
            return carry

        lax.fori_loop(0, UNITS, one, 0)

    return send_across, (stage_across, stage_line, stage_final, stage_half), sent


def back_scratch(shards, rows_of):
    bf16 = jnp.bfloat16
    rows = shards // 2
    _, shape = cutter(rows_of)
    return [pltpu.VMEM((UNITS, rows) + shape(2), bf16)] * 4 + [
        pltpu.VMEM((UNITS,) + shape(2), bf16),
        pltpu.VMEM((UNITS,) + shape(2), bf16),
        pltpu.VMEM((UNITS,) + shape(3), bf16),
        pltpu.VMEM((UNITS,) + shape(3), bf16),
    ] + [pltpu.SemaphoreType.DMA((UNITS,))] * 9


BACK_SCRATCH = 17


def small_steps(shards, seqn, small, scratch):
    got_small, mid_small, got_mid, got_all, small_send, small_recv = scratch
    dp, sq, row, side, deck, core = place()
    sibling = (dp, deck * 2 + 1 - core)

    def small_first():
        got_small[dp] = small[dp]

        def send(k, carry):
            to = lax.rem(dp + k, shards)
            remote(small.at[to], got_small.at[dp], small_send.at[0], small_recv.at[0], (to, sq)).start()
            return carry

        lax.fori_loop(1, shards, send, 0)

    def sum_of(ref, count):
        summed = ref[0]
        for i in range(1, count):
            summed = summed + ref[i]
        return summed

    def small_second():
        rest = got_small.at[pl.ds(0, shards - 1)]
        remote(rest, rest, small_send.at[0], small_recv.at[0], sibling).wait()
        summed = sum_of(got_small, shards)
        mid_small[0] = summed
        got_mid[sq] = summed

        def send(k, carry):
            to = (dp, lax.rem(sq + k, seqn))
            remote(mid_small.at[0], got_mid.at[sq], small_send.at[1], small_recv.at[1], to).start()
            return carry

        lax.fori_loop(1, seqn, send, 0)

    def small_third():
        rest = got_mid.at[pl.ds(0, seqn - 1)]
        remote(rest, rest, small_send.at[1], small_recv.at[1], sibling).wait()
        summed = sum_of(got_mid, seqn)
        mid_small[1] = summed
        got_all[dp] = summed

        def send(k, carry):
            to = (lax.rem(dp + k, shards), sq)
            remote(mid_small.at[1], got_all.at[dp], small_send.at[2], small_recv.at[2], to).start()
            return carry

        lax.fori_loop(1, shards, send, 0)

    def small_last(small_out):
        rest = got_all.at[pl.ds(0, shards - 1)]
        remote(rest, rest, small_send.at[2], small_recv.at[2], sibling).wait()
        small_out[...] = got_all[...]

    return small_first, small_second, small_third, small_last


def small_scratch(shards, seqn, small_shape):
    f32 = jnp.float32
    return [
        pltpu.VMEM(small_shape, f32),
        pltpu.VMEM((2,) + small_shape[1:], f32),
        pltpu.VMEM((seqn,) + small_shape[1:], f32),
        pltpu.VMEM(small_shape, f32),
    ] + [pltpu.SemaphoreType.DMA((3,))] * 2


SMALL_SCRATCH = 6


def dx_steps(dxs, scratch):
    f32, bf16 = jnp.float32, jnp.bfloat16
    dx_own, dx_core, dx_deck, load, send, recv = scratch
    dp, sq, row, side, deck, core = place()
    other_deck = (dp, (1 - deck) * 2 + core)
    sibling = (dp, deck * 2 + 1 - core)
    deck_dx = remote(dx_own.at[1 - deck], dx_deck, send.at[2], recv.at[2], other_deck)

    def first():
        for k in range(2):
            pltpu.make_async_copy(dxs.at[k * 2 + core], dx_own.at[k], load.at[k]).start()
            remote(dxs.at[k * 2 + 1 - core], dx_core.at[k], send.at[k], recv.at[k], sibling).start()

    def second():
        for k in range(2):
            pltpu.make_async_copy(dx_own.at[k], dx_own.at[k], load.at[k]).wait()
            remote(dx_core.at[k], dx_core.at[k], send.at[k], recv.at[k], sibling).wait()
            dx_own[k] = (dx_own[k].astype(f32) + dx_core[k].astype(f32)).astype(bf16)
        deck_dx.start()

    def third(dx_out):
        deck_dx.wait()
        dx_out[...] += dx_own[deck].astype(f32) + dx_deck[...].astype(f32)

    return first, second, third


def dx_scratch(own):
    bf16 = jnp.bfloat16
    dma = pltpu.SemaphoreType.DMA
    return [pltpu.VMEM((2,) + own, bf16), pltpu.VMEM((2,) + own, bf16), pltpu.VMEM(own, bf16), dma((2,)), dma((3,)), dma((3,))]


bucket_marks = (12, 16, 23, 32, 46, 64, 91)
MASKED = NB
TN = (((0,), (0,)), ((), ()))
NT = (((1,), (1,)), ((), ()))


def dot(left, right, dims=None):
    if dims is None:
        dims = (((1,), (0,)), ((), ()))
    return lax.dot_general(left, right, dims, preferred_element_type=jnp.float32)


def column_of(row):
    return jnp.broadcast_to(row.astype(jnp.float32), (row.shape[1], row.shape[1])).T


def fill_buckets(buckets, positions, lengths, base, seqs, block, span):
    for s in range(seqs):
        mine = column_of(positions[s : s + 1, pl.ds(pl.multiple_of(base, block), block)]).astype(jnp.int32)
        for c in range(span // block):
            cols = slice(c * block, (c + 1) * block)
            delta = positions[s : s + 1, cols] - mine
            dist = jnp.abs(delta)
            far = jnp.full(dist.shape, 8, jnp.int32)
            for mark in bucket_marks:
                far = far + (dist >= mark).astype(jnp.int32)
            bucket = jnp.where(dist < 8, dist, far) + 16 * (delta > 0).astype(jnp.int32)
            i = base + lax.broadcasted_iota(jnp.int32, (block, block), 0)
            j = c * block + lax.broadcasted_iota(jnp.int32, (block, block), 1)
            valid = j < lengths[s]
            buckets[s, 0, :, cols] = jnp.where(valid & (j <= i), bucket, MASKED)
            buckets[s, 1, :, cols] = jnp.where(valid & (j < jnp.maximum(i, 1)), bucket, MASKED)


def head_lanes(rows, half):
    lane = lax.broadcasted_iota(jnp.int32, (rows, 2 * HD), 1)
    return (lane < HD) if half == 0 else (lane >= HD)


def fill_bias(i, biases, buckets, table, block, span):
    s, head = i // H, lax.rem(i, H)
    entry = jnp.broadcast_to(table[pl.ds(head, 1), :], (block, 128))
    for c in range(span // 128):
        cols = slice(c * 128, (c + 1) * 128)
        value = jnp.take_along_axis(entry, buckets[s, 0, :, cols], axis=1, mode="promise_in_bounds")
        biases[i, 0, :, cols] = value
        biases[i, 1, :, cols] = jnp.where(buckets[s, 1, :, cols] == MASKED, -1e30, value)


def attend_pair(i, refs, block, span, low_out):
    attended, query, keys, values, biases = refs
    f32, bf16 = jnp.float32, jnp.bfloat16
    pairs = H // 2
    s, pair = i // pairs, lax.rem(i, pairs)
    lanes = pl.ds(pl.multiple_of(pair * 128, 128), 128)
    q = query[:, s, :, lanes].reshape(2 * block, 128)
    k = keys[s, :, lanes]
    v = values[s, :, lanes]
    outs = []
    for half in range(2):
        mine = head_lanes(2 * block, half)
        one = jnp.where(mine, q * 0.125, 0).astype(bf16)
        scores = dot(one, k, NT) + biases[i * 2 + half].reshape(2 * block, span)
        top = jnp.max(scores, axis=-1, keepdims=True)
        expo = jnp.exp(scores - top)
        low = (expo * (1.0 / jnp.sum(expo, axis=-1, keepdims=True))).astype(bf16)
        low_out[half] = low
        outs.append(dot(low, v))
    mixed = jnp.where(head_lanes(2 * block, 0), outs[0], outs[1]).astype(bf16)
    attended[:, s, :, lanes] = mixed.reshape(2, block, 128)


def center_of(value):
    center = value - jnp.mean(value, axis=-1, keepdims=True)
    var = jnp.mean(center * center, axis=-1, keepdims=True)
    inv = lax.rsqrt(var + 1e-05)
    return center * inv, inv


def norm_back(grad, gain, normed, inv):
    scaled = grad * gain
    return inv * (
        scaled
        - jnp.mean(scaled, axis=-1, keepdims=True)
        - normed * jnp.mean(scaled * normed, axis=-1, keepdims=True)
    )


EARLY = 9
BIAS_FROM = 3
BIAS_STEPS = 6
TILE = 256
LONG = 384
DOWNS = 4


def forward_kernel(
    shards, seqn, seqs, block, span, rows_of,
    lengths, wk, wv, wq, wo, wu, wd, xc, xc_in, xq_in, cot_c_in, cot_q_in, positions, predicted, rel_table,
    bq, bv, bo, g1, b1, c2, g2, b2, c1,
    squares, x_out, probs, attended_out, query_out, keys_out, values_out, y_c, y_q, dr1_out, da_out, grads, downs, dvec,
    full, xall, vall, vectors, keep, attended, table, xc_rows, xq_rows, cot_c, cot_q, io_sem, low_sem, row_sem, *scratch,
):
    f32, bf16 = jnp.float32, jnp.bfloat16
    width = H * HD
    half = seqs * block
    rows = 2 * half
    r = rows_of
    wide = 4 * r
    base = lax.axis_index("seq") * block
    me = lax.axis_index("dp")
    begin, step, whole, pass_x, wait_x, wait_vec, finish = gather_steps(
        shards, seqn, (wk, wv, wq, wo, wu, wd, xc), (full, xall, vall), scratch[: -FRONT_SCRATCH]
    )
    send_front, stage_core, stage_deck, front_sent = reduce_front(shards, r, DOWNS, scratch[-FRONT_SCRATCH:])
    acc = scratch[-FRONT_SCRATCH]
    vall[me] = jnp.zeros(vall.shape[1:], f32)
    for i, piece in enumerate((bq, bv, bo, g1, b1, c2, g2, b2)):
        vall[me, i : i + 1, 0:r] = piece[...].astype(f32)
    vall[me, 8:9, :] = c1[...].astype(f32).reshape(1, wide)
    begin()
    streams = [
        pltpu.make_async_copy(src, dst, row_sem.at[i])
        for i, (src, dst) in enumerate(((xc_in, xc_rows), (xq_in, xq_rows), (cot_c_in, cot_c), (cot_q_in, cot_q)))
    ]
    for copy in streams:
        copy.start()

    def one(n, carry):
        step(n)
        return carry

    def matrix(u):
        return full[pl.ds(u * shards, shards)].reshape(width, width)

    def columns(u, cols):
        size = cols.size
        return full[pl.ds(u * shards, shards), :, cols].reshape(width, size)

    def row_block(u, n):
        per = LONG // r
        return full[pl.ds(u * shards + n * per, per)].reshape(LONG, width)

    def attention(query, keys, values, buckets, low_two, biases):
        fill_buckets(buckets, positions, lengths, base, seqs, block, span)
        eye = (
            lax.broadcasted_iota(jnp.int32, (NB, 128), 0) == lax.broadcasted_iota(jnp.int32, (NB, 128), 1)
        )
        by_head = dot(rel_table[...], jnp.where(eye, 1.0, 0.0).astype(bf16))
        lane = lax.broadcasted_iota(jnp.int32, by_head.shape, 1)
        table[...] = jnp.where(lane < NB, by_head, -1e30)
        for s in range(seqs):
            live = base + lax.broadcasted_iota(jnp.int32, (block, 1), 0) < lengths[s]
            chosen = column_of(predicted[s : s + 1, :])[:, 0:1] > 0
            keep[s * block : (s + 1) * block, :] = jnp.where(live, 1.0, 0.0)
            keep[half + s * block : half + (s + 1) * block, :] = jnp.where(live & chosen, 1.0, 0.0)
        share = seqs * H // BIAS_STEPS

        def one_and_bias(n, carry):
            step(n)

            def bias(k, inner):
                fill_bias((n - BIAS_FROM) * share + k, biases, buckets, table, block, span)
                return inner

            return lax.fori_loop(0, share, bias, carry)

        lax.fori_loop(0, BIAS_FROM, one, 0)
        lax.fori_loop(BIAS_FROM, BIAS_FROM + 3, one_and_bias, 0)
        pass_x()
        lax.fori_loop(BIAS_FROM + 3, BIAS_FROM + BIAS_STEPS, one_and_bias, 0)
        lax.fori_loop(BIAS_FROM + BIAS_STEPS, EARLY, one, 0)
        wait_x()
        wait_vec()
        for copy in streams:
            copy.wait()
        vectors[...] = jnp.zeros_like(vectors)

        def spread(i, carry):
            row = lax.broadcasted_iota(jnp.int32, (r, width), 0)
            col = lax.broadcasted_iota(jnp.int32, (r, width), 1)
            at = jnp.where(col == row + i * r, 1.0, 0.0).astype(bf16)
            vectors[0:8, :] += dot(vall[i, 0:8, 0:r].astype(bf16), at)
            per = width // wide
            row = lax.broadcasted_iota(jnp.int32, (wide, width), 0)
            col = lax.broadcasted_iota(jnp.int32, (wide, width), 1)
            at = jnp.where(col == row + lax.rem(i, per) * wide, 1.0, 0.0).astype(bf16)
            vectors[pl.ds(8 + i // per, 1), :] += dot(vall[i, 8:9, :].astype(bf16), at)
            return carry

        lax.fori_loop(0, shards, spread, 0)
        for u in range(3):
            whole(u)

        def project(k, carry):
            @pl.when(k == 2)
            def _():
                step(EARLY)

            x = xall[k].reshape(half, width)
            at = pl.ds(pl.multiple_of(k * block, block), block)
            keys[:, at, :] = dot(x, matrix(0)).astype(bf16).reshape(seqs, block, width)
            values[:, at, :] = (dot(x, matrix(1)) + vectors[1:2, :]).astype(bf16).reshape(seqs, block, width)
            return carry

        lax.fori_loop(0, seqn, project, 0)
        for t, x in enumerate((xc_rows, xq_rows)):
            query[t] = (dot(x[...], matrix(2)) + vectors[0:1, :]).astype(bf16).reshape(seqs, block, width)
        puts = [
            pltpu.make_async_copy(src, dst, io_sem.at[i])
            for i, (src, dst) in enumerate(((query, query_out), (keys, keys_out), (values, values_out)))
        ]
        for copy in puts:
            copy.start()
        total = seqs * H // 2

        def put(i, slot):
            return pltpu.make_async_copy(low_two.at[slot], probs.at[i], low_sem.at[slot])

        def attend_one(i, carry):
            slot = lax.rem(i, 2)

            @pl.when(lax.rem(i, 3) == 1)
            def _():
                step(EARLY + 1 + i // 3)

            @pl.when(i >= 2)
            def _():
                put(i - 2, slot).wait()

            attend_pair(i, (attended, query, keys, values, biases), block, span, low_two.at[slot])
            put(i, slot).start()
            return carry

        lax.fori_loop(0, total, attend_one, 0)
        put(total - 2, (total - 2) % 2).wait()
        put(total - 1, (total - 1) % 2).wait()
        for copy in puts:
            copy.wait()

    pl.run_scoped(
        attention,
        pltpu.VMEM((2, seqs, block, width), bf16),
        pltpu.VMEM((seqs, span, width), bf16),
        pltpu.VMEM((seqs, span, width), bf16),
        pltpu.VMEM((seqs, 2, block, span), jnp.int32),
        pltpu.VMEM((2, 2, 2 * block, span), bf16),
        pltpu.VMEM((seqs * H, 2, block, span), f32),
    )
    done = EARLY + 1 + seqs * H // 6
    more = [
        pltpu.make_async_copy(full.at[pl.ds(0, 3 * shards)], squares, io_sem.at[3]),
        pltpu.make_async_copy(xall, x_out, io_sem.at[4]),
        pltpu.make_async_copy(attended, attended_out, io_sem.at[5]),
    ]
    for copy in more:
        copy.start()
    dvec[...] = jnp.zeros_like(dvec)
    vec = lambda i: vectors[i : i + 1, :]
    chunk = 128
    chunks = half // chunk

    def ffn(hidden, hidden_low, hidden_turn, normed1, inv1, active, slope, feed, dr2, dr2_low, dr1_low, da, stage, stage_down):
        step(done)
        whole(3)

        def phase_one(c, carry):
            t, s = c // seqs, lax.rem(c, seqs)
            at = pl.ds(pl.multiple_of(c * chunk, chunk), chunk)
            out = dot(attended[t, s], matrix(3)) + vec(2)
            inner = pl.ds(pl.multiple_of(s * chunk, chunk), chunk)
            x = jnp.where(t == 0, xc_rows[inner, :].astype(f32), xq_rows[inner, :].astype(f32))
            normed, inv = center_of(x + out)
            normed1[at, :] = normed
            inv1[at, :] = inv
            h = normed * vec(3) + vec(4)
            hidden[at, :] = h
            hidden_low[at, :] = h.astype(bf16)
            return carry

        lax.fori_loop(0, rows // chunk, phase_one, 0)
        hidden_turn[...] = hidden_low[...].T
        tiles = width // TILE

        def phase_two(j, carry):
            step(done + 1 + j)
            whole(4 + j)

            def tile(n, inner):
                cols = pl.ds(pl.multiple_of(n * TILE, TILE), TILE)
                u = dot(hidden_low[...], columns(4 + j, cols)) + vectors[pl.ds(8 + j, 1), cols]
                cdf = 0.5 * (1.0 + lax.erf(u * (2.0**-0.5)))
                active[j, :, cols] = (u * cdf).astype(bf16)
                slope[j, :, cols] = (cdf + u * (jnp.exp(-0.5 * u * u) * ((2.0 * jnp.pi) ** -0.5))).astype(bf16)
                return inner

            return lax.fori_loop(0, tiles, tile, carry)

        lax.fori_loop(0, 4, phase_two, 0)

        def last(u, carry):
            whole(u)
            return carry

        lax.fori_loop(done + 5, UNITS + shards // 2 + X_LAG + Y_LAG, one, 0)
        lax.fori_loop(8, UNITS, last, 0)

        def phase_feed(n, carry):
            cols = pl.ds(pl.multiple_of(n * TILE, TILE), TILE)
            feed[:, cols] = sum(dot(active[j], columns(8 + j, cols)) for j in range(4))
            return carry

        lax.fori_loop(0, tiles, phase_feed, 0)

        def phase_three(c, carry):
            t, s = c // seqs, lax.rem(c, seqs)
            at = pl.ds(pl.multiple_of(c * chunk, chunk), chunk)
            normed, inv = center_of(hidden[at, :] + feed[at, :] + vec(5))
            kept = keep[at, :]
            feed[at, :] = (normed * vec(6) + vec(7)) * kept
            inner = pl.ds(pl.multiple_of(s * chunk, chunk), chunk)
            cot = jnp.where(t == 0, cot_c[inner, :].astype(f32), cot_q[inner, :].astype(f32)) * kept
            d = norm_back(cot, vec(6), normed, inv)
            dvec[6:7, :] += jnp.sum(cot * normed, axis=0, keepdims=True)
            dvec[7:8, :] += jnp.sum(cot, axis=0, keepdims=True)
            dvec[5:6, :] += jnp.sum(d, axis=0, keepdims=True)
            dr2[at, :] = d
            dr2_low[at, :] = d.astype(bf16)
            return carry

        lax.fori_loop(0, rows // chunk, phase_three, 0)
        y_copies = [
            pltpu.make_async_copy(feed.at[pl.ds(0, half)], y_c, io_sem.at[6]),
            pltpu.make_async_copy(feed.at[pl.ds(half, half)], y_q, io_sem.at[7]),
        ]
        for copy in y_copies:
            copy.start()
        longs = width // LONG

        def phase_down(j, carry):
            grad = dot(active[j], dr2_low[...], TN).astype(bf16)
            stage_down[pl.ds(j * shards, shards)] = grad.reshape(shards, r, width)
            return carry

        lax.fori_loop(0, 4, phase_down, 0)

        def start_down(k, carry):
            send_front(k, lambda shard: stage_down.at[shard * 4 + k])
            return carry

        lax.fori_loop(0, DOWNS, start_down, 0)

        def phase_slope(j, carry):
            du = slope[j].astype(f32) * dot(dr2_low[...], matrix(8 + j), NT)
            dvec[pl.ds(8 + j, 1), :] = jnp.sum(du, axis=0, keepdims=True)
            active[j] = du.astype(bf16)
            stage_core(j)
            return carry

        lax.fori_loop(0, 4, phase_slope, 0)

        def phase_up(j, carry):
            grad = dot(hidden_turn[...], active[j]).astype(bf16)
            stage[1 + j] = grad.reshape(shards, r, width)
            pltpu.make_async_copy(
                stage.at[1 + j], grads.at[pl.ds((1 + j) * shards, shards)], io_sem.at[10 + j]
            ).start()
            return carry

        lax.fori_loop(0, 4, phase_up, 0)

        def put_down(k):
            return pltpu.make_async_copy(acc.at[k], downs.at[k], io_sem.at[14 + k])

        def finish_down(k):
            stage_deck(k)
            put_down(k).start()

        finish_down(0)

        def phase_hidden(n, carry):
            cols = pl.ds(pl.multiple_of(n * LONG, 128), LONG)
            dr2[:, cols] += sum(dot(active[j], row_block(4 + j, n), NT) for j in range(4))
            return carry

        lax.fori_loop(0, longs, phase_hidden, 0)
        for copy in y_copies:
            copy.wait()
        finish_down(1)

        def phase_five(c, carry):
            at = pl.ds(pl.multiple_of(c * chunk, chunk), chunk)
            dh = dr2[at, :]
            normed = normed1[at, :]
            d = norm_back(dh, vec(3), normed, inv1[at, :])
            dvec[3:4, :] += jnp.sum(dh * normed, axis=0, keepdims=True)
            dvec[4:5, :] += jnp.sum(dh, axis=0, keepdims=True)
            dvec[2:3, :] += jnp.sum(d, axis=0, keepdims=True)
            feed[at, :] = d
            low = d.astype(bf16)
            dr1_low[at, :] = low
            da[at, :] = dot(low, matrix(3), NT).astype(bf16)
            return carry

        lax.fori_loop(0, rows // chunk, phase_five, 0)
        finals = [
            pltpu.make_async_copy(feed, dr1_out, io_sem.at[6]),
            pltpu.make_async_copy(da, da_out, io_sem.at[7]),
        ]
        for copy in finals:
            copy.start()
        finish_down(2)
        turned = attended[...].reshape(rows, width).T

        def phase_out(n, carry):
            cols = pl.ds(pl.multiple_of(n * TILE, TILE), TILE)
            grad = dot(hidden_turn[...], dr1_low[:, cols]).astype(bf16)
            stage[0, :, :, cols] = grad.reshape(shards, r, TILE)
            return carry

        hidden_turn[...] = turned
        lax.fori_loop(0, tiles, phase_out, 0)
        out_copy = pltpu.make_async_copy(stage.at[0], grads.at[pl.ds(0, shards)], io_sem.at[9])
        out_copy.start()
        finish_down(3)
        for j in range(4):
            pltpu.make_async_copy(
                stage.at[1 + j], grads.at[pl.ds((1 + j) * shards, shards)], io_sem.at[10 + j]
            ).wait()
            put_down(j).wait()
        out_copy.wait()
        for copy in finals + more:
            copy.wait()
        front_sent()
        finish()

    pl.run_scoped(
        ffn,
        pltpu.VMEM((rows, width), f32),
        pltpu.VMEM((rows, width), bf16),
        pltpu.VMEM((width, rows), bf16),
        pltpu.VMEM((rows, width), f32),
        pltpu.VMEM((rows, 1), f32),
        pltpu.VMEM((4, rows, width), bf16),
        pltpu.VMEM((4, rows, width), bf16),
        pltpu.VMEM((rows, width), f32),
        pltpu.VMEM((rows, width), f32),
        pltpu.VMEM((rows, width), bf16),
        pltpu.VMEM((rows, width), bf16),
        pltpu.VMEM((rows, width), bf16),
        pltpu.VMEM((5, shards, r, width), bf16),
        pltpu.VMEM((4 * shards, r, width), bf16),
    )


def forward(wk, wv, wq, wo, wu, wd, xc, xq, cot_c, cot_q, vecs, lengths, positions, predicted, rel_table, shards, seqn):
    rows_of, width = wq.shape
    seqs, block, _ = xc.shape
    span = positions.shape[1]
    f32, bf16 = jnp.float32, jnp.bfloat16
    steps = seqs * H // 2
    half = seqs * block
    anywhere = pl.BlockSpec(memory_space=pl.ANY)
    vmem = pl.BlockSpec(memory_space=pltpu.VMEM)
    rows = shards // 2
    _, shape = cutter(rows_of)
    dma = pltpu.SemaphoreType.DMA
    flat = lambda a: a.reshape(half, width)
    stream = (2, seqs, block, width)
    return pl.pallas_call(
        functools.partial(forward_kernel, shards, seqn, seqs, block, span, rows_of),
        out_shape=(
            jax.ShapeDtypeStruct((3 * shards, rows_of, width), bf16),
            jax.ShapeDtypeStruct((seqn,) + xc.shape, bf16),
            jax.ShapeDtypeStruct((steps, 2, 2 * block, span), bf16),
            jax.ShapeDtypeStruct(stream, bf16),
            jax.ShapeDtypeStruct(stream, bf16),
            jax.ShapeDtypeStruct((seqs, span, width), bf16),
            jax.ShapeDtypeStruct((seqs, span, width), bf16),
            jax.ShapeDtypeStruct((half, width), f32),
            jax.ShapeDtypeStruct((half, width), f32),
            jax.ShapeDtypeStruct((2 * half, width), f32),
            jax.ShapeDtypeStruct((2 * half, width), bf16),
            jax.ShapeDtypeStruct((5 * shards, rows_of, width), bf16),
            jax.ShapeDtypeStruct((DOWNS, rows, 2) + shape(3), bf16),
            jax.ShapeDtypeStruct((UNITS, width), f32),
        ),
        in_specs=[pl.BlockSpec(memory_space=pltpu.SMEM)] + [anywhere] * 11 + [vmem] * 12,
        out_specs=(anywhere,) * 13 + (vmem,),
        scratch_shapes=[
            pltpu.VMEM((UNITS * shards, rows_of, width), bf16),
            pltpu.VMEM((seqn,) + xc.shape, bf16),
            pltpu.VMEM((shards, 9, 4 * rows_of), f32),
            pltpu.VMEM((UNITS, width), f32),
            pltpu.VMEM((2 * half, 1), f32),
            pltpu.VMEM(stream, bf16),
            pltpu.VMEM((H, 128), f32),
            pltpu.VMEM((half, width), bf16),
            pltpu.VMEM((half, width), bf16),
            pltpu.VMEM((half, width), bf16),
            pltpu.VMEM((half, width), bf16),
            dma((18,)),
            dma((2,)),
            dma((4,)),
        ]
        + gather_scratch(shards)
        + front_scratch(shards, rows_of, DOWNS),
        compiler_params=pltpu.CompilerParams(collective_id=0, has_side_effects=True, vmem_limit_bytes=67043328),
        name="gather_attend_ffn",
    )(
        lengths, wk, wv, wq, wo, wu, wd.reshape(4, rows_of, width), xc, flat(xc), flat(xq), flat(cot_c), flat(cot_q),
        positions, predicted, rel_table.T, *vecs,
    )


def attend_back_pair(i, refs, low, seqs, block, span):
    attended, d_attended, query, keys, values, buckets, dq, dk, dv, ds_sum, sums, counts = refs
    f32, bf16 = jnp.float32, jnp.bfloat16
    pairs = H // 2
    rows = 2 * block
    s, pair = i // pairs, lax.rem(i, pairs)
    lanes = pl.ds(pl.multiple_of(pair * 128, 128), 128)
    q = query[:, s, :, lanes].reshape(rows, 128)
    k = keys[s, :, lanes]
    v = values[s, :, lanes]
    da = d_attended[:, s, :, lanes].reshape(rows, 128)
    product = da.astype(f32) * attended[:, s, :, lanes].reshape(rows, 128).astype(f32)
    d_queries, dk_turn, dv_turn = [], 0.0, 0.0
    for half in range(2):
        mine = head_lanes(rows, half)
        one = jnp.where(mine, da, 0).astype(bf16)
        inner = jnp.sum(jnp.where(mine, product, 0.0), axis=-1, keepdims=True)
        ds = low[half].astype(f32) * (dot(one, v, NT) - inner)
        ds_sum[pair * 2 + half] = (ds[:block] + ds[block:]).astype(bf16)
        ds_low = ds.astype(bf16)
        d_queries.append(dot(ds_low, k))
        dk_turn += dot(jnp.where(mine, q, 0).astype(bf16), ds_low, TN)
        dv_turn += dot(one, low[half], TN)
    d_query = jnp.where(head_lanes(rows, 0), d_queries[0], d_queries[1]) * 0.125
    sums[0:1, lanes] += jnp.sum(d_query, axis=0, keepdims=True)
    dq[:, s, :, lanes] = d_query.reshape(2, block, 128).astype(bf16)
    dk[s, :, lanes] = (dk_turn * 0.125).T.astype(bf16)
    d_value = dv_turn.T
    sums[1:2, lanes] += jnp.sum(d_value, axis=0, keepdims=True)
    dv[s, :, lanes] = d_value.astype(bf16)

    @pl.when(pair == pairs - 1)
    def _():
        def count(g, carry):
            at = pl.ds(pl.multiple_of(g * 16, 16), 16)
            bucket = buckets[s, 0, at, :]
            hot = jnp.concatenate([jnp.where(bucket == n, 1.0, 0.0).astype(bf16) for n in range(NB)], axis=0)
            counts[...] += dot(hot, ds_sum[:, at, :].reshape(H * 16, span), NT)
            return carry

        lax.fori_loop(0, block // 16, count, 0)


def table_of(counts):
    row = lax.broadcasted_iota(jnp.int32, counts.shape, 0)
    col = lax.broadcasted_iota(jnp.int32, counts.shape, 1)
    kept = jnp.where(lax.rem(row, 16) == lax.rem(col, 16), counts, 0.0)
    folded = jnp.sum(kept.reshape(NB, 16, H * 16), axis=1)
    lane = lax.broadcasted_iota(jnp.int32, (H * 16, 128), 1)
    head = lax.broadcasted_iota(jnp.int32, (H * 16, 128), 0) // 16
    return jnp.dot(folded, jnp.where(lane == head, 1.0, 0.0), precision=lax.Precision.HIGHEST)


def backward_kernel(
    shards, seqn, seqs, block, span, rows_of,
    lengths, grads, downs, squares, xall, probs, attended_in, da_in, query_in, keys_in, values_in, dr1_in,
    xc, xq, dvec, positions,
    out, d_content, d_query_x, small_out,
    dq, dk, dv, late, w, x_every, dxs, sums, counts, small, io_sem, low_sem, *scratch,
):
    f32, bf16 = jnp.float32, jnp.bfloat16
    width = H * HD
    half = seqs * block
    total_pairs = seqs * H // 2
    front, scratch = scratch[:FRONT_SCRATCH], scratch[FRONT_SCRATCH:]
    back, scratch = scratch[:BACK_SCRATCH], scratch[BACK_SCRATCH:]
    send_front, stage_core, stage_deck, front_sent = reduce_front(shards, rows_of, UNITS - DOWNS, front)
    send_across, later, back_sent = reduce_back(shards, rows_of, out, back)
    small_first, small_second, small_third, small_last = small_steps(shards, seqn, small, scratch[:SMALL_SCRATCH])
    dx_first, dx_second, dx_third = dx_steps(dxs, scratch[SMALL_SCRATCH:])
    dp, sq = lax.axis_index("dp"), lax.axis_index("seq")
    acc = front[0]
    early = UNITS - DOWNS - 3
    order = lambda k: UNITS - 1 - k
    weights = [pltpu.make_async_copy(squares.at[pl.ds(u * shards, shards)], w.at[u], io_sem.at[5 + u]) for u in range(3)]
    slots = [
        pltpu.make_async_copy(xall.at[k], x_every.at[:, pl.ds(k * block, block)], io_sem.at[8 + k]) for k in range(seqn)
    ]

    def deck_and_across(u):
        stage_deck(u)
        send_across(u, acc.at[u])

    across, line, final, half_stage = later
    ready, late_from_unit = DOWNS, DOWNS + early
    plan = (
        (stage_core, ready, early, 1, 1),
        (across, 0, DOWNS, 6, 3),
        (deck_and_across, ready, early, 9, 3),
        (line, 0, DOWNS, 12, 3),
        (final, 0, DOWNS, 15, 3),
        (half_stage, 0, DOWNS, 18, 3),
        (across, ready, early, 18, 3),
        (stage_core, late_from_unit, 3, 18, 3),
        (line, ready, early, 24, 3),
        (deck_and_across, late_from_unit, 3, 24, 3),
        (final, ready, early, 27, 3),
        (half_stage, ready, early, 30, 3),
        (across, late_from_unit, 3, 32, 3),
        (line, late_from_unit, 3, 38, 3),
        (final, late_from_unit, 3, 42, 3),
        (half_stage, late_from_unit, 3, 45, 3),
    )
    ticks = 52

    def tick(t):
        for stage, first, count, start, gap in plan:
            d = t - start

            @pl.when((d >= 0) & (d < count * gap) & (lax.rem(d, gap) == 0))
            def _(stage=stage, first=first, d=d, gap=gap):
                stage(order(first + d // gap))

    def one(t, carry):
        tick(t)
        return carry

    def attention(attended, d_attended, query, keys, values, buckets, low_two, ds_sum):
        loads = [
            pltpu.make_async_copy(src, dst, io_sem.at[i])
            for i, (src, dst) in enumerate(
                ((attended_in, attended), (da_in, d_attended), (query_in, query), (keys_in, keys), (values_in, values))
            )
        ]

        def take(i, slot):
            return pltpu.make_async_copy(probs.at[i], low_two.at[slot], low_sem.at[slot])

        barrier, count = greet_all(dp, sq, shards, seqn)
        for load in loads:
            load.start()
        take(0, 0).start()
        for load in weights + slots:
            load.start()
        pl.semaphore_wait(barrier, count)

        def send(k, carry):
            u = order(DOWNS + k)
            send_front(u, lambda shard: grads.at[(u - 3) * shards + shard])
            return carry

        def send_down(k, carry):
            send_across(order(k), downs.at[order(k) - 8])
            return carry

        lax.fori_loop(0, early, send, 0)
        lax.fori_loop(0, DOWNS, send_down, 0)
        fill_buckets(buckets, positions, lengths, sq * block, seqs, block, span)
        counts[...] = jnp.zeros_like(counts)
        sums[...] = jnp.zeros_like(sums)
        for load in loads:
            load.wait()
        refs = (attended, d_attended, query, keys, values, buckets, dq, dk, dv, ds_sum, sums, counts)

        def pair(i, carry):
            slot = lax.rem(i, 2)

            tick(i)
            take(i, slot).wait()

            @pl.when(i + 1 < total_pairs)
            def _():
                take(i + 1, 1 - slot).start()

            attend_back_pair(i, refs, low_two.at[slot], seqs, block, span)
            return carry

        lax.fori_loop(0, total_pairs, pair, 0)

    pl.run_scoped(
        attention,
        pltpu.VMEM((2, seqs, block, width), bf16),
        pltpu.VMEM((2, seqs, block, width), bf16),
        pltpu.VMEM((2, seqs, block, width), bf16),
        pltpu.VMEM((seqs, span, width), bf16),
        pltpu.VMEM((seqs, span, width), bf16),
        pltpu.VMEM((seqs, 2, block, span), jnp.int32),
        pltpu.VMEM((2, 2, 2 * block, span), bf16),
        pltpu.VMEM((H, block, span), bf16),
    )

    tile = 256

    def weight_grads(dr1, turned, x_two):
        load = pltpu.make_async_copy(dr1_in, dr1, io_sem.at[0])
        load.start()
        loads = [pltpu.make_async_copy(x, x_two.at[t], io_sem.at[1 + t]) for t, x in enumerate((xc, xq))]
        for copy in loads:
            copy.start()
        for copy in weights + slots:
            copy.wait()
        matrix = lambda u: w[u].reshape(width, width)
        turned[...] = x_every[...].reshape(seqs * span, width).T

        def late_from(u, ref, first_tick):
            def tiles(n, carry):
                tick(first_tick + n)
                cols = pl.ds(pl.multiple_of(n * tile, tile), tile)
                grad = dot(turned[...], ref[:, :, cols].reshape(seqs * span, tile))
                late[u, :, :, cols] = grad.astype(bf16).reshape(shards, rows_of, tile)
                return carry

            lax.fori_loop(0, width // tile, tiles, 0)
            send_front(u, lambda shard: late.at[u, shard])

        for copy in loads:
            copy.wait()

        def tiles(n, carry):
            tick(12 + n)
            cols = pl.ds(pl.multiple_of(n * tile, tile), tile)
            grad = sum(
                dot(x_two[t].reshape(half, width), dq[t, :, :, cols].reshape(half, tile), TN) for t in range(2)
            )
            late[2, :, :, cols] = grad.astype(bf16).reshape(shards, rows_of, tile)
            return carry

        lax.fori_loop(0, width // tile, tiles, 0)
        send_front(2, lambda shard: late.at[2, shard])
        late_from(1, dv, 15)
        late_from(0, dk, 18)

        def every(n, carry):
            tick(21 + n)
            s, k = n // seqn, lax.rem(n, seqn)
            at = pl.ds(pl.multiple_of(k * block, block), block)
            part = dot(dk[s, at, :], matrix(0), NT) + dot(dv[s, at, :], matrix(1), NT)
            dxs[k, pl.ds(pl.multiple_of(s * block, block), block), :] = part.astype(bf16)
            return carry

        lax.fori_loop(0, seqs * seqn, every, 0)
        dx_first()
        load.wait()
        for t, d_x in enumerate((d_content, d_query_x)):
            d_x[...] = dr1[pl.ds(t * half, half), :] + dot(dq[t].reshape(half, width), matrix(2), NT)

    pl.run_scoped(
        weight_grads,
        pltpu.VMEM((2 * half, width), f32),
        pltpu.VMEM((width, seqs * span), bf16),
        pltpu.VMEM((2, seqs, block, width), bf16),
    )
    table = table_of(counts[...])
    vectors = jnp.concatenate([sums[0:2, :], dvec[2:, :], jnp.zeros((4, width), f32)], axis=0)
    pieces = [vectors[:, c * 128 : (c + 1) * 128] for c in range(width // 128)] + [table[:16], table[16:]]
    each = shards // 8
    size = 16 // each
    for p, piece in enumerate(pieces):
        for k in range(each):
            small[p * each + k] = piece[k * size : (k + 1) * size]
    small_first()
    lax.fori_loop(29, 31, one, 0)
    dx_second()
    lax.fori_loop(31, 33, one, 0)
    small_second()
    lax.fori_loop(33, 36, one, 0)
    small_third()
    lax.fori_loop(36, ticks, one, 0)
    dx_third(d_content)
    small_last(small_out)
    front_sent()
    back_sent()


def backward(lengths, grads, downs, squares, xall, probs, attended, d_attended, query, keys, values, dr1, xc, xq, dvec, positions, shards, seqn):
    rows_of, width = squares.shape[1:]
    seqs, block, _ = xc.shape
    span = positions.shape[1]
    f32, bf16 = jnp.float32, jnp.bfloat16
    anywhere = pl.BlockSpec(memory_space=pl.ANY)
    vmem = pl.BlockSpec(memory_space=pltpu.VMEM)
    own = (seqs * block, width)
    small_shape = (shards, 128 // shards, 128)
    dma = pltpu.SemaphoreType.DMA
    return pl.pallas_call(
        functools.partial(backward_kernel, shards, seqn, seqs, block, span, rows_of),
        out_shape=(
            jax.ShapeDtypeStruct((UNITS, rows_of, width), bf16),
            jax.ShapeDtypeStruct(own, f32),
            jax.ShapeDtypeStruct(own, f32),
            jax.ShapeDtypeStruct(small_shape, f32),
        ),
        in_specs=[pl.BlockSpec(memory_space=pltpu.SMEM)] + [anywhere] * 13 + [vmem] * 2,
        out_specs=(vmem,) * 4,
        scratch_shapes=[
            pltpu.VMEM((2, seqs, block, width), bf16),
            pltpu.VMEM((seqs, span, width), bf16),
            pltpu.VMEM((seqs, span, width), bf16),
            pltpu.VMEM((3, shards, rows_of, width), bf16),
            pltpu.VMEM((3, shards, rows_of, width), bf16),
            pltpu.VMEM((seqs, span, width), bf16),
            pltpu.VMEM((seqn,) + own, bf16),
            pltpu.VMEM((8, width), f32),
            pltpu.VMEM((NB * 16, H * 16), f32),
            pltpu.VMEM(small_shape, f32),
            dma((8 + seqn,)),
            dma((2,)),
        ]
        + front_scratch(shards, rows_of, UNITS - DOWNS)
        + back_scratch(shards, rows_of)
        + small_scratch(shards, seqn, small_shape)
        + dx_scratch(own),
        compiler_params=pltpu.CompilerParams(
            collective_id=1, has_side_effects=True, vmem_limit_bytes=67043328
        ),
        name="attend_back_reduce",
    )(lengths, grads, downs, squares, xall, probs, attended, d_attended, query, keys, values, dr1, xc, xq, dvec, positions)


def present_kernel(
    shards, rows_of,
    sums, small, y_c_in, y_q_in, g_c_in, g_q_in,
    y_c, y_q, g_c, g_q, wk, wv, wq, wo, wu, wd, *rest,
):
    vectors, table, wide_rows, low, units, passing, in_sem, out_sem, pass_sem = rest[:9], rest[9], *rest[10:]
    f32 = jnp.float32
    width = H * HD
    r = rows_of
    get = pltpu.make_async_copy(sums, low, in_sem.at[4])
    get.start()
    moves = []
    for i, (src, dst) in enumerate(((y_c_in, y_c), (y_q_in, y_q), (g_c_in, g_c), (g_q_in, g_q))):
        come = pltpu.make_async_copy(src, passing.at[i], in_sem.at[i])
        come.start()
        moves.append((come, pltpu.make_async_copy(passing.at[i], dst, pass_sem.at[i])))
    get.wait()
    pieces = [wk, wv, wq, wo] + [wu.at[:, pl.ds(j * width, width)] for j in range(4)]
    pieces += [wd.at[j] for j in range(4)]
    outs = [pltpu.make_async_copy(units.at[u], piece, out_sem.at[u]) for u, piece in enumerate(pieces)]
    for u, out in enumerate(outs):
        units[u] = low[u].astype(f32)
        out.start()
        if u % 3 == 2:
            come, go = moves[u // 3]
            come.wait()
            go.start()
    me = lax.axis_index("dp")
    whole = jnp.concatenate([small[c] for c in range(width // 128)], axis=1)
    place_of = lax.broadcasted_iota(jnp.int32, (width, r), 0)
    lane = lax.broadcasted_iota(jnp.int32, (width, r), 1)
    mine = jnp.dot(whole, jnp.where(place_of == me * r + lane, 1.0, 0.0), precision=lax.Precision.HIGHEST)
    for i in range(8):
        vectors[i][...] = mine[i]
    per = width // (4 * r)
    place_of = lax.broadcasted_iota(jnp.int32, (width, 4 * r), 0)
    lane = lax.broadcasted_iota(jnp.int32, (width, 4 * r), 1)
    at = jnp.where(place_of == lax.rem(me, per) * (4 * r) + lane, 1.0, 0.0)
    wide_rows[...] = jnp.dot(whole, at, precision=lax.Precision.HIGHEST)
    vectors[8][...] = wide_rows[pl.ds(8 + me // per, 1), :].reshape(4 * r)
    table[...] = jnp.concatenate([small[6], small[7]], axis=0).T[:H, :]
    for out in outs:
        out.wait()
    for come, go in moves:
        go.wait()


def present(sums, small, y_c, y_q, g_c, g_q, shards):
    _, r, width = sums.shape
    f32, bf16 = jnp.float32, jnp.bfloat16
    anywhere = pl.BlockSpec(memory_space=pl.ANY)
    vmem = pl.BlockSpec(memory_space=pltpu.VMEM)
    own = y_c.shape
    shape = lambda *dims: jax.ShapeDtypeStruct(dims, f32)
    dma = pltpu.SemaphoreType.DMA
    return pl.pallas_call(
        functools.partial(present_kernel, shards, r),
        out_shape=(shape(*own),) * 4
        + (shape(r, width),) * 4
        + (shape(r, 4 * width), shape(4, r, width))
        + (shape(r),) * 8
        + (shape(4 * r), shape(H, NB)),
        in_specs=[anywhere, vmem] + [anywhere] * 4,
        out_specs=(anywhere,) * 10 + (vmem,) * 10,
        scratch_shapes=[
            pltpu.VMEM((16, 4 * r), f32),
            pltpu.VMEM((UNITS, r, width), bf16),
            pltpu.VMEM((UNITS, r, width), f32),
            pltpu.VMEM((4,) + own, f32),
            dma((5,)),
            dma((UNITS,)),
            dma((4,)),
        ],
        compiler_params=pltpu.CompilerParams(vmem_limit_bytes=67043328),
        name="present",
    )(sums, small.reshape(8, 16, 128), y_c, y_q, g_c, g_q)


def per_device(
    x_content, x_query, cot_content, cot_query,
    w_query, b_query, w_key, w_value, b_value, w_out, b_out, gain_attn, shift_attn,
    w_up, b_up, w_down, b_down, gain_ffn, shift_ffn, rel_table, lengths, positions, predicted,
    *, shards, seqn,
):
    f32 = jnp.float32
    seqs, block, width = x_content.shape
    r = w_query.shape[0]
    vecs = [
        v.reshape(1, r) for v in (b_query, b_value, b_out, gain_attn, shift_attn, b_down, gain_ffn, shift_ffn)
    ] + [b_up]
    (squares, xall, probs, attended, query, keys, values, y_c, y_q, dr1, d_attended, grads, downs, dvec) = forward(
        w_key, w_value, w_query, w_out, w_up, w_down, x_content, x_query, cot_content, cot_query, vecs,
        lengths, positions, predicted, rel_table, shards, seqn,
    )
    sums, g_content, g_x_query, small = backward(
        lengths, grads, downs, squares, xall, probs, attended, d_attended.reshape(attended.shape),
        query, keys, values, dr1, x_content, x_query, dvec, positions, shards, seqn,
    )
    (
        y_c, y_q, g_content, g_x_query, g_wk, g_wv, g_wq, g_wo, g_w1, g_w2,
        g_bq, g_bv, g_bo, g_g1, g_b1, g_c2, g_g2, g_b2, g_c1, g_table,
    ) = present(sums, small, y_c, y_q, g_content, g_x_query, shards)
    shape = (seqs, block, width)
    return (
        y_c.reshape(shape), y_q.reshape(shape), g_content.reshape(shape), g_x_query.reshape(shape),
        g_wq, g_bq, g_wk, g_wv, g_bv, g_wo, g_bo, g_g1, g_b1,
        g_w1, g_c1, g_w2.reshape(4 * r, width), g_c2, g_g2, g_b2, g_table.T,
    )


def solution(mesh):
    in_specs = (
        P("dp", "seq", None),
        P("dp", "seq", None),
        P("dp", "seq", None),
        P("dp", "seq", None),
        P("dp", None),
        P("dp"),
        P("dp", None),
        P("dp", None),
        P("dp"),
        P("dp", None),
        P("dp"),
        P("dp"),
        P("dp"),
        P("dp", None),
        P("dp"),
        P("dp", None),
        P("dp"),
        P("dp"),
        P("dp"),
        P(),
        P("dp"),
        P("dp", None),
        P("dp", "seq"),
    )
    out_specs = (
        P("dp", "seq", None),
        P("dp", "seq", None),
        P("dp", "seq", None),
        P("dp", "seq", None),
        P("dp", None),
        P("dp"),
        P("dp", None),
        P("dp", None),
        P("dp"),
        P("dp", None),
        P("dp"),
        P("dp"),
        P("dp"),
        P("dp", None),
        P("dp"),
        P("dp", None),
        P("dp"),
        P("dp"),
        P("dp"),
        P(),
    )
    return jax.shard_map(
        functools.partial(per_device, shards=mesh.shape["dp"], seqn=mesh.shape["seq"]),
        mesh=mesh, in_specs=in_specs, out_specs=out_specs, check_vma=False
    )
```

```python
import functools

import jax
import jax.numpy as jnp
from jax import lax
from jax.experimental import pallas as pl
from jax.experimental.pallas import tpu as pltpu
from jax.sharding import PartitionSpec as P

H = 12
HD = 64
NB = 32

MESH = pl.DeviceIdType.MESH
UNITS = 12


def cutter(rows_of):
    by_rows = rows_of % 96 == 0
    piece = rows_of // 6 if by_rows else 128

    def cut(start, size):
        if not isinstance(start, int):
            start = pl.multiple_of(start * piece, 16 if by_rows else 128)
        else:
            start = start * piece
        inner = pl.ds(start, size * piece)
        return (inner, slice(None)) if by_rows else (slice(None), inner)

    def shape(size):
        return (size * piece, 768) if by_rows else (rows_of, size * piece)

    return cut, shape


def place():
    dp, sq = lax.axis_index("dp"), lax.axis_index("seq")
    row, side = dp // 2, dp % 2
    deck, core = sq // 2, sq % 2
    return dp, sq, row, side, deck, core


def tile_of(unit, shard, shards):
    down = unit // 8
    return (1 - down) * (unit * shards + shard) + down * (8 * shards + shard * 4 + unit - 8)


def remote(src, dst, send, recv, device):
    return pltpu.make_async_remote_copy(
        src_ref=src, dst_ref=dst, send_sem=send, recv_sem=recv, device_id=device, device_id_type=MESH
    )


def greet_all(dp, sq, shards, seqn):
    barrier = pltpu.get_barrier_semaphore()

    def greet(step, carry):
        pl.semaphore_signal(barrier, inc=1, device_id=(lax.rem(dp + step, shards), sq), device_id_type=MESH)
        return carry

    def greet_seq(step, carry):
        pl.semaphore_signal(barrier, inc=1, device_id=(dp, lax.rem(sq + step, seqn)), device_id_type=MESH)
        return carry

    lax.fori_loop(1, shards, greet, 0)
    lax.fori_loop(1, seqn, greet_seq, 0)
    return barrier, shards + seqn - 2


AHEAD = 2
X_LAG = 1
Y_LAG = 1


def gather_steps(shards, seqn, ins, outs, scratch):
    wk, wv, wq, wo, wu, wd, xc = ins
    full, xall, vall = outs
    (load_sem, zu_sem, zd_sem, xs_sem, ys_sem, cp_sem, cy_sem,
     zr_sem, xr_sem, yr_sem, cpr_sem, cyr_sem, xc_send, xc_recv, vec_send, vec_recv) = scratch
    dp, sq, row, side, deck, core = place()
    rows = shards // 2
    across = (row * 2 + 1 - side, sq)
    other_deck = (dp, (1 - deck) * 2 + core)
    sibling = (dp, deck * 2 + 1 - core)
    cut, _ = cutter(full.shape[1])
    plane = cut(core * 3 + deck, 2)
    solo = cut(core * 3 + deck * 2, 1)
    theirs = cut(core * 3 + (1 - deck) * 2, 1)

    def many(count, size):
        return full.at[(pl.ds(0, count),) + cut(0, size)]

    def part(unit, shard, piece):
        return full.at[(tile_of(unit, shard, shards),) + piece]

    pieces = [wk, wv, wq, wo] + [wu.at[:, pl.ds(j * 768, 768)] for j in range(4)] + [wd.at[j] for j in range(4)]
    loads = [
        pltpu.make_async_copy(piece, full.at[tile_of(u, dp, shards)], load_sem.at[u]) for u, piece in enumerate(pieces)
    ]
    x_mine = xall.at[sq]
    xload = pltpu.make_async_copy(xc, x_mine, load_sem.at[UNITS])
    x_deck = remote(x_mine, x_mine, xc_send.at[0], xc_recv.at[0], other_deck)
    x_core = remote(x_mine, x_mine, xc_send.at[1], xc_recv.at[1], sibling)
    x_theirs = xall.at[(1 - deck) * 2 + core]
    x_forward = remote(x_theirs, x_theirs, xc_send.at[2], xc_recv.at[2], sibling)

    up = ((row + 1) * 2 + side, sq)
    down = ((row - 1) * 2 + side, sq)

    def along(u, s, src):
        dst = part(u, s * 2 + side, plane)

        @pl.when((s <= row) & (row < rows - 1))
        def _():
            remote(src, dst, zu_sem.at[s], zr_sem.at[u, s], up).start()

        @pl.when((s >= row) & (row > 0))
        def _():
            remote(src, dst, zd_sem.at[s], zr_sem.at[u, s], down).start()

    def send_own(u):
        tile = full.at[tile_of(u, dp, shards)]
        pltpu.make_async_copy(tile, tile, load_sem.at[u]).wait()
        along(u, row, part(u, dp, plane))
        across_own(u)

    def across_own(u):
        ref = part(u, dp, plane)
        remote(ref, ref, xs_sem, xr_sem.at[u], across).start()

    def to_deck(u, shard):
        ref = part(u, shard, solo)
        remote(ref, ref, ys_sem, yr_sem.at[u], other_deck).start()

    def to_core(u, shard):
        ref = part(u, shard, plane)
        remote(ref, ref, cp_sem, cpr_sem.at[u], sibling).start()

    def begin():
        barrier, count = greet_all(dp, sq, shards, seqn)
        for load in loads:
            load.start()
        xload.start()
        pl.semaphore_wait(barrier, count)

        def send_vec(step, carry):
            to = (lax.rem(dp + step, shards), sq)
            remote(vall.at[dp], vall.at[dp], vec_send, vec_recv, to).start()
            return carry

        lax.fori_loop(1, shards, send_vec, 0)

        def first(u, carry):
            send_own(u)
            return carry

        lax.fori_loop(0, AHEAD, first, 0)

        xload.wait()
        x_deck.start()
        x_core.start()

    def step(n):
        @pl.when(n + AHEAD < UNITS)
        def _():
            send_own(n + AHEAD)

        def hop(t, carry):
            u = n - (t - 1)

            def arrived(s):
                ref = part(u, s * 2 + side, plane)
                remote(ref, ref, xs_sem, zr_sem.at[u, s], across).wait_recv()
                along(u, s, ref)
                remote(ref, ref, xs_sem, xr_sem.at[u], across).start()
                to_deck(u, s * 2 + side)
                to_core(u, s * 2 + side)

            @pl.when((u >= 0) & (u < UNITS))
            def _():
                pl.when(row - t >= 0)(lambda: arrived(row - t))
                pl.when(row + t < rows)(lambda: arrived(row + t))

            return carry

        lax.fori_loop(1, rows, hop, 0)
        ux = n - (rows - 1) - X_LAG

        @pl.when((ux >= 0) & (ux < UNITS))
        def _():
            remote(many(rows, 2), many(rows, 2), xs_sem, xr_sem.at[ux], across).wait_recv()

            def pass_on(s, carry):
                to_deck(ux, s * 2 + 1 - side)
                to_core(ux, s * 2 + 1 - side)
                return carry

            lax.fori_loop(0, rows, pass_on, 0)

        uy = n - rows - X_LAG - Y_LAG

        @pl.when((uy >= 0) & (uy < UNITS))
        def _():
            remote(many(shards - 1, 1), many(shards - 1, 1), ys_sem, yr_sem.at[uy], other_deck).wait_recv()

            def pass_on(k, carry):
                ref = part(uy, lax.rem(dp + k, shards), theirs)
                remote(ref, ref, cy_sem, cyr_sem.at[uy], sibling).start()
                return carry

            lax.fori_loop(1, shards, pass_on, 0)

    def pass_x():
        x_deck.wait_recv()
        x_forward.start()

    def wait_x():
        x_core.wait_recv()
        x_forward.wait_recv()

    def wait_vec():
        rest = vall.at[pl.ds(0, shards - 1)]
        remote(rest, rest, vec_send, vec_recv, sibling).wait_recv()

    def whole(u):
        remote(many(shards - 1, 2), many(shards - 1, 2), cp_sem, cpr_sem.at[u], sibling).wait_recv()
        remote(many(shards - 1, 1), many(shards - 1, 1), cy_sem, cyr_sem.at[u], sibling).wait_recv()

    def finish():
        x_deck.wait_send()
        x_core.wait_send()
        x_forward.wait_send()
        rest = vall.at[pl.ds(0, shards - 1)]
        remote(rest, rest, vec_send, vec_recv, sibling).wait_send()
        for count, size, sem in (
            (UNITS * rows, 2, xs_sem),
            (UNITS * (shards - 1), 1, ys_sem),
            (UNITS * (shards - 1), 1, cy_sem),
            (UNITS * (shards - 1), 2, cp_sem),
        ):
            ref = many(count, size)
            remote(ref, ref, sem, xr_sem.at[0], sibling).wait_send()

        def sent(s, carry):
            ref = many(UNITS, 2)

            @pl.when((s <= row) & (row < rows - 1))
            def _():
                remote(ref, ref, zu_sem.at[s], xr_sem.at[0], sibling).wait_send()

            @pl.when((s >= row) & (row > 0))
            def _():
                remote(ref, ref, zd_sem.at[s], xr_sem.at[0], sibling).wait_send()

            return carry

        lax.fori_loop(0, rows, sent, 0)

    return begin, step, whole, pass_x, wait_x, wait_vec, finish


def gather_scratch(shards):
    dma = pltpu.SemaphoreType.DMA
    return [dma((UNITS + 1,))] + [dma((shards // 2,))] * 2 + [dma(())] * 4 + [dma((UNITS, shards // 2))] + [dma((UNITS,))] * 4 + [dma((3,)), dma((3,)), dma(()), dma(())]


GATHER_SCRATCH = 16


def reduce_front(shards, rows_of, count, scratch):
    f32, bf16 = jnp.float32, jnp.bfloat16
    acc, got_core, got_deck, load_sem, core_send, core_recv, deck_send, deck_recv = scratch
    dp, sq, row, side, deck, core = place()
    rows = shards // 2
    other_deck = (dp, (1 - deck) * 2 + core)
    sibling = (dp, deck * 2 + 1 - core)
    cut, _ = cutter(rows_of)
    mine = cut(core * 3, 3)
    siblings = cut((1 - core) * 3, 3)
    solo = cut(deck * 2, 1)
    other_solo = cut((1 - deck) * 2, 1)

    def send(u, tiles):
        def one(s, carry):
            for b in range(2):
                tile = tiles(s * 2 + b)
                remote(tile.at[siblings], got_core.at[u, s, b], core_send.at[u], core_recv.at[u], sibling).start()
                pltpu.make_async_copy(tile.at[mine], acc.at[u, s, b], load_sem.at[u]).start()
            return carry

        lax.fori_loop(0, rows, one, 0)

    def core_copy(u):
        return remote(got_core.at[u], got_core.at[u], core_send.at[u], core_recv.at[u], sibling)

    def deck_copy(u):
        src = acc.at[(u, slice(None), slice(None)) + other_solo]
        return remote(src, got_deck.at[u], deck_send.at[u], deck_recv.at[u], other_deck)

    def stage_core(u):
        pltpu.make_async_copy(acc.at[u], acc.at[u], load_sem.at[u]).wait()
        core_copy(u).wait_recv()

        def add(s, carry):
            for b in range(2):
                acc[u, s, b] = total(acc[u, s, b], got_core[u, s, b])
            return carry

        lax.fori_loop(0, rows, add, 0)
        deck_copy(u).start()

    def stage_deck(u):
        deck_copy(u).wait_recv()

        def add(s, carry):
            for b in range(2):
                at = (u, s, b) + solo
                acc[at] = total(acc[at], got_deck[u, s, b])
            return carry

        lax.fori_loop(0, rows, add, 0)

    def sent():
        def one(u, carry):
            core_copy(u).wait_send()
            deck_copy(u).wait_send()
            return carry

        lax.fori_loop(0, count, one, 0)

    return send, stage_core, stage_deck, sent


def total(left, right):
    return left + right


def front_scratch(shards, rows_of, count):
    bf16 = jnp.bfloat16
    rows = shards // 2
    _, shape = cutter(rows_of)
    return [
        pltpu.VMEM((count, rows, 2) + shape(3), bf16),
        pltpu.VMEM((count, rows, 2) + shape(3), bf16),
        pltpu.VMEM((count, rows, 2) + shape(1), bf16),
    ] + [pltpu.SemaphoreType.DMA((count,))] * 5


FRONT_SCRATCH = 8


def reduce_back(shards, rows_of, out, scratch):
    f32, bf16 = jnp.float32, jnp.bfloat16
    (own_side, got_across, line, got_line, final, got_final, half, got_half,
     side_sem, across_send, across_recv, line_send, line_recv, final_send, final_recv, half_send, half_recv) = scratch
    dp, sq, row, side, deck, core = place()
    rows = shards // 2
    across = (row * 2 + 1 - side, sq)
    other_deck = (dp, (1 - deck) * 2 + core)
    sibling = (dp, deck * 2 + 1 - core)
    cut, _ = cutter(rows_of)
    mine = cut(core * 3, 3)
    siblings = cut((1 - core) * 3, 3)
    plane = cut(deck, 2)
    other_solo = cut((1 - deck) * 2, 1)

    def send_across(u, planes):
        remote(
            planes.at[(slice(None), 1 - side) + plane], got_across.at[u], across_send.at[u], across_recv.at[u], across
        ).start()
        pltpu.make_async_copy(planes.at[(slice(None), side) + plane], own_side.at[u], side_sem.at[u]).start()

    def across_copy(u):
        return remote(got_across.at[u], got_across.at[u], across_send.at[u], across_recv.at[u], across)

    def line_copy(u):
        ref = got_line.at[u, pl.ds(0, rows - 1)]
        return remote(ref, ref, line_send.at[u], line_recv.at[u], across)

    def final_copy(u):
        return remote(final.at[u], got_final.at[u], final_send.at[u], final_recv.at[u], other_deck)

    def half_copy(u):
        return remote(half.at[u], got_half.at[u], half_send.at[u], half_recv.at[u], sibling)

    def stage_across(u):
        pltpu.make_async_copy(own_side.at[u], own_side.at[u], side_sem.at[u]).wait()
        across_copy(u).wait_recv()

        def add(k, carry):
            s = lax.rem(row + k, rows)
            line[u, s] = total(own_side[u, s], got_across[u, s])

            @pl.when(k < rows)
            def _():
                remote(
                    line.at[u, s], got_line.at[u, rows - 1 - k], line_send.at[u], line_recv.at[u], (s * 2 + side, sq)
                ).start()

            return carry

        lax.fori_loop(1, rows + 1, add, 0)

    def stage_line(u):
        line_copy(u).wait_recv()
        summed = line[u, row].astype(f32)
        if rows <= 4:
            for k in range(rows - 1):
                summed = summed + got_line[u, k].astype(f32)
        else:
            summed = lax.fori_loop(0, rows - 1, lambda k, t: t + got_line[u, k].astype(f32), summed)
        final[u] = summed.astype(bf16)
        final_copy(u).start()

    def stage_final(u):
        final_copy(u).wait_recv()
        half[(u,) + plane] = final[u]
        half[(u,) + other_solo] = got_final[(u,) + cut(1 - deck, 1)]
        both = (u,) + cut(1, 1)
        half[both] = total(half[both], got_final[(u,) + cut(deck, 1)])
        half_copy(u).start()

    def stage_half(u):
        half_copy(u).wait_recv()
        out[(u,) + mine] = half[u]
        out[(u,) + siblings] = got_half[u]

    def sent():
        def one(u, carry):
            for copy in (across_copy, line_copy, final_copy, half_copy):
                copy(u).wait_send()
            return carry

        lax.fori_loop(0, UNITS, one, 0)

    return send_across, (stage_across, stage_line, stage_final, stage_half), sent


def back_scratch(shards, rows_of):
    bf16 = jnp.bfloat16
    rows = shards // 2
    _, shape = cutter(rows_of)
    return [pltpu.VMEM((UNITS, rows) + shape(2), bf16)] * 4 + [
        pltpu.VMEM((UNITS,) + shape(2), bf16),
        pltpu.VMEM((UNITS,) + shape(2), bf16),
        pltpu.VMEM((UNITS,) + shape(3), bf16),
        pltpu.VMEM((UNITS,) + shape(3), bf16),
    ] + [pltpu.SemaphoreType.DMA((UNITS,))] * 9


BACK_SCRATCH = 17


def small_steps(shards, seqn, small, scratch):
    got_small, mid_small, got_mid, got_all, small_send, small_recv = scratch
    dp, sq, row, side, deck, core = place()
    sibling = (dp, deck * 2 + 1 - core)

    def small_first():
        got_small[dp] = small[dp]

        def send(k, carry):
            to = lax.rem(dp + k, shards)
            remote(small.at[to], got_small.at[dp], small_send.at[0], small_recv.at[0], (to, sq)).start()
            return carry

        lax.fori_loop(1, shards, send, 0)

    def sum_of(ref, count):
        summed = ref[0]
        for i in range(1, count):
            summed = summed + ref[i]
        return summed

    def small_second():
        rest = got_small.at[pl.ds(0, shards - 1)]
        remote(rest, rest, small_send.at[0], small_recv.at[0], sibling).wait()
        summed = sum_of(got_small, shards)
        mid_small[0] = summed
        got_mid[sq] = summed

        def send(k, carry):
            to = (dp, lax.rem(sq + k, seqn))
            remote(mid_small.at[0], got_mid.at[sq], small_send.at[1], small_recv.at[1], to).start()
            return carry

        lax.fori_loop(1, seqn, send, 0)

    def small_third():
        rest = got_mid.at[pl.ds(0, seqn - 1)]
        remote(rest, rest, small_send.at[1], small_recv.at[1], sibling).wait()
        summed = sum_of(got_mid, seqn)
        mid_small[1] = summed
        got_all[dp] = summed

        def send(k, carry):
            to = (lax.rem(dp + k, shards), sq)
            remote(mid_small.at[1], got_all.at[dp], small_send.at[2], small_recv.at[2], to).start()
            return carry

        lax.fori_loop(1, shards, send, 0)

    def small_last(small_out):
        rest = got_all.at[pl.ds(0, shards - 1)]
        remote(rest, rest, small_send.at[2], small_recv.at[2], sibling).wait()
        small_out[...] = got_all[...]

    return small_first, small_second, small_third, small_last


def small_scratch(shards, seqn, small_shape):
    f32 = jnp.float32
    return [
        pltpu.VMEM(small_shape, f32),
        pltpu.VMEM((2,) + small_shape[1:], f32),
        pltpu.VMEM((seqn,) + small_shape[1:], f32),
        pltpu.VMEM(small_shape, f32),
    ] + [pltpu.SemaphoreType.DMA((3,))] * 2


SMALL_SCRATCH = 6


def dx_steps(dxs, scratch):
    f32, bf16 = jnp.float32, jnp.bfloat16
    dx_own, dx_core, dx_deck, load, send, recv = scratch
    dp, sq, row, side, deck, core = place()
    other_deck = (dp, (1 - deck) * 2 + core)
    sibling = (dp, deck * 2 + 1 - core)
    deck_dx = remote(dx_own.at[1 - deck], dx_deck, send.at[2], recv.at[2], other_deck)

    def first():
        for k in range(2):
            pltpu.make_async_copy(dxs.at[k * 2 + core], dx_own.at[k], load.at[k]).start()
            remote(dxs.at[k * 2 + 1 - core], dx_core.at[k], send.at[k], recv.at[k], sibling).start()

    def second():
        for k in range(2):
            pltpu.make_async_copy(dx_own.at[k], dx_own.at[k], load.at[k]).wait()
            remote(dx_core.at[k], dx_core.at[k], send.at[k], recv.at[k], sibling).wait()
            dx_own[k] = (dx_own[k].astype(f32) + dx_core[k].astype(f32)).astype(bf16)
        deck_dx.start()

    def third(dx_out):
        deck_dx.wait()
        dx_out[...] += dx_own[deck].astype(f32) + dx_deck[...].astype(f32)

    return first, second, third


def dx_scratch(own):
    bf16 = jnp.bfloat16
    dma = pltpu.SemaphoreType.DMA
    return [pltpu.VMEM((2,) + own, bf16), pltpu.VMEM((2,) + own, bf16), pltpu.VMEM(own, bf16), dma((2,)), dma((3,)), dma((3,))]


bucket_marks = (12, 16, 23, 32, 46, 64, 91)
MASKED = NB
TN = (((0,), (0,)), ((), ()))
NT = (((1,), (1,)), ((), ()))


def dot(left, right, dims=None):
    if dims is None:
        dims = (((1,), (0,)), ((), ()))
    return lax.dot_general(left, right, dims, preferred_element_type=jnp.float32)


def column_of(row):
    return jnp.broadcast_to(row.astype(jnp.float32), (row.shape[1], row.shape[1])).T


def fill_buckets(buckets, positions, lengths, base, seqs, block, span):
    for s in range(seqs):
        mine = column_of(positions[s : s + 1, pl.ds(pl.multiple_of(base, block), block)]).astype(jnp.int32)
        for c in range(span // block):
            cols = slice(c * block, (c + 1) * block)
            delta = positions[s : s + 1, cols] - mine
            dist = jnp.abs(delta)
            far = jnp.full(dist.shape, 8, jnp.int32)
            for mark in bucket_marks:
                far = far + (dist >= mark).astype(jnp.int32)
            bucket = jnp.where(dist < 8, dist, far) + 16 * (delta > 0).astype(jnp.int32)
            i = base + lax.broadcasted_iota(jnp.int32, (block, block), 0)
            j = c * block + lax.broadcasted_iota(jnp.int32, (block, block), 1)
            valid = j < lengths[s]
            buckets[s, 0, :, cols] = jnp.where(valid & (j <= i), bucket, MASKED)
            buckets[s, 1, :, cols] = jnp.where(valid & (j < jnp.maximum(i, 1)), bucket, MASKED)


def head_lanes(rows, half):
    lane = lax.broadcasted_iota(jnp.int32, (rows, 2 * HD), 1)
    return (lane < HD) if half == 0 else (lane >= HD)


def fill_bias(i, biases, buckets, table, block, span):
    s, head = i // H, lax.rem(i, H)
    entry = jnp.broadcast_to(table[pl.ds(head, 1), :], (block, 128))
    for c in range(span // 128):
        cols = slice(c * 128, (c + 1) * 128)
        value = jnp.take_along_axis(entry, buckets[s, 0, :, cols], axis=1, mode="promise_in_bounds")
        biases[i, 0, :, cols] = value
        biases[i, 1, :, cols] = jnp.where(buckets[s, 1, :, cols] == MASKED, -1e30, value)


def attend_pair(i, refs, block, span, low_out):
    attended, query, keys, values, biases = refs
    f32, bf16 = jnp.float32, jnp.bfloat16
    pairs = H // 2
    s, pair = i // pairs, lax.rem(i, pairs)
    lanes = pl.ds(pl.multiple_of(pair * 128, 128), 128)
    q = query[:, s, :, lanes].reshape(2 * block, 128)
    k = keys[s, :, lanes]
    v = values[s, :, lanes]
    outs = []
    for half in range(2):
        mine = head_lanes(2 * block, half)
        one = jnp.where(mine, q * 0.125, 0).astype(bf16)
        scores = dot(one, k, NT) + biases[i * 2 + half].reshape(2 * block, span)
        top = jnp.max(scores, axis=-1, keepdims=True)
        expo = jnp.exp(scores - top)
        low = (expo * (1.0 / jnp.sum(expo, axis=-1, keepdims=True))).astype(bf16)
        low_out[half] = low
        outs.append(dot(low, v))
    mixed = jnp.where(head_lanes(2 * block, 0), outs[0], outs[1]).astype(bf16)
    attended[:, s, :, lanes] = mixed.reshape(2, block, 128)


def center_of(value):
    center = value - jnp.mean(value, axis=-1, keepdims=True)
    var = jnp.mean(center * center, axis=-1, keepdims=True)
    inv = lax.rsqrt(var + 1e-05)
    return center * inv, inv


def norm_back(grad, gain, normed, inv):
    scaled = grad * gain
    return inv * (
        scaled
        - jnp.mean(scaled, axis=-1, keepdims=True)
        - normed * jnp.mean(scaled * normed, axis=-1, keepdims=True)
    )


EARLY = 9
BIAS_FROM = 3
BIAS_STEPS = 6
TILE = 256
LONG = 384
DOWNS = 4


def forward_kernel(
    shards, seqn, seqs, block, span, rows_of,
    lengths, wk, wv, wq, wo, wu, wd, xc, xc_in, xq_in, cot_c_in, cot_q_in, positions, predicted, rel_table,
    bq, bv, bo, g1, b1, c2, g2, b2, c1,
    squares, x_out, probs, attended_out, query_out, keys_out, values_out, y_c, y_q, dr1_out, da_out, grads, downs, dvec,
    full, xall, vall, vectors, keep, attended, table, xc_rows, xq_rows, cot_c, cot_q, io_sem, low_sem, row_sem, *scratch,
):
    f32, bf16 = jnp.float32, jnp.bfloat16
    width = H * HD
    half = seqs * block
    rows = 2 * half
    r = rows_of
    wide = 4 * r
    base = lax.axis_index("seq") * block
    me = lax.axis_index("dp")
    begin, step, whole, pass_x, wait_x, wait_vec, finish = gather_steps(
        shards, seqn, (wk, wv, wq, wo, wu, wd, xc), (full, xall, vall), scratch[: -FRONT_SCRATCH]
    )
    send_front, stage_core, stage_deck, front_sent = reduce_front(shards, r, DOWNS, scratch[-FRONT_SCRATCH:])
    acc = scratch[-FRONT_SCRATCH]
    vall[me] = jnp.zeros(vall.shape[1:], f32)
    for i, piece in enumerate((bq, bv, bo, g1, b1, c2, g2, b2)):
        vall[me, i : i + 1, 0:r] = piece[...].astype(f32)
    vall[me, 8:9, :] = c1[...].astype(f32).reshape(1, wide)
    begin()
    streams = [
        pltpu.make_async_copy(src, dst, row_sem.at[i])
        for i, (src, dst) in enumerate(((xc_in, xc_rows), (xq_in, xq_rows), (cot_c_in, cot_c), (cot_q_in, cot_q)))
    ]
    for copy in streams:
        copy.start()

    def one(n, carry):
        step(n)
        return carry

    def matrix(u):
        return full[pl.ds(u * shards, shards)].reshape(width, width)

    def columns(u, cols):
        size = cols.size
        return full[pl.ds(u * shards, shards), :, cols].reshape(width, size)

    def row_block(u, n):
        per = LONG // r
        return full[pl.ds(u * shards + n * per, per)].reshape(LONG, width)

    def attention(query, keys, values, buckets, low_two, biases):
        fill_buckets(buckets, positions, lengths, base, seqs, block, span)
        eye = (
            lax.broadcasted_iota(jnp.int32, (NB, 128), 0) == lax.broadcasted_iota(jnp.int32, (NB, 128), 1)
        )
        by_head = dot(rel_table[...], jnp.where(eye, 1.0, 0.0).astype(bf16))
        lane = lax.broadcasted_iota(jnp.int32, by_head.shape, 1)
        table[...] = jnp.where(lane < NB, by_head, -1e30)
        for s in range(seqs):
            live = base + lax.broadcasted_iota(jnp.int32, (block, 1), 0) < lengths[s]
            chosen = column_of(predicted[s : s + 1, :])[:, 0:1] > 0
            keep[s * block : (s + 1) * block, :] = jnp.where(live, 1.0, 0.0)
            keep[half + s * block : half + (s + 1) * block, :] = jnp.where(live & chosen, 1.0, 0.0)
        share = seqs * H // BIAS_STEPS

        def one_and_bias(n, carry):
            step(n)

            def bias(k, inner):
                fill_bias((n - BIAS_FROM) * share + k, biases, buckets, table, block, span)
                return inner

            return lax.fori_loop(0, share, bias, carry)

        lax.fori_loop(0, BIAS_FROM, one, 0)
        lax.fori_loop(BIAS_FROM, BIAS_FROM + 3, one_and_bias, 0)
        pass_x()
        lax.fori_loop(BIAS_FROM + 3, BIAS_FROM + BIAS_STEPS, one_and_bias, 0)
        lax.fori_loop(BIAS_FROM + BIAS_STEPS, EARLY, one, 0)
        wait_x()
        wait_vec()
        for copy in streams:
            copy.wait()
        vectors[...] = jnp.zeros_like(vectors)

        def spread(i, carry):
            row = lax.broadcasted_iota(jnp.int32, (r, width), 0)
            col = lax.broadcasted_iota(jnp.int32, (r, width), 1)
            at = jnp.where(col == row + i * r, 1.0, 0.0).astype(bf16)
            vectors[0:8, :] += dot(vall[i, 0:8, 0:r].astype(bf16), at)
            per = width // wide
            row = lax.broadcasted_iota(jnp.int32, (wide, width), 0)
            col = lax.broadcasted_iota(jnp.int32, (wide, width), 1)
            at = jnp.where(col == row + lax.rem(i, per) * wide, 1.0, 0.0).astype(bf16)
            vectors[pl.ds(8 + i // per, 1), :] += dot(vall[i, 8:9, :].astype(bf16), at)
            return carry

        lax.fori_loop(0, shards, spread, 0)
        for u in range(3):
            whole(u)

        def project(k, carry):
            @pl.when(k == 2)
            def _():
                step(EARLY)

            x = xall[k].reshape(half, width)
            at = pl.ds(pl.multiple_of(k * block, block), block)
            keys[:, at, :] = dot(x, matrix(0)).astype(bf16).reshape(seqs, block, width)
            values[:, at, :] = (dot(x, matrix(1)) + vectors[1:2, :]).astype(bf16).reshape(seqs, block, width)
            return carry

        lax.fori_loop(0, seqn, project, 0)
        for t, x in enumerate((xc_rows, xq_rows)):
            query[t] = (dot(x[...], matrix(2)) + vectors[0:1, :]).astype(bf16).reshape(seqs, block, width)
        puts = [
            pltpu.make_async_copy(src, dst, io_sem.at[i])
            for i, (src, dst) in enumerate(((query, query_out), (keys, keys_out), (values, values_out)))
        ]
        for copy in puts:
            copy.start()
        total = seqs * H // 2

        def put(i, slot):
            return pltpu.make_async_copy(low_two.at[slot], probs.at[i], low_sem.at[slot])

        def attend_one(i, carry):
            slot = lax.rem(i, 2)

            @pl.when(lax.rem(i, 3) == 1)
            def _():
                step(EARLY + 1 + i // 3)

            @pl.when(i >= 2)
            def _():
                put(i - 2, slot).wait()

            attend_pair(i, (attended, query, keys, values, biases), block, span, low_two.at[slot])
            put(i, slot).start()
            return carry

        lax.fori_loop(0, total, attend_one, 0)
        put(total - 2, (total - 2) % 2).wait()
        put(total - 1, (total - 1) % 2).wait()
        for copy in puts:
            copy.wait()

    pl.run_scoped(
        attention,
        pltpu.VMEM((2, seqs, block, width), bf16),
        pltpu.VMEM((seqs, span, width), bf16),
        pltpu.VMEM((seqs, span, width), bf16),
        pltpu.VMEM((seqs, 2, block, span), jnp.int32),
        pltpu.VMEM((2, 2, 2 * block, span), bf16),
        pltpu.VMEM((seqs * H, 2, block, span), f32),
    )
    done = EARLY + 1 + seqs * H // 6
    more = [
        pltpu.make_async_copy(full.at[pl.ds(0, 3 * shards)], squares, io_sem.at[3]),
        pltpu.make_async_copy(xall, x_out, io_sem.at[4]),
        pltpu.make_async_copy(attended, attended_out, io_sem.at[5]),
    ]
    for copy in more:
        copy.start()
    dvec[...] = jnp.zeros_like(dvec)
    vec = lambda i: vectors[i : i + 1, :]
    chunk = 128
    chunks = half // chunk

    def ffn(hidden, hidden_low, hidden_turn, normed1, inv1, active, slope, feed, dr2, dr2_low, dr1_low, da, stage, stage_down):
        step(done)
        whole(3)

        def phase_one(c, carry):
            t, s = c // seqs, lax.rem(c, seqs)
            at = pl.ds(pl.multiple_of(c * chunk, chunk), chunk)
            out = dot(attended[t, s], matrix(3)) + vec(2)
            inner = pl.ds(pl.multiple_of(s * chunk, chunk), chunk)
            x = jnp.where(t == 0, xc_rows[inner, :].astype(f32), xq_rows[inner, :].astype(f32))
            normed, inv = center_of(x + out)
            normed1[at, :] = normed
            inv1[at, :] = inv
            h = normed * vec(3) + vec(4)
            hidden[at, :] = h
            hidden_low[at, :] = h.astype(bf16)
            return carry

        lax.fori_loop(0, rows // chunk, phase_one, 0)
        hidden_turn[...] = hidden_low[...].T
        tiles = width // TILE

        def phase_two(j, carry):
            step(done + 1 + j)
            whole(4 + j)

            def tile(n, inner):
                cols = pl.ds(pl.multiple_of(n * TILE, TILE), TILE)
                u = dot(hidden_low[...], columns(4 + j, cols)) + vectors[pl.ds(8 + j, 1), cols]
                cdf = 0.5 * (1.0 + lax.erf(u * (2.0**-0.5)))
                active[j, :, cols] = (u * cdf).astype(bf16)
                slope[j, :, cols] = (cdf + u * (jnp.exp(-0.5 * u * u) * ((2.0 * jnp.pi) ** -0.5))).astype(bf16)
                return inner

            return lax.fori_loop(0, tiles, tile, carry)

        lax.fori_loop(0, 4, phase_two, 0)

        def last(u, carry):
            whole(u)
            return carry

        lax.fori_loop(done + 5, UNITS + shards // 2 + X_LAG + Y_LAG, one, 0)
        lax.fori_loop(8, UNITS, last, 0)

        def phase_feed(n, carry):
            cols = pl.ds(pl.multiple_of(n * TILE, TILE), TILE)
            feed[:, cols] = sum(dot(active[j], columns(8 + j, cols)) for j in range(4))
            return carry

        lax.fori_loop(0, tiles, phase_feed, 0)

        def phase_three(c, carry):
            t, s = c // seqs, lax.rem(c, seqs)
            at = pl.ds(pl.multiple_of(c * chunk, chunk), chunk)
            normed, inv = center_of(hidden[at, :] + feed[at, :] + vec(5))
            kept = keep[at, :]
            feed[at, :] = (normed * vec(6) + vec(7)) * kept
            inner = pl.ds(pl.multiple_of(s * chunk, chunk), chunk)
            cot = jnp.where(t == 0, cot_c[inner, :].astype(f32), cot_q[inner, :].astype(f32)) * kept
            d = norm_back(cot, vec(6), normed, inv)
            dvec[6:7, :] += jnp.sum(cot * normed, axis=0, keepdims=True)
            dvec[7:8, :] += jnp.sum(cot, axis=0, keepdims=True)
            dvec[5:6, :] += jnp.sum(d, axis=0, keepdims=True)
            dr2[at, :] = d
            dr2_low[at, :] = d.astype(bf16)
            return carry

        lax.fori_loop(0, rows // chunk, phase_three, 0)
        y_copies = [
            pltpu.make_async_copy(feed.at[pl.ds(0, half)], y_c, io_sem.at[6]),
            pltpu.make_async_copy(feed.at[pl.ds(half, half)], y_q, io_sem.at[7]),
        ]
        for copy in y_copies:
            copy.start()
        longs = width // LONG

        def phase_down(j, carry):
            grad = dot(active[j], dr2_low[...], TN).astype(bf16)
            stage_down[pl.ds(j * shards, shards)] = grad.reshape(shards, r, width)
            return carry

        lax.fori_loop(0, 4, phase_down, 0)

        def start_down(k, carry):
            send_front(k, lambda shard: stage_down.at[shard * 4 + k])
            return carry

        lax.fori_loop(0, DOWNS, start_down, 0)

        def phase_slope(j, carry):
            du = slope[j].astype(f32) * dot(dr2_low[...], matrix(8 + j), NT)
            dvec[pl.ds(8 + j, 1), :] = jnp.sum(du, axis=0, keepdims=True)
            active[j] = du.astype(bf16)
            stage_core(j)
            return carry

        lax.fori_loop(0, 4, phase_slope, 0)

        def phase_up(j, carry):
            grad = dot(hidden_turn[...], active[j]).astype(bf16)
            stage[1 + j] = grad.reshape(shards, r, width)
            pltpu.make_async_copy(
                stage.at[1 + j], grads.at[pl.ds((1 + j) * shards, shards)], io_sem.at[10 + j]
            ).start()
            return carry

        lax.fori_loop(0, 4, phase_up, 0)

        def put_down(k):
            return pltpu.make_async_copy(acc.at[k], downs.at[k], io_sem.at[14 + k])

        def finish_down(k):
            stage_deck(k)
            put_down(k).start()

        finish_down(0)

        def phase_hidden(n, carry):
            cols = pl.ds(pl.multiple_of(n * LONG, 128), LONG)
            dr2[:, cols] += sum(dot(active[j], row_block(4 + j, n), NT) for j in range(4))
            return carry

        lax.fori_loop(0, longs, phase_hidden, 0)
        for copy in y_copies:
            copy.wait()
        finish_down(1)

        def phase_five(c, carry):
            at = pl.ds(pl.multiple_of(c * chunk, chunk), chunk)
            dh = dr2[at, :]
            normed = normed1[at, :]
            d = norm_back(dh, vec(3), normed, inv1[at, :])
            dvec[3:4, :] += jnp.sum(dh * normed, axis=0, keepdims=True)
            dvec[4:5, :] += jnp.sum(dh, axis=0, keepdims=True)
            dvec[2:3, :] += jnp.sum(d, axis=0, keepdims=True)
            feed[at, :] = d
            low = d.astype(bf16)
            dr1_low[at, :] = low
            da[at, :] = dot(low, matrix(3), NT).astype(bf16)
            return carry

        lax.fori_loop(0, rows // chunk, phase_five, 0)
        finals = [
            pltpu.make_async_copy(feed, dr1_out, io_sem.at[6]),
            pltpu.make_async_copy(da, da_out, io_sem.at[7]),
        ]
        for copy in finals:
            copy.start()
        finish_down(2)
        turned = attended[...].reshape(rows, width).T

        def phase_out(n, carry):
            cols = pl.ds(pl.multiple_of(n * TILE, TILE), TILE)
            grad = dot(hidden_turn[...], dr1_low[:, cols]).astype(bf16)
            stage[0, :, :, cols] = grad.reshape(shards, r, TILE)
            return carry

        hidden_turn[...] = turned
        lax.fori_loop(0, tiles, phase_out, 0)
        out_copy = pltpu.make_async_copy(stage.at[0], grads.at[pl.ds(0, shards)], io_sem.at[9])
        out_copy.start()
        finish_down(3)
        for j in range(4):
            pltpu.make_async_copy(
                stage.at[1 + j], grads.at[pl.ds((1 + j) * shards, shards)], io_sem.at[10 + j]
            ).wait()
            put_down(j).wait()
        out_copy.wait()
        for copy in finals + more:
            copy.wait()
        front_sent()
        finish()

    pl.run_scoped(
        ffn,
        pltpu.VMEM((rows, width), f32),
        pltpu.VMEM((rows, width), bf16),
        pltpu.VMEM((width, rows), bf16),
        pltpu.VMEM((rows, width), f32),
        pltpu.VMEM((rows, 1), f32),
        pltpu.VMEM((4, rows, width), bf16),
        pltpu.VMEM((4, rows, width), bf16),
        pltpu.VMEM((rows, width), f32),
        pltpu.VMEM((rows, width), f32),
        pltpu.VMEM((rows, width), bf16),
        pltpu.VMEM((rows, width), bf16),
        pltpu.VMEM((rows, width), bf16),
        pltpu.VMEM((5, shards, r, width), bf16),
        pltpu.VMEM((4 * shards, r, width), bf16),
    )


def forward(wk, wv, wq, wo, wu, wd, xc, xq, cot_c, cot_q, vecs, lengths, positions, predicted, rel_table, shards, seqn):
    rows_of, width = wq.shape
    seqs, block, _ = xc.shape
    span = positions.shape[1]
    f32, bf16 = jnp.float32, jnp.bfloat16
    steps = seqs * H // 2
    half = seqs * block
    anywhere = pl.BlockSpec(memory_space=pl.ANY)
    vmem = pl.BlockSpec(memory_space=pltpu.VMEM)
    rows = shards // 2
    _, shape = cutter(rows_of)
    dma = pltpu.SemaphoreType.DMA
    flat = lambda a: a.reshape(half, width)
    stream = (2, seqs, block, width)
    return pl.pallas_call(
        functools.partial(forward_kernel, shards, seqn, seqs, block, span, rows_of),
        out_shape=(
            jax.ShapeDtypeStruct((3 * shards, rows_of, width), bf16),
            jax.ShapeDtypeStruct((seqn,) + xc.shape, bf16),
            jax.ShapeDtypeStruct((steps, 2, 2 * block, span), bf16),
            jax.ShapeDtypeStruct(stream, bf16),
            jax.ShapeDtypeStruct(stream, bf16),
            jax.ShapeDtypeStruct((seqs, span, width), bf16),
            jax.ShapeDtypeStruct((seqs, span, width), bf16),
            jax.ShapeDtypeStruct((half, width), f32),
            jax.ShapeDtypeStruct((half, width), f32),
            jax.ShapeDtypeStruct((2 * half, width), f32),
            jax.ShapeDtypeStruct((2 * half, width), bf16),
            jax.ShapeDtypeStruct((5 * shards, rows_of, width), bf16),
            jax.ShapeDtypeStruct((DOWNS, rows, 2) + shape(3), bf16),
            jax.ShapeDtypeStruct((UNITS, width), f32),
        ),
        in_specs=[pl.BlockSpec(memory_space=pltpu.SMEM)] + [anywhere] * 11 + [vmem] * 12,
        out_specs=(anywhere,) * 13 + (vmem,),
        scratch_shapes=[
            pltpu.VMEM((UNITS * shards, rows_of, width), bf16),
            pltpu.VMEM((seqn,) + xc.shape, bf16),
            pltpu.VMEM((shards, 9, 4 * rows_of), f32),
            pltpu.VMEM((UNITS, width), f32),
            pltpu.VMEM((2 * half, 1), f32),
            pltpu.VMEM(stream, bf16),
            pltpu.VMEM((H, 128), f32),
            pltpu.VMEM((half, width), bf16),
            pltpu.VMEM((half, width), bf16),
            pltpu.VMEM((half, width), bf16),
            pltpu.VMEM((half, width), bf16),
            dma((18,)),
            dma((2,)),
            dma((4,)),
        ]
        + gather_scratch(shards)
        + front_scratch(shards, rows_of, DOWNS),
        compiler_params=pltpu.CompilerParams(collective_id=0, has_side_effects=True, vmem_limit_bytes=67043328),
        name="gather_attend_ffn",
    )(
        lengths, wk, wv, wq, wo, wu, wd.reshape(4, rows_of, width), xc, flat(xc), flat(xq), flat(cot_c), flat(cot_q),
        positions, predicted, rel_table.T, *vecs,
    )


def attend_back_pair(i, refs, low, seqs, block, span):
    attended, d_attended, query, keys, values, buckets, dq, dk, dv, ds_sum, sums, counts = refs
    f32, bf16 = jnp.float32, jnp.bfloat16
    pairs = H // 2
    rows = 2 * block
    s, pair = i // pairs, lax.rem(i, pairs)
    lanes = pl.ds(pl.multiple_of(pair * 128, 128), 128)
    q = query[:, s, :, lanes].reshape(rows, 128)
    k = keys[s, :, lanes]
    v = values[s, :, lanes]
    da = d_attended[:, s, :, lanes].reshape(rows, 128)
    product = da.astype(f32) * attended[:, s, :, lanes].reshape(rows, 128).astype(f32)
    d_queries, dk_turn, dv_turn = [], 0.0, 0.0
    for half in range(2):
        mine = head_lanes(rows, half)
        one = jnp.where(mine, da, 0).astype(bf16)
        inner = jnp.sum(jnp.where(mine, product, 0.0), axis=-1, keepdims=True)
        ds = low[half].astype(f32) * (dot(one, v, NT) - inner)
        ds_sum[pair * 2 + half] = (ds[:block] + ds[block:]).astype(bf16)
        ds_low = ds.astype(bf16)
        d_queries.append(dot(ds_low, k))
        dk_turn += dot(jnp.where(mine, q, 0).astype(bf16), ds_low, TN)
        dv_turn += dot(one, low[half], TN)
    d_query = jnp.where(head_lanes(rows, 0), d_queries[0], d_queries[1]) * 0.125
    sums[0:1, lanes] += jnp.sum(d_query, axis=0, keepdims=True)
    dq[:, s, :, lanes] = d_query.reshape(2, block, 128).astype(bf16)
    dk[s, :, lanes] = (dk_turn * 0.125).T.astype(bf16)
    d_value = dv_turn.T
    sums[1:2, lanes] += jnp.sum(d_value, axis=0, keepdims=True)
    dv[s, :, lanes] = d_value.astype(bf16)

    @pl.when(pair == pairs - 1)
    def _():
        def count(g, carry):
            at = pl.ds(pl.multiple_of(g * 16, 16), 16)
            bucket = buckets[s, 0, at, :]
            hot = jnp.concatenate([jnp.where(bucket == n, 1.0, 0.0).astype(bf16) for n in range(NB)], axis=0)
            counts[...] += dot(hot, ds_sum[:, at, :].reshape(H * 16, span), NT)
            return carry

        lax.fori_loop(0, block // 16, count, 0)


def table_of(counts):
    row = lax.broadcasted_iota(jnp.int32, counts.shape, 0)
    col = lax.broadcasted_iota(jnp.int32, counts.shape, 1)
    kept = jnp.where(lax.rem(row, 16) == lax.rem(col, 16), counts, 0.0)
    folded = jnp.sum(kept.reshape(NB, 16, H * 16), axis=1)
    lane = lax.broadcasted_iota(jnp.int32, (H * 16, 128), 1)
    head = lax.broadcasted_iota(jnp.int32, (H * 16, 128), 0) // 16
    return jnp.dot(folded, jnp.where(lane == head, 1.0, 0.0), precision=lax.Precision.HIGHEST)


def backward_kernel(
    shards, seqn, seqs, block, span, rows_of,
    lengths, grads, downs, squares, xall, probs, attended_in, da_in, query_in, keys_in, values_in, dr1_in,
    xc, xq, dvec, positions,
    out, d_content, d_query_x, small_out,
    dq, dk, dv, late, w, x_every, dxs, sums, counts, small, io_sem, low_sem, *scratch,
):
    f32, bf16 = jnp.float32, jnp.bfloat16
    width = H * HD
    half = seqs * block
    total_pairs = seqs * H // 2
    front, scratch = scratch[:FRONT_SCRATCH], scratch[FRONT_SCRATCH:]
    back, scratch = scratch[:BACK_SCRATCH], scratch[BACK_SCRATCH:]
    send_front, stage_core, stage_deck, front_sent = reduce_front(shards, rows_of, UNITS - DOWNS, front)
    send_across, later, back_sent = reduce_back(shards, rows_of, out, back)
    small_first, small_second, small_third, small_last = small_steps(shards, seqn, small, scratch[:SMALL_SCRATCH])
    dx_first, dx_second, dx_third = dx_steps(dxs, scratch[SMALL_SCRATCH:])
    dp, sq = lax.axis_index("dp"), lax.axis_index("seq")
    acc = front[0]
    early = UNITS - DOWNS - 3
    order = lambda k: UNITS - 1 - k
    weights = [pltpu.make_async_copy(squares.at[pl.ds(u * shards, shards)], w.at[u], io_sem.at[5 + u]) for u in range(3)]
    slots = [
        pltpu.make_async_copy(xall.at[k], x_every.at[:, pl.ds(k * block, block)], io_sem.at[8 + k]) for k in range(seqn)
    ]

    def deck_and_across(u):
        stage_deck(u)
        send_across(u, acc.at[u])

    across, line, final, half_stage = later
    ready, late_from_unit = DOWNS, DOWNS + early
    plan = (
        (stage_core, ready, early, 1, 1),
        (across, 0, DOWNS, 6, 3),
        (deck_and_across, ready, early, 9, 3),
        (line, 0, DOWNS, 12, 3),
        (final, 0, DOWNS, 15, 3),
        (stage_core, late_from_unit, 3, 16, 3),
        (half_stage, 0, DOWNS, 18, 3),
        (across, ready, early, 18, 3),
        (deck_and_across, late_from_unit, 3, 21, 3),
        (line, ready, early, 24, 3),
        (final, ready, early, 27, 3),
        (half_stage, ready, early, 30, 3),
        (across, late_from_unit, 3, 30, 3),
        (line, late_from_unit, 3, 36, 3),
        (final, late_from_unit, 3, 40, 3),
        (half_stage, late_from_unit, 3, 43, 3),
    )
    ticks = 50

    def tick(t):
        for stage, first, count, start, gap in plan:
            d = t - start

            @pl.when((d >= 0) & (d < count * gap) & (lax.rem(d, gap) == 0))
            def _(stage=stage, first=first, d=d, gap=gap):
                stage(order(first + d // gap))

    def one(t, carry):
        tick(t)
        return carry

    def attention(attended, d_attended, query, keys, values, buckets, low_two, ds_sum):
        loads = [
            pltpu.make_async_copy(src, dst, io_sem.at[i])
            for i, (src, dst) in enumerate(
                ((attended_in, attended), (da_in, d_attended), (query_in, query), (keys_in, keys), (values_in, values))
            )
        ]

        def take(i, slot):
            return pltpu.make_async_copy(probs.at[i], low_two.at[slot], low_sem.at[slot])

        barrier, count = greet_all(dp, sq, shards, seqn)
        for load in loads:
            load.start()
        take(0, 0).start()
        for load in weights + slots:
            load.start()
        pl.semaphore_wait(barrier, count)

        def send(k, carry):
            u = order(DOWNS + k)
            send_front(u, lambda shard: grads.at[(u - 3) * shards + shard])
            return carry

        def send_down(k, carry):
            send_across(order(k), downs.at[order(k) - 8])
            return carry

        lax.fori_loop(0, early, send, 0)
        lax.fori_loop(0, DOWNS, send_down, 0)
        fill_buckets(buckets, positions, lengths, sq * block, seqs, block, span)
        counts[...] = jnp.zeros_like(counts)
        sums[...] = jnp.zeros_like(sums)
        for load in loads:
            load.wait()
        refs = (attended, d_attended, query, keys, values, buckets, dq, dk, dv, ds_sum, sums, counts)

        def pair(i, carry):
            slot = lax.rem(i, 2)

            tick(i)
            take(i, slot).wait()

            @pl.when(i + 1 < total_pairs)
            def _():
                take(i + 1, 1 - slot).start()

            attend_back_pair(i, refs, low_two.at[slot], seqs, block, span)
            return carry

        lax.fori_loop(0, total_pairs, pair, 0)

    pl.run_scoped(
        attention,
        pltpu.VMEM((2, seqs, block, width), bf16),
        pltpu.VMEM((2, seqs, block, width), bf16),
        pltpu.VMEM((2, seqs, block, width), bf16),
        pltpu.VMEM((seqs, span, width), bf16),
        pltpu.VMEM((seqs, span, width), bf16),
        pltpu.VMEM((seqs, 2, block, span), jnp.int32),
        pltpu.VMEM((2, 2, 2 * block, span), bf16),
        pltpu.VMEM((H, block, span), bf16),
    )

    tile = 256

    def weight_grads(dr1, turned, x_two):
        load = pltpu.make_async_copy(dr1_in, dr1, io_sem.at[0])
        load.start()
        loads = [pltpu.make_async_copy(x, x_two.at[t], io_sem.at[1 + t]) for t, x in enumerate((xc, xq))]
        for copy in loads:
            copy.start()
        for copy in weights + slots:
            copy.wait()
        matrix = lambda u: w[u].reshape(width, width)
        turned[...] = x_every[...].reshape(seqs * span, width).T

        def late_from(u, ref, first_tick):
            def tiles(n, carry):
                tick(first_tick + n)
                cols = pl.ds(pl.multiple_of(n * tile, tile), tile)
                grad = dot(turned[...], ref[:, :, cols].reshape(seqs * span, tile))
                late[u, :, :, cols] = grad.astype(bf16).reshape(shards, rows_of, tile)
                return carry

            lax.fori_loop(0, width // tile, tiles, 0)
            send_front(u, lambda shard: late.at[u, shard])

        for copy in loads:
            copy.wait()

        def tiles(n, carry):
            tick(12 + n)
            cols = pl.ds(pl.multiple_of(n * tile, tile), tile)
            grad = sum(
                dot(x_two[t].reshape(half, width), dq[t, :, :, cols].reshape(half, tile), TN) for t in range(2)
            )
            late[2, :, :, cols] = grad.astype(bf16).reshape(shards, rows_of, tile)
            return carry

        lax.fori_loop(0, width // tile, tiles, 0)
        send_front(2, lambda shard: late.at[2, shard])
        late_from(1, dv, 15)
        late_from(0, dk, 18)

        def every(n, carry):
            tick(21 + n)
            s, k = n // seqn, lax.rem(n, seqn)
            at = pl.ds(pl.multiple_of(k * block, block), block)
            part = dot(dk[s, at, :], matrix(0), NT) + dot(dv[s, at, :], matrix(1), NT)
            dxs[k, pl.ds(pl.multiple_of(s * block, block), block), :] = part.astype(bf16)
            return carry

        lax.fori_loop(0, seqs * seqn, every, 0)
        dx_first()
        load.wait()
        for t, d_x in enumerate((d_content, d_query_x)):
            d_x[...] = dr1[pl.ds(t * half, half), :] + dot(dq[t].reshape(half, width), matrix(2), NT)

    pl.run_scoped(
        weight_grads,
        pltpu.VMEM((2 * half, width), f32),
        pltpu.VMEM((width, seqs * span), bf16),
        pltpu.VMEM((2, seqs, block, width), bf16),
    )
    table = table_of(counts[...])
    vectors = jnp.concatenate([sums[0:2, :], dvec[2:, :], jnp.zeros((4, width), f32)], axis=0)
    pieces = [vectors[:, c * 128 : (c + 1) * 128] for c in range(width // 128)] + [table[:16], table[16:]]
    each = shards // 8
    size = 16 // each
    for p, piece in enumerate(pieces):
        for k in range(each):
            small[p * each + k] = piece[k * size : (k + 1) * size]
    small_first()
    lax.fori_loop(29, 31, one, 0)
    dx_second()
    lax.fori_loop(31, 33, one, 0)
    small_second()
    lax.fori_loop(33, 36, one, 0)
    small_third()
    lax.fori_loop(36, ticks, one, 0)
    dx_third(d_content)
    small_last(small_out)
    front_sent()
    back_sent()


def backward(lengths, grads, downs, squares, xall, probs, attended, d_attended, query, keys, values, dr1, xc, xq, dvec, positions, shards, seqn):
    rows_of, width = squares.shape[1:]
    seqs, block, _ = xc.shape
    span = positions.shape[1]
    f32, bf16 = jnp.float32, jnp.bfloat16
    anywhere = pl.BlockSpec(memory_space=pl.ANY)
    vmem = pl.BlockSpec(memory_space=pltpu.VMEM)
    own = (seqs * block, width)
    small_shape = (shards, 128 // shards, 128)
    dma = pltpu.SemaphoreType.DMA
    return pl.pallas_call(
        functools.partial(backward_kernel, shards, seqn, seqs, block, span, rows_of),
        out_shape=(
            jax.ShapeDtypeStruct((UNITS, rows_of, width), bf16),
            jax.ShapeDtypeStruct(own, f32),
            jax.ShapeDtypeStruct(own, f32),
            jax.ShapeDtypeStruct(small_shape, f32),
        ),
        in_specs=[pl.BlockSpec(memory_space=pltpu.SMEM)] + [anywhere] * 13 + [vmem] * 2,
        out_specs=(vmem,) * 4,
        scratch_shapes=[
            pltpu.VMEM((2, seqs, block, width), bf16),
            pltpu.VMEM((seqs, span, width), bf16),
            pltpu.VMEM((seqs, span, width), bf16),
            pltpu.VMEM((3, shards, rows_of, width), bf16),
            pltpu.VMEM((3, shards, rows_of, width), bf16),
            pltpu.VMEM((seqs, span, width), bf16),
            pltpu.VMEM((seqn,) + own, bf16),
            pltpu.VMEM((8, width), f32),
            pltpu.VMEM((NB * 16, H * 16), f32),
            pltpu.VMEM(small_shape, f32),
            dma((8 + seqn,)),
            dma((2,)),
        ]
        + front_scratch(shards, rows_of, UNITS - DOWNS)
        + back_scratch(shards, rows_of)
        + small_scratch(shards, seqn, small_shape)
        + dx_scratch(own),
        compiler_params=pltpu.CompilerParams(
            collective_id=1, has_side_effects=True, vmem_limit_bytes=67043328
        ),
        name="attend_back_reduce",
    )(lengths, grads, downs, squares, xall, probs, attended, d_attended, query, keys, values, dr1, xc, xq, dvec, positions)


def present_kernel(
    shards, rows_of,
    sums, small, y_c_in, y_q_in, g_c_in, g_q_in,
    y_c, y_q, g_c, g_q, wk, wv, wq, wo, wu, wd, *rest,
):
    vectors, table, wide_rows, low, units, passing, in_sem, out_sem, pass_sem = rest[:9], rest[9], *rest[10:]
    f32 = jnp.float32
    width = H * HD
    r = rows_of
    get = pltpu.make_async_copy(sums, low, in_sem.at[4])
    get.start()
    moves = []
    for i, (src, dst) in enumerate(((y_c_in, y_c), (y_q_in, y_q), (g_c_in, g_c), (g_q_in, g_q))):
        come = pltpu.make_async_copy(src, passing.at[i], in_sem.at[i])
        come.start()
        moves.append((come, pltpu.make_async_copy(passing.at[i], dst, pass_sem.at[i])))
    get.wait()
    pieces = [wk, wv, wq, wo] + [wu.at[:, pl.ds(j * width, width)] for j in range(4)]
    pieces += [wd.at[j] for j in range(4)]
    outs = [pltpu.make_async_copy(units.at[u], piece, out_sem.at[u]) for u, piece in enumerate(pieces)]
    for u, out in enumerate(outs):
        units[u] = low[u].astype(f32)
        out.start()
        if u % 3 == 2:
            come, go = moves[u // 3]
            come.wait()
            go.start()
    me = lax.axis_index("dp")
    whole = jnp.concatenate([small[c] for c in range(width // 128)], axis=1)
    place_of = lax.broadcasted_iota(jnp.int32, (width, r), 0)
    lane = lax.broadcasted_iota(jnp.int32, (width, r), 1)
    mine = jnp.dot(whole, jnp.where(place_of == me * r + lane, 1.0, 0.0), precision=lax.Precision.HIGHEST)
    for i in range(8):
        vectors[i][...] = mine[i]
    per = width // (4 * r)
    place_of = lax.broadcasted_iota(jnp.int32, (width, 4 * r), 0)
    lane = lax.broadcasted_iota(jnp.int32, (width, 4 * r), 1)
    at = jnp.where(place_of == lax.rem(me, per) * (4 * r) + lane, 1.0, 0.0)
    wide_rows[...] = jnp.dot(whole, at, precision=lax.Precision.HIGHEST)
    vectors[8][...] = wide_rows[pl.ds(8 + me // per, 1), :].reshape(4 * r)
    table[...] = jnp.concatenate([small[6], small[7]], axis=0).T[:H, :]
    for out in outs:
        out.wait()
    for come, go in moves:
        go.wait()


def present(sums, small, y_c, y_q, g_c, g_q, shards):
    _, r, width = sums.shape
    f32, bf16 = jnp.float32, jnp.bfloat16
    anywhere = pl.BlockSpec(memory_space=pl.ANY)
    vmem = pl.BlockSpec(memory_space=pltpu.VMEM)
    own = y_c.shape
    shape = lambda *dims: jax.ShapeDtypeStruct(dims, f32)
    dma = pltpu.SemaphoreType.DMA
    return pl.pallas_call(
        functools.partial(present_kernel, shards, r),
        out_shape=(shape(*own),) * 4
        + (shape(r, width),) * 4
        + (shape(r, 4 * width), shape(4, r, width))
        + (shape(r),) * 8
        + (shape(4 * r), shape(H, NB)),
        in_specs=[anywhere, vmem] + [anywhere] * 4,
        out_specs=(anywhere,) * 10 + (vmem,) * 10,
        scratch_shapes=[
            pltpu.VMEM((16, 4 * r), f32),
            pltpu.VMEM((UNITS, r, width), bf16),
            pltpu.VMEM((UNITS, r, width), f32),
            pltpu.VMEM((4,) + own, f32),
            dma((5,)),
            dma((UNITS,)),
            dma((4,)),
        ],
        compiler_params=pltpu.CompilerParams(vmem_limit_bytes=67043328),
        name="present",
    )(sums, small.reshape(8, 16, 128), y_c, y_q, g_c, g_q)


def per_device(
    x_content, x_query, cot_content, cot_query,
    w_query, b_query, w_key, w_value, b_value, w_out, b_out, gain_attn, shift_attn,
    w_up, b_up, w_down, b_down, gain_ffn, shift_ffn, rel_table, lengths, positions, predicted,
    *, shards, seqn,
):
    f32 = jnp.float32
    seqs, block, width = x_content.shape
    r = w_query.shape[0]
    vecs = [
        v.reshape(1, r) for v in (b_query, b_value, b_out, gain_attn, shift_attn, b_down, gain_ffn, shift_ffn)
    ] + [b_up]
    (squares, xall, probs, attended, query, keys, values, y_c, y_q, dr1, d_attended, grads, downs, dvec) = forward(
        w_key, w_value, w_query, w_out, w_up, w_down, x_content, x_query, cot_content, cot_query, vecs,
        lengths, positions, predicted, rel_table, shards, seqn,
    )
    sums, g_content, g_x_query, small = backward(
        lengths, grads, downs, squares, xall, probs, attended, d_attended.reshape(attended.shape),
        query, keys, values, dr1, x_content, x_query, dvec, positions, shards, seqn,
    )
    (
        y_c, y_q, g_content, g_x_query, g_wk, g_wv, g_wq, g_wo, g_w1, g_w2,
        g_bq, g_bv, g_bo, g_g1, g_b1, g_c2, g_g2, g_b2, g_c1, g_table,
    ) = present(sums, small, y_c, y_q, g_content, g_x_query, shards)
    shape = (seqs, block, width)
    return (
        y_c.reshape(shape), y_q.reshape(shape), g_content.reshape(shape), g_x_query.reshape(shape),
        g_wq, g_bq, g_wk, g_wv, g_bv, g_wo, g_bo, g_g1, g_b1,
        g_w1, g_c1, g_w2.reshape(4 * r, width), g_c2, g_g2, g_b2, g_table.T,
    )


def solution(mesh):
    in_specs = (
        P("dp", "seq", None),
        P("dp", "seq", None),
        P("dp", "seq", None),
        P("dp", "seq", None),
        P("dp", None),
        P("dp"),
        P("dp", None),
        P("dp", None),
        P("dp"),
        P("dp", None),
        P("dp"),
        P("dp"),
        P("dp"),
        P("dp", None),
        P("dp"),
        P("dp", None),
        P("dp"),
        P("dp"),
        P("dp"),
        P(),
        P("dp"),
        P("dp", None),
        P("dp", "seq"),
    )
    out_specs = (
        P("dp", "seq", None),
        P("dp", "seq", None),
        P("dp", "seq", None),
        P("dp", "seq", None),
        P("dp", None),
        P("dp"),
        P("dp", None),
        P("dp", None),
        P("dp"),
        P("dp", None),
        P("dp"),
        P("dp"),
        P("dp"),
        P("dp", None),
        P("dp"),
        P("dp", None),
        P("dp"),
        P("dp"),
        P("dp"),
        P(),
    )
    return jax.shard_map(
        functools.partial(per_device, shards=mesh.shape["dp"], seqn=mesh.shape["seq"]),
        mesh=mesh, in_specs=in_specs, out_specs=out_specs, check_vma=False
    )
```

```python
import functools

import jax
import jax.numpy as jnp
from jax import lax
from jax.experimental import pallas as pl
from jax.experimental.pallas import tpu as pltpu
from jax.sharding import PartitionSpec as P

H = 12
HD = 64
NB = 32

MESH = pl.DeviceIdType.MESH
UNITS = 12


def cutter(rows_of):
    by_rows = rows_of % 96 == 0
    piece = rows_of // 6 if by_rows else 128

    def cut(start, size):
        if not isinstance(start, int):
            start = pl.multiple_of(start * piece, 16 if by_rows else 128)
        else:
            start = start * piece
        inner = pl.ds(start, size * piece)
        return (inner, slice(None)) if by_rows else (slice(None), inner)

    def shape(size):
        return (size * piece, 768) if by_rows else (rows_of, size * piece)

    return cut, shape


def place():
    dp, sq = lax.axis_index("dp"), lax.axis_index("seq")
    row, side = dp // 2, dp % 2
    deck, core = sq // 2, sq % 2
    return dp, sq, row, side, deck, core


def tile_of(unit, shard, shards):
    down = unit // 8
    return (1 - down) * (unit * shards + shard) + down * (8 * shards + shard * 4 + unit - 8)


def remote(src, dst, send, recv, device):
    return pltpu.make_async_remote_copy(
        src_ref=src, dst_ref=dst, send_sem=send, recv_sem=recv, device_id=device, device_id_type=MESH
    )


def greet_all(dp, sq, shards, seqn):
    barrier = pltpu.get_barrier_semaphore()

    def greet(step, carry):
        pl.semaphore_signal(barrier, inc=1, device_id=(lax.rem(dp + step, shards), sq), device_id_type=MESH)
        return carry

    def greet_seq(step, carry):
        pl.semaphore_signal(barrier, inc=1, device_id=(dp, lax.rem(sq + step, seqn)), device_id_type=MESH)
        return carry

    lax.fori_loop(1, shards, greet, 0)
    lax.fori_loop(1, seqn, greet_seq, 0)
    return barrier, shards + seqn - 2


AHEAD = 2
X_LAG = 1
Y_LAG = 1


def gather_steps(shards, seqn, ins, outs, scratch):
    wk, wv, wq, wo, wu, wd, xc = ins
    full, xall, vall = outs
    (load_sem, zu_sem, zd_sem, xs_sem, ys_sem, cp_sem, cy_sem,
     zr_sem, xr_sem, yr_sem, cpr_sem, cyr_sem, xc_send, xc_recv, vec_send, vec_recv) = scratch
    dp, sq, row, side, deck, core = place()
    rows = shards // 2
    across = (row * 2 + 1 - side, sq)
    other_deck = (dp, (1 - deck) * 2 + core)
    sibling = (dp, deck * 2 + 1 - core)
    cut, _ = cutter(full.shape[1])
    plane = cut(core * 3 + deck, 2)
    solo = cut(core * 3 + deck * 2, 1)
    theirs = cut(core * 3 + (1 - deck) * 2, 1)

    def many(count, size):
        return full.at[(pl.ds(0, count),) + cut(0, size)]

    def part(unit, shard, piece):
        return full.at[(tile_of(unit, shard, shards),) + piece]

    pieces = [wk, wv, wq, wo] + [wu.at[:, pl.ds(j * 768, 768)] for j in range(4)] + [wd.at[j] for j in range(4)]
    loads = [
        pltpu.make_async_copy(piece, full.at[tile_of(u, dp, shards)], load_sem.at[u]) for u, piece in enumerate(pieces)
    ]
    x_mine = xall.at[sq]
    xload = pltpu.make_async_copy(xc, x_mine, load_sem.at[UNITS])
    x_deck = remote(x_mine, x_mine, xc_send.at[0], xc_recv.at[0], other_deck)
    x_core = remote(x_mine, x_mine, xc_send.at[1], xc_recv.at[1], sibling)
    x_theirs = xall.at[(1 - deck) * 2 + core]
    x_forward = remote(x_theirs, x_theirs, xc_send.at[2], xc_recv.at[2], sibling)

    up = ((row + 1) * 2 + side, sq)
    down = ((row - 1) * 2 + side, sq)

    def along(u, s, src):
        dst = part(u, s * 2 + side, plane)

        @pl.when((s <= row) & (row < rows - 1))
        def _():
            remote(src, dst, zu_sem.at[s], zr_sem.at[u, s], up).start()

        @pl.when((s >= row) & (row > 0))
        def _():
            remote(src, dst, zd_sem.at[s], zr_sem.at[u, s], down).start()

    def send_own(u):
        tile = full.at[tile_of(u, dp, shards)]
        pltpu.make_async_copy(tile, tile, load_sem.at[u]).wait()
        along(u, row, part(u, dp, plane))
        across_own(u)

    def across_own(u):
        ref = part(u, dp, plane)
        remote(ref, ref, xs_sem, xr_sem.at[u], across).start()

    def to_deck(u, shard):
        ref = part(u, shard, solo)
        remote(ref, ref, ys_sem, yr_sem.at[u], other_deck).start()

    def to_core(u, shard):
        ref = part(u, shard, plane)
        remote(ref, ref, cp_sem, cpr_sem.at[u], sibling).start()

    def begin():
        barrier, count = greet_all(dp, sq, shards, seqn)
        for load in loads:
            load.start()
        xload.start()
        pl.semaphore_wait(barrier, count)

        def send_vec(step, carry):
            to = (lax.rem(dp + step, shards), sq)
            remote(vall.at[dp], vall.at[dp], vec_send, vec_recv, to).start()
            return carry

        lax.fori_loop(1, shards, send_vec, 0)

        def first(u, carry):
            send_own(u)
            return carry

        lax.fori_loop(0, AHEAD, first, 0)

        xload.wait()
        x_deck.start()
        x_core.start()

    def step(n):
        @pl.when(n + AHEAD < UNITS)
        def _():
            send_own(n + AHEAD)

        def hop(t, carry):
            u = n - (t - 1)

            def arrived(s):
                ref = part(u, s * 2 + side, plane)
                remote(ref, ref, xs_sem, zr_sem.at[u, s], across).wait_recv()
                along(u, s, ref)
                remote(ref, ref, xs_sem, xr_sem.at[u], across).start()
                to_deck(u, s * 2 + side)
                to_core(u, s * 2 + side)

            @pl.when((u >= 0) & (u < UNITS))
            def _():
                pl.when(row - t >= 0)(lambda: arrived(row - t))
                pl.when(row + t < rows)(lambda: arrived(row + t))

            return carry

        lax.fori_loop(1, rows, hop, 0)
        ux = n - (rows - 1) - X_LAG

        @pl.when((ux >= 0) & (ux < UNITS))
        def _():
            remote(many(rows, 2), many(rows, 2), xs_sem, xr_sem.at[ux], across).wait_recv()

            def pass_on(s, carry):
                to_deck(ux, s * 2 + 1 - side)
                to_core(ux, s * 2 + 1 - side)
                return carry

            lax.fori_loop(0, rows, pass_on, 0)

        uy = n - rows - X_LAG - Y_LAG

        @pl.when((uy >= 0) & (uy < UNITS))
        def _():
            remote(many(shards - 1, 1), many(shards - 1, 1), ys_sem, yr_sem.at[uy], other_deck).wait_recv()

            def pass_on(k, carry):
                ref = part(uy, lax.rem(dp + k, shards), theirs)
                remote(ref, ref, cy_sem, cyr_sem.at[uy], sibling).start()
                return carry

            lax.fori_loop(1, shards, pass_on, 0)

    def pass_x():
        x_deck.wait_recv()
        x_forward.start()

    def wait_x():
        x_core.wait_recv()
        x_forward.wait_recv()

    def wait_vec():
        rest = vall.at[pl.ds(0, shards - 1)]
        remote(rest, rest, vec_send, vec_recv, sibling).wait_recv()

    def whole(u):
        remote(many(shards - 1, 2), many(shards - 1, 2), cp_sem, cpr_sem.at[u], sibling).wait_recv()
        remote(many(shards - 1, 1), many(shards - 1, 1), cy_sem, cyr_sem.at[u], sibling).wait_recv()

    def finish():
        x_deck.wait_send()
        x_core.wait_send()
        x_forward.wait_send()
        rest = vall.at[pl.ds(0, shards - 1)]
        remote(rest, rest, vec_send, vec_recv, sibling).wait_send()
        for count, size, sem in (
            (UNITS * rows, 2, xs_sem),
            (UNITS * (shards - 1), 1, ys_sem),
            (UNITS * (shards - 1), 1, cy_sem),
            (UNITS * (shards - 1), 2, cp_sem),
        ):
            ref = many(count, size)
            remote(ref, ref, sem, xr_sem.at[0], sibling).wait_send()

        def sent(s, carry):
            ref = many(UNITS, 2)

            @pl.when((s <= row) & (row < rows - 1))
            def _():
                remote(ref, ref, zu_sem.at[s], xr_sem.at[0], sibling).wait_send()

            @pl.when((s >= row) & (row > 0))
            def _():
                remote(ref, ref, zd_sem.at[s], xr_sem.at[0], sibling).wait_send()

            return carry

        lax.fori_loop(0, rows, sent, 0)

    return begin, step, whole, pass_x, wait_x, wait_vec, finish


def gather_scratch(shards):
    dma = pltpu.SemaphoreType.DMA
    return [dma((UNITS + 1,))] + [dma((shards // 2,))] * 2 + [dma(())] * 4 + [dma((UNITS, shards // 2))] + [dma((UNITS,))] * 4 + [dma((3,)), dma((3,)), dma(()), dma(())]


GATHER_SCRATCH = 16


def reduce_front(shards, rows_of, count, scratch):
    f32, bf16 = jnp.float32, jnp.bfloat16
    acc, got_core, got_deck, load_sem, core_send, core_recv, deck_send, deck_recv = scratch
    dp, sq, row, side, deck, core = place()
    rows = shards // 2
    other_deck = (dp, (1 - deck) * 2 + core)
    sibling = (dp, deck * 2 + 1 - core)
    cut, _ = cutter(rows_of)
    mine = cut(core * 3, 3)
    siblings = cut((1 - core) * 3, 3)
    solo = cut(deck * 2, 1)
    other_solo = cut((1 - deck) * 2, 1)

    def send(u, tiles):
        def one(s, carry):
            for b in range(2):
                tile = tiles(s * 2 + b)
                remote(tile.at[siblings], got_core.at[u, s, b], core_send.at[u], core_recv.at[u], sibling).start()
                pltpu.make_async_copy(tile.at[mine], acc.at[u, s, b], load_sem.at[u]).start()
            return carry

        lax.fori_loop(0, rows, one, 0)

    def core_copy(u):
        return remote(got_core.at[u], got_core.at[u], core_send.at[u], core_recv.at[u], sibling)

    def deck_copy(u):
        src = acc.at[(u, slice(None), slice(None)) + other_solo]
        return remote(src, got_deck.at[u], deck_send.at[u], deck_recv.at[u], other_deck)

    def stage_core(u):
        pltpu.make_async_copy(acc.at[u], acc.at[u], load_sem.at[u]).wait()
        core_copy(u).wait_recv()

        def add(s, carry):
            for b in range(2):
                acc[u, s, b] = total(acc[u, s, b], got_core[u, s, b])
            return carry

        lax.fori_loop(0, rows, add, 0)
        deck_copy(u).start()

    def stage_deck(u):
        deck_copy(u).wait_recv()

        def add(s, carry):
            for b in range(2):
                at = (u, s, b) + solo
                acc[at] = total(acc[at], got_deck[u, s, b])
            return carry

        lax.fori_loop(0, rows, add, 0)

    def sent():
        def one(u, carry):
            core_copy(u).wait_send()
            deck_copy(u).wait_send()
            return carry

        lax.fori_loop(0, count, one, 0)

    return send, stage_core, stage_deck, sent


def total(left, right):
    return left + right


def front_scratch(shards, rows_of, count):
    bf16 = jnp.bfloat16
    rows = shards // 2
    _, shape = cutter(rows_of)
    return [
        pltpu.VMEM((count, rows, 2) + shape(3), bf16),
        pltpu.VMEM((count, rows, 2) + shape(3), bf16),
        pltpu.VMEM((count, rows, 2) + shape(1), bf16),
    ] + [pltpu.SemaphoreType.DMA((count,))] * 5


FRONT_SCRATCH = 8


def reduce_back(shards, rows_of, out, scratch):
    f32, bf16 = jnp.float32, jnp.bfloat16
    (own_side, got_across, line, got_line, final, got_final, half, got_half,
     side_sem, across_send, across_recv, line_send, line_recv, final_send, final_recv, half_send, half_recv) = scratch
    dp, sq, row, side, deck, core = place()
    rows = shards // 2
    across = (row * 2 + 1 - side, sq)
    other_deck = (dp, (1 - deck) * 2 + core)
    sibling = (dp, deck * 2 + 1 - core)
    cut, _ = cutter(rows_of)
    mine = cut(core * 3, 3)
    siblings = cut((1 - core) * 3, 3)
    plane = cut(deck, 2)
    other_solo = cut((1 - deck) * 2, 1)

    def send_across(u, planes):
        remote(
            planes.at[(slice(None), 1 - side) + plane], got_across.at[u], across_send.at[u], across_recv.at[u], across
        ).start()
        pltpu.make_async_copy(planes.at[(slice(None), side) + plane], own_side.at[u], side_sem.at[u]).start()

    def across_copy(u):
        return remote(got_across.at[u], got_across.at[u], across_send.at[u], across_recv.at[u], across)

    def line_copy(u):
        ref = got_line.at[u, pl.ds(0, rows - 1)]
        return remote(ref, ref, line_send.at[u], line_recv.at[u], across)

    def final_copy(u):
        return remote(final.at[u], got_final.at[u], final_send.at[u], final_recv.at[u], other_deck)

    def half_copy(u):
        return remote(half.at[u], got_half.at[u], half_send.at[u], half_recv.at[u], sibling)

    def stage_across(u):
        pltpu.make_async_copy(own_side.at[u], own_side.at[u], side_sem.at[u]).wait()
        across_copy(u).wait_recv()

        def add(k, carry):
            s = lax.rem(row + k, rows)
            line[u, s] = total(own_side[u, s], got_across[u, s])

            @pl.when(k < rows)
            def _():
                remote(
                    line.at[u, s], got_line.at[u, rows - 1 - k], line_send.at[u], line_recv.at[u], (s * 2 + side, sq)
                ).start()

            return carry

        lax.fori_loop(1, rows + 1, add, 0)

    def stage_line(u):
        line_copy(u).wait_recv()
        summed = line[u, row].astype(f32)
        if rows <= 4:
            for k in range(rows - 1):
                summed = summed + got_line[u, k].astype(f32)
        else:
            summed = lax.fori_loop(0, rows - 1, lambda k, t: t + got_line[u, k].astype(f32), summed)
        final[u] = summed.astype(bf16)
        final_copy(u).start()

    def stage_final(u):
        final_copy(u).wait_recv()
        half[(u,) + plane] = final[u]
        half[(u,) + other_solo] = got_final[(u,) + cut(1 - deck, 1)]
        both = (u,) + cut(1, 1)
        half[both] = total(half[both], got_final[(u,) + cut(deck, 1)])
        half_copy(u).start()

    def stage_half(u):
        half_copy(u).wait_recv()
        out[(u,) + mine] = half[u]
        out[(u,) + siblings] = got_half[u]

    def sent():
        def one(u, carry):
            for copy in (across_copy, line_copy, final_copy, half_copy):
                copy(u).wait_send()
            return carry

        lax.fori_loop(0, UNITS, one, 0)

    return send_across, (stage_across, stage_line, stage_final, stage_half), sent


def back_scratch(shards, rows_of):
    bf16 = jnp.bfloat16
    rows = shards // 2
    _, shape = cutter(rows_of)
    return [pltpu.VMEM((UNITS, rows) + shape(2), bf16)] * 4 + [
        pltpu.VMEM((UNITS,) + shape(2), bf16),
        pltpu.VMEM((UNITS,) + shape(2), bf16),
        pltpu.VMEM((UNITS,) + shape(3), bf16),
        pltpu.VMEM((UNITS,) + shape(3), bf16),
    ] + [pltpu.SemaphoreType.DMA((UNITS,))] * 9


BACK_SCRATCH = 17


def small_steps(shards, seqn, small, scratch):
    got_small, mid_small, got_mid, got_all, small_send, small_recv = scratch
    dp, sq, row, side, deck, core = place()
    sibling = (dp, deck * 2 + 1 - core)

    def small_first():
        got_small[dp] = small[dp]

        def send(k, carry):
            to = lax.rem(dp + k, shards)
            remote(small.at[to], got_small.at[dp], small_send.at[0], small_recv.at[0], (to, sq)).start()
            return carry

        lax.fori_loop(1, shards, send, 0)

    def sum_of(ref, count):
        summed = ref[0]
        for i in range(1, count):
            summed = summed + ref[i]
        return summed

    def small_second():
        rest = got_small.at[pl.ds(0, shards - 1)]
        remote(rest, rest, small_send.at[0], small_recv.at[0], sibling).wait()
        summed = sum_of(got_small, shards)
        mid_small[0] = summed
        got_mid[sq] = summed

        def send(k, carry):
            to = (dp, lax.rem(sq + k, seqn))
            remote(mid_small.at[0], got_mid.at[sq], small_send.at[1], small_recv.at[1], to).start()
            return carry

        lax.fori_loop(1, seqn, send, 0)

    def small_third():
        rest = got_mid.at[pl.ds(0, seqn - 1)]
        remote(rest, rest, small_send.at[1], small_recv.at[1], sibling).wait()
        summed = sum_of(got_mid, seqn)
        mid_small[1] = summed
        got_all[dp] = summed

        def send(k, carry):
            to = (lax.rem(dp + k, shards), sq)
            remote(mid_small.at[1], got_all.at[dp], small_send.at[2], small_recv.at[2], to).start()
            return carry

        lax.fori_loop(1, shards, send, 0)

    def small_last(small_out):
        rest = got_all.at[pl.ds(0, shards - 1)]
        remote(rest, rest, small_send.at[2], small_recv.at[2], sibling).wait()
        small_out[...] = got_all[...]

    return small_first, small_second, small_third, small_last


def small_scratch(shards, seqn, small_shape):
    f32 = jnp.float32
    return [
        pltpu.VMEM(small_shape, f32),
        pltpu.VMEM((2,) + small_shape[1:], f32),
        pltpu.VMEM((seqn,) + small_shape[1:], f32),
        pltpu.VMEM(small_shape, f32),
    ] + [pltpu.SemaphoreType.DMA((3,))] * 2


SMALL_SCRATCH = 6


def dx_steps(dxs, scratch):
    f32, bf16 = jnp.float32, jnp.bfloat16
    dx_own, dx_core, dx_deck, load, send, recv = scratch
    dp, sq, row, side, deck, core = place()
    other_deck = (dp, (1 - deck) * 2 + core)
    sibling = (dp, deck * 2 + 1 - core)
    deck_dx = remote(dx_own.at[1 - deck], dx_deck, send.at[2], recv.at[2], other_deck)

    def first():
        for k in range(2):
            pltpu.make_async_copy(dxs.at[k * 2 + core], dx_own.at[k], load.at[k]).start()
            remote(dxs.at[k * 2 + 1 - core], dx_core.at[k], send.at[k], recv.at[k], sibling).start()

    def second():
        for k in range(2):
            pltpu.make_async_copy(dx_own.at[k], dx_own.at[k], load.at[k]).wait()
            remote(dx_core.at[k], dx_core.at[k], send.at[k], recv.at[k], sibling).wait()
            dx_own[k] = (dx_own[k].astype(f32) + dx_core[k].astype(f32)).astype(bf16)
        deck_dx.start()

    def third(dx_out):
        deck_dx.wait()
        dx_out[...] += dx_own[deck].astype(f32) + dx_deck[...].astype(f32)

    return first, second, third


def dx_scratch(own):
    bf16 = jnp.bfloat16
    dma = pltpu.SemaphoreType.DMA
    return [pltpu.VMEM((2,) + own, bf16), pltpu.VMEM((2,) + own, bf16), pltpu.VMEM(own, bf16), dma((2,)), dma((3,)), dma((3,))]


bucket_marks = (12, 16, 23, 32, 46, 64, 91)
MASKED = NB
TN = (((0,), (0,)), ((), ()))
NT = (((1,), (1,)), ((), ()))


def dot(left, right, dims=None):
    if dims is None:
        dims = (((1,), (0,)), ((), ()))
    return lax.dot_general(left, right, dims, preferred_element_type=jnp.float32)


def column_of(row):
    return jnp.broadcast_to(row.astype(jnp.float32), (row.shape[1], row.shape[1])).T


def fill_buckets(buckets, positions, lengths, base, seqs, block, span):
    for s in range(seqs):
        mine = column_of(positions[s : s + 1, pl.ds(pl.multiple_of(base, block), block)]).astype(jnp.int32)
        for c in range(span // block):
            cols = slice(c * block, (c + 1) * block)
            delta = positions[s : s + 1, cols] - mine
            dist = jnp.abs(delta)
            far = jnp.full(dist.shape, 8, jnp.int32)
            for mark in bucket_marks:
                far = far + (dist >= mark).astype(jnp.int32)
            bucket = jnp.where(dist < 8, dist, far) + 16 * (delta > 0).astype(jnp.int32)
            i = base + lax.broadcasted_iota(jnp.int32, (block, block), 0)
            j = c * block + lax.broadcasted_iota(jnp.int32, (block, block), 1)
            valid = j < lengths[s]
            buckets[s, 0, :, cols] = jnp.where(valid & (j <= i), bucket, MASKED)
            buckets[s, 1, :, cols] = jnp.where(valid & (j < jnp.maximum(i, 1)), bucket, MASKED)


def head_lanes(rows, half):
    lane = lax.broadcasted_iota(jnp.int32, (rows, 2 * HD), 1)
    return (lane < HD) if half == 0 else (lane >= HD)


def fill_bias(i, biases, buckets, table, block, span):
    s, head = i // H, lax.rem(i, H)
    entry = jnp.broadcast_to(table[pl.ds(head, 1), :], (block, 128))
    for c in range(span // 128):
        cols = slice(c * 128, (c + 1) * 128)
        value = jnp.take_along_axis(entry, buckets[s, 0, :, cols], axis=1, mode="promise_in_bounds")
        biases[i, 0, :, cols] = value
        biases[i, 1, :, cols] = jnp.where(buckets[s, 1, :, cols] == MASKED, -1e30, value)


def attend_pair(i, refs, block, span, low_out):
    attended, query, keys, values, biases = refs
    f32, bf16 = jnp.float32, jnp.bfloat16
    pairs = H // 2
    s, pair = i // pairs, lax.rem(i, pairs)
    lanes = pl.ds(pl.multiple_of(pair * 128, 128), 128)
    q = query[:, s, :, lanes].reshape(2 * block, 128)
    k = keys[s, :, lanes]
    v = values[s, :, lanes]
    outs = []
    for half in range(2):
        mine = head_lanes(2 * block, half)
        one = jnp.where(mine, q * 0.125, 0).astype(bf16)
        scores = dot(one, k, NT) + biases[i * 2 + half].reshape(2 * block, span)
        top = jnp.max(scores, axis=-1, keepdims=True)
        expo = jnp.exp(scores - top)
        low = (expo * (1.0 / jnp.sum(expo, axis=-1, keepdims=True))).astype(bf16)
        low_out[half] = low
        outs.append(dot(low, v))
    mixed = jnp.where(head_lanes(2 * block, 0), outs[0], outs[1]).astype(bf16)
    attended[:, s, :, lanes] = mixed.reshape(2, block, 128)


def center_of(value):
    center = value - jnp.mean(value, axis=-1, keepdims=True)
    var = jnp.mean(center * center, axis=-1, keepdims=True)
    inv = lax.rsqrt(var + 1e-05)
    return center * inv, inv


def norm_back(grad, gain, normed, inv):
    scaled = grad * gain
    return inv * (
        scaled
        - jnp.mean(scaled, axis=-1, keepdims=True)
        - normed * jnp.mean(scaled * normed, axis=-1, keepdims=True)
    )


EARLY = 9
BIAS_FROM = 3
BIAS_STEPS = 6
TILE = 256
LONG = 384
DOWNS = 3


def forward_kernel(
    shards, seqn, seqs, block, span, rows_of,
    lengths, wk, wv, wq, wo, wu, wd, xc, xc_in, xq_in, cot_c_in, cot_q_in, positions, predicted, rel_table,
    bq, bv, bo, g1, b1, c2, g2, b2, c1,
    squares, x_out, probs, attended_out, query_out, keys_out, values_out, y_c, y_q, dr1_out, da_out, grads, downs, rest,
    dvec,
    full, xall, vall, vectors, keep, attended, table, xc_rows, xq_rows, cot_c, cot_q, io_sem, low_sem, row_sem, *scratch,
):
    f32, bf16 = jnp.float32, jnp.bfloat16
    width = H * HD
    half = seqs * block
    rows = 2 * half
    r = rows_of
    wide = 4 * r
    base = lax.axis_index("seq") * block
    me = lax.axis_index("dp")
    begin, step, whole, pass_x, wait_x, wait_vec, finish = gather_steps(
        shards, seqn, (wk, wv, wq, wo, wu, wd, xc), (full, xall, vall), scratch[: -FRONT_SCRATCH]
    )
    send_front, stage_core, stage_deck, front_sent = reduce_front(shards, r, DOWNS, scratch[-FRONT_SCRATCH:])
    acc = scratch[-FRONT_SCRATCH]
    vall[me] = jnp.zeros(vall.shape[1:], f32)
    for i, piece in enumerate((bq, bv, bo, g1, b1, c2, g2, b2)):
        vall[me, i : i + 1, 0:r] = piece[...].astype(f32)
    vall[me, 8:9, :] = c1[...].astype(f32).reshape(1, wide)
    begin()
    streams = [
        pltpu.make_async_copy(src, dst, row_sem.at[i])
        for i, (src, dst) in enumerate(((xc_in, xc_rows), (xq_in, xq_rows), (cot_c_in, cot_c), (cot_q_in, cot_q)))
    ]
    for copy in streams:
        copy.start()

    def one(n, carry):
        step(n)
        return carry

    def matrix(u):
        return full[pl.ds(u * shards, shards)].reshape(width, width)

    def columns(u, cols):
        size = cols.size
        return full[pl.ds(u * shards, shards), :, cols].reshape(width, size)

    def row_block(u, n):
        per = LONG // r
        return full[pl.ds(u * shards + n * per, per)].reshape(LONG, width)

    def attention(query, keys, values, buckets, low_two, biases):
        fill_buckets(buckets, positions, lengths, base, seqs, block, span)
        eye = (
            lax.broadcasted_iota(jnp.int32, (NB, 128), 0) == lax.broadcasted_iota(jnp.int32, (NB, 128), 1)
        )
        by_head = dot(rel_table[...], jnp.where(eye, 1.0, 0.0).astype(bf16))
        lane = lax.broadcasted_iota(jnp.int32, by_head.shape, 1)
        table[...] = jnp.where(lane < NB, by_head, -1e30)
        for s in range(seqs):
            live = base + lax.broadcasted_iota(jnp.int32, (block, 1), 0) < lengths[s]
            chosen = column_of(predicted[s : s + 1, :])[:, 0:1] > 0
            keep[s * block : (s + 1) * block, :] = jnp.where(live, 1.0, 0.0)
            keep[half + s * block : half + (s + 1) * block, :] = jnp.where(live & chosen, 1.0, 0.0)
        share = seqs * H // BIAS_STEPS

        def one_and_bias(n, carry):
            step(n)

            def bias(k, inner):
                fill_bias((n - BIAS_FROM) * share + k, biases, buckets, table, block, span)
                return inner

            return lax.fori_loop(0, share, bias, carry)

        lax.fori_loop(0, BIAS_FROM, one, 0)
        lax.fori_loop(BIAS_FROM, BIAS_FROM + 3, one_and_bias, 0)
        pass_x()
        lax.fori_loop(BIAS_FROM + 3, BIAS_FROM + BIAS_STEPS, one_and_bias, 0)
        lax.fori_loop(BIAS_FROM + BIAS_STEPS, EARLY, one, 0)
        wait_x()
        wait_vec()
        for copy in streams:
            copy.wait()
        vectors[...] = jnp.zeros_like(vectors)

        def spread(i, carry):
            row = lax.broadcasted_iota(jnp.int32, (r, width), 0)
            col = lax.broadcasted_iota(jnp.int32, (r, width), 1)
            at = jnp.where(col == row + i * r, 1.0, 0.0).astype(bf16)
            vectors[0:8, :] += dot(vall[i, 0:8, 0:r].astype(bf16), at)
            per = width // wide
            row = lax.broadcasted_iota(jnp.int32, (wide, width), 0)
            col = lax.broadcasted_iota(jnp.int32, (wide, width), 1)
            at = jnp.where(col == row + lax.rem(i, per) * wide, 1.0, 0.0).astype(bf16)
            vectors[pl.ds(8 + i // per, 1), :] += dot(vall[i, 8:9, :].astype(bf16), at)
            return carry

        lax.fori_loop(0, shards, spread, 0)
        for u in range(3):
            whole(u)

        def project(k, carry):
            @pl.when(k == 2)
            def _():
                step(EARLY)

            x = xall[k].reshape(half, width)
            at = pl.ds(pl.multiple_of(k * block, block), block)
            keys[:, at, :] = dot(x, matrix(0)).astype(bf16).reshape(seqs, block, width)
            values[:, at, :] = (dot(x, matrix(1)) + vectors[1:2, :]).astype(bf16).reshape(seqs, block, width)
            return carry

        lax.fori_loop(0, seqn, project, 0)
        for t, x in enumerate((xc_rows, xq_rows)):
            query[t] = (dot(x[...], matrix(2)) + vectors[0:1, :]).astype(bf16).reshape(seqs, block, width)
        puts = [
            pltpu.make_async_copy(src, dst, io_sem.at[i])
            for i, (src, dst) in enumerate(((query, query_out), (keys, keys_out), (values, values_out)))
        ]
        for copy in puts:
            copy.start()
        total = seqs * H // 2

        def put(i, slot):
            return pltpu.make_async_copy(low_two.at[slot], probs.at[i], low_sem.at[slot])

        def attend_one(i, carry):
            slot = lax.rem(i, 2)

            @pl.when(lax.rem(i, 3) == 1)
            def _():
                step(EARLY + 1 + i // 3)

            @pl.when(i >= 2)
            def _():
                put(i - 2, slot).wait()

            attend_pair(i, (attended, query, keys, values, biases), block, span, low_two.at[slot])
            put(i, slot).start()
            return carry

        lax.fori_loop(0, total, attend_one, 0)
        put(total - 2, (total - 2) % 2).wait()
        put(total - 1, (total - 1) % 2).wait()
        for copy in puts:
            copy.wait()

    pl.run_scoped(
        attention,
        pltpu.VMEM((2, seqs, block, width), bf16),
        pltpu.VMEM((seqs, span, width), bf16),
        pltpu.VMEM((seqs, span, width), bf16),
        pltpu.VMEM((seqs, 2, block, span), jnp.int32),
        pltpu.VMEM((2, 2, 2 * block, span), bf16),
        pltpu.VMEM((seqs * H, 2, block, span), f32),
    )
    done = EARLY + 1 + seqs * H // 6
    more = [
        pltpu.make_async_copy(full.at[pl.ds(0, 3 * shards)], squares, io_sem.at[3]),
        pltpu.make_async_copy(xall, x_out, io_sem.at[4]),
        pltpu.make_async_copy(attended, attended_out, io_sem.at[5]),
    ]
    for copy in more:
        copy.start()
    dvec[...] = jnp.zeros_like(dvec)
    vec = lambda i: vectors[i : i + 1, :]
    chunk = 128
    chunks = half // chunk

    def ffn(hidden, hidden_low, hidden_turn, normed1, inv1, active, slope, feed, dr2, dr2_low, dr1_low, da, stage, stage_down):
        step(done)
        whole(3)

        def phase_one(c, carry):
            t, s = c // seqs, lax.rem(c, seqs)
            at = pl.ds(pl.multiple_of(c * chunk, chunk), chunk)
            out = dot(attended[t, s], matrix(3)) + vec(2)
            inner = pl.ds(pl.multiple_of(s * chunk, chunk), chunk)
            x = jnp.where(t == 0, xc_rows[inner, :].astype(f32), xq_rows[inner, :].astype(f32))
            normed, inv = center_of(x + out)
            normed1[at, :] = normed
            inv1[at, :] = inv
            h = normed * vec(3) + vec(4)
            hidden[at, :] = h
            hidden_low[at, :] = h.astype(bf16)
            return carry

        lax.fori_loop(0, rows // chunk, phase_one, 0)
        hidden_turn[...] = hidden_low[...].T
        tiles = width // TILE

        def phase_two(j, carry):
            step(done + 1 + j)
            whole(4 + j)

            def tile(n, inner):
                cols = pl.ds(pl.multiple_of(n * TILE, TILE), TILE)
                u = dot(hidden_low[...], columns(4 + j, cols)) + vectors[pl.ds(8 + j, 1), cols]
                cdf = 0.5 * (1.0 + lax.erf(u * (2.0**-0.5)))
                active[j, :, cols] = (u * cdf).astype(bf16)
                slope[j, :, cols] = (cdf + u * (jnp.exp(-0.5 * u * u) * ((2.0 * jnp.pi) ** -0.5))).astype(bf16)
                return inner

            return lax.fori_loop(0, tiles, tile, carry)

        lax.fori_loop(0, 4, phase_two, 0)

        def last(u, carry):
            whole(u)
            return carry

        lax.fori_loop(done + 5, UNITS + shards // 2 + X_LAG + Y_LAG, one, 0)
        lax.fori_loop(8, UNITS, last, 0)

        def phase_feed(n, carry):
            cols = pl.ds(pl.multiple_of(n * TILE, TILE), TILE)
            feed[:, cols] = sum(dot(active[j], columns(8 + j, cols)) for j in range(4))
            return carry

        lax.fori_loop(0, tiles, phase_feed, 0)

        def phase_three(c, carry):
            t, s = c // seqs, lax.rem(c, seqs)
            at = pl.ds(pl.multiple_of(c * chunk, chunk), chunk)
            normed, inv = center_of(hidden[at, :] + feed[at, :] + vec(5))
            kept = keep[at, :]
            feed[at, :] = (normed * vec(6) + vec(7)) * kept
            inner = pl.ds(pl.multiple_of(s * chunk, chunk), chunk)
            cot = jnp.where(t == 0, cot_c[inner, :].astype(f32), cot_q[inner, :].astype(f32)) * kept
            d = norm_back(cot, vec(6), normed, inv)
            dvec[6:7, :] += jnp.sum(cot * normed, axis=0, keepdims=True)
            dvec[7:8, :] += jnp.sum(cot, axis=0, keepdims=True)
            dvec[5:6, :] += jnp.sum(d, axis=0, keepdims=True)
            dr2[at, :] = d
            dr2_low[at, :] = d.astype(bf16)
            return carry

        lax.fori_loop(0, rows // chunk, phase_three, 0)
        y_copies = [
            pltpu.make_async_copy(feed.at[pl.ds(0, half)], y_c, io_sem.at[6]),
            pltpu.make_async_copy(feed.at[pl.ds(half, half)], y_q, io_sem.at[7]),
        ]
        for copy in y_copies:
            copy.start()
        longs = width // LONG

        def phase_down(j, carry):
            grad = dot(active[j], dr2_low[...], TN).astype(bf16)
            stage_down[pl.ds(j * shards, shards)] = grad.reshape(shards, r, width)
            return carry

        lax.fori_loop(0, 4, phase_down, 0)

        def start_down(k, carry):
            send_front(k, lambda shard: stage_down.at[shard * 4 + 4 - DOWNS + k])
            return carry

        lax.fori_loop(0, DOWNS, start_down, 0)
        rest_copy = pltpu.make_async_copy(stage_down, rest, io_sem.at[8])
        rest_copy.start()

        def phase_slope(j, carry):
            du = slope[j].astype(f32) * dot(dr2_low[...], matrix(8 + j), NT)
            dvec[pl.ds(8 + j, 1), :] = jnp.sum(du, axis=0, keepdims=True)
            active[j] = du.astype(bf16)
            pl.when(j < DOWNS)(lambda: stage_core(j))
            return carry

        lax.fori_loop(0, 4, phase_slope, 0)

        def phase_up(j, carry):
            grad = dot(hidden_turn[...], active[j]).astype(bf16)
            stage[1 + j] = grad.reshape(shards, r, width)
            pltpu.make_async_copy(
                stage.at[1 + j], grads.at[pl.ds((1 + j) * shards, shards)], io_sem.at[10 + j]
            ).start()
            return carry

        lax.fori_loop(0, 4, phase_up, 0)

        def put_down(k):
            return pltpu.make_async_copy(acc.at[k], downs.at[k], io_sem.at[14 + k])

        def finish_down(k):
            stage_deck(k)
            put_down(k).start()

        def phase_hidden(n, carry):
            cols = pl.ds(pl.multiple_of(n * LONG, 128), LONG)
            dr2[:, cols] += sum(dot(active[j], row_block(4 + j, n), NT) for j in range(4))
            return carry

        lax.fori_loop(0, longs, phase_hidden, 0)
        for copy in y_copies:
            copy.wait()
        finish_down(0)

        def phase_five(c, carry):
            at = pl.ds(pl.multiple_of(c * chunk, chunk), chunk)
            dh = dr2[at, :]
            normed = normed1[at, :]
            d = norm_back(dh, vec(3), normed, inv1[at, :])
            dvec[3:4, :] += jnp.sum(dh * normed, axis=0, keepdims=True)
            dvec[4:5, :] += jnp.sum(dh, axis=0, keepdims=True)
            dvec[2:3, :] += jnp.sum(d, axis=0, keepdims=True)
            feed[at, :] = d
            low = d.astype(bf16)
            dr1_low[at, :] = low
            da[at, :] = dot(low, matrix(3), NT).astype(bf16)
            return carry

        lax.fori_loop(0, rows // chunk, phase_five, 0)
        finals = [
            pltpu.make_async_copy(feed, dr1_out, io_sem.at[6]),
            pltpu.make_async_copy(da, da_out, io_sem.at[7]),
        ]
        for copy in finals:
            copy.start()
        for k in range(1, DOWNS - 1):
            finish_down(k)
        turned = attended[...].reshape(rows, width).T

        def phase_out(n, carry):
            cols = pl.ds(pl.multiple_of(n * TILE, TILE), TILE)
            grad = dot(hidden_turn[...], dr1_low[:, cols]).astype(bf16)
            stage[0, :, :, cols] = grad.reshape(shards, r, TILE)
            return carry

        hidden_turn[...] = turned
        lax.fori_loop(0, tiles, phase_out, 0)
        out_copy = pltpu.make_async_copy(stage.at[0], grads.at[pl.ds(0, shards)], io_sem.at[9])
        out_copy.start()
        finish_down(DOWNS - 1)
        for j in range(4):
            pltpu.make_async_copy(
                stage.at[1 + j], grads.at[pl.ds((1 + j) * shards, shards)], io_sem.at[10 + j]
            ).wait()
        for k in range(DOWNS):
            put_down(k).wait()
        rest_copy.wait()
        out_copy.wait()
        for copy in finals + more:
            copy.wait()
        front_sent()
        finish()

    pl.run_scoped(
        ffn,
        pltpu.VMEM((rows, width), f32),
        pltpu.VMEM((rows, width), bf16),
        pltpu.VMEM((width, rows), bf16),
        pltpu.VMEM((rows, width), f32),
        pltpu.VMEM((rows, 1), f32),
        pltpu.VMEM((4, rows, width), bf16),
        pltpu.VMEM((4, rows, width), bf16),
        pltpu.VMEM((rows, width), f32),
        pltpu.VMEM((rows, width), f32),
        pltpu.VMEM((rows, width), bf16),
        pltpu.VMEM((rows, width), bf16),
        pltpu.VMEM((rows, width), bf16),
        pltpu.VMEM((5, shards, r, width), bf16),
        pltpu.VMEM((4 * shards, r, width), bf16),
    )


def forward(wk, wv, wq, wo, wu, wd, xc, xq, cot_c, cot_q, vecs, lengths, positions, predicted, rel_table, shards, seqn):
    rows_of, width = wq.shape
    seqs, block, _ = xc.shape
    span = positions.shape[1]
    f32, bf16 = jnp.float32, jnp.bfloat16
    steps = seqs * H // 2
    half = seqs * block
    anywhere = pl.BlockSpec(memory_space=pl.ANY)
    vmem = pl.BlockSpec(memory_space=pltpu.VMEM)
    rows = shards // 2
    _, shape = cutter(rows_of)
    dma = pltpu.SemaphoreType.DMA
    flat = lambda a: a.reshape(half, width)
    stream = (2, seqs, block, width)
    return pl.pallas_call(
        functools.partial(forward_kernel, shards, seqn, seqs, block, span, rows_of),
        out_shape=(
            jax.ShapeDtypeStruct((3 * shards, rows_of, width), bf16),
            jax.ShapeDtypeStruct((seqn,) + xc.shape, bf16),
            jax.ShapeDtypeStruct((steps, 2, 2 * block, span), bf16),
            jax.ShapeDtypeStruct(stream, bf16),
            jax.ShapeDtypeStruct(stream, bf16),
            jax.ShapeDtypeStruct((seqs, span, width), bf16),
            jax.ShapeDtypeStruct((seqs, span, width), bf16),
            jax.ShapeDtypeStruct((half, width), f32),
            jax.ShapeDtypeStruct((half, width), f32),
            jax.ShapeDtypeStruct((2 * half, width), f32),
            jax.ShapeDtypeStruct((2 * half, width), bf16),
            jax.ShapeDtypeStruct((5 * shards, rows_of, width), bf16),
            jax.ShapeDtypeStruct((DOWNS, rows, 2) + shape(3), bf16),
            jax.ShapeDtypeStruct((4 * shards, rows_of, width), bf16),
            jax.ShapeDtypeStruct((UNITS, width), f32),
        ),
        in_specs=[pl.BlockSpec(memory_space=pltpu.SMEM)] + [anywhere] * 11 + [vmem] * 12,
        out_specs=(anywhere,) * 14 + (vmem,),
        scratch_shapes=[
            pltpu.VMEM((UNITS * shards, rows_of, width), bf16),
            pltpu.VMEM((seqn,) + xc.shape, bf16),
            pltpu.VMEM((shards, 9, 4 * rows_of), f32),
            pltpu.VMEM((UNITS, width), f32),
            pltpu.VMEM((2 * half, 1), f32),
            pltpu.VMEM(stream, bf16),
            pltpu.VMEM((H, 128), f32),
            pltpu.VMEM((half, width), bf16),
            pltpu.VMEM((half, width), bf16),
            pltpu.VMEM((half, width), bf16),
            pltpu.VMEM((half, width), bf16),
            dma((18,)),
            dma((2,)),
            dma((4,)),
        ]
        + gather_scratch(shards)
        + front_scratch(shards, rows_of, DOWNS),
        compiler_params=pltpu.CompilerParams(collective_id=0, has_side_effects=True, vmem_limit_bytes=67043328),
        name="gather_attend_ffn",
    )(
        lengths, wk, wv, wq, wo, wu, wd.reshape(4, rows_of, width), xc, flat(xc), flat(xq), flat(cot_c), flat(cot_q),
        positions, predicted, rel_table.T, *vecs,
    )


def attend_back_pair(i, refs, low, seqs, block, span):
    attended, d_attended, query, keys, values, buckets, dq, dk, dv, ds_sum, sums, counts = refs
    f32, bf16 = jnp.float32, jnp.bfloat16
    pairs = H // 2
    rows = 2 * block
    s, pair = i // pairs, lax.rem(i, pairs)
    lanes = pl.ds(pl.multiple_of(pair * 128, 128), 128)
    q = query[:, s, :, lanes].reshape(rows, 128)
    k = keys[s, :, lanes]
    v = values[s, :, lanes]
    da = d_attended[:, s, :, lanes].reshape(rows, 128)
    product = da.astype(f32) * attended[:, s, :, lanes].reshape(rows, 128).astype(f32)
    d_queries, dk_turn, dv_turn = [], 0.0, 0.0
    for half in range(2):
        mine = head_lanes(rows, half)
        one = jnp.where(mine, da, 0).astype(bf16)
        inner = jnp.sum(jnp.where(mine, product, 0.0), axis=-1, keepdims=True)
        ds = low[half].astype(f32) * (dot(one, v, NT) - inner)
        ds_sum[pair * 2 + half] = (ds[:block] + ds[block:]).astype(bf16)
        ds_low = ds.astype(bf16)
        d_queries.append(dot(ds_low, k))
        dk_turn += dot(jnp.where(mine, q, 0).astype(bf16), ds_low, TN)
        dv_turn += dot(one, low[half], TN)
    d_query = jnp.where(head_lanes(rows, 0), d_queries[0], d_queries[1]) * 0.125
    sums[0:1, lanes] += jnp.sum(d_query, axis=0, keepdims=True)
    dq[:, s, :, lanes] = d_query.reshape(2, block, 128).astype(bf16)
    dk[s, :, lanes] = (dk_turn * 0.125).T.astype(bf16)
    d_value = dv_turn.T
    sums[1:2, lanes] += jnp.sum(d_value, axis=0, keepdims=True)
    dv[s, :, lanes] = d_value.astype(bf16)

    @pl.when(pair == pairs - 1)
    def _():
        def count(g, carry):
            at = pl.ds(pl.multiple_of(g * 16, 16), 16)
            bucket = buckets[s, 0, at, :]
            hot = jnp.concatenate([jnp.where(bucket == n, 1.0, 0.0).astype(bf16) for n in range(NB)], axis=0)
            counts[...] += dot(hot, ds_sum[:, at, :].reshape(H * 16, span), NT)
            return carry

        lax.fori_loop(0, block // 16, count, 0)


def table_of(counts):
    row = lax.broadcasted_iota(jnp.int32, counts.shape, 0)
    col = lax.broadcasted_iota(jnp.int32, counts.shape, 1)
    kept = jnp.where(lax.rem(row, 16) == lax.rem(col, 16), counts, 0.0)
    folded = jnp.sum(kept.reshape(NB, 16, H * 16), axis=1)
    lane = lax.broadcasted_iota(jnp.int32, (H * 16, 128), 1)
    head = lax.broadcasted_iota(jnp.int32, (H * 16, 128), 0) // 16
    return jnp.dot(folded, jnp.where(lane == head, 1.0, 0.0), precision=lax.Precision.HIGHEST)


def backward_kernel(
    shards, seqn, seqs, block, span, rows_of,
    lengths, grads, downs, rest, squares, xall, probs, attended_in, da_in, query_in, keys_in, values_in, dr1_in,
    xc, xq, dvec, positions,
    out, d_content, d_query_x, small_out,
    dq, dk, dv, late, w, x_every, dxs, sums, counts, small, io_sem, low_sem, *scratch,
):
    f32, bf16 = jnp.float32, jnp.bfloat16
    width = H * HD
    half = seqs * block
    total_pairs = seqs * H // 2
    front, scratch = scratch[:FRONT_SCRATCH], scratch[FRONT_SCRATCH:]
    back, scratch = scratch[:BACK_SCRATCH], scratch[BACK_SCRATCH:]
    send_front, stage_core, stage_deck, front_sent = reduce_front(shards, rows_of, UNITS - DOWNS, front)
    send_across, later, back_sent = reduce_back(shards, rows_of, out, back)
    small_first, small_second, small_third, small_last = small_steps(shards, seqn, small, scratch[:SMALL_SCRATCH])
    dx_first, dx_second, dx_third = dx_steps(dxs, scratch[SMALL_SCRATCH:])
    dp, sq = lax.axis_index("dp"), lax.axis_index("seq")
    acc = front[0]
    early = UNITS - DOWNS - 3
    order = lambda k: UNITS - 1 - k
    weights = [pltpu.make_async_copy(squares.at[pl.ds(u * shards, shards)], w.at[u], io_sem.at[5 + u]) for u in range(3)]
    slots = [
        pltpu.make_async_copy(xall.at[k], x_every.at[:, pl.ds(k * block, block)], io_sem.at[8 + k]) for k in range(seqn)
    ]

    def deck_and_across(u):
        stage_deck(u)
        send_across(u, acc.at[u])

    across, line, final, half_stage = later
    ready, late_from_unit = DOWNS, DOWNS + early
    plan = (
        (stage_core, ready, early, 1, 1),
        (across, 0, DOWNS, 6, 3),
        (deck_and_across, ready, early, 9, 3),
        (line, 0, DOWNS, 12, 3),
        (final, 0, DOWNS, 15, 3),
        (stage_core, late_from_unit, 3, 16, 3),
        (half_stage, 0, DOWNS, 18, 3),
        (across, ready, early, 18, 3),
        (deck_and_across, late_from_unit, 3, 21, 3),
        (line, ready, early, 24, 3),
        (final, ready, early, 27, 3),
        (half_stage, ready, early, 30, 3),
        (across, late_from_unit, 3, 30, 3),
        (line, late_from_unit, 3, 36, 3),
        (final, late_from_unit, 3, 40, 3),
        (half_stage, late_from_unit, 3, 43, 3),
    )
    ticks = 50

    def tick(t):
        for stage, first, count, start, gap in plan:
            d = t - start

            @pl.when((d >= 0) & (d < count * gap) & (lax.rem(d, gap) == 0))
            def _(stage=stage, first=first, d=d, gap=gap):
                stage(order(first + d // gap))

    def one(t, carry):
        tick(t)
        return carry

    def attention(attended, d_attended, query, keys, values, buckets, low_two, ds_sum):
        loads = [
            pltpu.make_async_copy(src, dst, io_sem.at[i])
            for i, (src, dst) in enumerate(
                ((attended_in, attended), (da_in, d_attended), (query_in, query), (keys_in, keys), (values_in, values))
            )
        ]

        def take(i, slot):
            return pltpu.make_async_copy(probs.at[i], low_two.at[slot], low_sem.at[slot])

        barrier, count = greet_all(dp, sq, shards, seqn)
        for load in loads:
            load.start()
        take(0, 0).start()
        for load in weights + slots:
            load.start()
        pl.semaphore_wait(barrier, count)

        def send_rest(k, carry):
            u = order(DOWNS + k)
            send_front(u, lambda shard: rest.at[shard * 4 + u - 8])
            return carry

        def send(k, carry):
            u = order(4 + k)
            send_front(u, lambda shard: grads.at[(u - 3) * shards + shard])
            return carry

        def send_down(k, carry):
            send_across(order(k), downs.at[order(k) - (UNITS - DOWNS)])
            return carry

        lax.fori_loop(0, 4 - DOWNS, send_rest, 0)
        lax.fori_loop(0, 5, send, 0)
        lax.fori_loop(0, DOWNS, send_down, 0)
        fill_buckets(buckets, positions, lengths, sq * block, seqs, block, span)
        counts[...] = jnp.zeros_like(counts)
        sums[...] = jnp.zeros_like(sums)
        for load in loads:
            load.wait()
        refs = (attended, d_attended, query, keys, values, buckets, dq, dk, dv, ds_sum, sums, counts)

        def pair(i, carry):
            slot = lax.rem(i, 2)

            tick(i)
            take(i, slot).wait()

            @pl.when(i + 1 < total_pairs)
            def _():
                take(i + 1, 1 - slot).start()

            attend_back_pair(i, refs, low_two.at[slot], seqs, block, span)
            return carry

        lax.fori_loop(0, total_pairs, pair, 0)

    pl.run_scoped(
        attention,
        pltpu.VMEM((2, seqs, block, width), bf16),
        pltpu.VMEM((2, seqs, block, width), bf16),
        pltpu.VMEM((2, seqs, block, width), bf16),
        pltpu.VMEM((seqs, span, width), bf16),
        pltpu.VMEM((seqs, span, width), bf16),
        pltpu.VMEM((seqs, 2, block, span), jnp.int32),
        pltpu.VMEM((2, 2, 2 * block, span), bf16),
        pltpu.VMEM((H, block, span), bf16),
    )

    tile = 256

    def weight_grads(dr1, turned, x_two):
        load = pltpu.make_async_copy(dr1_in, dr1, io_sem.at[0])
        load.start()
        loads = [pltpu.make_async_copy(x, x_two.at[t], io_sem.at[1 + t]) for t, x in enumerate((xc, xq))]
        for copy in loads:
            copy.start()
        for copy in weights + slots:
            copy.wait()
        matrix = lambda u: w[u].reshape(width, width)
        turned[...] = x_every[...].reshape(seqs * span, width).T

        def late_from(u, ref, first_tick):
            def tiles(n, carry):
                tick(first_tick + n)
                cols = pl.ds(pl.multiple_of(n * tile, tile), tile)
                grad = dot(turned[...], ref[:, :, cols].reshape(seqs * span, tile))
                late[u, :, :, cols] = grad.astype(bf16).reshape(shards, rows_of, tile)
                return carry

            lax.fori_loop(0, width // tile, tiles, 0)
            send_front(u, lambda shard: late.at[u, shard])

        for copy in loads:
            copy.wait()

        def tiles(n, carry):
            tick(12 + n)
            cols = pl.ds(pl.multiple_of(n * tile, tile), tile)
            grad = sum(
                dot(x_two[t].reshape(half, width), dq[t, :, :, cols].reshape(half, tile), TN) for t in range(2)
            )
            late[2, :, :, cols] = grad.astype(bf16).reshape(shards, rows_of, tile)
            return carry

        lax.fori_loop(0, width // tile, tiles, 0)
        send_front(2, lambda shard: late.at[2, shard])
        late_from(1, dv, 15)
        late_from(0, dk, 18)

        def every(n, carry):
            tick(21 + n)
            s, k = n // seqn, lax.rem(n, seqn)
            at = pl.ds(pl.multiple_of(k * block, block), block)
            part = dot(dk[s, at, :], matrix(0), NT) + dot(dv[s, at, :], matrix(1), NT)
            dxs[k, pl.ds(pl.multiple_of(s * block, block), block), :] = part.astype(bf16)
            return carry

        lax.fori_loop(0, seqs * seqn, every, 0)
        dx_first()
        load.wait()
        for t, d_x in enumerate((d_content, d_query_x)):
            d_x[...] = dr1[pl.ds(t * half, half), :] + dot(dq[t].reshape(half, width), matrix(2), NT)

    pl.run_scoped(
        weight_grads,
        pltpu.VMEM((2 * half, width), f32),
        pltpu.VMEM((width, seqs * span), bf16),
        pltpu.VMEM((2, seqs, block, width), bf16),
    )
    table = table_of(counts[...])
    vectors = jnp.concatenate([sums[0:2, :], dvec[2:, :], jnp.zeros((4, width), f32)], axis=0)
    pieces = [vectors[:, c * 128 : (c + 1) * 128] for c in range(width // 128)] + [table[:16], table[16:]]
    each = shards // 8
    size = 16 // each
    for p, piece in enumerate(pieces):
        for k in range(each):
            small[p * each + k] = piece[k * size : (k + 1) * size]
    small_first()
    lax.fori_loop(29, 31, one, 0)
    dx_second()
    lax.fori_loop(31, 33, one, 0)
    small_second()
    lax.fori_loop(33, 36, one, 0)
    small_third()
    lax.fori_loop(36, ticks, one, 0)
    dx_third(d_content)
    small_last(small_out)
    front_sent()
    back_sent()


def backward(lengths, grads, downs, rest, squares, xall, probs, attended, d_attended, query, keys, values, dr1, xc, xq, dvec, positions, shards, seqn):
    rows_of, width = squares.shape[1:]
    seqs, block, _ = xc.shape
    span = positions.shape[1]
    f32, bf16 = jnp.float32, jnp.bfloat16
    anywhere = pl.BlockSpec(memory_space=pl.ANY)
    vmem = pl.BlockSpec(memory_space=pltpu.VMEM)
    own = (seqs * block, width)
    small_shape = (shards, 128 // shards, 128)
    dma = pltpu.SemaphoreType.DMA
    return pl.pallas_call(
        functools.partial(backward_kernel, shards, seqn, seqs, block, span, rows_of),
        out_shape=(
            jax.ShapeDtypeStruct((UNITS, rows_of, width), bf16),
            jax.ShapeDtypeStruct(own, f32),
            jax.ShapeDtypeStruct(own, f32),
            jax.ShapeDtypeStruct(small_shape, f32),
        ),
        in_specs=[pl.BlockSpec(memory_space=pltpu.SMEM)] + [anywhere] * 14 + [vmem] * 2,
        out_specs=(vmem,) * 4,
        scratch_shapes=[
            pltpu.VMEM((2, seqs, block, width), bf16),
            pltpu.VMEM((seqs, span, width), bf16),
            pltpu.VMEM((seqs, span, width), bf16),
            pltpu.VMEM((3, shards, rows_of, width), bf16),
            pltpu.VMEM((3, shards, rows_of, width), bf16),
            pltpu.VMEM((seqs, span, width), bf16),
            pltpu.VMEM((seqn,) + own, bf16),
            pltpu.VMEM((8, width), f32),
            pltpu.VMEM((NB * 16, H * 16), f32),
            pltpu.VMEM(small_shape, f32),
            dma((8 + seqn,)),
            dma((2,)),
        ]
        + front_scratch(shards, rows_of, UNITS - DOWNS)
        + back_scratch(shards, rows_of)
        + small_scratch(shards, seqn, small_shape)
        + dx_scratch(own),
        compiler_params=pltpu.CompilerParams(
            collective_id=1, has_side_effects=True, vmem_limit_bytes=67043328
        ),
        name="attend_back_reduce",
    )(lengths, grads, downs, rest, squares, xall, probs, attended, d_attended, query, keys, values, dr1, xc, xq, dvec, positions)


def present_kernel(
    shards, rows_of,
    sums, small, y_c_in, y_q_in, g_c_in, g_q_in,
    y_c, y_q, g_c, g_q, wk, wv, wq, wo, wu, wd, *rest,
):
    vectors, table, wide_rows, low, units, passing, in_sem, out_sem, pass_sem = rest[:9], rest[9], *rest[10:]
    f32 = jnp.float32
    width = H * HD
    r = rows_of
    get = pltpu.make_async_copy(sums, low, in_sem.at[4])
    get.start()
    moves = []
    for i, (src, dst) in enumerate(((y_c_in, y_c), (y_q_in, y_q), (g_c_in, g_c), (g_q_in, g_q))):
        come = pltpu.make_async_copy(src, passing.at[i], in_sem.at[i])
        come.start()
        moves.append((come, pltpu.make_async_copy(passing.at[i], dst, pass_sem.at[i])))
    get.wait()
    pieces = [wk, wv, wq, wo] + [wu.at[:, pl.ds(j * width, width)] for j in range(4)]
    pieces += [wd.at[j] for j in range(4)]
    outs = [pltpu.make_async_copy(units.at[u], piece, out_sem.at[u]) for u, piece in enumerate(pieces)]
    for u, out in enumerate(outs):
        units[u] = low[u].astype(f32)
        out.start()
        if u % 3 == 2:
            come, go = moves[u // 3]
            come.wait()
            go.start()
    me = lax.axis_index("dp")
    whole = jnp.concatenate([small[c] for c in range(width // 128)], axis=1)
    place_of = lax.broadcasted_iota(jnp.int32, (width, r), 0)
    lane = lax.broadcasted_iota(jnp.int32, (width, r), 1)
    mine = jnp.dot(whole, jnp.where(place_of == me * r + lane, 1.0, 0.0), precision=lax.Precision.HIGHEST)
    for i in range(8):
        vectors[i][...] = mine[i]
    per = width // (4 * r)
    place_of = lax.broadcasted_iota(jnp.int32, (width, 4 * r), 0)
    lane = lax.broadcasted_iota(jnp.int32, (width, 4 * r), 1)
    at = jnp.where(place_of == lax.rem(me, per) * (4 * r) + lane, 1.0, 0.0)
    wide_rows[...] = jnp.dot(whole, at, precision=lax.Precision.HIGHEST)
    vectors[8][...] = wide_rows[pl.ds(8 + me // per, 1), :].reshape(4 * r)
    table[...] = jnp.concatenate([small[6], small[7]], axis=0).T[:H, :]
    for out in outs:
        out.wait()
    for come, go in moves:
        go.wait()


def present(sums, small, y_c, y_q, g_c, g_q, shards):
    _, r, width = sums.shape
    f32, bf16 = jnp.float32, jnp.bfloat16
    anywhere = pl.BlockSpec(memory_space=pl.ANY)
    vmem = pl.BlockSpec(memory_space=pltpu.VMEM)
    own = y_c.shape
    shape = lambda *dims: jax.ShapeDtypeStruct(dims, f32)
    dma = pltpu.SemaphoreType.DMA
    return pl.pallas_call(
        functools.partial(present_kernel, shards, r),
        out_shape=(shape(*own),) * 4
        + (shape(r, width),) * 4
        + (shape(r, 4 * width), shape(4, r, width))
        + (shape(r),) * 8
        + (shape(4 * r), shape(H, NB)),
        in_specs=[anywhere, vmem] + [anywhere] * 4,
        out_specs=(anywhere,) * 10 + (vmem,) * 10,
        scratch_shapes=[
            pltpu.VMEM((16, 4 * r), f32),
            pltpu.VMEM((UNITS, r, width), bf16),
            pltpu.VMEM((UNITS, r, width), f32),
            pltpu.VMEM((4,) + own, f32),
            dma((5,)),
            dma((UNITS,)),
            dma((4,)),
        ],
        compiler_params=pltpu.CompilerParams(vmem_limit_bytes=67043328),
        name="present",
    )(sums, small.reshape(8, 16, 128), y_c, y_q, g_c, g_q)


def per_device(
    x_content, x_query, cot_content, cot_query,
    w_query, b_query, w_key, w_value, b_value, w_out, b_out, gain_attn, shift_attn,
    w_up, b_up, w_down, b_down, gain_ffn, shift_ffn, rel_table, lengths, positions, predicted,
    *, shards, seqn,
):
    f32 = jnp.float32
    seqs, block, width = x_content.shape
    r = w_query.shape[0]
    vecs = [
        v.reshape(1, r) for v in (b_query, b_value, b_out, gain_attn, shift_attn, b_down, gain_ffn, shift_ffn)
    ] + [b_up]
    (squares, xall, probs, attended, query, keys, values, y_c, y_q, dr1, d_attended, grads, downs, rest, dvec) = forward(
        w_key, w_value, w_query, w_out, w_up, w_down, x_content, x_query, cot_content, cot_query, vecs,
        lengths, positions, predicted, rel_table, shards, seqn,
    )
    sums, g_content, g_x_query, small = backward(
        lengths, grads, downs, rest, squares, xall, probs, attended, d_attended.reshape(attended.shape),
        query, keys, values, dr1, x_content, x_query, dvec, positions, shards, seqn,
    )
    (
        y_c, y_q, g_content, g_x_query, g_wk, g_wv, g_wq, g_wo, g_w1, g_w2,
        g_bq, g_bv, g_bo, g_g1, g_b1, g_c2, g_g2, g_b2, g_c1, g_table,
    ) = present(sums, small, y_c, y_q, g_content, g_x_query, shards)
    shape = (seqs, block, width)
    return (
        y_c.reshape(shape), y_q.reshape(shape), g_content.reshape(shape), g_x_query.reshape(shape),
        g_wq, g_bq, g_wk, g_wv, g_bv, g_wo, g_bo, g_g1, g_b1,
        g_w1, g_c1, g_w2.reshape(4 * r, width), g_c2, g_g2, g_b2, g_table.T,
    )


def solution(mesh):
    in_specs = (
        P("dp", "seq", None),
        P("dp", "seq", None),
        P("dp", "seq", None),
        P("dp", "seq", None),
        P("dp", None),
        P("dp"),
        P("dp", None),
        P("dp", None),
        P("dp"),
        P("dp", None),
        P("dp"),
        P("dp"),
        P("dp"),
        P("dp", None),
        P("dp"),
        P("dp", None),
        P("dp"),
        P("dp"),
        P("dp"),
        P(),
        P("dp"),
        P("dp", None),
        P("dp", "seq"),
    )
    out_specs = (
        P("dp", "seq", None),
        P("dp", "seq", None),
        P("dp", "seq", None),
        P("dp", "seq", None),
        P("dp", None),
        P("dp"),
        P("dp", None),
        P("dp", None),
        P("dp"),
        P("dp", None),
        P("dp"),
        P("dp"),
        P("dp"),
        P("dp", None),
        P("dp"),
        P("dp", None),
        P("dp"),
        P("dp"),
        P("dp"),
        P(),
    )
    return jax.shard_map(
        functools.partial(per_device, shards=mesh.shape["dp"], seqn=mesh.shape["seq"]),
        mesh=mesh, in_specs=in_specs, out_specs=out_specs, check_vma=False
    )
```
